32 devices in a mesh: band: 4 (over y, x), domain: 8 (over z, core).
Axes of the slice: x: 2, y: 2, z: 4, core: 2. Of those that a mesh axis runs over, the one named last changes fastest.
Arguments:
- orbitals: float32 [6144, 512], P('domain', 'band'), may hold values from -6 to 6
- potential: float32 [6144], P('domain'), may hold values from -1 to 1
- occupation: float32 [512], P('band'), may hold values from 0 to 0.0068359375, as said below
- cell_matrix: bfloat16 [343, 343], replicated, may hold values from -1 to 2, as said below
- cell_nodes: int32 [32, 343], P('domain'), may hold values from 0 to 936, as said below
- face_order: int32 [8, 169], P('domain'), may hold values from 0 to 168, as said below
- pois_matrix: float32 [729, 729], replicated, may hold values from -1 to 2, as said below
- pois_nodes: int32 [16, 729], P('domain'), may hold values from 0 to 848, as said below
- pois_face: int32 [8, 81], P('domain'), may hold values from 0 to 80, as said below
- screening: float32 [6144], P('domain'), may hold values from 0.5 to 2
- block_owner: int32 [8, 8], P('domain'), may hold values from 0 to 7, as said below
Outputs:
- filtered: float32 [6144, 512], P('domain', 'band')
- hartree: float32 [6144], P('domain')
The draws below stay inside these ranges and needn't reach their ends.
Inputs may be any that keep to these rules, and one draw needn't show every extreme that they name: `occupation`: positive weights. `cell_matrix`: symmetric. `pois_matrix`: symmetric. `cell_nodes`: cell c (counted from 0 within its domain) uses the local nodes (c * 234 + k) mod 937 for k < 343, in a drawn order. `pois_nodes`: cell c (counted from 0 within its domain) uses the local nodes (c * 424 + k) mod 849 for k < 729, in a drawn order. `face_order`: each row is a permutation. `pois_face`: each row is a permutation. `block_owner`: each row is a permutation.
All inputs are finite; a program needn't handle non-finite values.
Results may differ from the reference program's by a relative error of at most 0.0065.
The reference program's roundings to bfloat16 on the way count: a program that leaves them out, or rounds other values in their place, can miss the bound.
Values may be sent and summed in bfloat16 or wider, within the bound.
No kernel may reach another device: no remote copies, remote signals or barrier semaphores. Data moves between devices by JAX's collectives and lax.ppermute only.
A program may use at most 64 MiB of HBM per device.

```python
import math
import jax
import jax.numpy as jnp
from jax import lax

CELLS = 4
NPC = 343
SHARE = 169
PNPC = 729
PSHARE = 81
NOWN = 768
NLOC = 937
PNLOC = 849
PCELLS = 2
ORBITALS = 512
NODES = 6144
BLK = 96
N_DOMAIN = 8


def symmetric_matrix(key, order_size):
    raw = jax.random.normal(key, (order_size, order_size), jnp.float32)
    return jnp.eye(order_size, dtype=jnp.float32) + (raw + raw.T) * (0.25 / order_size ** 0.5)


def window_nodes(key, cell_count, per_cell, local_count):
    total_cells = N_DOMAIN * cell_count
    keys = jax.random.split(key, total_cells)
    orders = jax.vmap(lambda one_key: jax.random.permutation(one_key, per_cell))(keys)
    stride = local_count // cell_count
    starts = jnp.arange(total_cells, dtype=jnp.int32) % cell_count * stride
    return ((starts[:, None] + orders.astype(jnp.int32)) % local_count).astype(jnp.int32)


def permuted_rows(key, row_count, length):
    keys = jax.random.split(key, row_count)
    return jax.vmap(lambda one_key: jax.random.permutation(one_key, length))(keys).astype(jnp.int32)


def draw_occupation(key, part):
    index = jnp.arange(ORBITALS, dtype=jnp.float32)
    factor = jax.random.uniform(jax.random.fold_in(key, 3), (ORBITALS,), jnp.float32, 0.5, 1.5)
    return 2.0 / ORBITALS * (1.0 - 0.7 * index / ORBITALS) * factor


def draw_cell_matrix(key, part):
    return symmetric_matrix(jax.random.fold_in(key, 11), NPC).astype(jnp.bfloat16)


def draw_pois_matrix(key, part):
    return symmetric_matrix(jax.random.fold_in(key, 13), PNPC)


def draw_cell_nodes(key, part):
    return window_nodes(jax.random.fold_in(key, 21), CELLS, NPC, NLOC)


def draw_pois_nodes(key, part):
    return window_nodes(jax.random.fold_in(key, 23), PCELLS, PNPC, PNLOC)


def draw_face_order(key, part):
    return permuted_rows(jax.random.fold_in(key, 31), N_DOMAIN, SHARE)


def draw_pois_face(key, part):
    return permuted_rows(jax.random.fold_in(key, 33), N_DOMAIN, PSHARE)


def draw_block_owner(key, part):
    return permuted_rows(jax.random.fold_in(key, 41), N_DOMAIN, N_DOMAIN)


def level_of(rng, extent, pieces, low, top_value):
    loudness = 1.0
    for axis_at, parts in pieces:
        heights = jax.random.uniform(jax.random.fold_in(jax.random.fold_in(rng, 6), axis_at), (parts,), jnp.float32, low / len(pieces), top_value / len(pieces))
        loudness = loudness * jnp.repeat(jnp.exp(heights), extent[axis_at] // parts).reshape((-1,) + (1,) * (len(extent) - 1 - axis_at))
    return loudness


def gaussian(rng, extent, deviation, bound, pieces=(), kind=jnp.bfloat16):
    factor_of = level_of(rng, extent, pieces, -0.22, 0.18) if pieces else 1.0
    drawn = jax.random.normal(rng, extent, jnp.float32) * deviation * factor_of
    return jnp.minimum(jnp.maximum(drawn, -bound), bound).astype(kind)


def setup_inputs(seed: int = 0) -> dict:
    key_of = jax.random.split(jax.random.key(seed), 12)
    orbitals = gaussian(key_of[0], (NODES, ORBITALS), 1.0, 6.0, ((0, 8), (1, 4)), jnp.float32)
    potential = jnp.clip(jax.random.uniform(key_of[1], (NODES,), jnp.float32, -1.0, 1.0) * level_of(key_of[1], (NODES,), ((0, 8),), -0.4, 0.0), -1.0, 1.0)
    occupation = draw_occupation(jax.random.fold_in(key_of[11], 71), 0)
    cell_matrix = draw_cell_matrix(jax.random.fold_in(key_of[11], 71), 0)
    cell_nodes = draw_cell_nodes(jax.random.fold_in(key_of[11], 71), 0)
    face_order = draw_face_order(jax.random.fold_in(key_of[11], 71), 0)
    pois_matrix = draw_pois_matrix(jax.random.fold_in(key_of[11], 71), 0)
    pois_nodes = draw_pois_nodes(jax.random.fold_in(key_of[11], 71), 0)
    pois_face = draw_pois_face(jax.random.fold_in(key_of[11], 71), 0)
    screening = jnp.clip(jnp.exp(math.log(2.0) - 1.3862944 * jax.random.uniform(key_of[9], (NODES,), jnp.float32) ** level_of(key_of[9], (NODES,), ((0, 8),), -0.2, 0.2)), 0.5, 2.0)
    block_owner = draw_block_owner(jax.random.fold_in(key_of[11], 71), 0)
    return {"orbitals": orbitals, "potential": potential, "occupation": occupation, "cell_matrix": cell_matrix, "cell_nodes": cell_nodes, "face_order": face_order, "pois_matrix": pois_matrix, "pois_nodes": pois_nodes, "pois_face": pois_face, "screening": screening, "block_owner": block_owner}


filter_center = 1.8
filter_half = 2.7
solve_center = 3.25
solve_half = 2.75
solve_ratio = solve_center / solve_half
weight_zero = 1.0 / solve_ratio
weight_one = 1.0 / (2.0 * solve_ratio - weight_zero)
weight_two = 1.0 / (2.0 * solve_ratio - weight_one)


def filter_step(applied, current, earlier):
    if earlier is None:
        return (applied - filter_center * current) / filter_half
    return 2.0 * (applied - filter_center * current) / filter_half - earlier


def assemble(blocks, face_rows, node_ids, terms):
    shared = face_rows.shape[1]
    owned_count = blocks.shape[1]
    following = jnp.roll(blocks[:, :shared], -1, axis=0)
    upper_rows = jax.vmap(lambda values, order_row: jnp.take(values, order_row, axis=0))(following, face_rows)
    local_rows = jnp.concatenate([blocks, upper_rows], axis=1)
    partial_value = lax.map(lambda domain_pair: terms(domain_pair[0], domain_pair[1]), (local_rows, node_ids))
    ordered = jax.vmap(lambda values, order_row: jnp.zeros_like(values).at[order_row].set(values))(partial_value[:, owned_count:], face_rows)
    arrived = jnp.roll(ordered, 1, axis=0)
    return partial_value[:, :owned_count].at[:, :shared].add(arrived)


def reference(orbitals, potential, occupation, cell_matrix, cell_nodes, face_order, pois_matrix, pois_nodes, pois_face, screening, block_owner):
    cell_float = cell_matrix.astype(jnp.float32)
    orbital_ids = cell_nodes.reshape(N_DOMAIN, CELLS, NPC)
    field_ids = pois_nodes.reshape(N_DOMAIN, PCELLS, PNPC)

    def orbital_terms(local_rows, node_ids):
        cell_vals = jnp.take(local_rows.astype(jnp.bfloat16), node_ids, axis=0).astype(jnp.float32)
        product = jnp.einsum("pq,cqm->cpm", cell_float, cell_vals, precision=lax.Precision.HIGHEST)
        columns = local_rows.shape[1]
        return jnp.zeros(local_rows.shape, jnp.float32).at[node_ids.reshape(-1)].add(product.reshape(-1, columns))

    def field_terms(local_rows, node_ids):
        cell_vals = jnp.take(local_rows, node_ids, axis=0)
        product = jnp.einsum("pq,cq->cp", pois_matrix, cell_vals, precision=lax.Precision.HIGHEST)
        return jnp.zeros(local_rows.shape, jnp.float32).at[node_ids.reshape(-1)].add(product.reshape(-1))

    def hamiltonian(vector, potential_in):
        return assemble(vector, face_order, orbital_ids, orbital_terms) + potential_in[:, :, None] * vector

    screen_blocks = screening.reshape(N_DOMAIN, NOWN)

    def field_operator(vector):
        return assemble(vector, pois_face, field_ids, field_terms) + screen_blocks * vector

    potential_now = potential.reshape(N_DOMAIN, NOWN)
    filter_zero = orbitals.reshape(N_DOMAIN, NOWN, ORBITALS)
    filter_one = filter_step(hamiltonian(filter_zero, potential_now), filter_zero, None)
    filter_two = filter_step(hamiltonian(filter_one, potential_now), filter_one, filter_zero)
    filter_three = filter_step(hamiltonian(filter_two, potential_now), filter_two, filter_one)
    density = jnp.einsum("dnm,m->dn", filter_three * filter_three, occupation, precision=lax.Precision.HIGHEST)
    domain_ids = jnp.arange(N_DOMAIN, dtype=jnp.int32)[:, None]
    blocks = density.reshape(N_DOMAIN, N_DOMAIN, BLK)
    source = jnp.zeros_like(blocks).at[block_owner, domain_ids].set(blocks).reshape(N_DOMAIN, NOWN)
    step_one = source / solve_center
    residual = source - field_operator(step_one)
    step_two = (weight_one * weight_zero) * step_one + (2.0 * weight_one / solve_half) * residual
    residual = residual - field_operator(step_two)
    step_three = (weight_two * weight_one) * step_two + (2.0 * weight_two / solve_half) * residual
    solution = step_one + step_two + step_three
    hartree = solution.reshape(N_DOMAIN, N_DOMAIN, BLK)[block_owner, domain_ids].reshape(N_DOMAIN, NOWN)
    potential_new = potential_now + hartree
    refilter_one = filter_step(hamiltonian(filter_three, potential_new), filter_three, None)
    refilter_two = filter_step(hamiltonian(refilter_one, potential_new), refilter_one, filter_three)
    return refilter_two.reshape(NODES, ORBITALS), hartree.reshape(NODES)
```

```python
import functools

import jax
import jax.numpy as jnp
from jax import lax
from jax.experimental import pallas as pl
from jax.experimental.pallas import tpu as pltpu
from jax.sharding import PartitionSpec as P

filter_center = 1.8
filter_half = 2.7
solve_center = 3.25
solve_half = 2.75
solve_ratio = solve_center / solve_half
weight_zero = 1.0 / solve_ratio
weight_one = 1.0 / (2.0 * solve_ratio - weight_zero)
weight_two = 1.0 / (2.0 * solve_ratio - weight_one)

BF = jnp.bfloat16
F32 = jnp.float32
I32 = jnp.int32
LANES = 128
SUBLANES = 8


def up_to(n, m):
    return -(-n // m) * m


def from_behind(array, axis, by):
    length = lax.axis_size(axis)
    return lax.ppermute(array, axis, [(i, (i + by) % length) for i in range(length)])


class Window:
    def __init__(self, start, npc, own, nloc):
        end = start + npc
        self.lo = start // 16 * 16
        self.hi = min(up_to(min(end, own), 16), own)
        self.touches = end > own
        self.low = up_to(max(0, end - nloc), 16)
        self.rows = self.hi - self.lo + self.low


class Geometry:
    def __init__(self, own, share, cells, npc):
        self.own, self.share, self.cells, self.npc = own, share, cells, npc
        nloc = own + share
        stride = nloc // cells
        self.sp = up_to(share, 16)
        self.npl = up_to(npc, LANES)
        self.windows = [Window(c * stride, npc, own, nloc) for c in range(cells)]
        self.touching = [c for c in range(cells) if self.windows[c].touches]
        self.dn_lo = min(self.windows[c].lo for c in self.touching)
        self.low = max(w.low for w in self.windows)
        self.dn_rows = own - self.dn_lo + self.low


def dot(a, b):
    return lax.dot_general(a, b, (((1,), (0,)), ((), ())), preferred_element_type=F32)


def dot_t(a, b):
    return lax.dot_general(a, b, (((1,), (1,)), ((), ())), preferred_element_type=F32)


def vmem_call(kernel, out_shape, scratch=(), in_specs=None, cost=None):
    kwargs = {}
    if in_specs is not None:
        kwargs["in_specs"] = in_specs
    return pl.pallas_call(
        kernel,
        out_shape=out_shape,
        scratch_shapes=list(scratch),
        cost_estimate=cost,
        compiler_params=pltpu.CompilerParams(vmem_limit_bytes=56 * 1024 * 1024),
        **kwargs,
    )


def sds(shape, dtype):
    return jax.ShapeDtypeStruct(shape, dtype)


def one_hot_rows(count, first, nodes):
    ids = lax.broadcasted_iota(I32, (count, nodes.shape[1]), 0) + first
    return jnp.where(ids == nodes, 1.0, 0.0).astype(BF)


def place_tables(geo, nodes_ref, face_ref, matrix_ref, nodes_pad, face_pad, matrix_pad):
    nodes_pad[...] = jnp.full(nodes_pad.shape, -1, I32)
    nodes_pad[0 : geo.cells, 0 : geo.npc] = nodes_ref[...]
    face_pad[...] = jnp.full(face_pad.shape, -1, I32)
    face_pad[0:1, 0 : geo.share] = face_ref[...]
    matrix_pad[...] = jnp.zeros(matrix_pad.shape, F32)
    matrix_pad[0 : geo.npc, 0 : geo.npc] = matrix_ref[...].astype(F32)


def table_scratch(geo):
    return [
        pltpu.VMEM((up_to(geo.cells, SUBLANES), geo.npl), I32),
        pltpu.VMEM((SUBLANES, up_to(geo.share, LANES)), I32),
        pltpu.VMEM((geo.npl, geo.npl), F32),
    ]


def owned_picks(geo, c, nodes):
    w = geo.windows[c]
    picks = one_hot_rows(w.hi - w.lo, w.lo, nodes)
    if w.low:
        picks = jnp.concatenate([picks, one_hot_rows(w.low, 0, nodes)], axis=0)
    return picks


def upper_picks(geo, nodes, face):
    by_local = one_hot_rows(face.shape[1], geo.own, nodes)
    by_owner = one_hot_rows(geo.sp, 0, face)
    return dot(by_owner, by_local).astype(BF)


def own_matrices_kernel(geo, *refs):
    nodes_ref, face_ref, matrix_ref, pot_ref = refs[:4]
    outs = refs[4:-3]
    nodes_pad, face_pad, matrix_pad = refs[-3:]
    place_tables(geo, nodes_ref, face_ref, matrix_ref, nodes_pad, face_pad, matrix_pad)
    matrix = matrix_pad[...].astype(BF)
    face = face_pad[0:1, :]
    for c in range(geo.cells):
        nodes = nodes_pad[c : c + 1, :]
        own = owned_picks(geo, c, nodes)
        left = dot(own, matrix).astype(BF)
        outs[c][...] = dot_t(left, own).astype(BF)
        if c in geo.touching:
            at = geo.cells + geo.touching.index(c)
            outs[at][...] = dot_t(left, upper_picks(geo, nodes, face)).astype(BF)
    column = outs[-1]
    for r in range(geo.own // LANES):
        row = jnp.broadcast_to(pot_ref[r : r + 1, :], (LANES, LANES))
        column[r * LANES : (r + 1) * LANES, :] = row.T


def own_matrices(geo, cell_nodes, face_order, cell_matrix, potential):
    shapes = [sds((w.rows, w.rows), BF) for w in geo.windows]
    shapes += [sds((geo.windows[c].rows, geo.sp), BF) for c in geo.touching]
    shapes += [sds((geo.own, LANES), F32)]
    outs = vmem_call(
        functools.partial(own_matrices_kernel, geo), shapes, table_scratch(geo), cost=cost_of(3.0)
    )(cell_nodes, face_order, cell_matrix, potential.reshape(geo.own // LANES, LANES))
    n = geo.cells
    return outs[:n], outs[n:-1], outs[-1]


def behind_matrices_kernel(geo, *refs):
    nodes_ref, face_ref, matrix_ref = refs[:3]
    outs = refs[3:-3]
    nodes_pad, face_pad, matrix_pad = refs[-3:]
    place_tables(geo, nodes_ref, face_ref, matrix_ref, nodes_pad, face_pad, matrix_pad)
    matrix = matrix_pad[...].astype(BF)
    face = face_pad[0:1, :]
    count = len(geo.touching)
    for at, c in enumerate(geo.touching):
        nodes = nodes_pad[c : c + 1, :]
        upper = upper_picks(geo, nodes, face)
        left = dot(upper, matrix).astype(BF)
        outs[at][...] = dot_t(left, owned_picks(geo, c, nodes)).astype(BF)
        outs[count + at][...] = dot_t(left, upper).astype(BF)


def behind_matrices(geo, nodes, face, cell_matrix):
    shapes = [sds((geo.sp, geo.windows[c].rows), BF) for c in geo.touching]
    shapes += [sds((geo.sp, geo.sp), BF) for _ in geo.touching]
    outs = vmem_call(
        functools.partial(behind_matrices_kernel, geo), shapes, table_scratch(geo), cost=cost_of(1.5)
    )(nodes, face, cell_matrix)
    n = len(geo.touching)
    return outs[:n], outs[n:]


def cost_of(us):
    return pl.CostEstimate(flops=0, bytes_accessed=int(us * 3.0e6), transcendentals=0)


def write_sends(geo, y_ref, dn_ref, up_ref):
    top = geo.own - geo.dn_lo
    dn_ref[0:top, :] = y_ref[geo.dn_lo : geo.own, :].astype(BF)
    dn_ref[top : top + geo.low, :] = y_ref[0 : geo.low, :].astype(BF)
    up_ref[...] = y_ref[0 : geo.sp, :].astype(BF)


def send_shapes(geo, columns):
    return [sds((geo.dn_rows, columns), BF), sds((geo.sp, columns), BF)]


def pack_kernel(geo, y_ref, dn_ref, up_ref):
    write_sends(geo, y_ref, dn_ref, up_ref)


def pack(geo, y):
    return vmem_call(
        functools.partial(pack_kernel, geo), send_shapes(geo, y.shape[1]), cost=cost_of(0.5)
    )(y)


def owned_part_kernel(geo, scale, has_prev, has_field, has_upper, *refs):
    refs = list(refs)
    base_ref = refs.pop()
    y_ref = refs.pop(0)
    prev_ref = refs.pop(0) if has_prev else None
    pot_ref = refs.pop(0)
    field_ref = refs.pop(0) if has_field else None
    mats = [refs.pop(0) for _ in range(geo.cells)]
    y = y_ref[...]
    factor = pot_ref[...]
    if has_field:
        factor = factor + field_ref[...]
    value = ((factor - filter_center) * scale) * y
    if has_prev:
        value = value - prev_ref[...]
    base_ref[...] = value
    x = y.astype(BF)
    for c in range(geo.cells):
        w = geo.windows[c]
        own = w.hi - w.lo
        rows = x[w.lo : w.hi, :]
        if w.low:
            rows = jnp.concatenate([rows, x[0 : w.low, :]], axis=0)
        product = dot(mats[c][...], rows) * scale
        base_ref[w.lo : w.hi, :] += product[:own]
        if w.low:
            base_ref[0 : w.low, :] += product[own:]
    if has_upper:
        for upper in refs:
            base_ref[0 : geo.sp, :] += dot(upper[...], x[0 : geo.sp, :]) * scale


def owned_part(geo, scale, y, prev, pot, field, mats, uppers):
    args = [y] + ([prev] if prev is not None else []) + [pot]
    args += [field] if field is not None else []
    args += list(mats) + list(uppers)
    return vmem_call(
        functools.partial(
            owned_part_kernel, geo, scale, prev is not None, field is not None, bool(uppers)
        ),
        sds(y.shape, F32),
        cost=cost_of(2.0),
    )(*args)


def add_halo(geo, scale, y_ref, up_ref, dn_ref, crosses, behinds, uppers, own_up_ref):
    h_up = up_ref[...]
    h_dn = dn_ref[...]
    for at, c in enumerate(geo.touching):
        w = geo.windows[c]
        own = w.hi - w.lo
        product = dot(crosses[at][...], h_up) * scale
        y_ref[w.lo : w.hi, :] += product[:own]
        if w.low:
            y_ref[0 : w.low, :] += product[own:]
    total = None
    for at, c in enumerate(geo.touching):
        w = geo.windows[c]
        first = w.lo - geo.dn_lo
        term = dot(behinds[at][...], h_dn[first : first + w.rows, :])
        total = term if total is None else total + term
        if uppers:
            total = total + dot(uppers[at][...], own_up_ref[...])
    y_ref[0 : geo.sp, :] += total * scale


def write_density(y_ref, occ_ref, dens_ref, row_pad):
    parts, blocks, _ = dens_ref.shape
    own = y_ref.shape[0]
    length = own // blocks
    y = y_ref[...]
    terms = y * y * occ_ref[...]
    high = terms.astype(BF)
    low = (terms - high.astype(F32)).astype(BF)
    ones = jnp.ones((SUBLANES, terms.shape[1]), BF)
    summed = dot_t(ones, high) + dot_t(ones, low)
    row_pad[...] = jnp.zeros(row_pad.shape, F32)
    for j in range(blocks):
        row_pad[j : j + 1, 0:length] = summed[0:1, j * length : (j + 1) * length]
    dens_ref[...] = jnp.broadcast_to(row_pad[...][None], dens_ref.shape)


def finish_kernel(geo, scale, has_upper, mode, *refs):
    refs = list(refs)
    n = len(geo.touching)
    base_ref, up_ref, dn_ref = refs[:3]
    refs = refs[3:]
    crosses, refs = refs[:n], refs[n:]
    behinds, refs = refs[:n], refs[n:]
    uppers, own_up = [], None
    if has_upper:
        uppers, refs = refs[:n], refs[n:]
        own_up = refs.pop(0)
    occ_ref = refs.pop(0) if mode == "density" else None
    y_ref = refs.pop(0)
    y_ref[...] = base_ref[...]
    add_halo(geo, scale, y_ref, up_ref, dn_ref, crosses, behinds, uppers, own_up)
    if mode != "last":
        write_sends(geo, y_ref, refs[0], refs[1])
    if mode == "density":
        write_density(y_ref, occ_ref, refs[2], refs[3])


def finish(geo, scale, base, halo, crosses, behinds, uppers=(), own_up=None, occ=None, parts=None, last=False):
    columns = base.shape[1]
    args = [base, halo[0], halo[1], *crosses, *behinds, *uppers]
    if uppers:
        args.append(own_up)
    shapes = [sds(base.shape, F32)]
    scratch = []
    mode = "plain"
    if last:
        mode = "last"
    else:
        shapes += send_shapes(geo, columns)
    if occ is not None:
        mode = "density"
        args.append(occ)
        shapes.append(sds(parts, F32))
        scratch.append(pltpu.VMEM(parts[1:], F32))
    return vmem_call(
        functools.partial(finish_kernel, geo, scale, bool(uppers), mode),
        shapes,
        scratch,
        cost=cost_of(1.0),
    )(*args)


class FieldGeometry:
    def __init__(self, domains, own, share, cells, npc):
        self.domains, self.own, self.share, self.cells, self.npc = domains, own, share, cells, npc
        self.block = own // domains
        self.rows = up_to(npc, LANES) // LANES
        self.blocks = domains + 1
        self.at_inverse = cells * self.rows
        self.at_face = self.at_inverse + cells * self.blocks
        self.at_face_inverse = self.at_face + 1
        self.at_owner = self.at_face + 2
        self.at_screen = self.at_face + 3
        self.table_rows = up_to(self.at_screen + domains, SUBLANES)
        self.fits = (
            domains == SUBLANES
            and own % domains == 0
            and share <= self.block <= LANES
        )


def column_of(row):
    return jnp.broadcast_to(row, (LANES, LANES)).T


def field_tables_kernel(fg, nodes_ref, face_ref, owner_ref, screen_ref, matrix_ref, table_ref, high_ref, low_ref, pad, one, wide):
    lane = lax.broadcasted_iota(I32, (1, LANES), 1)
    one[...] = jnp.full(one.shape, -1.0, F32)
    pad[...] = jnp.full(pad.shape, -1, I32)
    pad[0 : fg.cells, 0 : fg.npc] = nodes_ref[...]
    sub = lax.broadcasted_iota(I32, (LANES, LANES), 0)
    wide_lane = lax.broadcasted_iota(I32, (LANES, LANES), 1)
    for c in range(fg.cells):
        columns = []
        for r in range(fg.rows):
            nodes = pad[c : c + 1, r * LANES : (r + 1) * LANES]
            block = jnp.zeros((1, LANES), I32)
            for b in range(1, fg.blocks):
                block = block + jnp.where(nodes >= b * fg.block, 1, 0)
            code = jnp.where(nodes < 0, -1, nodes + block * (LANES - fg.block))
            code = code.astype(F32)
            at = c * fg.rows + r
            one[at : at + 1, :] = code
            columns.append(column_of(code))
        for b in range(fg.blocks):
            target = (wide_lane + b * LANES).astype(F32)
            found = jnp.zeros((LANES, LANES), F32)
            for r in range(fg.rows):
                position = (sub + (r * LANES + 1)).astype(F32)
                found = found + jnp.where(columns[r] == target, position, 0.0)
            at = fg.at_inverse + c * fg.blocks + b
            one[at : at + 1, :] = jnp.sum(found, axis=0, keepdims=True) - 1.0
    one[fg.at_face : fg.at_face + 1, 0 : fg.share] = face_ref[...].astype(F32)
    column = column_of(one[fg.at_face : fg.at_face + 1, :])
    hits = jnp.where(column == wide_lane.astype(F32), (sub + 1).astype(F32), 0.0)
    one[fg.at_face_inverse : fg.at_face_inverse + 1, :] = jnp.sum(hits, axis=0, keepdims=True) - 1.0
    one[fg.at_owner : fg.at_owner + 1, 0 : fg.domains] = owner_ref[...].astype(F32)
    one[fg.at_screen : fg.at_screen + fg.domains, 0 : fg.block] = screen_ref[...]
    table_ref[...] = jnp.broadcast_to(one[...][None], table_ref.shape)
    wide[...] = jnp.zeros(wide.shape, F32)
    wide[0 : fg.npc, 0 : fg.npc] = matrix_ref[...]
    full = wide[...]
    high = full.astype(BF)
    high_ref[...] = high
    low_ref[...] = (full - high.astype(F32)).astype(BF)


def field_tables(fg, pois_nodes, pois_face, block_owner, screening, pois_matrix):
    size = fg.rows * LANES
    return vmem_call(
        functools.partial(field_tables_kernel, fg),
        [
            sds((fg.domains, fg.table_rows, LANES), F32),
            sds((size, size), BF),
            sds((size, size), BF),
        ],
        [
            pltpu.VMEM((up_to(fg.cells, SUBLANES), size), I32),
            pltpu.VMEM((fg.table_rows, LANES), F32),
            pltpu.VMEM((size, size), F32),
        ],
        cost=cost_of(3.0),
    )(pois_nodes, pois_face, block_owner, screening.reshape(fg.domains, fg.block), pois_matrix)


def lanes_of(values, index):
    return jnp.take_along_axis(values, index, axis=1, mode="promise_in_bounds")


def field_solve(fg, dens_ref, table_ref, high_ref, low_ref, codes, rows):
    domains, cells = fg.domains, fg.cells
    bands = dens_ref.shape[0] // domains
    valid = lax.broadcasted_iota(I32, (domains, LANES), 1) < fg.block

    def table(at):
        return table_ref[:, at, :]

    for at in range(fg.at_owner):
        codes[at] = table(at).astype(I32)
    owner = table(fg.at_owner)
    part = lax.broadcasted_iota(I32, (domains, LANES), 0).astype(F32)
    source = []
    for q in range(domains):
        density = dens_ref[q]
        for b in range(1, bands):
            density = density + dens_ref[b * domains + q]
        placed = jnp.zeros((domains, LANES), F32)
        for j in range(domains):
            who = jnp.broadcast_to(owner[q : q + 1, j : j + 1], (domains, LANES))
            placed = placed + jnp.where(who == part, jnp.broadcast_to(density[j : j + 1, :], (domains, LANES)), 0.0)
        source.append(placed)
    screen = [table(fg.at_screen + q) for q in range(domains)]

    def lookup(sources, code):
        lane = jnp.bitwise_and(code, LANES - 1)
        which = jnp.right_shift(code, 7)
        total = jnp.zeros((domains, LANES), F32)
        for b, values in enumerate(sources):
            total = jnp.where(which == b, lanes_of(values, lane), total)
        return total

    def operator(field):
        ahead = pltpu.roll(field[0], domains - 1, 0)
        face = codes[fg.at_face]
        upper = lookup([ahead], face)
        local = list(field) + [upper]
        for c in range(cells):
            for r in range(fg.rows):
                rows[c * domains : (c + 1) * domains, r * LANES : (r + 1) * LANES] = lookup(local, codes[c * fg.rows + r])
        picked = rows[...]
        high = picked.astype(BF)
        low = (picked - high.astype(F32)).astype(BF)
        product = dot(high, high_ref[...]) + (dot(low, high_ref[...]) + dot(high, low_ref[...]))
        out = []
        for b in range(fg.blocks):
            total = None
            for c in range(cells):
                sources = [
                    product[c * domains : (c + 1) * domains, r * LANES : (r + 1) * LANES]
                    for r in range(fg.rows)
                ]
                term = lookup(sources, codes[fg.at_inverse + c * fg.blocks + b])
                total = term if total is None else total + term
            out.append(total)
        arriving = pltpu.roll(out[domains], 1, 0)
        home = pltpu.roll(codes[fg.at_face_inverse], 1, 0)
        out[0] = out[0] + lookup([arriving], home)
        return [jnp.where(valid, screen[q] * field[q] + out[q], 0.0) for q in range(domains)]

    step_one = [s * (1.0 / solve_center) for s in source]
    applied = operator(step_one)
    residual = [s - a for s, a in zip(source, applied)]
    a1, b1 = weight_one * weight_zero, 2.0 * weight_one / solve_half
    step_two = [a1 * e + b1 * r for e, r in zip(step_one, residual)]
    applied = operator(step_two)
    residual = [r - a for r, a in zip(residual, applied)]
    a2, b2 = weight_two * weight_one, 2.0 * weight_two / solve_half
    step_three = [a2 * e + b2 * r for e, r in zip(step_two, residual)]
    return [(x + y) + z for x, y, z in zip(step_one, step_two, step_three)]


def field_kernel(geo, fg, scale, *refs):
    refs = list(refs)
    n = len(geo.touching)
    dens_ref, table_ref, high_ref, low_ref, owner_ref = refs[:5]
    base_ref, up_ref, dn_ref, y_ref = refs[5:9]
    refs = refs[9:]
    crosses, refs = refs[:n], refs[n:]
    behinds, refs = refs[:n], refs[n:]
    z_ref, dn_out, up_out, column_ref, hartree_ref = refs[:5]
    codes, rows, phi = refs[5:]
    blocks = field_solve(fg, dens_ref, table_ref, high_ref, low_ref, codes, rows)
    for q in range(fg.domains):
        phi[q] = blocks[q]
    here = lax.axis_index("domain")
    for j in range(fg.domains):
        hartree_ref[j : j + 1, :] = phi[here, pl.ds(owner_ref[0, j], 1), :]
    for j in range(fg.domains):
        column = column_of(hartree_ref[j : j + 1, :])
        column_ref[j * fg.block : (j + 1) * fg.block, :] = column[0 : fg.block, :]
    z_ref[...] = base_ref[...] + (column_ref[...] * scale) * y_ref[...]
    add_halo(geo, scale, z_ref, up_ref, dn_ref, crosses, behinds, [], None)
    write_sends(geo, z_ref, dn_out, up_out)


def field_step(geo, fg, scale, dens, table, high, low, block_owner, base, halo, y, crosses, behinds):
    columns = y.shape[1]
    vmem = pl.BlockSpec(memory_space=pltpu.VMEM)
    args = [dens, table, high, low, block_owner, base, halo[0], halo[1], y, *crosses, *behinds]
    specs = [vmem] * len(args)
    specs[4] = pl.BlockSpec(memory_space=pltpu.SMEM)
    return vmem_call(
        functools.partial(field_kernel, geo, fg, scale),
        [sds(y.shape, F32), *send_shapes(geo, columns), sds((geo.own, LANES), F32), sds((fg.domains, LANES), F32)],
        [
            pltpu.VMEM((fg.at_owner, fg.domains, LANES), I32),
            pltpu.VMEM((fg.cells * fg.domains, fg.rows * LANES), F32),
            pltpu.VMEM((fg.domains, fg.domains, LANES), F32),
        ],
        in_specs=specs,
        cost=cost_of(5.0),
    )(*args)


def assembled(owned_rows, face_row, terms):
    owned_count = owned_rows.shape[0]
    shared = face_row.shape[0]
    coming = jnp.take(from_behind(owned_rows[:shared], "domain", -1), face_row, axis=0)
    partial_value = terms(jnp.concatenate([owned_rows, coming], axis=0))
    upper_rows = partial_value[owned_count:]
    ordered = jnp.zeros_like(upper_rows).at[face_row].set(upper_rows)
    arrived = from_behind(ordered, "domain", 1)
    return partial_value[:owned_count].at[:shared].add(arrived)


def field_terms(local_rows, pois_matrix, node_ids):
    cell_vals = jnp.take(local_rows, node_ids, axis=0)
    product = jnp.einsum(
        "pq,cq->cp",
        pois_matrix,
        cell_vals,
        precision=lax.Precision.HIGHEST,
        preferred_element_type=F32,
    )
    return jnp.zeros(local_rows.shape, F32).at[node_ids.reshape(-1)].add(product.reshape(-1))


def reshuffle(blocks):
    return lax.all_to_all(blocks, "domain", split_axis=0, concat_axis=0, tiled=True)


def distributed_field(y, occupation, owner_row, pois_matrix, pois_nodes, field_face, screening):
    owned_count = y.shape[0]
    domains = lax.axis_size("domain")
    block_len = owned_count // domains
    partial_value = jnp.dot(
        y * y, occupation, precision=lax.Precision.HIGHEST, preferred_element_type=F32
    )
    summed = lax.psum(partial_value, "band")
    arranged = (
        jnp.zeros((domains, block_len), F32)
        .at[owner_row]
        .set(summed.reshape(domains, block_len))
    )
    source = reshuffle(arranged).reshape(owned_count)

    def field_operator(vector):
        return (
            assembled(
                vector, field_face, lambda local: field_terms(local, pois_matrix, pois_nodes)
            )
            + screening * vector
        )

    step_one = source / solve_center
    residual = source - field_operator(step_one)
    step_two = weight_one * weight_zero * step_one + 2.0 * weight_one / solve_half * residual
    residual = residual - field_operator(step_two)
    step_three = weight_two * weight_one * step_two + 2.0 * weight_two / solve_half * residual
    solved = step_one + step_two + step_three
    returned = reshuffle(solved.reshape(domains, block_len))
    return jnp.take(returned, owner_row, axis=0).reshape(owned_count)


def exchange(sends):
    dn, up = sends
    h_dn = from_behind(dn, "domain", 1)
    h_up = from_behind(up, "domain", -1)
    return h_up, h_dn


def per_device(
    orbitals,
    potential,
    occupation,
    cell_matrix,
    cell_nodes,
    face_order,
    pois_matrix,
    pois_nodes,
    pois_face,
    screening,
    block_owner,
):
    domains = lax.axis_size("domain")
    bands = lax.axis_size("band")
    own, columns = orbitals.shape
    geo = Geometry(own, face_order.shape[1], cell_nodes.shape[0], cell_nodes.shape[1])
    fg = FieldGeometry(domains, own, pois_face.shape[1], pois_nodes.shape[0], pois_nodes.shape[1])
    first, later = 1.0 / filter_half, 2.0 / filter_half

    sends = pack(geo, orbitals)
    halo = exchange(sends)
    behind_nodes = from_behind(cell_nodes, "domain", 1)
    behind_face = from_behind(face_order, "domain", 1)
    mats, crosses, pot = own_matrices(geo, cell_nodes, face_order, cell_matrix, potential)
    if fg.fits:
        table, high, low = field_tables(fg, pois_nodes, pois_face, block_owner, screening, pois_matrix)
        tables = lax.all_to_all(table, "domain", 0, 0, tiled=True)

    base = owned_part(geo, first, orbitals, None, pot, None, mats, ())
    behinds, uppers = behind_matrices(geo, behind_nodes, behind_face, cell_matrix)
    y1, *sends1 = finish(geo, first, base, halo, crosses, behinds, uppers, sends[1])

    halo = exchange(sends1)
    base = owned_part(geo, later, y1, orbitals, pot, None, mats, uppers)
    y2, *sends2 = finish(geo, later, base, halo, crosses, behinds)

    halo = exchange(sends2)
    base = owned_part(geo, later, y2, y1, pot, None, mats, uppers)
    if fg.fits:
        parts = (domains * bands, domains, LANES)
        y3, dn, up, spread = finish(
            geo, later, base, halo, crosses, behinds, occ=occupation.reshape(1, columns), parts=parts
        )
        dens = lax.all_to_all(spread, ("band", "domain"), 0, 0, tiled=True)
        halo = exchange((dn, up))
        base = owned_part(geo, first, y3, None, pot, None, mats, uppers)
        z1, dn, up, column, packed = field_step(
            geo, fg, first, dens, tables, high, low, block_owner, base, halo, y3, crosses, behinds
        )
        hartree = packed[:, : fg.block].reshape(own)
        sends4 = (dn, up)
    else:
        y3, *sends3 = finish(geo, later, base, halo, crosses, behinds)
        halo = exchange(sends3)
        hartree = distributed_field(
            y3, occupation, block_owner[0], pois_matrix, pois_nodes, pois_face[0], screening
        )
        column = jnp.broadcast_to(hartree[:, None], (own, LANES))
        base = owned_part(geo, first, y3, None, pot, column, mats, uppers)
        z1, *sends4 = finish(geo, first, base, halo, crosses, behinds)

    halo = exchange(sends4)
    base = owned_part(geo, later, z1, y3, pot, column, mats, uppers)
    (filtered,) = finish(geo, later, base, halo, crosses, behinds, last=True)
    return filtered, hartree


def solution(mesh):
    return jax.shard_map(
        per_device,
        mesh=mesh,
        in_specs=(
            P("domain", "band"),
            P("domain"),
            P("band"),
            P(),
            P("domain", None),
            P("domain", None),
            P(),
            P("domain", None),
            P("domain", None),
            P("domain"),
            P("domain", None),
        ),
        out_specs=(P("domain", "band"), P("domain")),
        check_vma=False,
    )
```

```python
import functools

import jax
import jax.numpy as jnp
from jax import lax
from jax.experimental import pallas as pl
from jax.experimental.pallas import tpu as pltpu
from jax.sharding import PartitionSpec as P

filter_center = 1.8
filter_half = 2.7
solve_center = 3.25
solve_half = 2.75
solve_ratio = solve_center / solve_half
weight_zero = 1.0 / solve_ratio
weight_one = 1.0 / (2.0 * solve_ratio - weight_zero)
weight_two = 1.0 / (2.0 * solve_ratio - weight_one)

BF = jnp.bfloat16
F32 = jnp.float32
I32 = jnp.int32
LANES = 128
SUBLANES = 8


def up_to(n, m):
    return -(-n // m) * m


def from_behind(array, axis, by):
    length = lax.axis_size(axis)
    return lax.ppermute(array, axis, [(i, (i + by) % length) for i in range(length)])


class Window:
    def __init__(self, start, npc, own, nloc):
        end = start + npc
        self.lo = start // 16 * 16
        self.hi = min(up_to(min(end, own), 16), own)
        self.touches = end > own
        self.low = up_to(max(0, end - nloc), 16)
        self.rows = self.hi - self.lo + self.low


class Geometry:
    def __init__(self, own, share, cells, npc):
        self.own, self.share, self.cells, self.npc = own, share, cells, npc
        nloc = own + share
        stride = nloc // cells
        self.sp = up_to(share, 16)
        self.npl = up_to(npc, LANES)
        self.windows = [Window(c * stride, npc, own, nloc) for c in range(cells)]
        self.touching = [c for c in range(cells) if self.windows[c].touches]
        self.dn_lo = min(self.windows[c].lo for c in self.touching)
        self.low = max(w.low for w in self.windows)
        self.dn_rows = own - self.dn_lo + self.low


def dot(a, b):
    return lax.dot_general(a, b, (((1,), (0,)), ((), ())), preferred_element_type=F32)


def dot_t(a, b):
    return lax.dot_general(a, b, (((1,), (1,)), ((), ())), preferred_element_type=F32)


def vmem_call(kernel, out_shape, scratch=(), in_specs=None, cost=None):
    kwargs = {}
    if in_specs is not None:
        kwargs["in_specs"] = in_specs
    return pl.pallas_call(
        kernel,
        out_shape=out_shape,
        scratch_shapes=list(scratch),
        cost_estimate=cost,
        compiler_params=pltpu.CompilerParams(vmem_limit_bytes=16 * 1024 * 1024),
        **kwargs,
    )


def sds(shape, dtype):
    return jax.ShapeDtypeStruct(shape, dtype)


def one_hot_rows(count, first, nodes):
    ids = lax.broadcasted_iota(I32, (count, nodes.shape[1]), 0) + first
    return jnp.where(ids == nodes, 1.0, 0.0).astype(BF)


def place_tables(geo, nodes_ref, face_ref, matrix_ref, nodes_pad, face_pad, matrix_pad):
    nodes_pad[...] = jnp.full(nodes_pad.shape, -1, I32)
    nodes_pad[0 : geo.cells, 0 : geo.npc] = nodes_ref[...]
    face_pad[...] = jnp.full(face_pad.shape, -1, I32)
    face_pad[0:1, 0 : geo.share] = face_ref[...]
    matrix_pad[...] = jnp.zeros(matrix_pad.shape, F32)
    matrix_pad[0 : geo.npc, 0 : geo.npc] = matrix_ref[...].astype(F32)


def table_scratch(geo):
    return [
        pltpu.VMEM((up_to(geo.cells, SUBLANES), geo.npl), I32),
        pltpu.VMEM((SUBLANES, up_to(geo.share, LANES)), I32),
        pltpu.VMEM((geo.npl, geo.npl), F32),
    ]


def owned_picks(geo, c, nodes):
    w = geo.windows[c]
    picks = one_hot_rows(w.hi - w.lo, w.lo, nodes)
    if w.low:
        picks = jnp.concatenate([picks, one_hot_rows(w.low, 0, nodes)], axis=0)
    return picks


def upper_picks(geo, nodes, face):
    by_local = one_hot_rows(face.shape[1], geo.own, nodes)
    by_owner = one_hot_rows(geo.sp, 0, face)
    return dot(by_owner, by_local).astype(BF)


def own_matrices_kernel(geo, *refs):
    nodes_ref, face_ref, matrix_ref, pot_ref = refs[:4]
    outs = refs[4:-3]
    nodes_pad, face_pad, matrix_pad = refs[-3:]
    place_tables(geo, nodes_ref, face_ref, matrix_ref, nodes_pad, face_pad, matrix_pad)
    matrix = matrix_pad[...].astype(BF)
    face = face_pad[0:1, :]
    for c in range(geo.cells):
        nodes = nodes_pad[c : c + 1, :]
        own = owned_picks(geo, c, nodes)
        left = dot(own, matrix).astype(BF)
        outs[c][...] = dot_t(left, own).astype(BF)
        if c in geo.touching:
            at = geo.cells + geo.touching.index(c)
            outs[at][...] = dot_t(left, upper_picks(geo, nodes, face)).astype(BF)
    column = outs[-1]
    for r in range(geo.own // LANES):
        row = jnp.broadcast_to(pot_ref[r : r + 1, :], (LANES, LANES))
        column[r * LANES : (r + 1) * LANES, :] = row.T


def own_matrices(geo, cell_nodes, face_order, cell_matrix, potential):
    shapes = [sds((w.rows, w.rows), BF) for w in geo.windows]
    shapes += [sds((geo.windows[c].rows, geo.sp), BF) for c in geo.touching]
    shapes += [sds((geo.own, LANES), F32)]
    outs = vmem_call(
        functools.partial(own_matrices_kernel, geo), shapes, table_scratch(geo), cost=cost_of(3.0)
    )(cell_nodes, face_order, cell_matrix, potential.reshape(geo.own // LANES, LANES))
    n = geo.cells
    return outs[:n], outs[n:-1], outs[-1]


def behind_matrices_kernel(geo, *refs):
    nodes_ref, face_ref, matrix_ref = refs[:3]
    outs = refs[3:-3]
    nodes_pad, face_pad, matrix_pad = refs[-3:]
    place_tables(geo, nodes_ref, face_ref, matrix_ref, nodes_pad, face_pad, matrix_pad)
    matrix = matrix_pad[...].astype(BF)
    face = face_pad[0:1, :]
    count = len(geo.touching)
    for at, c in enumerate(geo.touching):
        nodes = nodes_pad[c : c + 1, :]
        upper = upper_picks(geo, nodes, face)
        left = dot(upper, matrix).astype(BF)
        outs[at][...] = dot_t(left, owned_picks(geo, c, nodes)).astype(BF)
        outs[count + at][...] = dot_t(left, upper).astype(BF)


def behind_matrices(geo, nodes, face, cell_matrix):
    shapes = [sds((geo.sp, geo.windows[c].rows), BF) for c in geo.touching]
    shapes += [sds((geo.sp, geo.sp), BF) for _ in geo.touching]
    outs = vmem_call(
        functools.partial(behind_matrices_kernel, geo), shapes, table_scratch(geo), cost=cost_of(1.5)
    )(nodes, face, cell_matrix)
    n = len(geo.touching)
    return outs[:n], outs[n:]


def cost_of(us):
    return pl.CostEstimate(flops=0, bytes_accessed=int(us * 3.0e6), transcendentals=0)


def write_sends(geo, y_ref, dn_ref, up_ref):
    top = geo.own - geo.dn_lo
    dn_ref[0:top, :] = y_ref[geo.dn_lo : geo.own, :].astype(BF)
    dn_ref[top : top + geo.low, :] = y_ref[0 : geo.low, :].astype(BF)
    up_ref[...] = y_ref[0 : geo.sp, :].astype(BF)


def send_shapes(geo, columns):
    return [sds((geo.dn_rows, columns), BF), sds((geo.sp, columns), BF)]


def pack_kernel(geo, y_ref, dn_ref, up_ref):
    write_sends(geo, y_ref, dn_ref, up_ref)


def pack(geo, y):
    return vmem_call(
        functools.partial(pack_kernel, geo), send_shapes(geo, y.shape[1]), cost=cost_of(0.5)
    )(y)


def owned_part_kernel(geo, scale, has_prev, has_field, has_upper, *refs):
    refs = list(refs)
    base_ref = refs.pop()
    y_ref = refs.pop(0)
    prev_ref = refs.pop(0) if has_prev else None
    pot_ref = refs.pop(0)
    field_ref = refs.pop(0) if has_field else None
    mats = [refs.pop(0) for _ in range(geo.cells)]
    y = y_ref[...]
    factor = pot_ref[...]
    if has_field:
        factor = factor + field_ref[...]
    value = ((factor - filter_center) * scale) * y
    if has_prev:
        value = value - prev_ref[...]
    base_ref[...] = value
    x = y.astype(BF)
    for c in range(geo.cells):
        w = geo.windows[c]
        own = w.hi - w.lo
        rows = x[w.lo : w.hi, :]
        if w.low:
            rows = jnp.concatenate([rows, x[0 : w.low, :]], axis=0)
        product = dot(mats[c][...], rows) * scale
        base_ref[w.lo : w.hi, :] += product[:own]
        if w.low:
            base_ref[0 : w.low, :] += product[own:]
    if has_upper:
        for upper in refs:
            base_ref[0 : geo.sp, :] += dot(upper[...], x[0 : geo.sp, :]) * scale


def owned_part(geo, scale, y, prev, pot, field, mats, uppers):
    args = [y] + ([prev] if prev is not None else []) + [pot]
    args += [field] if field is not None else []
    args += list(mats) + list(uppers)
    return vmem_call(
        functools.partial(
            owned_part_kernel, geo, scale, prev is not None, field is not None, bool(uppers)
        ),
        sds(y.shape, F32),
        cost=cost_of(2.0),
    )(*args)


def add_halo(geo, scale, y_ref, up_ref, dn_ref, crosses, behinds, uppers, own_up_ref):
    h_up = up_ref[...]
    h_dn = dn_ref[...]
    for at, c in enumerate(geo.touching):
        w = geo.windows[c]
        own = w.hi - w.lo
        product = dot(crosses[at][...], h_up) * scale
        y_ref[w.lo : w.hi, :] += product[:own]
        if w.low:
            y_ref[0 : w.low, :] += product[own:]
    total = None
    for at, c in enumerate(geo.touching):
        w = geo.windows[c]
        first = w.lo - geo.dn_lo
        term = dot(behinds[at][...], h_dn[first : first + w.rows, :])
        total = term if total is None else total + term
        if uppers:
            total = total + dot(uppers[at][...], own_up_ref[...])
    y_ref[0 : geo.sp, :] += total * scale


def write_density(y_ref, occ_ref, dens_ref, row_pad):
    parts, blocks, _ = dens_ref.shape
    own = y_ref.shape[0]
    length = own // blocks
    y = y_ref[...]
    terms = y * y * occ_ref[...]
    high = terms.astype(BF)
    low = (terms - high.astype(F32)).astype(BF)
    ones = jnp.ones((SUBLANES, terms.shape[1]), BF)
    summed = dot_t(ones, high) + dot_t(ones, low)
    row_pad[...] = jnp.zeros(row_pad.shape, F32)
    for j in range(blocks):
        row_pad[j : j + 1, 0:length] = summed[0:1, j * length : (j + 1) * length]
    dens_ref[...] = jnp.broadcast_to(row_pad[...][None], dens_ref.shape)


def finish_kernel(geo, scale, has_upper, mode, *refs):
    refs = list(refs)
    n = len(geo.touching)
    base_ref, up_ref, dn_ref = refs[:3]
    refs = refs[3:]
    crosses, refs = refs[:n], refs[n:]
    behinds, refs = refs[:n], refs[n:]
    uppers, own_up = [], None
    if has_upper:
        uppers, refs = refs[:n], refs[n:]
        own_up = refs.pop(0)
    occ_ref = refs.pop(0) if mode == "density" else None
    y_ref = refs.pop(0)
    y_ref[...] = base_ref[...]
    add_halo(geo, scale, y_ref, up_ref, dn_ref, crosses, behinds, uppers, own_up)
    if mode != "last":
        write_sends(geo, y_ref, refs[0], refs[1])
    if mode == "density":
        write_density(y_ref, occ_ref, refs[2], refs[3])


def finish(geo, scale, base, halo, crosses, behinds, uppers=(), own_up=None, occ=None, parts=None, last=False):
    columns = base.shape[1]
    args = [base, halo[0], halo[1], *crosses, *behinds, *uppers]
    if uppers:
        args.append(own_up)
    shapes = [sds(base.shape, F32)]
    scratch = []
    mode = "plain"
    if last:
        mode = "last"
    else:
        shapes += send_shapes(geo, columns)
    if occ is not None:
        mode = "density"
        args.append(occ)
        shapes.append(sds(parts, F32))
        scratch.append(pltpu.VMEM(parts[1:], F32))
    return vmem_call(
        functools.partial(finish_kernel, geo, scale, bool(uppers), mode),
        shapes,
        scratch,
        cost=cost_of(1.0),
    )(*args)


class FieldGeometry:
    def __init__(self, domains, own, share, cells, npc):
        self.domains, self.own, self.share, self.cells, self.npc = domains, own, share, cells, npc
        self.block = own // domains
        self.rows = up_to(npc, LANES) // LANES
        self.blocks = domains + 1
        self.at_inverse = cells * self.rows
        self.at_face = self.at_inverse + cells * self.blocks
        self.at_face_inverse = self.at_face + 1
        self.at_owner = self.at_face + 2
        self.at_screen = self.at_face + 3
        self.table_rows = up_to(self.at_screen + domains, SUBLANES)
        self.fits = (
            domains == SUBLANES
            and own % domains == 0
            and share <= self.block <= LANES
        )


def column_of(row):
    return jnp.broadcast_to(row, (LANES, LANES)).T


def field_tables_kernel(fg, nodes_ref, face_ref, owner_ref, screen_ref, matrix_ref, table_ref, high_ref, low_ref, pad, one, wide):
    lane = lax.broadcasted_iota(I32, (1, LANES), 1)
    one[...] = jnp.full(one.shape, -1.0, F32)
    pad[...] = jnp.full(pad.shape, -1, I32)
    pad[0 : fg.cells, 0 : fg.npc] = nodes_ref[...]
    sub = lax.broadcasted_iota(I32, (LANES, LANES), 0)
    wide_lane = lax.broadcasted_iota(I32, (LANES, LANES), 1)
    for c in range(fg.cells):
        columns = []
        for r in range(fg.rows):
            nodes = pad[c : c + 1, r * LANES : (r + 1) * LANES]
            block = jnp.zeros((1, LANES), I32)
            for b in range(1, fg.blocks):
                block = block + jnp.where(nodes >= b * fg.block, 1, 0)
            code = jnp.where(nodes < 0, -1, nodes + block * (LANES - fg.block))
            code = code.astype(F32)
            at = c * fg.rows + r
            one[at : at + 1, :] = code
            columns.append(column_of(code))
        for b in range(fg.blocks):
            target = (wide_lane + b * LANES).astype(F32)
            found = jnp.zeros((LANES, LANES), F32)
            for r in range(fg.rows):
                position = (sub + (r * LANES + 1)).astype(F32)
                found = found + jnp.where(columns[r] == target, position, 0.0)
            at = fg.at_inverse + c * fg.blocks + b
            one[at : at + 1, :] = jnp.sum(found, axis=0, keepdims=True) - 1.0
    one[fg.at_face : fg.at_face + 1, 0 : fg.share] = face_ref[...].astype(F32)
    column = column_of(one[fg.at_face : fg.at_face + 1, :])
    hits = jnp.where(column == wide_lane.astype(F32), (sub + 1).astype(F32), 0.0)
    one[fg.at_face_inverse : fg.at_face_inverse + 1, :] = jnp.sum(hits, axis=0, keepdims=True) - 1.0
    one[fg.at_owner : fg.at_owner + 1, 0 : fg.domains] = owner_ref[...].astype(F32)
    one[fg.at_screen : fg.at_screen + fg.domains, 0 : fg.block] = screen_ref[...]
    table_ref[...] = jnp.broadcast_to(one[...][None], table_ref.shape)
    wide[...] = jnp.zeros(wide.shape, F32)
    wide[0 : fg.npc, 0 : fg.npc] = matrix_ref[...]
    full = wide[...]
    high = full.astype(BF)
    high_ref[...] = high
    low_ref[...] = (full - high.astype(F32)).astype(BF)


def field_tables(fg, pois_nodes, pois_face, block_owner, screening, pois_matrix):
    size = fg.rows * LANES
    return vmem_call(
        functools.partial(field_tables_kernel, fg),
        [
            sds((fg.domains, fg.table_rows, LANES), F32),
            sds((size, size), BF),
            sds((size, size), BF),
        ],
        [
            pltpu.VMEM((up_to(fg.cells, SUBLANES), size), I32),
            pltpu.VMEM((fg.table_rows, LANES), F32),
            pltpu.VMEM((size, size), F32),
        ],
        cost=cost_of(3.0),
    )(pois_nodes, pois_face, block_owner, screening.reshape(fg.domains, fg.block), pois_matrix)


def lanes_of(values, index):
    return jnp.take_along_axis(values, index, axis=1, mode="promise_in_bounds")


def field_solve(fg, dens_ref, table_ref, high_ref, low_ref, codes, rows):
    domains, cells = fg.domains, fg.cells
    bands = dens_ref.shape[0] // domains
    valid = lax.broadcasted_iota(I32, (domains, LANES), 1) < fg.block

    def table(at):
        return table_ref[:, at, :]

    for at in range(fg.at_owner):
        codes[at] = table(at).astype(I32)
    owner = table(fg.at_owner)
    part = lax.broadcasted_iota(I32, (domains, LANES), 0).astype(F32)
    source = []
    for q in range(domains):
        density = dens_ref[q]
        for b in range(1, bands):
            density = density + dens_ref[b * domains + q]
        placed = jnp.zeros((domains, LANES), F32)
        for j in range(domains):
            who = jnp.broadcast_to(owner[q : q + 1, j : j + 1], (domains, LANES))
            placed = placed + jnp.where(who == part, jnp.broadcast_to(density[j : j + 1, :], (domains, LANES)), 0.0)
        source.append(placed)
    screen = [table(fg.at_screen + q) for q in range(domains)]

    def lookup(sources, code):
        lane = jnp.bitwise_and(code, LANES - 1)
        which = jnp.right_shift(code, 7)
        total = jnp.zeros((domains, LANES), F32)
        for b, values in enumerate(sources):
            total = jnp.where(which == b, lanes_of(values, lane), total)
        return total

    def operator(field):
        ahead = pltpu.roll(field[0], domains - 1, 0)
        face = codes[fg.at_face]
        upper = lookup([ahead], face)
        local = list(field) + [upper]
        for c in range(cells):
            for r in range(fg.rows):
                rows[c * domains : (c + 1) * domains, r * LANES : (r + 1) * LANES] = lookup(local, codes[c * fg.rows + r])
        picked = rows[...]
        high = picked.astype(BF)
        low = (picked - high.astype(F32)).astype(BF)
        product = dot(high, high_ref[...]) + (dot(low, high_ref[...]) + dot(high, low_ref[...]))
        out = []
        for b in range(fg.blocks):
            total = None
            for c in range(cells):
                sources = [
                    product[c * domains : (c + 1) * domains, r * LANES : (r + 1) * LANES]
                    for r in range(fg.rows)
                ]
                term = lookup(sources, codes[fg.at_inverse + c * fg.blocks + b])
                total = term if total is None else total + term
            out.append(total)
        arriving = pltpu.roll(out[domains], 1, 0)
        home = pltpu.roll(codes[fg.at_face_inverse], 1, 0)
        out[0] = out[0] + lookup([arriving], home)
        return [jnp.where(valid, screen[q] * field[q] + out[q], 0.0) for q in range(domains)]

    step_one = [s * (1.0 / solve_center) for s in source]
    applied = operator(step_one)
    residual = [s - a for s, a in zip(source, applied)]
    a1, b1 = weight_one * weight_zero, 2.0 * weight_one / solve_half
    step_two = [a1 * e + b1 * r for e, r in zip(step_one, residual)]
    applied = operator(step_two)
    residual = [r - a for r, a in zip(residual, applied)]
    a2, b2 = weight_two * weight_one, 2.0 * weight_two / solve_half
    step_three = [a2 * e + b2 * r for e, r in zip(step_two, residual)]
    return [(x + y) + z for x, y, z in zip(step_one, step_two, step_three)]


def field_kernel(geo, fg, scale, *refs):
    refs = list(refs)
    n = len(geo.touching)
    dens_ref, table_ref, high_ref, low_ref, owner_ref = refs[:5]
    base_ref, up_ref, dn_ref, y_ref = refs[5:9]
    refs = refs[9:]
    crosses, refs = refs[:n], refs[n:]
    behinds, refs = refs[:n], refs[n:]
    z_ref, dn_out, up_out, column_ref, hartree_ref = refs[:5]
    codes, rows, phi = refs[5:]
    blocks = field_solve(fg, dens_ref, table_ref, high_ref, low_ref, codes, rows)
    for q in range(fg.domains):
        phi[q] = blocks[q]
    here = lax.axis_index("domain")
    for j in range(fg.domains):
        hartree_ref[j : j + 1, :] = phi[here, pl.ds(owner_ref[0, j], 1), :]
    for j in range(fg.domains):
        column = column_of(hartree_ref[j : j + 1, :])
        column_ref[j * fg.block : (j + 1) * fg.block, :] = column[0 : fg.block, :]
    z_ref[...] = base_ref[...] + (column_ref[...] * scale) * y_ref[...]
    add_halo(geo, scale, z_ref, up_ref, dn_ref, crosses, behinds, [], None)
    write_sends(geo, z_ref, dn_out, up_out)


def field_step(geo, fg, scale, dens, table, high, low, block_owner, base, halo, y, crosses, behinds):
    columns = y.shape[1]
    vmem = pl.BlockSpec(memory_space=pltpu.VMEM)
    args = [dens, table, high, low, block_owner, base, halo[0], halo[1], y, *crosses, *behinds]
    specs = [vmem] * len(args)
    specs[4] = pl.BlockSpec(memory_space=pltpu.SMEM)
    return vmem_call(
        functools.partial(field_kernel, geo, fg, scale),
        [sds(y.shape, F32), *send_shapes(geo, columns), sds((geo.own, LANES), F32), sds((fg.domains, LANES), F32)],
        [
            pltpu.VMEM((fg.at_owner, fg.domains, LANES), I32),
            pltpu.VMEM((fg.cells * fg.domains, fg.rows * LANES), F32),
            pltpu.VMEM((fg.domains, fg.domains, LANES), F32),
        ],
        in_specs=specs,
        cost=cost_of(5.0),
    )(*args)


def assembled(owned_rows, face_row, terms):
    owned_count = owned_rows.shape[0]
    shared = face_row.shape[0]
    coming = jnp.take(from_behind(owned_rows[:shared], "domain", -1), face_row, axis=0)
    partial_value = terms(jnp.concatenate([owned_rows, coming], axis=0))
    upper_rows = partial_value[owned_count:]
    ordered = jnp.zeros_like(upper_rows).at[face_row].set(upper_rows)
    arrived = from_behind(ordered, "domain", 1)
    return partial_value[:owned_count].at[:shared].add(arrived)


def field_terms(local_rows, pois_matrix, node_ids):
    cell_vals = jnp.take(local_rows, node_ids, axis=0)
    product = jnp.einsum(
        "pq,cq->cp",
        pois_matrix,
        cell_vals,
        precision=lax.Precision.HIGHEST,
        preferred_element_type=F32,
    )
    return jnp.zeros(local_rows.shape, F32).at[node_ids.reshape(-1)].add(product.reshape(-1))


def reshuffle(blocks):
    return lax.all_to_all(blocks, "domain", split_axis=0, concat_axis=0, tiled=True)


def distributed_field(y, occupation, owner_row, pois_matrix, pois_nodes, field_face, screening):
    owned_count = y.shape[0]
    domains = lax.axis_size("domain")
    block_len = owned_count // domains
    partial_value = jnp.dot(
        y * y, occupation, precision=lax.Precision.HIGHEST, preferred_element_type=F32
    )
    summed = lax.psum(partial_value, "band")
    arranged = (
        jnp.zeros((domains, block_len), F32)
        .at[owner_row]
        .set(summed.reshape(domains, block_len))
    )
    source = reshuffle(arranged).reshape(owned_count)

    def field_operator(vector):
        return (
            assembled(
                vector, field_face, lambda local: field_terms(local, pois_matrix, pois_nodes)
            )
            + screening * vector
        )

    step_one = source / solve_center
    residual = source - field_operator(step_one)
    step_two = weight_one * weight_zero * step_one + 2.0 * weight_one / solve_half * residual
    residual = residual - field_operator(step_two)
    step_three = weight_two * weight_one * step_two + 2.0 * weight_two / solve_half * residual
    solved = step_one + step_two + step_three
    returned = reshuffle(solved.reshape(domains, block_len))
    return jnp.take(returned, owner_row, axis=0).reshape(owned_count)


def exchange(sends):
    dn, up = sends
    h_dn = from_behind(dn, "domain", 1)
    h_up = from_behind(up, "domain", -1)
    return h_up, h_dn


def per_device(
    orbitals,
    potential,
    occupation,
    cell_matrix,
    cell_nodes,
    face_order,
    pois_matrix,
    pois_nodes,
    pois_face,
    screening,
    block_owner,
):
    domains = lax.axis_size("domain")
    bands = lax.axis_size("band")
    own, columns = orbitals.shape
    geo = Geometry(own, face_order.shape[1], cell_nodes.shape[0], cell_nodes.shape[1])
    fg = FieldGeometry(domains, own, pois_face.shape[1], pois_nodes.shape[0], pois_nodes.shape[1])
    first, later = 1.0 / filter_half, 2.0 / filter_half

    sends = pack(geo, orbitals)
    halo = exchange(sends)
    behind_nodes = from_behind(cell_nodes, "domain", 1)
    behind_face = from_behind(face_order, "domain", 1)
    mats, crosses, pot = own_matrices(geo, cell_nodes, face_order, cell_matrix, potential)
    if fg.fits:
        table, high, low = field_tables(fg, pois_nodes, pois_face, block_owner, screening, pois_matrix)
        tables = lax.all_to_all(table, "domain", 0, 0, tiled=True)

    base = owned_part(geo, first, orbitals, None, pot, None, mats, ())
    behinds, uppers = behind_matrices(geo, behind_nodes, behind_face, cell_matrix)
    y1, *sends1 = finish(geo, first, base, halo, crosses, behinds, uppers, sends[1])

    halo = exchange(sends1)
    base = owned_part(geo, later, y1, orbitals, pot, None, mats, uppers)
    y2, *sends2 = finish(geo, later, base, halo, crosses, behinds)

    halo = exchange(sends2)
    base = owned_part(geo, later, y2, y1, pot, None, mats, uppers)
    if fg.fits:
        parts = (domains * bands, domains, LANES)
        y3, dn, up, spread = finish(
            geo, later, base, halo, crosses, behinds, occ=occupation.reshape(1, columns), parts=parts
        )
        dens = lax.all_to_all(spread, ("band", "domain"), 0, 0, tiled=True)
        halo = exchange((dn, up))
        base = owned_part(geo, first, y3, None, pot, None, mats, uppers)
        z1, dn, up, column, packed = field_step(
            geo, fg, first, dens, tables, high, low, block_owner, base, halo, y3, crosses, behinds
        )
        hartree = packed[:, : fg.block].reshape(own)
        sends4 = (dn, up)
    else:
        y3, *sends3 = finish(geo, later, base, halo, crosses, behinds)
        halo = exchange(sends3)
        hartree = distributed_field(
            y3, occupation, block_owner[0], pois_matrix, pois_nodes, pois_face[0], screening
        )
        column = jnp.broadcast_to(hartree[:, None], (own, LANES))
        base = owned_part(geo, first, y3, None, pot, column, mats, uppers)
        z1, *sends4 = finish(geo, first, base, halo, crosses, behinds)

    halo = exchange(sends4)
    base = owned_part(geo, later, z1, y3, pot, column, mats, uppers)
    (filtered,) = finish(geo, later, base, halo, crosses, behinds, last=True)
    return filtered, hartree


def solution(mesh):
    return jax.shard_map(
        per_device,
        mesh=mesh,
        in_specs=(
            P("domain", "band"),
            P("domain"),
            P("band"),
            P(),
            P("domain", None),
            P("domain", None),
            P(),
            P("domain", None),
            P("domain", None),
            P("domain"),
            P("domain", None),
        ),
        out_specs=(P("domain", "band"), P("domain")),
        check_vma=False,
    )
```

```python
import functools

import jax
import jax.numpy as jnp
from jax import lax
from jax.experimental import pallas as pl
from jax.experimental.pallas import tpu as pltpu
from jax.sharding import PartitionSpec as P

filter_center = 1.8
filter_half = 2.7
solve_center = 3.25
solve_half = 2.75
solve_ratio = solve_center / solve_half
weight_zero = 1.0 / solve_ratio
weight_one = 1.0 / (2.0 * solve_ratio - weight_zero)
weight_two = 1.0 / (2.0 * solve_ratio - weight_one)

BF = jnp.bfloat16
F32 = jnp.float32
I32 = jnp.int32
LANES = 128
SUBLANES = 8


def up_to(n, m):
    return -(-n // m) * m


def from_behind(array, axis, by):
    length = lax.axis_size(axis)
    return lax.ppermute(array, axis, [(i, (i + by) % length) for i in range(length)])


class Window:
    def __init__(self, start, npc, own, nloc):
        end = start + npc
        self.lo = start // 16 * 16
        self.hi = min(up_to(min(end, own), 16), own)
        self.touches = end > own
        self.low = up_to(max(0, end - nloc), 16)
        self.rows = self.hi - self.lo + self.low


class Geometry:
    def __init__(self, own, share, cells, npc):
        self.own, self.share, self.cells, self.npc = own, share, cells, npc
        nloc = own + share
        stride = nloc // cells
        self.sp = up_to(share, 16)
        self.npl = up_to(npc, LANES)
        self.windows = [Window(c * stride, npc, own, nloc) for c in range(cells)]
        self.touching = [c for c in range(cells) if self.windows[c].touches]
        self.dn_lo = min(self.windows[c].lo for c in self.touching)
        self.low = max(w.low for w in self.windows)
        self.dn_rows = own - self.dn_lo + self.low
        self.table_rows = up_to(cells + 1, SUBLANES)
        self.table_lanes = up_to(max(npc, share), LANES)
        self.table_tiles = self.table_lanes // LANES


def dot(a, b):
    return lax.dot_general(a, b, (((1,), (0,)), ((), ())), preferred_element_type=F32)


def dot_t(a, b):
    return lax.dot_general(a, b, (((1,), (1,)), ((), ())), preferred_element_type=F32)


def vmem_call(kernel, out_shape, scratch=(), in_specs=None, cost=None):
    kwargs = {}
    if in_specs is not None:
        kwargs["in_specs"] = in_specs
    return pl.pallas_call(
        kernel,
        out_shape=out_shape,
        scratch_shapes=list(scratch),
        cost_estimate=cost,
        compiler_params=pltpu.CompilerParams(vmem_limit_bytes=12 * 1024 * 1024),
        **kwargs,
    )


def in_hbm(*arrays):
    return [pltpu.with_memory_space_constraint(a, pltpu.HBM) for a in arrays]


def sds(shape, dtype):
    return jax.ShapeDtypeStruct(shape, dtype)


def one_hot_rows(count, first, nodes):
    ids = lax.broadcasted_iota(I32, (count, nodes.shape[1]), 0) + first
    return jnp.where(ids == nodes, 1.0, 0.0).astype(BF)


def place_table(geo, nodes_ref, face_ref, table):
    table[...] = jnp.full(table.shape, -1, I32)
    table[0 : geo.cells, 0 : geo.npc] = nodes_ref[...]
    table[geo.cells : geo.cells + 1, 0 : geo.share] = face_ref[...]


def place_matrix(geo, matrix_ref, matrix_pad):
    matrix_pad[...] = jnp.zeros(matrix_pad.shape, F32)
    matrix_pad[0 : geo.npc, 0 : geo.npc] = matrix_ref[...].astype(F32)
    return matrix_pad[...].astype(BF)


def table_scratch(geo):
    return pltpu.VMEM((geo.table_rows, geo.table_lanes), I32)


def matrix_scratch(geo):
    return pltpu.VMEM((geo.npl, geo.npl), F32)


def nodes_of(geo, table, c):
    return table[c : c + 1, 0 : geo.npl]


def face_of(geo, table):
    return table[geo.cells : geo.cells + 1, 0 : up_to(geo.share, LANES)]


def owned_picks(geo, c, nodes):
    w = geo.windows[c]
    picks = one_hot_rows(w.hi - w.lo, w.lo, nodes)
    if w.low:
        picks = jnp.concatenate([picks, one_hot_rows(w.low, 0, nodes)], axis=0)
    return picks


def upper_picks(geo, nodes, face):
    by_local = one_hot_rows(face.shape[1], geo.own, nodes)
    by_owner = one_hot_rows(geo.sp, 0, face)
    return dot(by_owner, by_local).astype(BF)


def own_matrices_kernel(geo, *refs):
    outs = refs[4:-7]
    nodes_ref, face_ref, matrix_ref, pot_ref, table, matrix_pad, sems = refs[-7:]
    copies = fetch(list(zip(refs[:4], (nodes_ref, face_ref, matrix_ref, pot_ref))), sems)
    for copy in copies:
        copy.wait()
    place_table(geo, nodes_ref, face_ref, table)
    matrix = place_matrix(geo, matrix_ref, matrix_pad)
    face = face_of(geo, table)
    for c in range(geo.cells):
        nodes = nodes_of(geo, table, c)
        own = owned_picks(geo, c, nodes)
        left = dot(own, matrix).astype(BF)
        outs[c][...] = dot_t(left, own).astype(BF)
        if c in geo.touching:
            at = geo.cells + geo.touching.index(c)
            outs[at][...] = dot_t(left, upper_picks(geo, nodes, face)).astype(BF)
    column = outs[-1]
    for r in range(geo.own // LANES):
        row = jnp.broadcast_to(pot_ref[r : r + 1, :], (LANES, LANES))
        column[r * LANES : (r + 1) * LANES, :] = row.T


def own_matrices(geo, cell_nodes, face_order, cell_matrix, potential):
    shapes = [sds((w.rows, w.rows), BF) for w in geo.windows]
    shapes += [sds((geo.windows[c].rows, geo.sp), BF) for c in geo.touching]
    shapes += [sds((geo.own, LANES), F32)]
    outs = vmem_call(
        functools.partial(own_matrices_kernel, geo),
        shapes,
        [
            pltpu.VMEM(cell_nodes.shape, I32),
            pltpu.VMEM(face_order.shape, I32),
            pltpu.VMEM(cell_matrix.shape, BF),
            pltpu.VMEM((geo.own // LANES, LANES), F32),
            table_scratch(geo),
            matrix_scratch(geo),
            pltpu.SemaphoreType.DMA((4,)),
        ],
        in_specs=[pl.BlockSpec(memory_space=pltpu.HBM)] * 4,
        cost=cost_of(2.0),
    )(*in_hbm(cell_nodes, face_order, cell_matrix, potential.reshape(geo.own // LANES, LANES)))
    n = geo.cells
    return outs[:n], outs[n:-1], outs[-1]


def behind_matrices_kernel(geo, *refs):
    sent_ref, matrix_ref = refs[:2]
    outs = refs[2:-2]
    table, matrix_pad = refs[-2:]
    for t in range(geo.table_tiles):
        at = geo.dn_rows + 2 * t * geo.table_rows
        digits = sent_ref[at : at + 2 * geo.table_rows, :].astype(F32)
        value = digits[: geo.table_rows] * LANES + digits[geo.table_rows :] - 1.0
        table[:, t * LANES : (t + 1) * LANES] = value.astype(I32)
    matrix = place_matrix(geo, matrix_ref, matrix_pad)
    face = face_of(geo, table)
    count = len(geo.touching)
    for at, c in enumerate(geo.touching):
        nodes = nodes_of(geo, table, c)
        upper = upper_picks(geo, nodes, face)
        left = dot(upper, matrix).astype(BF)
        outs[at][...] = dot_t(left, owned_picks(geo, c, nodes)).astype(BF)
        outs[count + at][...] = dot_t(left, upper).astype(BF)


def behind_matrices(geo, sent, cell_matrix):
    shapes = [sds((geo.sp, geo.windows[c].rows), BF) for c in geo.touching]
    shapes += [sds((geo.sp, geo.sp), BF) for _ in geo.touching]
    outs = vmem_call(
        functools.partial(behind_matrices_kernel, geo),
        shapes,
        [table_scratch(geo), matrix_scratch(geo)],
        cost=cost_of(1.0),
    )(sent, cell_matrix)
    n = len(geo.touching)
    return outs[:n], outs[n:]


def cost_of(us):
    return pl.CostEstimate(flops=0, bytes_accessed=int(us * 3.0e6), transcendentals=0)


def write_sends(geo, y_ref, dn_ref, up_ref):
    top = geo.own - geo.dn_lo
    dn_ref[0:top, :] = y_ref[geo.dn_lo : geo.own, :].astype(BF)
    dn_ref[top : top + geo.low, :] = y_ref[0 : geo.low, :].astype(BF)
    up_ref[...] = y_ref[0 : geo.sp, :].astype(BF)


def send_shapes(geo, columns):
    return [sds((geo.dn_rows, columns), BF), sds((geo.sp, columns), BF)]


def fetch(pairs, sems):
    copies = [pltpu.make_async_copy(src, dst, sems.at[i]) for i, (src, dst) in enumerate(pairs)]
    for copy in copies:
        copy.start()
    return copies


def pack_kernel(geo, y_hbm, nodes_hbm, face_hbm, dn_ref, up_ref, y, nodes, face, table, sems):
    cuts = sorted({0, max(geo.sp, geo.low), geo.dn_lo, geo.own})
    spans = list(zip(cuts[:-1], cuts[1:]))
    pairs = [(nodes_hbm, nodes), (face_hbm, face)]
    pairs += [(y_hbm.at[pl.ds(a, b - a)], y.at[pl.ds(a, b - a)]) for a, b in spans]
    copies = fetch(pairs, sems)
    copies[0].wait()
    copies[1].wait()
    place_table(geo, nodes, face, table)
    for t in range(geo.table_tiles):
        at = geo.dn_rows + 2 * t * geo.table_rows
        value = table[:, t * LANES : (t + 1) * LANES] + 1
        high = jnp.right_shift(value, 7).astype(F32)
        low = jnp.bitwise_and(value, LANES - 1).astype(F32)
        digits = jnp.concatenate([high, low], axis=0).astype(BF)
        dn_ref[at : at + 2 * geo.table_rows, :] = digits
    for copy in copies[2:]:
        copy.wait()
    write_sends(geo, y, dn_ref, up_ref)


def pack(geo, y, cell_nodes, face_order):
    _, up = send_shapes(geo, y.shape[1])
    rows = geo.dn_rows + 2 * geo.table_rows * geo.table_tiles
    return vmem_call(
        functools.partial(pack_kernel, geo),
        [sds((rows, y.shape[1]), BF), up, sds(y.shape, F32)],
        [
            pltpu.VMEM(cell_nodes.shape, I32),
            pltpu.VMEM(face_order.shape, I32),
            table_scratch(geo),
            pltpu.SemaphoreType.DMA((5,)),
        ],
        in_specs=[pl.BlockSpec(memory_space=pltpu.HBM)] * 3,
        cost=cost_of(1.0),
    )(*in_hbm(y, cell_nodes, face_order))


def owned_part_kernel(geo, scale, has_prev, has_field, has_upper, *refs):
    refs = list(refs)
    base_ref = refs.pop()
    y_ref = refs.pop(0)
    prev_ref = refs.pop(0) if has_prev else None
    pot_ref = refs.pop(0)
    field_ref = refs.pop(0) if has_field else None
    mats = [refs.pop(0) for _ in range(geo.cells)]
    y = y_ref[...]
    factor = pot_ref[...]
    if has_field:
        factor = factor + field_ref[...]
    value = ((factor - filter_center) * scale) * y
    if has_prev:
        value = value - prev_ref[...]
    base_ref[...] = value
    x = y.astype(BF)
    for c in range(geo.cells):
        w = geo.windows[c]
        own = w.hi - w.lo
        rows = x[w.lo : w.hi, :]
        if w.low:
            rows = jnp.concatenate([rows, x[0 : w.low, :]], axis=0)
        product = dot(mats[c][...], rows) * scale
        base_ref[w.lo : w.hi, :] += product[:own]
        if w.low:
            base_ref[0 : w.low, :] += product[own:]
    if has_upper:
        for upper in refs:
            base_ref[0 : geo.sp, :] += dot(upper[...], x[0 : geo.sp, :]) * scale


def owned_part(geo, scale, y, prev, pot, field, mats, uppers):
    args = [y] + ([prev] if prev is not None else []) + [pot]
    args += [field] if field is not None else []
    args += list(mats) + list(uppers)
    return vmem_call(
        functools.partial(
            owned_part_kernel, geo, scale, prev is not None, field is not None, bool(uppers)
        ),
        sds(y.shape, F32),
        cost=cost_of(2.0),
    )(*args)


def add_halo(geo, scale, y_ref, up_ref, dn_ref, crosses, behinds, uppers, own_up_ref):
    h_up = up_ref[...]
    h_dn = dn_ref[...]
    for at, c in enumerate(geo.touching):
        w = geo.windows[c]
        own = w.hi - w.lo
        product = dot(crosses[at][...], h_up) * scale
        y_ref[w.lo : w.hi, :] += product[:own]
        if w.low:
            y_ref[0 : w.low, :] += product[own:]
    total = None
    for at, c in enumerate(geo.touching):
        w = geo.windows[c]
        first = w.lo - geo.dn_lo
        term = dot(behinds[at][...], h_dn[first : first + w.rows, :])
        total = term if total is None else total + term
        if uppers:
            total = total + dot(uppers[at][...], own_up_ref[...])
    y_ref[0 : geo.sp, :] += total * scale


def write_density(y_ref, occ_ref, dens_ref, row_pad):
    _, blocks, _ = dens_ref.shape
    own = y_ref.shape[0]
    length = own // blocks
    y = y_ref[...]
    terms = y * y * occ_ref[...]
    high = terms.astype(BF)
    low = (terms - high.astype(F32)).astype(BF)
    ones = jnp.ones((SUBLANES, terms.shape[1]), BF)
    summed = dot_t(ones, high) + dot_t(ones, low)
    row_pad[...] = jnp.zeros(row_pad.shape, F32)
    for j in range(blocks):
        row_pad[j : j + 1, 0:length] = summed[0:1, j * length : (j + 1) * length]
    dens_ref[...] = jnp.broadcast_to(row_pad[...][None], dens_ref.shape)


def finish_kernel(geo, scale, has_upper, mode, *refs):
    refs = list(refs)
    n = len(geo.touching)
    base_ref, up_ref, dn_ref = refs[:3]
    refs = refs[3:]
    crosses, refs = refs[:n], refs[n:]
    behinds, refs = refs[:n], refs[n:]
    uppers, own_up = [], None
    if has_upper:
        uppers, refs = refs[:n], refs[n:]
        own_up = refs.pop(0)
    occ_ref = refs.pop(0) if mode == "density" else None
    if mode == "field":
        column_ref, before_ref = refs.pop(0), refs.pop(0)
    y_ref = refs.pop(0)
    if mode == "field":
        y_ref[...] = base_ref[...] + (column_ref[...] * scale) * before_ref[...]
    else:
        y_ref[...] = base_ref[...]
    add_halo(geo, scale, y_ref, up_ref, dn_ref, crosses, behinds, uppers, own_up)
    if mode != "last":
        write_sends(geo, y_ref, refs[0], refs[1])
    if mode == "density":
        write_density(y_ref, occ_ref, refs[2], refs[3])


def finish(geo, scale, base, halo, crosses, behinds, uppers=(), own_up=None, occ=None, parts=None, field=None, last=False):
    columns = base.shape[1]
    args = [base, halo[0], halo[1], *crosses, *behinds, *uppers]
    if uppers:
        args.append(own_up)
    shapes = [sds(base.shape, F32)]
    scratch = []
    mode = "plain"
    if last:
        mode = "last"
    else:
        shapes += send_shapes(geo, columns)
    if field is not None:
        mode = "field"
        args += list(field)
    if occ is not None:
        mode = "density"
        args.append(occ)
        shapes.append(sds(parts, F32))
        scratch.append(pltpu.VMEM(parts[1:], F32))
    return vmem_call(
        functools.partial(finish_kernel, geo, scale, bool(uppers), mode),
        shapes,
        scratch,
        cost=cost_of(1.0),
    )(*args)


class FieldGeometry:
    def __init__(self, domains, own, share, cells, npc):
        self.domains, self.own, self.share, self.cells, self.npc = domains, own, share, cells, npc
        self.block = own // domains
        self.rows = up_to(npc, LANES) // LANES
        self.blocks = domains + 1
        self.at_inverse = cells * self.rows
        self.at_face = self.at_inverse + cells * self.blocks
        self.at_face_inverse = self.at_face + 1
        self.at_owner = self.at_face + 2
        self.codes = self.at_face + 3
        self.at_screen = up_to(self.codes, 2) // 2
        self.table_rows = up_to(self.at_screen + domains, SUBLANES)
        self.size = self.rows * LANES
        self.fits = (
            domains == SUBLANES
            and own % (domains * SUBLANES) == 0
            and own % LANES == 0
            and share <= self.block <= LANES
            and max(npc, self.blocks * LANES) < CODE_BASE - 1
        )


CODE_BASE = 2048
CODE_BITS = 11


def pieces(length, blocks):
    found = []
    for j in range(blocks):
        done = 0
        while done < length:
            at = j * length + done
            count = min(length - done, LANES - at % LANES)
            found.append((at // LANES, at % LANES, j, done, count))
            done += count
    return found


def column_of(row):
    return jnp.broadcast_to(row, (LANES, LANES)).T


def field_tables_kernel(fg, *refs):
    sources, table_ref = refs[:4], refs[5]
    nodes_ref, face_ref, owner_ref, screen_ref, pad, one, packed, sems = refs[6:]
    copies = fetch(list(zip(sources, (nodes_ref, face_ref, owner_ref, screen_ref))), sems)
    for copy in copies:
        copy.wait()
    one[...] = jnp.full(one.shape, -1.0, F32)
    pad[...] = jnp.full(pad.shape, -1, I32)
    pad[0 : fg.cells, 0 : fg.npc] = nodes_ref[...]
    sub = lax.broadcasted_iota(I32, (LANES, LANES), 0)
    wide_lane = lax.broadcasted_iota(I32, (LANES, LANES), 1)
    for c in range(fg.cells):
        columns = []
        for r in range(fg.rows):
            nodes = pad[c : c + 1, r * LANES : (r + 1) * LANES]
            block = jnp.zeros((1, LANES), I32)
            for b in range(1, fg.blocks):
                block = block + jnp.where(nodes >= b * fg.block, 1, 0)
            code = jnp.where(nodes < 0, -1, nodes + block * (LANES - fg.block))
            code = code.astype(F32)
            at = c * fg.rows + r
            one[at : at + 1, :] = code
            columns.append(column_of(code))
        for b in range(fg.blocks):
            target = (wide_lane + b * LANES).astype(F32)
            found = jnp.zeros((LANES, LANES), F32)
            for r in range(fg.rows):
                position = (sub + (r * LANES + 1)).astype(F32)
                found = jnp.where(columns[r] == target, position, found)
            at = fg.at_inverse + c * fg.blocks + b
            one[at : at + 1, :] = jnp.sum(found, axis=0, keepdims=True) - 1.0
    one[fg.at_face : fg.at_face + 1, 0 : fg.share] = face_ref[...].astype(F32)
    column = column_of(one[fg.at_face : fg.at_face + 1, :])
    hits = jnp.where(column == wide_lane.astype(F32), (sub + 1).astype(F32), 0.0)
    one[fg.at_face_inverse : fg.at_face_inverse + 1, :] = jnp.sum(hits, axis=0, keepdims=True) - 1.0
    one[fg.at_owner : fg.at_owner + 1, 0 : fg.domains] = owner_ref[...].astype(F32)
    packed[...] = jnp.zeros(packed.shape, F32)
    half = fg.at_screen
    packed[0:half, :] = (one[0:half, :] + 1.0) + (one[half : 2 * half, :] + 1.0) * CODE_BASE
    for row, lane, j, offset, count in pieces(fg.block, fg.domains):
        at = fg.at_screen + j
        packed[at : at + 1, offset : offset + count] = screen_ref[row : row + 1, lane : lane + count]
    table_ref[...] = jnp.broadcast_to(packed[...][None], table_ref.shape)


def field_tables(fg, pois_nodes, pois_face, block_owner, screening, after):
    specs = [pl.BlockSpec(memory_space=pltpu.HBM)] * 4 + [pl.BlockSpec(memory_space=pl.ANY)]
    lines = screening.reshape(fg.own // LANES, LANES)
    return vmem_call(
        functools.partial(field_tables_kernel, fg),
        sds((fg.domains, fg.table_rows, LANES), F32),
        [
            pltpu.VMEM(pois_nodes.shape, I32),
            pltpu.VMEM(pois_face.shape, I32),
            pltpu.VMEM(block_owner.shape, I32),
            pltpu.VMEM(lines.shape, F32),
            pltpu.VMEM((up_to(fg.cells, SUBLANES), fg.size), I32),
            pltpu.VMEM((up_to(2 * fg.at_screen, SUBLANES), LANES), F32),
            pltpu.VMEM((fg.table_rows, LANES), F32),
            pltpu.SemaphoreType.DMA((4,)),
        ],
        in_specs=specs,
        cost=cost_of(1.5),
    )(*in_hbm(pois_nodes, pois_face, block_owner, lines), after)


def lanes_of(values, index):
    return jnp.take_along_axis(values, index, axis=1, mode="promise_in_bounds")


def field_solve(fg, dens_ref, table_ref, matrix_ref, high_ref, low_ref, codes, rows, copies):
    domains, cells = fg.domains, fg.cells
    bands = dens_ref.shape[0] // domains
    valid = lax.broadcasted_iota(I32, (domains, LANES), 1) < fg.block

    half = fg.at_screen
    for at in range(half):
        both = table_ref[:, at, :].astype(I32)
        codes[at] = jnp.bitwise_and(both, CODE_BASE - 1) - 1
        codes[half + at] = jnp.right_shift(both, CODE_BITS) - 1
    owner = codes[fg.at_owner].astype(F32)
    part = lax.broadcasted_iota(I32, (domains, LANES), 0).astype(F32)
    source = []
    for q in range(domains):
        density = dens_ref[q]
        for b in range(1, bands):
            density = density + dens_ref[b * domains + q]
        placed = jnp.zeros((domains, LANES), F32)
        for j in range(domains):
            who = jnp.broadcast_to(owner[q : q + 1, j : j + 1], (domains, LANES))
            placed = placed + jnp.where(who == part, jnp.broadcast_to(density[j : j + 1, :], (domains, LANES)), 0.0)
        source.append(placed)
    screen = [table_ref[:, fg.at_screen + q, :] for q in range(domains)]

    def lookup(sources, code):
        lane = jnp.bitwise_and(code, LANES - 1)
        which = jnp.right_shift(code, 7)
        total = jnp.zeros((domains, LANES), F32)
        for b, values in enumerate(sources):
            total = jnp.where(which == b, lanes_of(values, lane), total)
        return total

    def operator(field):
        ahead = pltpu.roll(field[0], domains - 1, 0)
        face = codes[fg.at_face]
        upper = lookup([ahead], face)
        local = list(field) + [upper]
        for c in range(cells):
            for r in range(fg.rows):
                rows[c * domains : (c + 1) * domains, r * LANES : (r + 1) * LANES] = lookup(local, codes[c * fg.rows + r])
        if copies:
            copies.pop().wait()
            full = matrix_ref[...]
            top = full.astype(BF)
            high_ref[...] = top
            low_ref[...] = (full - top.astype(F32)).astype(BF)
        picked = rows[:, 0 : fg.npc]
        high = picked.astype(BF)
        low = (picked - high.astype(F32)).astype(BF)
        both = dot(jnp.concatenate([high, low], axis=0), high_ref[...])
        half_rows = cells * domains
        rows[:, 0 : fg.npc] = both[:half_rows] + (both[half_rows:] + dot(high, low_ref[...]))
        out = []
        for b in range(fg.blocks):
            total = None
            for c in range(cells):
                sources = [
                    rows[c * domains : (c + 1) * domains, r * LANES : (r + 1) * LANES]
                    for r in range(fg.rows)
                ]
                term = lookup(sources, codes[fg.at_inverse + c * fg.blocks + b])
                total = term if total is None else total + term
            out.append(total)
        arriving = pltpu.roll(out[domains], 1, 0)
        home = pltpu.roll(codes[fg.at_face_inverse], 1, 0)
        out[0] = out[0] + lookup([arriving], home)
        return [jnp.where(valid, screen[q] * field[q] + out[q], 0.0) for q in range(domains)]

    step_one = [s * (1.0 / solve_center) for s in source]
    applied = operator(step_one)
    residual = [s - a for s, a in zip(source, applied)]
    a1, b1 = weight_one * weight_zero, 2.0 * weight_one / solve_half
    step_two = [a1 * e + b1 * r for e, r in zip(step_one, residual)]
    applied = operator(step_two)
    residual = [r - a for r, a in zip(residual, applied)]
    a2, b2 = weight_two * weight_one, 2.0 * weight_two / solve_half
    step_three = [a2 * e + b2 * r for e, r in zip(step_two, residual)]
    return [(x + y) + z for x, y, z in zip(step_one, step_two, step_three)]


def field_kernel(fg, dens_ref, table_ref, matrix_hbm, owner_ref, column_ref, hartree_ref, codes, rows, phi, mine, matrix_ref, high_ref, low_ref, sems):
    copies = fetch([(matrix_hbm, matrix_ref)], sems)
    blocks = field_solve(fg, dens_ref, table_ref, matrix_ref, high_ref, low_ref, codes, rows, copies)
    for q in range(fg.domains):
        phi[q] = blocks[q]
    here = lax.axis_index("domain")
    for j in range(fg.domains):
        mine[j : j + 1, :] = phi[here, pl.ds(owner_ref[0, j], 1), :]
    for j in range(fg.domains):
        column = column_of(mine[j : j + 1, :])
        column_ref[j * fg.block : (j + 1) * fg.block, :] = column[0 : fg.block, :]
    for row, lane, j, offset, count in pieces(fg.block, fg.domains):
        hartree_ref[row : row + 1, lane : lane + count] = mine[j : j + 1, offset : offset + count]


def field_step(fg, dens, table, matrix, block_owner):
    vmem = pl.BlockSpec(memory_space=pltpu.VMEM)
    tile = (fg.domains, LANES)
    return vmem_call(
        functools.partial(field_kernel, fg),
        [sds((fg.own, LANES), F32), sds((fg.own // LANES, LANES), F32)],
        [
            pltpu.VMEM((2 * fg.at_screen, *tile), I32),
            pltpu.VMEM((fg.cells * fg.domains, fg.size), F32),
            pltpu.VMEM((fg.domains, *tile), F32),
            pltpu.VMEM(tile, F32),
            pltpu.VMEM(matrix.shape, F32),
            pltpu.VMEM(matrix.shape, BF),
            pltpu.VMEM(matrix.shape, BF),
            pltpu.SemaphoreType.DMA((1,)),
        ],
        in_specs=[vmem] * 2
        + [pl.BlockSpec(memory_space=pltpu.HBM)]
        + [pl.BlockSpec(memory_space=pltpu.SMEM)],
        cost=cost_of(4.0),
    )(dens, table, *in_hbm(matrix), block_owner)


def assembled(owned_rows, face_row, terms):
    owned_count = owned_rows.shape[0]
    shared = face_row.shape[0]
    coming = jnp.take(from_behind(owned_rows[:shared], "domain", -1), face_row, axis=0)
    partial_value = terms(jnp.concatenate([owned_rows, coming], axis=0))
    upper_rows = partial_value[owned_count:]
    ordered = jnp.zeros_like(upper_rows).at[face_row].set(upper_rows)
    arrived = from_behind(ordered, "domain", 1)
    return partial_value[:owned_count].at[:shared].add(arrived)


def field_terms(local_rows, pois_matrix, node_ids):
    cell_vals = jnp.take(local_rows, node_ids, axis=0)
    product = jnp.einsum(
        "pq,cq->cp",
        pois_matrix,
        cell_vals,
        precision=lax.Precision.HIGHEST,
        preferred_element_type=F32,
    )
    return jnp.zeros(local_rows.shape, F32).at[node_ids.reshape(-1)].add(product.reshape(-1))


def reshuffle(blocks):
    return lax.all_to_all(blocks, "domain", split_axis=0, concat_axis=0, tiled=True)


def distributed_field(y, occupation, owner_row, pois_matrix, pois_nodes, field_face, screening):
    owned_count = y.shape[0]
    domains = lax.axis_size("domain")
    block_len = owned_count // domains
    partial_value = jnp.dot(
        y * y, occupation, precision=lax.Precision.HIGHEST, preferred_element_type=F32
    )
    summed = lax.psum(partial_value, "band")
    arranged = (
        jnp.zeros((domains, block_len), F32)
        .at[owner_row]
        .set(summed.reshape(domains, block_len))
    )
    source = reshuffle(arranged).reshape(owned_count)

    def field_operator(vector):
        return (
            assembled(
                vector, field_face, lambda local: field_terms(local, pois_matrix, pois_nodes)
            )
            + screening * vector
        )

    step_one = source / solve_center
    residual = source - field_operator(step_one)
    step_two = weight_one * weight_zero * step_one + 2.0 * weight_one / solve_half * residual
    residual = residual - field_operator(step_two)
    step_three = weight_two * weight_one * step_two + 2.0 * weight_two / solve_half * residual
    solved = step_one + step_two + step_three
    returned = reshuffle(solved.reshape(domains, block_len))
    return jnp.take(returned, owner_row, axis=0).reshape(owned_count)


def exchange(sends):
    dn, up = sends
    h_dn = from_behind(dn, "domain", 1)
    h_up = from_behind(up, "domain", -1)
    return h_up, h_dn


def on_device(
    orbitals,
    potential,
    occupation,
    cell_matrix,
    cell_nodes,
    face_order,
    pois_matrix,
    pois_nodes,
    pois_face,
    screening,
    block_owner,
):
    domains = lax.axis_size("domain")
    bands = lax.axis_size("band")
    own, columns = orbitals.shape
    geo = Geometry(own, face_order.shape[1], cell_nodes.shape[0], cell_nodes.shape[1])
    fg = FieldGeometry(domains, own, pois_face.shape[1], pois_nodes.shape[0], pois_nodes.shape[1])
    first, later = 1.0 / filter_half, 2.0 / filter_half

    *sends, y0 = pack(geo, orbitals, cell_nodes, face_order)
    halo = exchange(sends)
    mats, crosses, pot = own_matrices(geo, cell_nodes, face_order, cell_matrix, potential)
    base = owned_part(geo, first, y0, None, pot, None, mats, ())
    behinds, uppers = behind_matrices(geo, halo[1], cell_matrix)
    y1, *sends1 = finish(geo, first, base, halo, crosses, behinds, uppers, sends[1])

    halo = exchange(sends1)
    base = owned_part(geo, later, y1, y0, pot, None, mats, uppers)
    if fg.fits:
        table = field_tables(fg, pois_nodes, pois_face, block_owner, screening, base)
    y2, *sends2 = finish(geo, later, base, halo, crosses, behinds)

    halo = exchange(sends2)
    base = owned_part(geo, later, y2, y1, pot, None, mats, uppers)
    if fg.fits:
        table, base = lax.optimization_barrier((table, base))
        tables = lax.all_to_all(table, "domain", 0, 0, tiled=True)
        parts = (domains * bands, domains, LANES)
        y3, dn, up, spread = finish(
            geo, later, base, halo, crosses, behinds, occ=occupation.reshape(1, columns), parts=parts
        )
        dens = lax.all_to_all(spread, ("band", "domain"), 0, 0, tiled=True)
        halo = exchange((dn, up))
        base = owned_part(geo, first, y3, None, pot, None, mats, uppers)
        column, packed = field_step(fg, dens, tables, pois_matrix, block_owner)
        hartree = packed.reshape(own)
        z1, *sends4 = finish(geo, first, base, halo, crosses, behinds, field=(column, y3))
    else:
        y3, *sends3 = finish(geo, later, base, halo, crosses, behinds)
        halo = exchange(sends3)
        hartree = distributed_field(
            y3, occupation, block_owner[0], pois_matrix, pois_nodes, pois_face[0], screening
        )
        column = jnp.broadcast_to(hartree[:, None], (own, LANES))
        base = owned_part(geo, first, y3, None, pot, column, mats, uppers)
        z1, *sends4 = finish(geo, first, base, halo, crosses, behinds)

    halo = exchange(sends4)
    base = owned_part(geo, later, z1, y3, pot, column, mats, uppers)
    (filtered,) = finish(geo, later, base, halo, crosses, behinds, last=True)
    return filtered, hartree


def solution(mesh):
    return jax.shard_map(
        on_device,
        mesh=mesh,
        in_specs=(
            P("domain", "band"),
            P("domain"),
            P("band"),
            P(),
            P("domain", None),
            P("domain", None),
            P(),
            P("domain", None),
            P("domain", None),
            P("domain"),
            P("domain", None),
        ),
        out_specs=(P("domain", "band"), P("domain")),
        check_vma=False,
    )
```

```python
import functools

import jax
import jax.numpy as jnp
from jax import lax
from jax.experimental import pallas as pl
from jax.experimental.pallas import tpu as pltpu
from jax.sharding import PartitionSpec as P

filter_center = 1.8
filter_half = 2.7
solve_center = 3.25
solve_half = 2.75
solve_ratio = solve_center / solve_half
weight_zero = 1.0 / solve_ratio
weight_one = 1.0 / (2.0 * solve_ratio - weight_zero)
weight_two = 1.0 / (2.0 * solve_ratio - weight_one)

BF = jnp.bfloat16
F32 = jnp.float32
I32 = jnp.int32
LANES = 128
SUBLANES = 8


def up_to(n, m):
    return -(-n // m) * m


def from_behind(array, axis, by):
    length = lax.axis_size(axis)
    return lax.ppermute(array, axis, [(i, (i + by) % length) for i in range(length)])


class Window:
    def __init__(self, start, npc, own, nloc):
        end = start + npc
        self.lo = start // 16 * 16
        self.hi = min(up_to(min(end, own), 16), own)
        self.touches = end > own
        self.low = up_to(max(0, end - nloc), 16)
        self.rows = self.hi - self.lo + self.low


class Geometry:
    def __init__(self, own, share, cells, npc):
        self.own, self.share, self.cells, self.npc = own, share, cells, npc
        nloc = own + share
        stride = nloc // cells
        self.sp = up_to(share, 16)
        self.npl = up_to(npc, LANES)
        self.windows = [Window(c * stride, npc, own, nloc) for c in range(cells)]
        self.touching = [c for c in range(cells) if self.windows[c].touches]
        self.dn_lo = min(self.windows[c].lo for c in self.touching)
        self.low = max(w.low for w in self.windows)
        self.dn_rows = own - self.dn_lo + self.low
        self.table_rows = up_to(cells + 1, SUBLANES)
        self.table_lanes = up_to(max(npc, share), LANES)
        self.table_tiles = self.table_lanes // LANES


def dot(a, b):
    return lax.dot_general(a, b, (((1,), (0,)), ((), ())), preferred_element_type=F32)


def dot_t(a, b):
    return lax.dot_general(a, b, (((1,), (1,)), ((), ())), preferred_element_type=F32)


def vmem_call(kernel, out_shape, scratch=(), in_specs=None, cost=None):
    kwargs = {}
    if in_specs is not None:
        kwargs["in_specs"] = in_specs
    return pl.pallas_call(
        kernel,
        out_shape=out_shape,
        scratch_shapes=list(scratch),
        cost_estimate=cost,
        compiler_params=pltpu.CompilerParams(vmem_limit_bytes=12 * 1024 * 1024),
        **kwargs,
    )


def in_hbm(*arrays):
    return [pltpu.with_memory_space_constraint(a, pltpu.HBM) for a in arrays]


def sds(shape, dtype):
    return jax.ShapeDtypeStruct(shape, dtype)


def one_hot_rows(count, first, nodes):
    ids = lax.broadcasted_iota(I32, (count, nodes.shape[1]), 0) + first
    return jnp.where(ids == nodes, 1.0, 0.0).astype(BF)


def place_table(geo, nodes_ref, face_ref, table):
    table[...] = jnp.full(table.shape, -1, I32)
    table[0 : geo.cells, 0 : geo.npc] = nodes_ref[...]
    table[geo.cells : geo.cells + 1, 0 : geo.share] = face_ref[...]


def place_matrix(geo, matrix_ref, matrix_pad):
    matrix_pad[...] = jnp.zeros(matrix_pad.shape, F32)
    matrix_pad[0 : geo.npc, 0 : geo.npc] = matrix_ref[...].astype(F32)
    return matrix_pad[...].astype(BF)


def table_scratch(geo):
    return pltpu.VMEM((geo.table_rows, geo.table_lanes), I32)


def matrix_scratch(geo):
    return pltpu.VMEM((geo.npl, geo.npl), F32)


def nodes_of(geo, table, c):
    return table[c : c + 1, 0 : geo.npl]


def face_of(geo, table):
    return table[geo.cells : geo.cells + 1, 0 : up_to(geo.share, LANES)]


def owned_picks(geo, c, nodes):
    w = geo.windows[c]
    picks = one_hot_rows(w.hi - w.lo, w.lo, nodes)
    if w.low:
        picks = jnp.concatenate([picks, one_hot_rows(w.low, 0, nodes)], axis=0)
    return picks


def upper_picks(geo, nodes, face):
    by_local = one_hot_rows(face.shape[1], geo.own, nodes)
    by_owner = one_hot_rows(geo.sp, 0, face)
    return dot(by_owner, by_local).astype(BF)


def own_matrices_kernel(geo, *refs):
    table, matrix_ref, pot_ref = refs[:3]
    outs, matrix_pad = refs[3:-1], refs[-1]
    matrix = place_matrix(geo, matrix_ref, matrix_pad)
    face = face_of(geo, table)
    for c in range(geo.cells):
        nodes = nodes_of(geo, table, c)
        own = owned_picks(geo, c, nodes)
        left = dot(own, matrix).astype(BF)
        outs[c][...] = dot_t(left, own).astype(BF)
        if c in geo.touching:
            at = geo.cells + geo.touching.index(c)
            outs[at][...] = dot_t(left, upper_picks(geo, nodes, face)).astype(BF)
    column = outs[-1]
    for r in range(geo.own // LANES):
        row = jnp.broadcast_to(pot_ref[r : r + 1, :], (LANES, LANES))
        column[r * LANES : (r + 1) * LANES, :] = row.T


def own_matrices(geo, table, cell_matrix, lines):
    shapes = [sds((w.rows, w.rows), BF) for w in geo.windows]
    shapes += [sds((geo.windows[c].rows, geo.sp), BF) for c in geo.touching]
    shapes += [sds((geo.own, LANES), F32)]
    outs = vmem_call(
        functools.partial(own_matrices_kernel, geo),
        shapes,
        [matrix_scratch(geo)],
        cost=cost_of(2.0),
    )(table, cell_matrix, lines)
    n = geo.cells
    return outs[:n], outs[n:-1], outs[-1]


def behind_matrices_kernel(geo, *refs):
    sent_ref, matrix_ref = refs[:2]
    outs = refs[2:-2]
    table, matrix_pad = refs[-2:]
    for t in range(geo.table_tiles):
        at = geo.dn_rows + 2 * t * geo.table_rows
        digits = sent_ref[at : at + 2 * geo.table_rows, :].astype(F32)
        value = digits[: geo.table_rows] * LANES + digits[geo.table_rows :] - 1.0
        table[:, t * LANES : (t + 1) * LANES] = value.astype(I32)
    matrix = place_matrix(geo, matrix_ref, matrix_pad)
    face = face_of(geo, table)
    count = len(geo.touching)
    for at, c in enumerate(geo.touching):
        nodes = nodes_of(geo, table, c)
        upper = upper_picks(geo, nodes, face)
        left = dot(upper, matrix).astype(BF)
        outs[at][...] = dot_t(left, owned_picks(geo, c, nodes)).astype(BF)
        outs[count + at][...] = dot_t(left, upper).astype(BF)


def behind_matrices(geo, sent, cell_matrix):
    shapes = [sds((geo.sp, geo.windows[c].rows), BF) for c in geo.touching]
    shapes += [sds((geo.sp, geo.sp), BF) for _ in geo.touching]
    outs = vmem_call(
        functools.partial(behind_matrices_kernel, geo),
        shapes,
        [table_scratch(geo), matrix_scratch(geo)],
        cost=cost_of(1.0),
    )(sent, cell_matrix)
    n = len(geo.touching)
    return outs[:n], outs[n:]


def cost_of(us):
    return pl.CostEstimate(flops=0, bytes_accessed=int(us * 3.0e6), transcendentals=0)


def write_sends(geo, y_ref, dn_ref, up_ref):
    top = geo.own - geo.dn_lo
    dn_ref[0:top, :] = y_ref[geo.dn_lo : geo.own, :].astype(BF)
    dn_ref[top : top + geo.low, :] = y_ref[0 : geo.low, :].astype(BF)
    up_ref[...] = y_ref[0 : geo.sp, :].astype(BF)


def send_shapes(geo, columns):
    return [sds((geo.dn_rows, columns), BF), sds((geo.sp, columns), BF)]


def fetch(pairs, sems):
    copies = [pltpu.make_async_copy(src, dst, sems.at[i]) for i, (src, dst) in enumerate(pairs)]
    for copy in copies:
        copy.start()
    return copies


def pack_kernel(geo, extra, y_hbm, nodes_hbm, face_hbm, *refs):
    sources, refs = refs[:extra], refs[extra:]
    dn_ref, up_ref, y, table = refs[:4]
    kept, (nodes, face, sems) = refs[4 : 4 + extra], refs[4 + extra :]
    cuts = sorted({0, max(geo.sp, geo.low), geo.dn_lo, geo.own})
    spans = list(zip(cuts[:-1], cuts[1:]))
    pairs = [(nodes_hbm, nodes), (face_hbm, face)]
    pairs += [(y_hbm.at[pl.ds(a, b - a)], y.at[pl.ds(a, b - a)]) for a, b in spans]
    pairs += list(zip(sources, kept))
    copies = fetch(pairs, sems)
    copies[0].wait()
    copies[1].wait()
    place_table(geo, nodes, face, table)
    for t in range(geo.table_tiles):
        at = geo.dn_rows + 2 * t * geo.table_rows
        value = table[:, t * LANES : (t + 1) * LANES] + 1
        high = jnp.right_shift(value, 7).astype(F32)
        low = jnp.bitwise_and(value, LANES - 1).astype(F32)
        digits = jnp.concatenate([high, low], axis=0).astype(BF)
        dn_ref[at : at + 2 * geo.table_rows, :] = digits
    for copy in copies[2:]:
        copy.wait()
    write_sends(geo, y, dn_ref, up_ref)


def pack(geo, y, cell_nodes, face_order, *others):
    dn, up = send_shapes(geo, y.shape[1])
    rows = geo.dn_rows + 2 * geo.table_rows * geo.table_tiles
    dn, up, y, table, *others = vmem_call(
        functools.partial(pack_kernel, geo, len(others)),
        [
            sds((rows, y.shape[1]), BF),
            up,
            sds(y.shape, F32),
            sds((geo.table_rows, geo.table_lanes), I32),
            *[sds(a.shape, a.dtype) for a in others],
        ],
        [
            pltpu.VMEM(cell_nodes.shape, I32),
            pltpu.VMEM(face_order.shape, I32),
            pltpu.SemaphoreType.DMA((5 + len(others),)),
        ],
        in_specs=[pl.BlockSpec(memory_space=pltpu.HBM)] * (3 + len(others)),
        cost=cost_of(1.0),
    )(*in_hbm(y, cell_nodes, face_order, *others))
    return (dn, up), y, table, others


def owned_part_kernel(geo, scale, has_prev, has_field, has_upper, *refs):
    refs = list(refs)
    base_ref = refs.pop()
    y_ref = refs.pop(0)
    prev_ref = refs.pop(0) if has_prev else None
    pot_ref = refs.pop(0)
    field_ref = refs.pop(0) if has_field else None
    mats = [refs.pop(0) for _ in range(geo.cells)]
    y = y_ref[...]
    factor = pot_ref[...]
    if has_field:
        factor = factor + field_ref[...]
    value = ((factor - filter_center) * scale) * y
    if has_prev:
        value = value - prev_ref[...]
    base_ref[...] = value
    x = y.astype(BF)
    for c in range(geo.cells):
        w = geo.windows[c]
        own = w.hi - w.lo
        rows = x[w.lo : w.hi, :]
        if w.low:
            rows = jnp.concatenate([rows, x[0 : w.low, :]], axis=0)
        product = dot(mats[c][...], rows) * scale
        base_ref[w.lo : w.hi, :] += product[:own]
        if w.low:
            base_ref[0 : w.low, :] += product[own:]
    if has_upper:
        for upper in refs:
            base_ref[0 : geo.sp, :] += dot(upper[...], x[0 : geo.sp, :]) * scale


def owned_part(geo, scale, y, prev, pot, field, mats, uppers):
    args = [y] + ([prev] if prev is not None else []) + [pot]
    args += [field] if field is not None else []
    args += list(mats) + list(uppers)
    return vmem_call(
        functools.partial(
            owned_part_kernel, geo, scale, prev is not None, field is not None, bool(uppers)
        ),
        sds(y.shape, F32),
        cost=cost_of(2.0),
    )(*args)


def add_halo(geo, scale, y_ref, up_ref, dn_ref, crosses, behinds, uppers, own_up_ref):
    h_up = up_ref[...]
    h_dn = dn_ref[...]
    for at, c in enumerate(geo.touching):
        w = geo.windows[c]
        own = w.hi - w.lo
        product = dot(crosses[at][...], h_up) * scale
        y_ref[w.lo : w.hi, :] += product[:own]
        if w.low:
            y_ref[0 : w.low, :] += product[own:]
    total = None
    for at, c in enumerate(geo.touching):
        w = geo.windows[c]
        first = w.lo - geo.dn_lo
        term = dot(behinds[at][...], h_dn[first : first + w.rows, :])
        total = term if total is None else total + term
        if uppers:
            total = total + dot(uppers[at][...], own_up_ref[...])
    y_ref[0 : geo.sp, :] += total * scale


def write_density(y_ref, occ_ref, dens_ref, row_pad):
    _, blocks, _ = dens_ref.shape
    own = y_ref.shape[0]
    length = own // blocks
    y = y_ref[...]
    terms = y * y * occ_ref[...]
    high = terms.astype(BF)
    low = (terms - high.astype(F32)).astype(BF)
    ones = jnp.ones((SUBLANES, terms.shape[1]), BF)
    summed = dot_t(ones, high) + dot_t(ones, low)
    row_pad[...] = jnp.zeros(row_pad.shape, F32)
    for j in range(blocks):
        row_pad[j : j + 1, 0:length] = summed[0:1, j * length : (j + 1) * length]
    dens_ref[...] = jnp.broadcast_to(row_pad[...][None], dens_ref.shape)


def finish_kernel(geo, scale, has_upper, mode, *refs):
    refs = list(refs)
    n = len(geo.touching)
    base_ref, up_ref, dn_ref = refs[:3]
    refs = refs[3:]
    crosses, refs = refs[:n], refs[n:]
    behinds, refs = refs[:n], refs[n:]
    uppers, own_up = [], None
    if has_upper:
        uppers, refs = refs[:n], refs[n:]
        own_up = refs.pop(0)
    occ_ref = refs.pop(0) if mode == "density" else None
    if mode == "field":
        column_ref, before_ref = refs.pop(0), refs.pop(0)
    y_ref = refs.pop(0)
    if mode == "field":
        y_ref[...] = base_ref[...] + (column_ref[...] * scale) * before_ref[...]
    else:
        y_ref[...] = base_ref[...]
    add_halo(geo, scale, y_ref, up_ref, dn_ref, crosses, behinds, uppers, own_up)
    if mode != "last":
        write_sends(geo, y_ref, refs[0], refs[1])
    if mode == "density":
        write_density(y_ref, occ_ref, refs[2], refs[3])


def finish(geo, scale, base, halo, crosses, behinds, uppers=(), own_up=None, occ=None, parts=None, field=None, last=False):
    columns = base.shape[1]
    args = [base, halo[0], halo[1], *crosses, *behinds, *uppers]
    if uppers:
        args.append(own_up)
    shapes = [sds(base.shape, F32)]
    scratch = []
    mode = "plain"
    if last:
        mode = "last"
    else:
        shapes += send_shapes(geo, columns)
    if field is not None:
        mode = "field"
        args += list(field)
    if occ is not None:
        mode = "density"
        args.append(occ)
        shapes.append(sds(parts, F32))
        scratch.append(pltpu.VMEM(parts[1:], F32))
    return vmem_call(
        functools.partial(finish_kernel, geo, scale, bool(uppers), mode),
        shapes,
        scratch,
        cost=cost_of(1.0),
    )(*args)


class FieldGeometry:
    def __init__(self, domains, own, share, cells, npc):
        self.domains, self.own, self.share, self.cells, self.npc = domains, own, share, cells, npc
        self.block = own // domains
        self.rows = up_to(npc, LANES) // LANES
        self.blocks = domains + 1
        self.at_inverse = cells * self.rows
        self.at_face = self.at_inverse + cells * self.blocks
        self.at_face_inverse = self.at_face + 1
        self.at_owner = self.at_face + 2
        self.codes = self.at_face + 3
        self.at_screen = up_to(self.codes, 2) // 2
        self.table_rows = up_to(self.at_screen + domains, SUBLANES)
        self.size = self.rows * LANES
        self.fits = (
            domains == SUBLANES
            and own % (domains * SUBLANES) == 0
            and own % LANES == 0
            and share <= self.block <= LANES
            and max(npc, self.blocks * LANES) < CODE_BASE - 1
        )


CODE_BASE = 2048
CODE_BITS = 11


def pieces(length, blocks):
    found = []
    for j in range(blocks):
        done = 0
        while done < length:
            at = j * length + done
            count = min(length - done, LANES - at % LANES)
            found.append((at // LANES, at % LANES, j, done, count))
            done += count
    return found


def column_of(row):
    return jnp.broadcast_to(row, (LANES, LANES)).T


def field_tables_kernel(fg, *refs):
    nodes_ref, face_ref, owner_ref, screen_ref = refs[:4]
    table_ref, pad, one, packed = refs[5:]
    one[...] = jnp.full(one.shape, -1.0, F32)
    pad[...] = jnp.full(pad.shape, -1, I32)
    pad[0 : fg.cells, 0 : fg.npc] = nodes_ref[...]
    sub = lax.broadcasted_iota(I32, (LANES, LANES), 0)
    wide_lane = lax.broadcasted_iota(I32, (LANES, LANES), 1)
    for c in range(fg.cells):
        columns = []
        for r in range(fg.rows):
            nodes = pad[c : c + 1, r * LANES : (r + 1) * LANES]
            block = jnp.zeros((1, LANES), I32)
            for b in range(1, fg.blocks):
                block = block + jnp.where(nodes >= b * fg.block, 1, 0)
            code = jnp.where(nodes < 0, -1, nodes + block * (LANES - fg.block))
            code = code.astype(F32)
            at = c * fg.rows + r
            one[at : at + 1, :] = code
            columns.append(column_of(code))
        for b in range(fg.blocks):
            target = (wide_lane + b * LANES).astype(F32)
            found = jnp.zeros((LANES, LANES), F32)
            for r in range(fg.rows):
                position = (sub + (r * LANES + 1)).astype(F32)
                found = jnp.where(columns[r] == target, position, found)
            at = fg.at_inverse + c * fg.blocks + b
            one[at : at + 1, :] = jnp.sum(found, axis=0, keepdims=True) - 1.0
    one[fg.at_face : fg.at_face + 1, 0 : fg.share] = face_ref[...].astype(F32)
    column = column_of(one[fg.at_face : fg.at_face + 1, :])
    hits = jnp.where(column == wide_lane.astype(F32), (sub + 1).astype(F32), 0.0)
    one[fg.at_face_inverse : fg.at_face_inverse + 1, :] = jnp.sum(hits, axis=0, keepdims=True) - 1.0
    one[fg.at_owner : fg.at_owner + 1, 0 : fg.domains] = owner_ref[...].astype(F32)
    packed[...] = jnp.zeros(packed.shape, F32)
    half = fg.at_screen
    packed[0:half, :] = (one[0:half, :] + 1.0) + (one[half : 2 * half, :] + 1.0) * CODE_BASE
    for row, lane, j, offset, count in pieces(fg.block, fg.domains):
        at = fg.at_screen + j
        packed[at : at + 1, offset : offset + count] = screen_ref[row : row + 1, lane : lane + count]
    table_ref[...] = jnp.broadcast_to(packed[...][None], table_ref.shape)


def field_tables(fg, pois_nodes, pois_face, block_owner, lines, after):
    specs = [pl.BlockSpec(memory_space=pltpu.VMEM)] * 4 + [pl.BlockSpec(memory_space=pl.ANY)]
    return vmem_call(
        functools.partial(field_tables_kernel, fg),
        sds((fg.domains, fg.table_rows, LANES), F32),
        [
            pltpu.VMEM((up_to(fg.cells, SUBLANES), fg.size), I32),
            pltpu.VMEM((up_to(2 * fg.at_screen, SUBLANES), LANES), F32),
            pltpu.VMEM((fg.table_rows, LANES), F32),
        ],
        in_specs=specs,
        cost=cost_of(1.0),
    )(pois_nodes, pois_face, block_owner, lines, after)


def lanes_of(values, index):
    return jnp.take_along_axis(values, index, axis=1, mode="promise_in_bounds")


def field_codes_kernel(fg, table_ref, codes_ref, screen_ref, lines):
    domains, half = fg.domains, fg.at_screen
    for at in range(fg.table_rows):
        for d in range(domains):
            lines[at, d : d + 1, :] = table_ref[d, at : at + 1, :]
    for at in range(half):
        both = lines[at].astype(I32)
        for here, code in ((at, jnp.bitwise_and(both, CODE_BASE - 1) - 1), (half + at, jnp.right_shift(both, CODE_BITS) - 1)):
            if here == fg.at_face_inverse:
                code = pltpu.roll(code, 1, 0)
            if here < fg.at_owner:
                codes_ref[here] = code
            elif here == fg.at_owner:
                owner = code.astype(F32)
    part = lax.broadcasted_iota(I32, (domains, LANES), 0).astype(F32)
    mine = jnp.zeros((domains, LANES), F32)
    here = lax.axis_index("domain").astype(F32)
    for q in range(domains):
        column = column_of(owner[q : q + 1, :])[0:domains, :]
        inverse = jnp.zeros((domains, LANES), F32)
        for j in range(domains):
            inverse = jnp.where(column[j : j + 1, :] == part, float(j), inverse)
        codes_ref[fg.at_owner + q] = inverse.astype(I32)
        mine = jnp.where(here == float(q), column, mine)
    codes_ref[fg.at_owner + domains] = mine.astype(I32)
    for q in range(domains):
        screen_ref[q] = lines[fg.at_screen + q]


def field_codes(fg, table):
    return vmem_call(
        functools.partial(field_codes_kernel, fg),
        [
            sds((fg.at_owner + fg.domains + 1, fg.domains, LANES), I32),
            sds((fg.domains, fg.domains, LANES), F32),
        ],
        [pltpu.VMEM((fg.table_rows, fg.domains, LANES), F32)],
        cost=cost_of(1.0),
    )(table)


def rows_of(values, index):
    return jnp.take_along_axis(values, index, axis=0, mode="promise_in_bounds")


def field_solve(fg, dens_ref, codes, screen_ref, matrix_ref, high_ref, low_ref, rows, copies):
    domains, cells = fg.domains, fg.cells
    bands = dens_ref.shape[0] // domains
    valid = lax.broadcasted_iota(I32, (domains, LANES), 1) < fg.block
    source = []
    for q in range(domains):
        density = dens_ref[q]
        for b in range(1, bands):
            density = density + dens_ref[b * domains + q]
        source.append(rows_of(density, codes[fg.at_owner + q]))
    screen = [screen_ref[q] for q in range(domains)]

    def lookup(sources, code):
        lane = jnp.bitwise_and(code, LANES - 1)
        which = jnp.right_shift(code, 7)
        total = jnp.zeros((domains, LANES), F32)
        for b, values in enumerate(sources):
            total = jnp.where(which == b, lanes_of(values, lane), total)
        return total

    def operator(field):
        ahead = pltpu.roll(field[0], domains - 1, 0)
        upper = lookup([ahead], codes[fg.at_face])
        local = list(field) + [upper]
        for c in range(cells):
            for r in range(fg.rows):
                rows[c * domains : (c + 1) * domains, r * LANES : (r + 1) * LANES] = lookup(local, codes[c * fg.rows + r])
        if copies:
            copies.pop().wait()
            full = matrix_ref[...]
            top = full.astype(BF)
            high_ref[...] = top
            low_ref[...] = (full - top.astype(F32)).astype(BF)
        picked = rows[:, 0 : fg.npc]
        high = picked.astype(BF)
        low = (picked - high.astype(F32)).astype(BF)
        both = dot(jnp.concatenate([high, low], axis=0), high_ref[...])
        half_rows = cells * domains
        rows[:, 0 : fg.npc] = both[:half_rows] + (both[half_rows:] + dot(high, low_ref[...]))
        out = []
        for b in range(fg.blocks):
            total = None
            for c in range(cells):
                sources = [
                    rows[c * domains : (c + 1) * domains, r * LANES : (r + 1) * LANES]
                    for r in range(fg.rows)
                ]
                term = lookup(sources, codes[fg.at_inverse + c * fg.blocks + b])
                total = term if total is None else total + term
            out.append(total)
        arriving = pltpu.roll(out[domains], 1, 0)
        out[0] = out[0] + lookup([arriving], codes[fg.at_face_inverse])
        return [jnp.where(valid, screen[q] * field[q] + out[q], 0.0) for q in range(domains)]

    step_one = [s * (1.0 / solve_center) for s in source]
    applied = operator(step_one)
    residual = [s - a for s, a in zip(source, applied)]
    a1, b1 = weight_one * weight_zero, 2.0 * weight_one / solve_half
    step_two = [a1 * e + b1 * r for e, r in zip(step_one, residual)]
    applied = operator(step_two)
    residual = [r - a for r, a in zip(residual, applied)]
    a2, b2 = weight_two * weight_one, 2.0 * weight_two / solve_half
    step_three = [a2 * e + b2 * r for e, r in zip(step_two, residual)]
    return [(x + y) + z for x, y, z in zip(step_one, step_two, step_three)]


def field_kernel(fg, dens_ref, codes, screen_ref, matrix_hbm, column_ref, hartree_ref, rows, phi, mine, matrix_ref, high_ref, low_ref, sems):
    copies = fetch([(matrix_hbm, matrix_ref)], sems)
    blocks = field_solve(fg, dens_ref, codes, screen_ref, matrix_ref, high_ref, low_ref, rows, copies)
    for q in range(fg.domains):
        phi[q] = blocks[q]
    here = lax.axis_index("domain")
    mine[...] = rows_of(phi[here], codes[fg.at_owner + fg.domains])
    for j in range(fg.domains):
        column = column_of(mine[j : j + 1, :])
        column_ref[j * fg.block : (j + 1) * fg.block, :] = column[0 : fg.block, :]
    for row, lane, j, offset, count in pieces(fg.block, fg.domains):
        hartree_ref[row : row + 1, lane : lane + count] = mine[j : j + 1, offset : offset + count]


def field_step(fg, dens, codes, screen, matrix):
    vmem = pl.BlockSpec(memory_space=pltpu.VMEM)
    tile = (fg.domains, LANES)
    return vmem_call(
        functools.partial(field_kernel, fg),
        [sds((fg.own, LANES), F32), sds((fg.own // LANES, LANES), F32)],
        [
            pltpu.VMEM((fg.cells * fg.domains, fg.size), F32),
            pltpu.VMEM((fg.domains, *tile), F32),
            pltpu.VMEM(tile, F32),
            pltpu.VMEM(matrix.shape, F32),
            pltpu.VMEM(matrix.shape, BF),
            pltpu.VMEM(matrix.shape, BF),
            pltpu.SemaphoreType.DMA((1,)),
        ],
        in_specs=[vmem] * 3 + [pl.BlockSpec(memory_space=pltpu.HBM)],
        cost=cost_of(4.0),
    )(dens, codes, screen, *in_hbm(matrix))


def assembled(owned_rows, face_row, terms):
    owned_count = owned_rows.shape[0]
    shared = face_row.shape[0]
    coming = jnp.take(from_behind(owned_rows[:shared], "domain", -1), face_row, axis=0)
    partial_value = terms(jnp.concatenate([owned_rows, coming], axis=0))
    upper_rows = partial_value[owned_count:]
    ordered = jnp.zeros_like(upper_rows).at[face_row].set(upper_rows)
    arrived = from_behind(ordered, "domain", 1)
    return partial_value[:owned_count].at[:shared].add(arrived)


def field_terms(local_rows, pois_matrix, node_ids):
    cell_vals = jnp.take(local_rows, node_ids, axis=0)
    product = jnp.einsum(
        "pq,cq->cp",
        pois_matrix,
        cell_vals,
        precision=lax.Precision.HIGHEST,
        preferred_element_type=F32,
    )
    return jnp.zeros(local_rows.shape, F32).at[node_ids.reshape(-1)].add(product.reshape(-1))


def reshuffle(blocks):
    return lax.all_to_all(blocks, "domain", split_axis=0, concat_axis=0, tiled=True)


def distributed_field(y, occupation, owner_row, pois_matrix, pois_nodes, field_face, screening):
    owned_count = y.shape[0]
    domains = lax.axis_size("domain")
    block_len = owned_count // domains
    partial_value = jnp.dot(
        y * y, occupation, precision=lax.Precision.HIGHEST, preferred_element_type=F32
    )
    summed = lax.psum(partial_value, "band")
    arranged = (
        jnp.zeros((domains, block_len), F32)
        .at[owner_row]
        .set(summed.reshape(domains, block_len))
    )
    source = reshuffle(arranged).reshape(owned_count)

    def field_operator(vector):
        return (
            assembled(
                vector, field_face, lambda local: field_terms(local, pois_matrix, pois_nodes)
            )
            + screening * vector
        )

    step_one = source / solve_center
    residual = source - field_operator(step_one)
    step_two = weight_one * weight_zero * step_one + 2.0 * weight_one / solve_half * residual
    residual = residual - field_operator(step_two)
    step_three = weight_two * weight_one * step_two + 2.0 * weight_two / solve_half * residual
    solved = step_one + step_two + step_three
    returned = reshuffle(solved.reshape(domains, block_len))
    return jnp.take(returned, owner_row, axis=0).reshape(owned_count)


def exchange(sends):
    dn, up = sends
    h_dn = from_behind(dn, "domain", 1)
    h_up = from_behind(up, "domain", -1)
    return h_up, h_dn


def on_device(
    orbitals,
    potential,
    occupation,
    cell_matrix,
    cell_nodes,
    face_order,
    pois_matrix,
    pois_nodes,
    pois_face,
    screening,
    block_owner,
):
    domains = lax.axis_size("domain")
    bands = lax.axis_size("band")
    own, columns = orbitals.shape
    geo = Geometry(own, face_order.shape[1], cell_nodes.shape[0], cell_nodes.shape[1])
    fg = FieldGeometry(domains, own, pois_face.shape[1], pois_nodes.shape[0], pois_nodes.shape[1])
    first, later = 1.0 / filter_half, 2.0 / filter_half

    others = [cell_matrix, potential.reshape(own // LANES, LANES)]
    if fg.fits:
        others += [pois_nodes, pois_face, block_owner, screening.reshape(own // LANES, LANES)]
        others.append(occupation.reshape(1, columns))
    sends, y0, nodes, (matrix, lines, *others) = pack(geo, orbitals, cell_nodes, face_order, *others)
    halo = exchange(sends)
    mats, crosses, pot = own_matrices(geo, nodes, matrix, lines)
    base = owned_part(geo, first, y0, None, pot, None, mats, ())
    behinds, uppers = behind_matrices(geo, halo[1], matrix)
    y1, *sends1 = finish(geo, first, base, halo, crosses, behinds, uppers, sends[1])

    halo = exchange(sends1)
    base = owned_part(geo, later, y1, y0, pot, None, mats, uppers)
    if fg.fits:
        *others, weights = others
        table = field_tables(fg, *others, base)
        tables = lax.all_to_all(table, "domain", 0, 0, tiled=True)
    y2, *sends2 = finish(geo, later, base, halo, crosses, behinds)

    halo = exchange(sends2)
    base = owned_part(geo, later, y2, y1, pot, None, mats, uppers)
    if fg.fits:
        parts = (domains * bands, domains, LANES)
        y3, dn, up, spread = finish(
            geo, later, base, halo, crosses, behinds, occ=weights, parts=parts
        )
        dens = lax.all_to_all(spread, ("band", "domain"), 0, 0, tiled=True)
        halo = exchange((dn, up))
        base = owned_part(geo, first, y3, None, pot, None, mats, uppers)
        codes, screen = field_codes(fg, tables)
        column, packed = field_step(fg, dens, codes, screen, pois_matrix)
        hartree = packed.reshape(own)
        z1, *sends4 = finish(geo, first, base, halo, crosses, behinds, field=(column, y3))
    else:
        y3, *sends3 = finish(geo, later, base, halo, crosses, behinds)
        halo = exchange(sends3)
        hartree = distributed_field(
            y3, occupation, block_owner[0], pois_matrix, pois_nodes, pois_face[0], screening
        )
        column = jnp.broadcast_to(hartree[:, None], (own, LANES))
        base = owned_part(geo, first, y3, None, pot, column, mats, uppers)
        z1, *sends4 = finish(geo, first, base, halo, crosses, behinds)

    halo = exchange(sends4)
    base = owned_part(geo, later, z1, y3, pot, column, mats, uppers)
    (filtered,) = finish(geo, later, base, halo, crosses, behinds, last=True)
    return filtered, hartree


def solution(mesh):
    return jax.shard_map(
        on_device,
        mesh=mesh,
        in_specs=(
            P("domain", "band"),
            P("domain"),
            P("band"),
            P(),
            P("domain", None),
            P("domain", None),
            P(),
            P("domain", None),
            P("domain", None),
            P("domain"),
            P("domain", None),
        ),
        out_specs=(P("domain", "band"), P("domain")),
        check_vma=False,
    )
```

```python
import functools

import jax
import jax.numpy as jnp
from jax import lax
from jax.experimental import pallas as pl
from jax.experimental.pallas import tpu as pltpu
from jax.sharding import PartitionSpec as P

filter_center = 1.8
filter_half = 2.7
solve_center = 3.25
solve_half = 2.75
solve_ratio = solve_center / solve_half
weight_zero = 1.0 / solve_ratio
weight_one = 1.0 / (2.0 * solve_ratio - weight_zero)
weight_two = 1.0 / (2.0 * solve_ratio - weight_one)

BF = jnp.bfloat16
F32 = jnp.float32
I32 = jnp.int32
LANES = 128
SUBLANES = 8


def up_to(n, m):
    return -(-n // m) * m


def from_behind(array, axis, by):
    length = lax.axis_size(axis)
    return lax.ppermute(array, axis, [(i, (i + by) % length) for i in range(length)])


class Window:
    def __init__(self, start, npc, own, nloc):
        end = start + npc
        self.lo = start // 16 * 16
        self.hi = min(up_to(min(end, own), 16), own)
        self.touches = end > own
        self.low = up_to(max(0, end - nloc), 16)
        self.rows = self.hi - self.lo + self.low


class Geometry:
    def __init__(self, own, share, cells, npc):
        self.own, self.share, self.cells, self.npc = own, share, cells, npc
        nloc = own + share
        stride = nloc // cells
        self.sp = up_to(share, 16)
        self.npl = up_to(npc, LANES)
        self.windows = [Window(c * stride, npc, own, nloc) for c in range(cells)]
        self.touching = [c for c in range(cells) if self.windows[c].touches]
        self.dn_lo = min(self.windows[c].lo for c in self.touching)
        self.low = max(w.low for w in self.windows)
        self.dn_rows = own - self.dn_lo + self.low
        self.table_rows = up_to(cells + 1, SUBLANES)
        self.table_lanes = up_to(max(npc, share), LANES)
        self.table_tiles = self.table_lanes // LANES


def dot(a, b):
    return lax.dot_general(a, b, (((1,), (0,)), ((), ())), preferred_element_type=F32)


def dot_t(a, b):
    return lax.dot_general(a, b, (((1,), (1,)), ((), ())), preferred_element_type=F32)


def vmem_call(kernel, out_shape, scratch=(), in_specs=None, cost=None):
    kwargs = {}
    if in_specs is not None:
        kwargs["in_specs"] = in_specs
    return pl.pallas_call(
        kernel,
        out_shape=out_shape,
        scratch_shapes=list(scratch),
        cost_estimate=cost,
        compiler_params=pltpu.CompilerParams(vmem_limit_bytes=12 * 1024 * 1024),
        **kwargs,
    )


def in_hbm(*arrays):
    return [pltpu.with_memory_space_constraint(a, pltpu.HBM) for a in arrays]


def sds(shape, dtype):
    return jax.ShapeDtypeStruct(shape, dtype)


def one_hot_rows(count, first, nodes):
    ids = lax.broadcasted_iota(I32, (count, nodes.shape[1]), 0) + first
    return jnp.where(ids == nodes, 1.0, 0.0).astype(BF)


def place_table(geo, nodes_ref, face_ref, table):
    table[...] = jnp.full(table.shape, -1, I32)
    table[0 : geo.cells, 0 : geo.npc] = nodes_ref[...]
    table[geo.cells : geo.cells + 1, 0 : geo.share] = face_ref[...]


def place_matrix(geo, matrix_ref, matrix_pad):
    matrix_pad[...] = jnp.zeros(matrix_pad.shape, F32)
    matrix_pad[0 : geo.npc, 0 : geo.npc] = matrix_ref[...].astype(F32)
    return matrix_pad[...].astype(BF)


def table_scratch(geo):
    return pltpu.VMEM((geo.table_rows, geo.table_lanes), I32)


def matrix_scratch(geo):
    return pltpu.VMEM((geo.npl, geo.npl), F32)


def nodes_of(geo, table, c):
    return table[c : c + 1, 0 : geo.npl]


def face_of(geo, table):
    return table[geo.cells : geo.cells + 1, 0 : up_to(geo.share, LANES)]


def owned_picks(geo, c, nodes):
    w = geo.windows[c]
    picks = one_hot_rows(w.hi - w.lo, w.lo, nodes)
    if w.low:
        picks = jnp.concatenate([picks, one_hot_rows(w.low, 0, nodes)], axis=0)
    return picks


def upper_picks(geo, nodes, face):
    by_local = one_hot_rows(face.shape[1], geo.own, nodes)
    by_owner = one_hot_rows(geo.sp, 0, face)
    return dot(by_owner, by_local).astype(BF)


def own_matrices_kernel(geo, *refs):
    table, matrix_ref, pot_ref = refs[:3]
    outs, matrix_pad = refs[3:-1], refs[-1]
    matrix = place_matrix(geo, matrix_ref, matrix_pad)
    face = face_of(geo, table)
    for c in range(geo.cells):
        nodes = nodes_of(geo, table, c)
        own = owned_picks(geo, c, nodes)
        left = dot(own, matrix).astype(BF)
        outs[c][...] = dot_t(left, own).astype(BF)
        if c in geo.touching:
            at = geo.cells + geo.touching.index(c)
            outs[at][...] = dot_t(left, upper_picks(geo, nodes, face)).astype(BF)
    column = outs[-1]
    for r in range(geo.own // LANES):
        row = jnp.broadcast_to(pot_ref[r : r + 1, :], (LANES, LANES))
        column[r * LANES : (r + 1) * LANES, :] = row.T


def own_matrices(geo, table, cell_matrix, lines):
    shapes = [sds((w.rows, w.rows), BF) for w in geo.windows]
    shapes += [sds((geo.windows[c].rows, geo.sp), BF) for c in geo.touching]
    shapes += [sds((geo.own, LANES), F32)]
    outs = vmem_call(
        functools.partial(own_matrices_kernel, geo),
        shapes,
        [matrix_scratch(geo)],
        cost=cost_of(2.0),
    )(table, cell_matrix, lines)
    n = geo.cells
    return outs[:n], outs[n:-1], outs[-1]


def behind_matrices_kernel(geo, *refs):
    sent_ref, matrix_ref = refs[:2]
    outs = refs[2:-2]
    table, matrix_pad = refs[-2:]
    for t in range(geo.table_tiles):
        at = geo.dn_rows + 2 * t * geo.table_rows
        digits = sent_ref[at : at + 2 * geo.table_rows, :].astype(F32)
        value = digits[: geo.table_rows] * LANES + digits[geo.table_rows :] - 1.0
        table[:, t * LANES : (t + 1) * LANES] = value.astype(I32)
    matrix = place_matrix(geo, matrix_ref, matrix_pad)
    face = face_of(geo, table)
    count = len(geo.touching)
    for at, c in enumerate(geo.touching):
        nodes = nodes_of(geo, table, c)
        upper = upper_picks(geo, nodes, face)
        left = dot(upper, matrix).astype(BF)
        outs[at][...] = dot_t(left, owned_picks(geo, c, nodes)).astype(BF)
        outs[count + at][...] = dot_t(left, upper).astype(BF)


def behind_matrices(geo, sent, cell_matrix):
    shapes = [sds((geo.sp, geo.windows[c].rows), BF) for c in geo.touching]
    shapes += [sds((geo.sp, geo.sp), BF) for _ in geo.touching]
    outs = vmem_call(
        functools.partial(behind_matrices_kernel, geo),
        shapes,
        [table_scratch(geo), matrix_scratch(geo)],
        cost=cost_of(1.0),
    )(sent, cell_matrix)
    n = len(geo.touching)
    return outs[:n], outs[n:]


def cost_of(us):
    return pl.CostEstimate(flops=0, bytes_accessed=int(us * 3.0e6), transcendentals=0)


def write_sends(geo, y_ref, dn_ref, up_ref):
    top = geo.own - geo.dn_lo
    dn_ref[0:top, :] = y_ref[geo.dn_lo : geo.own, :].astype(BF)
    dn_ref[top : top + geo.low, :] = y_ref[0 : geo.low, :].astype(BF)
    up_ref[...] = y_ref[0 : geo.sp, :].astype(BF)


def send_shapes(geo, columns):
    return [sds((geo.dn_rows, columns), BF), sds((geo.sp, columns), BF)]


def fetch(pairs, sems):
    copies = [pltpu.make_async_copy(src, dst, sems.at[i]) for i, (src, dst) in enumerate(pairs)]
    for copy in copies:
        copy.start()
    return copies


def pack_kernel(geo, extra, y_hbm, nodes_hbm, face_hbm, *refs):
    sources, refs = refs[:extra], refs[extra:]
    dn_ref, up_ref, y, table = refs[:4]
    kept, (nodes, face, sems) = refs[4 : 4 + extra], refs[4 + extra :]
    cuts = sorted({0, max(geo.sp, geo.low), geo.dn_lo, geo.own})
    spans = list(zip(cuts[:-1], cuts[1:]))
    pairs = [(nodes_hbm, nodes), (face_hbm, face)]
    pairs += [(y_hbm.at[pl.ds(a, b - a)], y.at[pl.ds(a, b - a)]) for a, b in spans]
    pairs += list(zip(sources, kept))
    copies = fetch(pairs, sems)
    copies[0].wait()
    copies[1].wait()
    place_table(geo, nodes, face, table)
    for t in range(geo.table_tiles):
        at = geo.dn_rows + 2 * t * geo.table_rows
        value = table[:, t * LANES : (t + 1) * LANES] + 1
        high = jnp.right_shift(value, 7).astype(F32)
        low = jnp.bitwise_and(value, LANES - 1).astype(F32)
        digits = jnp.concatenate([high, low], axis=0).astype(BF)
        dn_ref[at : at + 2 * geo.table_rows, :] = digits
    for copy in copies[2:]:
        copy.wait()
    write_sends(geo, y, dn_ref, up_ref)


def pack(geo, y, cell_nodes, face_order, *others):
    dn, up = send_shapes(geo, y.shape[1])
    rows = geo.dn_rows + 2 * geo.table_rows * geo.table_tiles
    dn, up, y, table, *others = vmem_call(
        functools.partial(pack_kernel, geo, len(others)),
        [
            sds((rows, y.shape[1]), BF),
            up,
            sds(y.shape, F32),
            sds((geo.table_rows, geo.table_lanes), I32),
            *[sds(a.shape, a.dtype) for a in others],
        ],
        [
            pltpu.VMEM(cell_nodes.shape, I32),
            pltpu.VMEM(face_order.shape, I32),
            pltpu.SemaphoreType.DMA((5 + len(others),)),
        ],
        in_specs=[pl.BlockSpec(memory_space=pltpu.HBM)] * (3 + len(others)),
        cost=cost_of(1.0),
    )(*in_hbm(y, cell_nodes, face_order, *others))
    return (dn, up), y, table, others


def owned_part_kernel(geo, scale, has_prev, has_field, has_upper, *refs):
    refs = list(refs)
    base_ref = refs.pop()
    y_ref = refs.pop(0)
    prev_ref = refs.pop(0) if has_prev else None
    pot_ref = refs.pop(0)
    field_ref = refs.pop(0) if has_field else None
    mats = [refs.pop(0) for _ in range(geo.cells)]
    y = y_ref[...]
    factor = pot_ref[...]
    if has_field:
        factor = factor + field_ref[...]
    value = ((factor - filter_center) * scale) * y
    if has_prev:
        value = value - prev_ref[...]
    base_ref[...] = value
    x = y.astype(BF)
    for c in range(geo.cells):
        w = geo.windows[c]
        own = w.hi - w.lo
        rows = x[w.lo : w.hi, :]
        if w.low:
            rows = jnp.concatenate([rows, x[0 : w.low, :]], axis=0)
        product = dot(mats[c][...], rows) * scale
        base_ref[w.lo : w.hi, :] += product[:own]
        if w.low:
            base_ref[0 : w.low, :] += product[own:]
    if has_upper:
        for upper in refs:
            base_ref[0 : geo.sp, :] += dot(upper[...], x[0 : geo.sp, :]) * scale


def owned_part(geo, scale, y, prev, pot, field, mats, uppers):
    args = [y] + ([prev] if prev is not None else []) + [pot]
    args += [field] if field is not None else []
    args += list(mats) + list(uppers)
    return vmem_call(
        functools.partial(
            owned_part_kernel, geo, scale, prev is not None, field is not None, bool(uppers)
        ),
        sds(y.shape, F32),
        cost=cost_of(2.0),
    )(*args)


def add_halo(geo, scale, y_ref, up_ref, dn_ref, crosses, behinds, uppers, own_up_ref):
    h_up = up_ref[...]
    h_dn = dn_ref[...]
    for at, c in enumerate(geo.touching):
        w = geo.windows[c]
        own = w.hi - w.lo
        product = dot(crosses[at][...], h_up) * scale
        y_ref[w.lo : w.hi, :] += product[:own]
        if w.low:
            y_ref[0 : w.low, :] += product[own:]
    total = None
    for at, c in enumerate(geo.touching):
        w = geo.windows[c]
        first = w.lo - geo.dn_lo
        term = dot(behinds[at][...], h_dn[first : first + w.rows, :])
        total = term if total is None else total + term
        if uppers:
            total = total + dot(uppers[at][...], own_up_ref[...])
    y_ref[0 : geo.sp, :] += total * scale


def write_density(y_ref, occ_ref, table_ref, part_rows, dens_ref):
    parts = dens_ref.shape[0]
    own = y_ref.shape[0]
    y = y_ref[...]
    terms = y * y * occ_ref[...]
    high = terms.astype(BF)
    low = (terms - high.astype(F32)).astype(BF)
    ones = jnp.ones((SUBLANES, terms.shape[1]), BF)
    summed = dot_t(ones, high) + dot_t(ones, low)
    dens_ref[:, 0, 0:own] = jnp.broadcast_to(summed[0:1, :], (parts, own))
    band = lax.axis_index("band")
    for r in range(part_rows):
        row = table_ref[band, r : r + 1, :]
        dens_ref[:, 0, own + r * LANES : own + (r + 1) * LANES] = jnp.broadcast_to(row, (parts, LANES))


def finish_kernel(geo, scale, has_upper, mode, part_rows, *refs):
    refs = list(refs)
    n = len(geo.touching)
    base_ref, up_ref, dn_ref = refs[:3]
    refs = refs[3:]
    crosses, refs = refs[:n], refs[n:]
    behinds, refs = refs[:n], refs[n:]
    uppers, own_up = [], None
    if has_upper:
        uppers, refs = refs[:n], refs[n:]
        own_up = refs.pop(0)
    if mode == "density":
        occ_ref, table_ref = refs.pop(0), refs.pop(0)
    if mode == "field":
        column_ref, before_ref = refs.pop(0), refs.pop(0)
    y_ref = refs.pop(0)
    if mode == "field":
        y_ref[...] = base_ref[...] + (column_ref[...] * scale) * before_ref[...]
    else:
        y_ref[...] = base_ref[...]
    add_halo(geo, scale, y_ref, up_ref, dn_ref, crosses, behinds, uppers, own_up)
    if mode != "last":
        write_sends(geo, y_ref, refs[0], refs[1])
    if mode == "density":
        write_density(y_ref, occ_ref, table_ref, part_rows, refs[2])


def finish(geo, scale, base, halo, crosses, behinds, uppers=(), own_up=None, density=None, field=None, last=False):
    columns = base.shape[1]
    args = [base, halo[0], halo[1], *crosses, *behinds, *uppers]
    if uppers:
        args.append(own_up)
    shapes = [sds(base.shape, F32)]
    mode, part_rows = "plain", 0
    if last:
        mode = "last"
    else:
        shapes += send_shapes(geo, columns)
    if field is not None:
        mode = "field"
        args += list(field)
    if density is not None:
        mode = "density"
        fg, weights, table = density
        part_rows = fg.part_rows
        args += [weights, table]
        shapes.append(sds((fg.bands * fg.domains, 1, fg.width), F32))
    return vmem_call(
        functools.partial(finish_kernel, geo, scale, bool(uppers), mode, part_rows),
        shapes,
        cost=cost_of(1.0),
    )(*args)


class FieldGeometry:
    def __init__(self, bands, domains, own, share, cells, npc):
        self.domains, self.own, self.share, self.cells, self.npc = domains, own, share, cells, npc
        self.block = own // domains
        self.rows = up_to(npc, LANES) // LANES
        self.blocks = domains + 1
        self.at_inverse = cells * self.rows
        self.at_face = self.at_inverse + cells * self.blocks
        self.at_face_inverse = self.at_face + 1
        self.at_owner = self.at_face + 2
        self.at_owner_inverse = self.at_face + 3
        self.codes = self.at_face + 4
        self.at_screen = up_to(self.codes, 2) // 2
        self.lines = own // LANES
        self.part_rows = -(-(self.at_screen + self.lines) // bands)
        self.table_rows = up_to(self.part_rows * bands, SUBLANES)
        self.bands = bands
        self.width = own + self.part_rows * LANES
        self.size = self.rows * LANES
        self.fits = (
            domains == SUBLANES
            and own % (domains * SUBLANES) == 0
            and own % LANES == 0
            and share <= self.block <= LANES
            and max(npc, self.blocks * LANES) < CODE_BASE - 1
        )


CODE_BASE = 2048
CODE_BITS = 11


def pieces(length, blocks):
    found = []
    for j in range(blocks):
        done = 0
        while done < length:
            at = j * length + done
            count = min(length - done, LANES - at % LANES)
            found.append((at // LANES, at % LANES, j, done, count))
            done += count
    return found


def column_of(row):
    return jnp.broadcast_to(row, (LANES, LANES)).T


def field_tables_kernel(fg, *refs):
    nodes_ref, face_ref, owner_ref, screen_ref = refs[:4]
    table_ref, pad, one, packed = refs[5:]
    one[...] = jnp.full(one.shape, -1.0, F32)
    pad[...] = jnp.full(pad.shape, -1, I32)
    pad[0 : fg.cells, 0 : fg.npc] = nodes_ref[...]
    sub = lax.broadcasted_iota(I32, (LANES, LANES), 0)
    wide_lane = lax.broadcasted_iota(I32, (LANES, LANES), 1)
    for c in range(fg.cells):
        columns = []
        for r in range(fg.rows):
            nodes = pad[c : c + 1, r * LANES : (r + 1) * LANES]
            block = jnp.zeros((1, LANES), I32)
            for b in range(1, fg.blocks):
                block = block + jnp.where(nodes >= b * fg.block, 1, 0)
            code = jnp.where(nodes < 0, -1, nodes + block * (LANES - fg.block))
            code = code.astype(F32)
            at = c * fg.rows + r
            one[at : at + 1, :] = code
            columns.append(column_of(code))
        for b in range(fg.blocks):
            target = (wide_lane + b * LANES).astype(F32)
            found = jnp.zeros((LANES, LANES), F32)
            for r in range(fg.rows):
                position = (sub + (r * LANES + 1)).astype(F32)
                found = jnp.where(columns[r] == target, position, found)
            at = fg.at_inverse + c * fg.blocks + b
            one[at : at + 1, :] = jnp.sum(found, axis=0, keepdims=True) - 1.0
    one[fg.at_face : fg.at_face + 1, 0 : fg.share] = face_ref[...].astype(F32)
    column = column_of(one[fg.at_face : fg.at_face + 1, :])
    hits = jnp.where(column == wide_lane.astype(F32), (sub + 1).astype(F32), 0.0)
    one[fg.at_face_inverse : fg.at_face_inverse + 1, :] = jnp.sum(hits, axis=0, keepdims=True) - 1.0
    one[fg.at_owner : fg.at_owner + 1, 0 : fg.domains] = owner_ref[...].astype(F32)
    column = column_of(one[fg.at_owner : fg.at_owner + 1, :])
    hits = jnp.where(column == wide_lane.astype(F32), (sub + 1).astype(F32), 0.0)
    hits = jnp.where(sub < fg.domains, hits, 0.0)
    one[fg.at_owner_inverse : fg.at_owner_inverse + 1, :] = jnp.sum(hits, axis=0, keepdims=True) - 1.0
    packed[...] = jnp.zeros(packed.shape, F32)
    half = fg.at_screen
    packed[0:half, :] = (one[0:half, :] + 1.0) + (one[half : 2 * half, :] + 1.0) * CODE_BASE
    packed[half : half + fg.lines, :] = screen_ref[...]
    for b in range(fg.bands):
        table_ref[b, 0 : fg.part_rows, :] = packed[b * fg.part_rows : (b + 1) * fg.part_rows, :]


def field_tables(fg, pois_nodes, pois_face, block_owner, lines, after):
    specs = [pl.BlockSpec(memory_space=pltpu.VMEM)] * 4 + [pl.BlockSpec(memory_space=pl.ANY)]
    return vmem_call(
        functools.partial(field_tables_kernel, fg),
        sds((fg.bands, up_to(fg.part_rows, SUBLANES), LANES), F32),
        [
            pltpu.VMEM((up_to(fg.cells, SUBLANES), fg.size), I32),
            pltpu.VMEM((up_to(2 * fg.at_screen, SUBLANES), LANES), F32),
            pltpu.VMEM((fg.table_rows, LANES), F32),
        ],
        in_specs=specs,
        cost=cost_of(1.0),
    )(pois_nodes, pois_face, block_owner, lines, after)


def lanes_of(values, index):
    return jnp.take_along_axis(values, index, axis=1, mode="promise_in_bounds")


def decode(fg, got_ref, codes):
    domains, half, own = fg.domains, fg.at_screen, fg.own

    def tile(at):
        band, row = at // fg.part_rows, at % fg.part_rows
        first = own + row * LANES
        return got_ref[band * domains : (band + 1) * domains, 0, first : first + LANES]

    for at in range(half):
        both = tile(at).astype(I32)
        low = jnp.bitwise_and(both, CODE_BASE - 1) - 1
        codes[at] = low
        codes[half + at] = jnp.right_shift(both, CODE_BITS) - 1
    codes[fg.at_face_inverse] = pltpu.roll(codes[fg.at_face_inverse], 1, 0)
    lines = [tile(half + g) for g in range(fg.lines)]
    lane = lax.broadcasted_iota(I32, (domains, LANES), 1)
    screens = []
    for q in range(domains):
        screen = jnp.zeros((domains, LANES), F32)
        for row, start, j, offset, count in pieces(fg.block, domains):
            if j == q:
                moved = pltpu.roll(lines[row], (offset - start) % LANES, 1)
                screen = jnp.where((lane >= offset) & (lane < offset + count), moved, screen)
        screens.append(screen)
    inverse = codes[fg.at_owner_inverse].astype(F32).T[0:domains, :]
    places = []
    for q in range(domains):
        block = jnp.broadcast_to(inverse[:, q : q + 1], (domains, LANES)).astype(I32)
        places.append(block * fg.block + lane)
    owners = codes[fg.at_owner].astype(F32).T[0:domains, :]
    here = lax.axis_index("domain")
    narrow = lax.broadcasted_iota(I32, (domains, domains), 1)
    mine = jnp.sum(jnp.where(narrow == here, owners, 0.0), axis=1, keepdims=True)
    return places, jnp.broadcast_to(mine, (domains, LANES)).astype(I32), screens


def rows_of(values, index):
    return jnp.take_along_axis(values, index, axis=0, mode="promise_in_bounds")


def field_solve(fg, got_ref, codes, places, screen, matrix_ref, high_ref, low_ref, rows, copies):
    domains, cells = fg.domains, fg.cells
    valid = lax.broadcasted_iota(I32, (domains, LANES), 1) < fg.block

    def lookup(sources, code):
        lane = jnp.bitwise_and(code, LANES - 1)
        which = jnp.right_shift(code, 7)
        total = jnp.zeros((domains, LANES), F32)
        for b, values in enumerate(sources):
            total = jnp.where(which == b, lanes_of(values, lane), total)
        return total

    def operator(field):
        ahead = pltpu.roll(field[0], domains - 1, 0)
        upper = lookup([ahead], codes[fg.at_face])
        local = list(field) + [upper]
        for c in range(cells):
            for r in range(fg.rows):
                rows[c * domains : (c + 1) * domains, r * LANES : (r + 1) * LANES] = lookup(local, codes[c * fg.rows + r])
        if copies:
            copies.pop().wait()
            full = matrix_ref[...]
            top = full.astype(BF)
            high_ref[...] = top
            low_ref[...] = (full - top.astype(F32)).astype(BF)
        picked = rows[:, 0 : fg.npc]
        high = picked.astype(BF)
        low = (picked - high.astype(F32)).astype(BF)
        both = dot(jnp.concatenate([high, low], axis=0), high_ref[...])
        half_rows = cells * domains
        rows[:, 0 : fg.npc] = both[:half_rows] + (both[half_rows:] + dot(high, low_ref[...]))
        out = []
        for b in range(fg.blocks):
            total = None
            for c in range(cells):
                sources = [
                    rows[c * domains : (c + 1) * domains, r * LANES : (r + 1) * LANES]
                    for r in range(fg.rows)
                ]
                term = lookup(sources, codes[fg.at_inverse + c * fg.blocks + b])
                total = term if total is None else total + term
            out.append(total)
        arriving = pltpu.roll(out[domains], 1, 0)
        out[0] = out[0] + lookup([arriving], codes[fg.at_face_inverse])
        return [jnp.where(valid, screen[q] * field[q] + out[q], 0.0) for q in range(domains)]

    density = []
    for g in range(fg.lines):
        at = slice(g * LANES, (g + 1) * LANES)
        total = got_ref[0:domains, 0, at]
        for b in range(1, fg.bands):
            total = total + got_ref[b * domains : (b + 1) * domains, 0, at]
        density.append(total)
    source = []
    for q in range(domains):
        spread = [jnp.broadcast_to(d[q : q + 1, :], (domains, LANES)) for d in density]
        source.append(jnp.where(valid, lookup(spread, places[q]), 0.0))
    step_one = [s * (1.0 / solve_center) for s in source]
    applied = operator(step_one)
    residual = [s - a for s, a in zip(source, applied)]
    a1, b1 = weight_one * weight_zero, 2.0 * weight_one / solve_half
    step_two = [a1 * e + b1 * r for e, r in zip(step_one, residual)]
    applied = operator(step_two)
    residual = [r - a for r, a in zip(residual, applied)]
    a2, b2 = weight_two * weight_one, 2.0 * weight_two / solve_half
    step_three = [a2 * e + b2 * r for e, r in zip(step_two, residual)]
    return [(x + y) + z for x, y, z in zip(step_one, step_two, step_three)]


def field_kernel(fg, got_ref, matrix_hbm, column_ref, hartree_ref, codes, rows, phi, mine, matrix_ref, high_ref, low_ref, sems):
    copies = fetch([(matrix_hbm, matrix_ref)], sems)
    places, owner, screens = decode(fg, got_ref, codes)
    blocks = field_solve(fg, got_ref, codes, places, screens, matrix_ref, high_ref, low_ref, rows, copies)
    for q in range(fg.domains):
        phi[q] = blocks[q]
    mine[...] = rows_of(phi[lax.axis_index("domain")], owner)
    for j in range(fg.domains):
        column = column_of(mine[j : j + 1, :])
        column_ref[j * fg.block : (j + 1) * fg.block, :] = column[0 : fg.block, :]
    for row, lane, j, offset, count in pieces(fg.block, fg.domains):
        hartree_ref[row : row + 1, lane : lane + count] = mine[j : j + 1, offset : offset + count]


def field_step(fg, got, matrix):
    tile = (fg.domains, LANES)
    return vmem_call(
        functools.partial(field_kernel, fg),
        [sds((fg.own, LANES), F32), sds((fg.lines, LANES), F32)],
        [
            pltpu.VMEM((2 * fg.at_screen, *tile), I32),
            pltpu.VMEM((fg.cells * fg.domains, fg.size), F32),
            pltpu.VMEM((fg.domains, *tile), F32),
            pltpu.VMEM(tile, F32),
            pltpu.VMEM(matrix.shape, F32),
            pltpu.VMEM(matrix.shape, BF),
            pltpu.VMEM(matrix.shape, BF),
            pltpu.SemaphoreType.DMA((1,)),
        ],
        in_specs=[pl.BlockSpec(memory_space=pltpu.VMEM), pl.BlockSpec(memory_space=pltpu.HBM)],
        cost=cost_of(4.0),
    )(got, *in_hbm(matrix))


def assembled(owned_rows, face_row, terms):
    owned_count = owned_rows.shape[0]
    shared = face_row.shape[0]
    coming = jnp.take(from_behind(owned_rows[:shared], "domain", -1), face_row, axis=0)
    partial_value = terms(jnp.concatenate([owned_rows, coming], axis=0))
    upper_rows = partial_value[owned_count:]
    ordered = jnp.zeros_like(upper_rows).at[face_row].set(upper_rows)
    arrived = from_behind(ordered, "domain", 1)
    return partial_value[:owned_count].at[:shared].add(arrived)


def field_terms(local_rows, pois_matrix, node_ids):
    cell_vals = jnp.take(local_rows, node_ids, axis=0)
    product = jnp.einsum(
        "pq,cq->cp",
        pois_matrix,
        cell_vals,
        precision=lax.Precision.HIGHEST,
        preferred_element_type=F32,
    )
    return jnp.zeros(local_rows.shape, F32).at[node_ids.reshape(-1)].add(product.reshape(-1))


def reshuffle(blocks):
    return lax.all_to_all(blocks, "domain", split_axis=0, concat_axis=0, tiled=True)


def distributed_field(y, occupation, owner_row, pois_matrix, pois_nodes, field_face, screening):
    owned_count = y.shape[0]
    domains = lax.axis_size("domain")
    block_len = owned_count // domains
    partial_value = jnp.dot(
        y * y, occupation, precision=lax.Precision.HIGHEST, preferred_element_type=F32
    )
    summed = lax.psum(partial_value, "band")
    arranged = (
        jnp.zeros((domains, block_len), F32)
        .at[owner_row]
        .set(summed.reshape(domains, block_len))
    )
    source = reshuffle(arranged).reshape(owned_count)

    def field_operator(vector):
        return (
            assembled(
                vector, field_face, lambda local: field_terms(local, pois_matrix, pois_nodes)
            )
            + screening * vector
        )

    step_one = source / solve_center
    residual = source - field_operator(step_one)
    step_two = weight_one * weight_zero * step_one + 2.0 * weight_one / solve_half * residual
    residual = residual - field_operator(step_two)
    step_three = weight_two * weight_one * step_two + 2.0 * weight_two / solve_half * residual
    solved = step_one + step_two + step_three
    returned = reshuffle(solved.reshape(domains, block_len))
    return jnp.take(returned, owner_row, axis=0).reshape(owned_count)


def exchange(sends):
    dn, up = sends
    h_dn = from_behind(dn, "domain", 1)
    h_up = from_behind(up, "domain", -1)
    return h_up, h_dn


def on_device(
    orbitals,
    potential,
    occupation,
    cell_matrix,
    cell_nodes,
    face_order,
    pois_matrix,
    pois_nodes,
    pois_face,
    screening,
    block_owner,
):
    domains = lax.axis_size("domain")
    bands = lax.axis_size("band")
    own, columns = orbitals.shape
    geo = Geometry(own, face_order.shape[1], cell_nodes.shape[0], cell_nodes.shape[1])
    fg = FieldGeometry(bands, domains, own, pois_face.shape[1], pois_nodes.shape[0], pois_nodes.shape[1])
    first, later = 1.0 / filter_half, 2.0 / filter_half

    others = [cell_matrix, potential.reshape(own // LANES, LANES)]
    if fg.fits:
        others += [pois_nodes, pois_face, block_owner, screening.reshape(own // LANES, LANES)]
        others.append(occupation.reshape(1, columns))
    sends, y0, nodes, (matrix, lines, *others) = pack(geo, orbitals, cell_nodes, face_order, *others)
    halo = exchange(sends)
    mats, crosses, pot = own_matrices(geo, nodes, matrix, lines)
    base = owned_part(geo, first, y0, None, pot, None, mats, ())
    behinds, uppers = behind_matrices(geo, halo[1], matrix)
    y1, *sends1 = finish(geo, first, base, halo, crosses, behinds, uppers, sends[1])

    halo = exchange(sends1)
    base = owned_part(geo, later, y1, y0, pot, None, mats, uppers)
    if fg.fits:
        *others, weights = others
        table = field_tables(fg, *others, base)
    y2, *sends2 = finish(geo, later, base, halo, crosses, behinds)

    halo = exchange(sends2)
    base = owned_part(geo, later, y2, y1, pot, None, mats, uppers)
    if fg.fits:
        y3, dn, up, spread = finish(
            geo, later, base, halo, crosses, behinds, density=(fg, weights, table)
        )
        dens = lax.all_to_all(spread, ("band", "domain"), 0, 0, tiled=True)
        halo = exchange((dn, up))
        base = owned_part(geo, first, y3, None, pot, None, mats, uppers)
        column, packed = field_step(fg, dens, pois_matrix)
        hartree = packed.reshape(own)
        z1, *sends4 = finish(geo, first, base, halo, crosses, behinds, field=(column, y3))
    else:
        y3, *sends3 = finish(geo, later, base, halo, crosses, behinds)
        halo = exchange(sends3)
        hartree = distributed_field(
            y3, occupation, block_owner[0], pois_matrix, pois_nodes, pois_face[0], screening
        )
        column = jnp.broadcast_to(hartree[:, None], (own, LANES))
        base = owned_part(geo, first, y3, None, pot, column, mats, uppers)
        z1, *sends4 = finish(geo, first, base, halo, crosses, behinds)

    halo = exchange(sends4)
    base = owned_part(geo, later, z1, y3, pot, column, mats, uppers)
    (filtered,) = finish(geo, later, base, halo, crosses, behinds, last=True)
    return filtered, hartree


def solution(mesh):
    return jax.shard_map(
        on_device,
        mesh=mesh,
        in_specs=(
            P("domain", "band"),
            P("domain"),
            P("band"),
            P(),
            P("domain", None),
            P("domain", None),
            P(),
            P("domain", None),
            P("domain", None),
            P("domain"),
            P("domain", None),
        ),
        out_specs=(P("domain", "band"), P("domain")),
        check_vma=False,
    )
```

```python
import functools

import jax
import jax.numpy as jnp
from jax import lax
from jax.experimental import pallas as pl
from jax.experimental.pallas import tpu as pltpu
from jax.sharding import PartitionSpec as P

filter_center = 1.8
filter_half = 2.7
solve_center = 3.25
solve_half = 2.75
solve_ratio = solve_center / solve_half
weight_zero = 1.0 / solve_ratio
weight_one = 1.0 / (2.0 * solve_ratio - weight_zero)
weight_two = 1.0 / (2.0 * solve_ratio - weight_one)

BF = jnp.bfloat16
F32 = jnp.float32
I32 = jnp.int32
LANES = 128
SUBLANES = 8


def up_to(n, m):
    return -(-n // m) * m


def from_behind(array, axis, by):
    length = lax.axis_size(axis)
    return lax.ppermute(array, axis, [(i, (i + by) % length) for i in range(length)])


class Window:
    def __init__(self, start, npc, own, nloc):
        end = start + npc
        self.lo = start // 16 * 16
        self.hi = min(up_to(min(end, own), 16), own)
        self.touches = end > own
        self.low = up_to(max(0, end - nloc), 16)
        self.rows = self.hi - self.lo + self.low


class Geometry:
    def __init__(self, own, share, cells, npc):
        self.own, self.share, self.cells, self.npc = own, share, cells, npc
        nloc = own + share
        stride = nloc // cells
        self.sp = up_to(share, 16)
        self.npl = up_to(npc, LANES)
        self.windows = [Window(c * stride, npc, own, nloc) for c in range(cells)]
        self.touching = [c for c in range(cells) if self.windows[c].touches]
        self.dn_lo = min(self.windows[c].lo for c in self.touching)
        self.low = max(w.low for w in self.windows)
        self.dn_rows = own - self.dn_lo + self.low
        self.table_rows = up_to(cells + 1, SUBLANES)
        self.table_lanes = up_to(max(npc, share), LANES)
        self.table_tiles = self.table_lanes // LANES


def dot(a, b):
    return lax.dot_general(a, b, (((1,), (0,)), ((), ())), preferred_element_type=F32)


def dot_t(a, b):
    return lax.dot_general(a, b, (((1,), (1,)), ((), ())), preferred_element_type=F32)


def vmem_call(kernel, out_shape, scratch=(), in_specs=None, out_specs=None, cost=None):
    kwargs = {}
    if in_specs is not None:
        kwargs["in_specs"] = in_specs
    if out_specs is not None:
        kwargs["out_specs"] = out_specs
    return pl.pallas_call(
        kernel,
        out_shape=out_shape,
        scratch_shapes=list(scratch),
        cost_estimate=cost,
        compiler_params=pltpu.CompilerParams(vmem_limit_bytes=12 * 1024 * 1024),
        **kwargs,
    )


def in_hbm(*arrays):
    return [pltpu.with_memory_space_constraint(a, pltpu.HBM) for a in arrays]


def sds(shape, dtype):
    return jax.ShapeDtypeStruct(shape, dtype)


def one_hot_rows(count, first, nodes):
    ids = lax.broadcasted_iota(I32, (count, nodes.shape[1]), 0) + first
    return jnp.where(ids == nodes, 1.0, 0.0).astype(BF)


def place_table(geo, nodes_ref, face_ref, table):
    table[...] = jnp.full(table.shape, -1, I32)
    table[0 : geo.cells, 0 : geo.npc] = nodes_ref[...]
    table[geo.cells : geo.cells + 1, 0 : geo.share] = face_ref[...]


def place_matrix(geo, matrix_ref, matrix_pad):
    matrix_pad[...] = jnp.zeros(matrix_pad.shape, F32)
    matrix_pad[0 : geo.npc, 0 : geo.npc] = matrix_ref[...].astype(F32)
    return matrix_pad[...].astype(BF)


def table_scratch(geo):
    return pltpu.VMEM((geo.table_rows, geo.table_lanes), I32)


def matrix_scratch(geo):
    return pltpu.VMEM((geo.npl, geo.npl), F32)


def nodes_of(geo, table, c):
    return table[c : c + 1, 0 : geo.npl]


def face_of(geo, table):
    return table[geo.cells : geo.cells + 1, 0 : up_to(geo.share, LANES)]


def owned_picks(geo, c, nodes):
    w = geo.windows[c]
    picks = one_hot_rows(w.hi - w.lo, w.lo, nodes)
    if w.low:
        picks = jnp.concatenate([picks, one_hot_rows(w.low, 0, nodes)], axis=0)
    return picks


def upper_picks(geo, nodes, face):
    by_local = one_hot_rows(face.shape[1], geo.own, nodes)
    by_owner = one_hot_rows(geo.sp, 0, face)
    return dot(by_owner, by_local).astype(BF)


def own_matrices_kernel(geo, *refs):
    table, matrix_ref, pot_ref = refs[:3]
    outs, matrix_pad = refs[3:-1], refs[-1]
    matrix = place_matrix(geo, matrix_ref, matrix_pad)
    face = face_of(geo, table)
    for c in range(geo.cells):
        nodes = nodes_of(geo, table, c)
        own = owned_picks(geo, c, nodes)
        left = dot(own, matrix).astype(BF)
        outs[c][...] = dot_t(left, own).astype(BF)
        if c in geo.touching:
            at = geo.cells + geo.touching.index(c)
            outs[at][...] = dot_t(left, upper_picks(geo, nodes, face)).astype(BF)
    column = outs[-1]
    for r in range(geo.own // LANES):
        row = jnp.broadcast_to(pot_ref[r : r + 1, :], (LANES, LANES))
        column[r * LANES : (r + 1) * LANES, :] = row.T


def own_matrices(geo, table, cell_matrix, lines):
    shapes = [sds((w.rows, w.rows), BF) for w in geo.windows]
    shapes += [sds((geo.windows[c].rows, geo.sp), BF) for c in geo.touching]
    shapes += [sds((geo.own, LANES), F32)]
    outs = vmem_call(
        functools.partial(own_matrices_kernel, geo),
        shapes,
        [matrix_scratch(geo)],
        cost=cost_of(2.0),
    )(table, cell_matrix, lines)
    n = geo.cells
    return outs[:n], outs[n:-1], outs[-1]


def behind_matrices_kernel(geo, *refs):
    sent_ref, matrix_ref = refs[:2]
    outs = refs[2:-2]
    table, matrix_pad = refs[-2:]
    for t in range(geo.table_tiles):
        at = geo.dn_rows + 2 * t * geo.table_rows
        digits = sent_ref[at : at + 2 * geo.table_rows, :].astype(F32)
        value = digits[: geo.table_rows] * LANES + digits[geo.table_rows :] - 1.0
        table[:, t * LANES : (t + 1) * LANES] = value.astype(I32)
    matrix = place_matrix(geo, matrix_ref, matrix_pad)
    face = face_of(geo, table)
    count = len(geo.touching)
    for at, c in enumerate(geo.touching):
        nodes = nodes_of(geo, table, c)
        upper = upper_picks(geo, nodes, face)
        left = dot(upper, matrix).astype(BF)
        outs[at][...] = dot_t(left, owned_picks(geo, c, nodes)).astype(BF)
        outs[count + at][...] = dot_t(left, upper).astype(BF)


def behind_matrices(geo, sent, cell_matrix):
    shapes = [sds((geo.sp, geo.windows[c].rows), BF) for c in geo.touching]
    shapes += [sds((geo.sp, geo.sp), BF) for _ in geo.touching]
    outs = vmem_call(
        functools.partial(behind_matrices_kernel, geo),
        shapes,
        [table_scratch(geo), matrix_scratch(geo)],
        cost=cost_of(1.0),
    )(sent, cell_matrix)
    n = len(geo.touching)
    return outs[:n], outs[n:]


def cost_of(us):
    return pl.CostEstimate(flops=0, bytes_accessed=int(us * 3.0e6), transcendentals=0)


def write_sends(geo, y_ref, dn_ref, up_ref):
    top = geo.own - geo.dn_lo
    dn_ref[0:top, :] = y_ref[geo.dn_lo : geo.own, :].astype(BF)
    dn_ref[top : top + geo.low, :] = y_ref[0 : geo.low, :].astype(BF)
    up_ref[...] = y_ref[0 : geo.sp, :].astype(BF)


def send_shapes(geo, columns):
    return [sds((geo.dn_rows, columns), BF), sds((geo.sp, columns), BF)]


def fetch(pairs, sems):
    copies = [pltpu.make_async_copy(src, dst, sems.at[i]) for i, (src, dst) in enumerate(pairs)]
    for copy in copies:
        copy.start()
    return copies


def pack_kernel(geo, extra, y_hbm, nodes_hbm, face_hbm, *refs):
    sources, refs = refs[:extra], refs[extra:]
    dn_ref, up_ref, y, table = refs[:4]
    kept, (nodes, face, sems) = refs[4 : 4 + extra], refs[4 + extra :]
    cuts = sorted({0, max(geo.sp, geo.low), geo.dn_lo, geo.own})
    spans = list(zip(cuts[:-1], cuts[1:]))
    pairs = [(nodes_hbm, nodes), (face_hbm, face)]
    pairs += [(y_hbm.at[pl.ds(a, b - a)], y.at[pl.ds(a, b - a)]) for a, b in spans]
    pairs += list(zip(sources, kept))
    copies = fetch(pairs, sems)
    copies[0].wait()
    copies[1].wait()
    place_table(geo, nodes, face, table)
    for t in range(geo.table_tiles):
        at = geo.dn_rows + 2 * t * geo.table_rows
        value = table[:, t * LANES : (t + 1) * LANES] + 1
        high = jnp.right_shift(value, 7).astype(F32)
        low = jnp.bitwise_and(value, LANES - 1).astype(F32)
        digits = jnp.concatenate([high, low], axis=0).astype(BF)
        dn_ref[at : at + 2 * geo.table_rows, :] = digits
    for copy in copies[2:]:
        copy.wait()
    write_sends(geo, y, dn_ref, up_ref)


def pack(geo, y, cell_nodes, face_order, *others):
    dn, up = send_shapes(geo, y.shape[1])
    rows = geo.dn_rows + 2 * geo.table_rows * geo.table_tiles
    dn, up, y, table, *others = vmem_call(
        functools.partial(pack_kernel, geo, len(others)),
        [
            sds((rows, y.shape[1]), BF),
            up,
            sds(y.shape, F32),
            sds((geo.table_rows, geo.table_lanes), I32),
            *[sds(a.shape, a.dtype) for a in others],
        ],
        [
            pltpu.VMEM(cell_nodes.shape, I32),
            pltpu.VMEM(face_order.shape, I32),
            pltpu.SemaphoreType.DMA((5 + len(others),)),
        ],
        in_specs=[pl.BlockSpec(memory_space=pltpu.HBM)] * (3 + len(others)),
        cost=cost_of(1.0),
    )(*in_hbm(y, cell_nodes, face_order, *others))
    return (dn, up), y, table, others


def owned_part_kernel(geo, scale, has_prev, has_field, has_upper, *refs):
    refs = list(refs)
    base_ref = refs.pop()
    y_ref = refs.pop(0)
    prev_ref = refs.pop(0) if has_prev else None
    pot_ref = refs.pop(0)
    field_ref = refs.pop(0) if has_field else None
    mats = [refs.pop(0) for _ in range(geo.cells)]
    y = y_ref[...]
    factor = pot_ref[...]
    if has_field:
        factor = factor + field_ref[...]
    value = ((factor - filter_center) * scale) * y
    if has_prev:
        value = value - prev_ref[...]
    base_ref[...] = value
    x = y.astype(BF)
    for c in range(geo.cells):
        w = geo.windows[c]
        own = w.hi - w.lo
        rows = x[w.lo : w.hi, :]
        if w.low:
            rows = jnp.concatenate([rows, x[0 : w.low, :]], axis=0)
        product = dot(mats[c][...], rows) * scale
        base_ref[w.lo : w.hi, :] += product[:own]
        if w.low:
            base_ref[0 : w.low, :] += product[own:]
    if has_upper:
        for upper in refs:
            base_ref[0 : geo.sp, :] += dot(upper[...], x[0 : geo.sp, :]) * scale


def owned_part(geo, scale, y, prev, pot, field, mats, uppers):
    args = [y] + ([prev] if prev is not None else []) + [pot]
    args += [field] if field is not None else []
    args += list(mats) + list(uppers)
    return vmem_call(
        functools.partial(
            owned_part_kernel, geo, scale, prev is not None, field is not None, bool(uppers)
        ),
        sds(y.shape, F32),
        cost=cost_of(2.0),
    )(*args)


def add_halo(geo, scale, y_ref, up_ref, dn_ref, crosses, behinds, uppers, own_up_ref):
    h_up = up_ref[...]
    h_dn = dn_ref[...]
    for at, c in enumerate(geo.touching):
        w = geo.windows[c]
        own = w.hi - w.lo
        product = dot(crosses[at][...], h_up) * scale
        y_ref[w.lo : w.hi, :] += product[:own]
        if w.low:
            y_ref[0 : w.low, :] += product[own:]
    total = None
    for at, c in enumerate(geo.touching):
        w = geo.windows[c]
        first = w.lo - geo.dn_lo
        term = dot(behinds[at][...], h_dn[first : first + w.rows, :])
        total = term if total is None else total + term
        if uppers:
            total = total + dot(uppers[at][...], own_up_ref[...])
    y_ref[0 : geo.sp, :] += total * scale


def write_density(y_ref, occ_ref, table_ref, part_rows, dens_ref):
    parts = dens_ref.shape[0]
    own = y_ref.shape[0]
    y = y_ref[...]
    terms = y * y * occ_ref[...]
    high = terms.astype(BF)
    low = (terms - high.astype(F32)).astype(BF)
    ones = jnp.ones((SUBLANES, terms.shape[1]), BF)
    summed = dot_t(ones, high) + dot_t(ones, low)
    dens_ref[:, 0, 0:own] = jnp.broadcast_to(summed[0:1, :], (parts, own))
    band = lax.axis_index("band")
    for r in range(part_rows):
        row = table_ref[band, r : r + 1, :]
        dens_ref[:, 0, own + r * LANES : own + (r + 1) * LANES] = jnp.broadcast_to(row, (parts, LANES))


def finish_kernel(geo, scale, has_upper, mode, part_rows, *refs):
    refs = list(refs)
    n = len(geo.touching)
    base_ref, up_ref, dn_ref = refs[:3]
    refs = refs[3:]
    crosses, refs = refs[:n], refs[n:]
    behinds, refs = refs[:n], refs[n:]
    uppers, own_up = [], None
    if has_upper:
        uppers, refs = refs[:n], refs[n:]
        own_up = refs.pop(0)
    halo = (up_ref, dn_ref, crosses, behinds, uppers, own_up)
    if mode == "last":
        finish_last(geo, scale, base_ref, halo, *refs)
        return
    if mode == "density":
        occ_ref, table_ref = refs.pop(0), refs.pop(0)
    if mode == "field":
        column_ref, before_ref = refs.pop(0), refs.pop(0)
    y_ref = refs.pop(0)
    if mode == "field":
        y_ref[...] = base_ref[...] + (column_ref[...] * scale) * before_ref[...]
    else:
        y_ref[...] = base_ref[...]
    add_halo(geo, scale, y_ref, *halo)
    if mode == "density":
        _, _, out_hbm, dens, sem = refs
        write_density(y_ref, occ_ref, table_ref, part_rows, dens)
        copy = pltpu.make_async_copy(dens, out_hbm, sem)
        copy.start()
    write_sends(geo, y_ref, refs[0], refs[1])
    if mode == "density":
        copy.wait()


def finish_last(geo, scale, base_ref, halo, *refs):
    extras = (len(refs) - 3) // 2
    sources, out_hbm, targets = refs[:extras], refs[extras], refs[extras + 1 : -2]
    y_ref, sems = refs[-2:]
    top = max(geo.sp, geo.low)
    inner = pl.ds(top, geo.dn_lo - top)
    copies = fetch([(base_ref.at[inner], out_hbm.at[inner]), *zip(sources, targets)], sems)
    edges = [(0, top), (geo.dn_lo, geo.own)]
    for a, b in edges:
        y_ref[a:b, :] = base_ref[a:b, :]
    add_halo(geo, scale, y_ref, *halo)
    for i, (a, b) in enumerate(edges):
        edge = pl.ds(a, b - a)
        copy = pltpu.make_async_copy(y_ref.at[edge], out_hbm.at[edge], sems.at[1 + extras + i])
        copy.start()
        copies.append(copy)
    for copy in copies:
        copy.wait()


def finish(geo, scale, base, halo, crosses, behinds, uppers=(), own_up=None, density=None, field=None, last=None):
    columns = base.shape[1]
    args = [base, halo[0], halo[1], *crosses, *behinds, *uppers]
    if uppers:
        args.append(own_up)
    mode, part_rows = "plain", 0
    shapes = [sds(base.shape, F32)]
    scratch = []
    vmem, hbm = pl.BlockSpec(memory_space=pltpu.VMEM), pl.BlockSpec(memory_space=pltpu.HBM)
    out_specs = [vmem, vmem, vmem]
    if last is not None:
        mode = "last"
        args += last
        shapes += [sds(a.shape, a.dtype) for a in last]
        out_specs = [hbm] * len(shapes)
        scratch = [pltpu.VMEM(base.shape, F32), pltpu.SemaphoreType.DMA((3 + len(last),))]
    else:
        shapes += send_shapes(geo, columns)
    if field is not None:
        mode = "field"
        args += list(field)
    if density is not None:
        mode = "density"
        fg, weights, table = density
        part_rows = fg.part_rows
        args += [weights, table]
        spread = (fg.bands * fg.domains, 1, fg.width)
        shapes.append(sds(spread, F32))
        out_specs.append(hbm)
        scratch = [pltpu.VMEM(spread, F32), pltpu.SemaphoreType.DMA(())]
    return vmem_call(
        functools.partial(finish_kernel, geo, scale, bool(uppers), mode, part_rows),
        shapes,
        scratch,
        out_specs=out_specs,
        cost=cost_of(1.0),
    )(*args)


class FieldGeometry:
    def __init__(self, bands, domains, own, share, cells, npc):
        self.domains, self.own, self.share, self.cells, self.npc = domains, own, share, cells, npc
        self.block = own // domains
        self.rows = up_to(npc, LANES) // LANES
        self.blocks = domains + 1
        self.at_inverse = cells * self.rows
        self.at_face = self.at_inverse + cells * self.blocks
        self.at_face_inverse = self.at_face + 1
        self.at_owner = self.at_face + 2
        self.at_owner_inverse = self.at_face + 3
        self.codes = self.at_face + 4
        self.at_screen = up_to(self.codes, 2) // 2
        self.lines = own // LANES
        self.part_rows = -(-(self.at_screen + self.lines) // bands)
        self.table_rows = up_to(self.part_rows * bands, SUBLANES)
        self.bands = bands
        self.width = own + self.part_rows * LANES
        self.size = self.rows * LANES
        self.fits = (
            domains == SUBLANES
            and own % (domains * SUBLANES) == 0
            and own % LANES == 0
            and share <= self.block <= LANES
            and max(npc, self.blocks * LANES) < CODE_BASE - 1
        )


CODE_BASE = 2048
CODE_BITS = 11


def pieces(length, blocks):
    found = []
    for j in range(blocks):
        done = 0
        while done < length:
            at = j * length + done
            count = min(length - done, LANES - at % LANES)
            found.append((at // LANES, at % LANES, j, done, count))
            done += count
    return found


def column_of(row):
    return jnp.broadcast_to(row, (LANES, LANES)).T


def field_tables_kernel(fg, *refs):
    nodes_ref, face_ref, owner_ref, screen_ref = refs[:4]
    table_ref, pad, one, packed = refs[5:]
    one[...] = jnp.full(one.shape, -1.0, F32)
    pad[...] = jnp.full(pad.shape, -1, I32)
    pad[0 : fg.cells, 0 : fg.npc] = nodes_ref[...]
    sub = lax.broadcasted_iota(I32, (LANES, LANES), 0)
    wide_lane = lax.broadcasted_iota(I32, (LANES, LANES), 1)
    for c in range(fg.cells):
        columns = []
        for r in range(fg.rows):
            nodes = pad[c : c + 1, r * LANES : (r + 1) * LANES]
            block = jnp.zeros((1, LANES), I32)
            for b in range(1, fg.blocks):
                block = block + jnp.where(nodes >= b * fg.block, 1, 0)
            code = jnp.where(nodes < 0, -1, nodes + block * (LANES - fg.block))
            code = code.astype(F32)
            at = c * fg.rows + r
            one[at : at + 1, :] = code
            columns.append(column_of(code))
        for b in range(fg.blocks):
            target = (wide_lane + b * LANES).astype(F32)
            found = jnp.zeros((LANES, LANES), F32)
            for r in range(fg.rows):
                position = (sub + (r * LANES + 1)).astype(F32)
                found = jnp.where(columns[r] == target, position, found)
            at = fg.at_inverse + c * fg.blocks + b
            one[at : at + 1, :] = jnp.sum(found, axis=0, keepdims=True) - 1.0
    one[fg.at_face : fg.at_face + 1, 0 : fg.share] = face_ref[...].astype(F32)
    column = column_of(one[fg.at_face : fg.at_face + 1, :])
    hits = jnp.where(column == wide_lane.astype(F32), (sub + 1).astype(F32), 0.0)
    one[fg.at_face_inverse : fg.at_face_inverse + 1, :] = jnp.sum(hits, axis=0, keepdims=True) - 1.0
    one[fg.at_owner : fg.at_owner + 1, 0 : fg.domains] = owner_ref[...].astype(F32)
    column = column_of(one[fg.at_owner : fg.at_owner + 1, :])
    hits = jnp.where(column == wide_lane.astype(F32), (sub + 1).astype(F32), 0.0)
    hits = jnp.where(sub < fg.domains, hits, 0.0)
    one[fg.at_owner_inverse : fg.at_owner_inverse + 1, :] = jnp.sum(hits, axis=0, keepdims=True) - 1.0
    packed[...] = jnp.zeros(packed.shape, F32)
    half = fg.at_screen
    packed[0:half, :] = (one[0:half, :] + 1.0) + (one[half : 2 * half, :] + 1.0) * CODE_BASE
    packed[half : half + fg.lines, :] = screen_ref[...]
    for b in range(fg.bands):
        table_ref[b, 0 : fg.part_rows, :] = packed[b * fg.part_rows : (b + 1) * fg.part_rows, :]


def field_tables(fg, pois_nodes, pois_face, block_owner, lines, after):
    specs = [pl.BlockSpec(memory_space=pltpu.VMEM)] * 4 + [pl.BlockSpec(memory_space=pl.ANY)]
    return vmem_call(
        functools.partial(field_tables_kernel, fg),
        sds((fg.bands, up_to(fg.part_rows, SUBLANES), LANES), F32),
        [
            pltpu.VMEM((up_to(fg.cells, SUBLANES), fg.size), I32),
            pltpu.VMEM((up_to(2 * fg.at_screen, SUBLANES), LANES), F32),
            pltpu.VMEM((fg.table_rows, LANES), F32),
        ],
        in_specs=specs,
        cost=cost_of(1.0),
    )(pois_nodes, pois_face, block_owner, lines, after)


def lanes_of(values, index):
    return jnp.take_along_axis(values, index, axis=1, mode="promise_in_bounds")


def decode(fg, got_ref, codes):
    domains, half, own = fg.domains, fg.at_screen, fg.own

    def tile(at):
        band, row = at // fg.part_rows, at % fg.part_rows
        first = own + row * LANES
        return got_ref[band * domains : (band + 1) * domains, 0, first : first + LANES]

    for at in range(half):
        both = tile(at).astype(I32)
        low = jnp.bitwise_and(both, CODE_BASE - 1) - 1
        codes[at] = low
        codes[half + at] = jnp.right_shift(both, CODE_BITS) - 1
    codes[fg.at_face_inverse] = pltpu.roll(codes[fg.at_face_inverse], 1, 0)
    lines = [tile(half + g) for g in range(fg.lines)]
    lane = lax.broadcasted_iota(I32, (domains, LANES), 1)
    screens = []
    for q in range(domains):
        screen = jnp.zeros((domains, LANES), F32)
        for row, start, j, offset, count in pieces(fg.block, domains):
            if j == q:
                moved = pltpu.roll(lines[row], (offset - start) % LANES, 1)
                screen = jnp.where((lane >= offset) & (lane < offset + count), moved, screen)
        screens.append(screen)
    inverse = codes[fg.at_owner_inverse].astype(F32).T[0:domains, :]
    places = []
    for q in range(domains):
        block = jnp.broadcast_to(inverse[:, q : q + 1], (domains, LANES)).astype(I32)
        places.append(block * fg.block + lane)
    owners = codes[fg.at_owner].astype(F32).T[0:domains, :]
    here = lax.axis_index("domain")
    narrow = lax.broadcasted_iota(I32, (domains, domains), 1)
    mine = jnp.sum(jnp.where(narrow == here, owners, 0.0), axis=1, keepdims=True)
    return places, jnp.broadcast_to(mine, (domains, LANES)).astype(I32), screens


def rows_of(values, index):
    return jnp.take_along_axis(values, index, axis=0, mode="promise_in_bounds")


def field_solve(fg, got_ref, codes, places, screen, matrix_ref, high_ref, low_ref, rows, copies):
    domains, cells = fg.domains, fg.cells
    valid = lax.broadcasted_iota(I32, (domains, LANES), 1) < fg.block

    def lookup(sources, code):
        lane = jnp.bitwise_and(code, LANES - 1)
        which = jnp.right_shift(code, 7)
        total = jnp.zeros((domains, LANES), F32)
        for b, values in enumerate(sources):
            total = jnp.where(which == b, lanes_of(values, lane), total)
        return total

    def operator(field):
        ahead = pltpu.roll(field[0], domains - 1, 0)
        upper = lookup([ahead], codes[fg.at_face])
        local = list(field) + [upper]
        for r in range(fg.rows):
            for c in range(cells):
                rows[c * domains : (c + 1) * domains, r * LANES : (r + 1) * LANES] = lookup(local, codes[c * fg.rows + r])
            if copies:
                copies.pop(0).wait()
                span = slice(r * LANES, min((r + 1) * LANES, fg.npc))
                full = matrix_ref[span, :]
                top = full.astype(BF)
                high_ref[span, :] = top
                low_ref[span, :] = (full - top.astype(F32)).astype(BF)
        picked = rows[:, 0 : fg.npc]
        high = picked.astype(BF)
        low = (picked - high.astype(F32)).astype(BF)
        both = dot(jnp.concatenate([high, low], axis=0), high_ref[...])
        half_rows = cells * domains
        rows[:, 0 : fg.npc] = both[:half_rows] + (both[half_rows:] + dot(high, low_ref[...]))
        out = []
        for b in range(fg.blocks):
            total = None
            for c in range(cells):
                sources = [
                    rows[c * domains : (c + 1) * domains, r * LANES : (r + 1) * LANES]
                    for r in range(fg.rows)
                ]
                term = lookup(sources, codes[fg.at_inverse + c * fg.blocks + b])
                total = term if total is None else total + term
            out.append(total)
        arriving = pltpu.roll(out[domains], 1, 0)
        out[0] = out[0] + lookup([arriving], codes[fg.at_face_inverse])
        return [jnp.where(valid, screen[q] * field[q] + out[q], 0.0) for q in range(domains)]

    density = []
    for g in range(fg.lines):
        at = slice(g * LANES, (g + 1) * LANES)
        total = got_ref[0:domains, 0, at]
        for b in range(1, fg.bands):
            total = total + got_ref[b * domains : (b + 1) * domains, 0, at]
        density.append(total)
    source = []
    for q in range(domains):
        spread = [jnp.broadcast_to(d[q : q + 1, :], (domains, LANES)) for d in density]
        source.append(jnp.where(valid, lookup(spread, places[q]), 0.0))
    step_one = [s * (1.0 / solve_center) for s in source]
    applied = operator(step_one)
    residual = [s - a for s, a in zip(source, applied)]
    a1, b1 = weight_one * weight_zero, 2.0 * weight_one / solve_half
    step_two = [a1 * e + b1 * r for e, r in zip(step_one, residual)]
    applied = operator(step_two)
    residual = [r - a for r, a in zip(residual, applied)]
    a2, b2 = weight_two * weight_one, 2.0 * weight_two / solve_half
    step_three = [a2 * e + b2 * r for e, r in zip(step_two, residual)]
    return [(x + y) + z for x, y, z in zip(step_one, step_two, step_three)]


def field_kernel(fg, got_ref, matrix_hbm, column_ref, hartree_ref, codes, rows, phi, mine, matrix_ref, high_ref, low_ref, sems):
    spans = [pl.ds(r * LANES, min(LANES, fg.npc - r * LANES)) for r in range(fg.rows)]
    copies = fetch([(matrix_hbm.at[span], matrix_ref.at[span]) for span in spans], sems)
    places, owner, screens = decode(fg, got_ref, codes)
    blocks = field_solve(fg, got_ref, codes, places, screens, matrix_ref, high_ref, low_ref, rows, copies)
    for q in range(fg.domains):
        phi[q] = blocks[q]
    mine[...] = rows_of(phi[lax.axis_index("domain")], owner)
    for j in range(fg.domains):
        column = column_of(mine[j : j + 1, :])
        column_ref[j * fg.block : (j + 1) * fg.block, :] = column[0 : fg.block, :]
    for row, lane, j, offset, count in pieces(fg.block, fg.domains):
        hartree_ref[row : row + 1, lane : lane + count] = mine[j : j + 1, offset : offset + count]


def field_step(fg, got, matrix):
    tile = (fg.domains, LANES)
    return vmem_call(
        functools.partial(field_kernel, fg),
        [sds((fg.own, LANES), F32), sds((fg.lines, LANES), F32)],
        [
            pltpu.VMEM((2 * fg.at_screen, *tile), I32),
            pltpu.VMEM((fg.cells * fg.domains, fg.size), F32),
            pltpu.VMEM((fg.domains, *tile), F32),
            pltpu.VMEM(tile, F32),
            pltpu.VMEM(matrix.shape, F32),
            pltpu.VMEM(matrix.shape, BF),
            pltpu.VMEM(matrix.shape, BF),
            pltpu.SemaphoreType.DMA((fg.rows,)),
        ],
        in_specs=[pl.BlockSpec(memory_space=pltpu.VMEM), pl.BlockSpec(memory_space=pltpu.HBM)],
        cost=cost_of(4.0),
    )(got, *in_hbm(matrix))


def assembled(owned_rows, face_row, terms):
    owned_count = owned_rows.shape[0]
    shared = face_row.shape[0]
    coming = jnp.take(from_behind(owned_rows[:shared], "domain", -1), face_row, axis=0)
    partial_value = terms(jnp.concatenate([owned_rows, coming], axis=0))
    upper_rows = partial_value[owned_count:]
    ordered = jnp.zeros_like(upper_rows).at[face_row].set(upper_rows)
    arrived = from_behind(ordered, "domain", 1)
    return partial_value[:owned_count].at[:shared].add(arrived)


def field_terms(local_rows, pois_matrix, node_ids):
    cell_vals = jnp.take(local_rows, node_ids, axis=0)
    product = jnp.einsum(
        "pq,cq->cp",
        pois_matrix,
        cell_vals,
        precision=lax.Precision.HIGHEST,
        preferred_element_type=F32,
    )
    return jnp.zeros(local_rows.shape, F32).at[node_ids.reshape(-1)].add(product.reshape(-1))


def reshuffle(blocks):
    return lax.all_to_all(blocks, "domain", split_axis=0, concat_axis=0, tiled=True)


def distributed_field(y, occupation, owner_row, pois_matrix, pois_nodes, field_face, screening):
    owned_count = y.shape[0]
    domains = lax.axis_size("domain")
    block_len = owned_count // domains
    partial_value = jnp.dot(
        y * y, occupation, precision=lax.Precision.HIGHEST, preferred_element_type=F32
    )
    summed = lax.psum(partial_value, "band")
    arranged = (
        jnp.zeros((domains, block_len), F32)
        .at[owner_row]
        .set(summed.reshape(domains, block_len))
    )
    source = reshuffle(arranged).reshape(owned_count)

    def field_operator(vector):
        return (
            assembled(
                vector, field_face, lambda local: field_terms(local, pois_matrix, pois_nodes)
            )
            + screening * vector
        )

    step_one = source / solve_center
    residual = source - field_operator(step_one)
    step_two = weight_one * weight_zero * step_one + 2.0 * weight_one / solve_half * residual
    residual = residual - field_operator(step_two)
    step_three = weight_two * weight_one * step_two + 2.0 * weight_two / solve_half * residual
    solved = step_one + step_two + step_three
    returned = reshuffle(solved.reshape(domains, block_len))
    return jnp.take(returned, owner_row, axis=0).reshape(owned_count)


def exchange(sends):
    dn, up = sends
    h_dn = from_behind(dn, "domain", 1)
    h_up = from_behind(up, "domain", -1)
    return h_up, h_dn


def on_device(
    orbitals,
    potential,
    occupation,
    cell_matrix,
    cell_nodes,
    face_order,
    pois_matrix,
    pois_nodes,
    pois_face,
    screening,
    block_owner,
):
    domains = lax.axis_size("domain")
    bands = lax.axis_size("band")
    own, columns = orbitals.shape
    geo = Geometry(own, face_order.shape[1], cell_nodes.shape[0], cell_nodes.shape[1])
    fg = FieldGeometry(bands, domains, own, pois_face.shape[1], pois_nodes.shape[0], pois_nodes.shape[1])
    first, later = 1.0 / filter_half, 2.0 / filter_half

    others = [cell_matrix, potential.reshape(own // LANES, LANES)]
    if fg.fits:
        others += [pois_nodes, pois_face, block_owner, screening.reshape(own // LANES, LANES)]
        others.append(occupation.reshape(1, columns))
    sends, y0, nodes, (matrix, lines, *others) = pack(geo, orbitals, cell_nodes, face_order, *others)
    halo = exchange(sends)
    mats, crosses, pot = own_matrices(geo, nodes, matrix, lines)
    base = owned_part(geo, first, y0, None, pot, None, mats, ())
    behinds, uppers = behind_matrices(geo, halo[1], matrix)
    y1, *sends1 = finish(geo, first, base, halo, crosses, behinds, uppers, sends[1])

    halo = exchange(sends1)
    base = owned_part(geo, later, y1, y0, pot, None, mats, uppers)
    if fg.fits:
        *others, weights = others
        table = field_tables(fg, *others, base)
    y2, *sends2 = finish(geo, later, base, halo, crosses, behinds)

    halo = exchange(sends2)
    base = owned_part(geo, later, y2, y1, pot, None, mats, uppers)
    if fg.fits:
        y3, dn, up, spread = finish(
            geo, later, base, halo, crosses, behinds, density=(fg, weights, table)
        )
        dens = lax.all_to_all(spread, ("band", "domain"), 0, 0, tiled=True)
        halo = exchange((dn, up))
        base = owned_part(geo, first, y3, None, pot, None, mats, uppers)
        column, packed = field_step(fg, dens, pois_matrix)
        z1, *sends4 = finish(geo, first, base, halo, crosses, behinds, field=(column, y3))
    else:
        y3, *sends3 = finish(geo, later, base, halo, crosses, behinds)
        halo = exchange(sends3)
        hartree = distributed_field(
            y3, occupation, block_owner[0], pois_matrix, pois_nodes, pois_face[0], screening
        )
        column = jnp.broadcast_to(hartree[:, None], (own, LANES))
        base = owned_part(geo, first, y3, None, pot, column, mats, uppers)
        z1, *sends4 = finish(geo, first, base, halo, crosses, behinds)

    halo = exchange(sends4)
    base = owned_part(geo, later, z1, y3, pot, column, mats, uppers)
    last = [packed] if fg.fits else []
    filtered, *rest = finish(geo, later, base, halo, crosses, behinds, last=last)
    if fg.fits:
        hartree = rest[0].reshape(own)
    return filtered, hartree


def solution(mesh):
    return jax.shard_map(
        on_device,
        mesh=mesh,
        in_specs=(
            P("domain", "band"),
            P("domain"),
            P("band"),
            P(),
            P("domain", None),
            P("domain", None),
            P(),
            P("domain", None),
            P("domain", None),
            P("domain"),
            P("domain", None),
        ),
        out_specs=(P("domain", "band"), P("domain")),
        check_vma=False,
    )
```

```python
import functools

import jax
import jax.numpy as jnp
from jax import lax
from jax.experimental import pallas as pl
from jax.experimental.pallas import tpu as pltpu
from jax.sharding import PartitionSpec as P

filter_center = 1.8
filter_half = 2.7
solve_center = 3.25
solve_half = 2.75
solve_ratio = solve_center / solve_half
weight_zero = 1.0 / solve_ratio
weight_one = 1.0 / (2.0 * solve_ratio - weight_zero)
weight_two = 1.0 / (2.0 * solve_ratio - weight_one)

BF = jnp.bfloat16
F32 = jnp.float32
I32 = jnp.int32
LANES = 128
SUBLANES = 8


def up_to(n, m):
    return -(-n // m) * m


def from_behind(array, axis, by):
    length = lax.axis_size(axis)
    return lax.ppermute(array, axis, [(i, (i + by) % length) for i in range(length)])


class Window:
    def __init__(self, start, npc, own, nloc):
        end = start + npc
        self.lo = start // 16 * 16
        self.hi = min(up_to(min(end, own), 16), own)
        self.touches = end > own
        self.low = up_to(max(0, end - nloc), 16)
        self.rows = self.hi - self.lo + self.low


class Geometry:
    def __init__(self, own, share, cells, npc):
        self.own, self.share, self.cells, self.npc = own, share, cells, npc
        nloc = own + share
        stride = nloc // cells
        self.sp = up_to(share, 16)
        self.npl = up_to(npc, LANES)
        self.windows = [Window(c * stride, npc, own, nloc) for c in range(cells)]
        self.touching = [c for c in range(cells) if self.windows[c].touches]
        self.dn_lo = min(self.windows[c].lo for c in self.touching)
        self.low = max(w.low for w in self.windows)
        self.dn_rows = own - self.dn_lo + self.low
        self.table_rows = up_to(cells, SUBLANES)
        self.table_lanes = up_to(npc, LANES)
        self.table_tiles = self.table_lanes // LANES


def dot(a, b):
    return lax.dot_general(a, b, (((1,), (0,)), ((), ())), preferred_element_type=F32)


def dot_t(a, b):
    return lax.dot_general(a, b, (((1,), (1,)), ((), ())), preferred_element_type=F32)


def vmem_call(kernel, out_shape, scratch=(), in_specs=None, out_specs=None, cost=None):
    kwargs = {}
    if in_specs is not None:
        kwargs["in_specs"] = in_specs
    if out_specs is not None:
        kwargs["out_specs"] = out_specs
    return pl.pallas_call(
        kernel,
        out_shape=out_shape,
        scratch_shapes=list(scratch),
        cost_estimate=cost,
        compiler_params=pltpu.CompilerParams(vmem_limit_bytes=12 * 1024 * 1024),
        **kwargs,
    )


def in_hbm(*arrays):
    return [pltpu.with_memory_space_constraint(a, pltpu.HBM) for a in arrays]


def sds(shape, dtype):
    return jax.ShapeDtypeStruct(shape, dtype)


def one_hot_rows(count, first, nodes):
    ids = lax.broadcasted_iota(I32, (count, nodes.shape[1]), 0) + first
    return jnp.where(ids == nodes, 1.0, 0.0).astype(BF)


def place_table(geo, nodes_ref, face_ref, table, faces):
    table[...] = jnp.full(table.shape, -1, I32)
    table[0 : geo.cells, 0 : geo.npc] = nodes_ref[...]
    faces[...] = jnp.zeros(faces.shape, I32)
    faces[0:1, 0 : geo.share] = face_ref[...]
    for t in range(geo.table_tiles):
        lanes = slice(t * LANES, (t + 1) * LANES)
        nodes = table[:, lanes]
        beyond = nodes - geo.own
        at = jnp.bitwise_and(beyond, LANES - 1)
        which = jnp.right_shift(beyond, 7)
        for f in range(faces.shape[1] // LANES):
            row = jnp.broadcast_to(faces[0:1, f * LANES : (f + 1) * LANES], nodes.shape)
            nodes = jnp.where(which == f, lanes_of(row, at) + geo.own, nodes)
        table[:, lanes] = nodes


def place_matrix(geo, matrix_ref, matrix_pad):
    matrix_pad[...] = jnp.zeros(matrix_pad.shape, F32)
    matrix_pad[0 : geo.npc, 0 : geo.npc] = matrix_ref[...].astype(F32)
    return matrix_pad[...].astype(BF)


def table_scratch(geo):
    return pltpu.VMEM((geo.table_rows, geo.table_lanes), I32)


def matrix_scratch(geo):
    return pltpu.VMEM((geo.npl, geo.npl), F32)


def nodes_of(geo, table, c):
    return table[c : c + 1, 0 : geo.npl]


def owned_picks(geo, c, nodes):
    w = geo.windows[c]
    picks = one_hot_rows(w.hi - w.lo, w.lo, nodes)
    if w.low:
        picks = jnp.concatenate([picks, one_hot_rows(w.low, 0, nodes)], axis=0)
    return picks


def upper_picks(geo, nodes):
    return one_hot_rows(geo.sp, geo.own, nodes)


def own_matrices_kernel(geo, *refs):
    table, matrix_ref, pot_ref = refs[:3]
    outs, matrix_pad = refs[3:-1], refs[-1]
    matrix = place_matrix(geo, matrix_ref, matrix_pad)
    for c in range(geo.cells):
        nodes = nodes_of(geo, table, c)
        own = owned_picks(geo, c, nodes)
        left = dot(own, matrix).astype(BF)
        outs[c][...] = dot_t(left, own).astype(BF)
        if c in geo.touching:
            at = geo.cells + geo.touching.index(c)
            outs[at][...] = dot_t(left, upper_picks(geo, nodes)).astype(BF)
    column = outs[-1]
    for r in range(geo.own // LANES):
        row = jnp.broadcast_to(pot_ref[r : r + 1, :], (LANES, LANES))
        column[r * LANES : (r + 1) * LANES, :] = row.T


def own_matrices(geo, table, cell_matrix, lines):
    shapes = [sds((w.rows, w.rows), BF) for w in geo.windows]
    shapes += [sds((geo.windows[c].rows, geo.sp), BF) for c in geo.touching]
    shapes += [sds((geo.own, LANES), F32)]
    outs = vmem_call(
        functools.partial(own_matrices_kernel, geo),
        shapes,
        [matrix_scratch(geo)],
        cost=cost_of(2.0),
    )(table, cell_matrix, lines)
    n = geo.cells
    return outs[:n], outs[n:-1], outs[-1]


def build_behind(geo, sent_ref, matrix_ref, table, matrix_pad, outs):
    for t in range(geo.table_tiles):
        at = geo.dn_rows + 2 * t * geo.table_rows
        digits = sent_ref[at : at + 2 * geo.table_rows, :].astype(F32)
        value = digits[: geo.table_rows] * LANES + digits[geo.table_rows :] - 1.0
        table[:, t * LANES : (t + 1) * LANES] = value.astype(I32)
    matrix = place_matrix(geo, matrix_ref, matrix_pad)
    count = len(geo.touching)
    for at, c in enumerate(geo.touching):
        nodes = nodes_of(geo, table, c)
        upper = upper_picks(geo, nodes)
        left = dot(upper, matrix).astype(BF)
        outs[at][...] = dot_t(left, owned_picks(geo, c, nodes)).astype(BF)
        outs[count + at][...] = dot_t(left, upper).astype(BF)


def behind_shapes(geo):
    shapes = [sds((geo.sp, geo.windows[c].rows), BF) for c in geo.touching]
    return shapes + [sds((geo.sp, geo.sp), BF) for _ in geo.touching]


def cost_of(us):
    return pl.CostEstimate(flops=0, bytes_accessed=int(us * 3.0e6), transcendentals=0)


def write_sends(geo, y_ref, dn_ref, up_ref):
    top = geo.own - geo.dn_lo
    dn_ref[0:top, :] = y_ref[geo.dn_lo : geo.own, :].astype(BF)
    dn_ref[top : top + geo.low, :] = y_ref[0 : geo.low, :].astype(BF)
    up_ref[...] = y_ref[0 : geo.sp, :].astype(BF)


def send_shapes(geo, columns):
    return [sds((geo.dn_rows, columns), BF), sds((geo.sp, columns), BF)]


def fetch(pairs, sems):
    copies = [pltpu.make_async_copy(src, dst, sems.at[i]) for i, (src, dst) in enumerate(pairs)]
    for copy in copies:
        copy.start()
    return copies


def pack_kernel(geo, extra, y_hbm, nodes_hbm, face_hbm, *refs):
    sources, refs = refs[:extra], refs[extra:]
    dn_ref, up_ref, y, table = refs[:4]
    kept, (nodes, face, faces, sems) = refs[4 : 4 + extra], refs[4 + extra :]
    cuts = sorted({0, max(geo.sp, geo.low), geo.dn_lo, geo.own})
    spans = list(zip(cuts[:-1], cuts[1:]))
    pairs = [(nodes_hbm, nodes), (face_hbm, face)]
    pairs += [(y_hbm.at[pl.ds(a, b - a)], y.at[pl.ds(a, b - a)]) for a, b in spans]
    pairs += list(zip(sources, kept))
    copies = fetch(pairs, sems)
    copies[0].wait()
    copies[1].wait()
    place_table(geo, nodes, face, table, faces)
    for t in range(geo.table_tiles):
        at = geo.dn_rows + 2 * t * geo.table_rows
        value = table[:, t * LANES : (t + 1) * LANES] + 1
        high = jnp.right_shift(value, 7).astype(F32)
        low = jnp.bitwise_and(value, LANES - 1).astype(F32)
        digits = jnp.concatenate([high, low], axis=0).astype(BF)
        dn_ref[at : at + 2 * geo.table_rows, :] = digits
    for copy in copies[2:]:
        copy.wait()
    write_sends(geo, y, dn_ref, up_ref)


def pack(geo, y, cell_nodes, face_order, *others):
    dn, up = send_shapes(geo, y.shape[1])
    rows = geo.dn_rows + 2 * geo.table_rows * geo.table_tiles
    dn, up, y, table, *others = vmem_call(
        functools.partial(pack_kernel, geo, len(others)),
        [
            sds((rows, y.shape[1]), BF),
            up,
            sds(y.shape, F32),
            sds((geo.table_rows, geo.table_lanes), I32),
            *[sds(a.shape, a.dtype) for a in others],
        ],
        [
            pltpu.VMEM(cell_nodes.shape, I32),
            pltpu.VMEM(face_order.shape, I32),
            pltpu.VMEM((1, up_to(geo.share, LANES)), I32),
            pltpu.SemaphoreType.DMA((5 + len(others),)),
        ],
        in_specs=[pl.BlockSpec(memory_space=pltpu.HBM)] * (3 + len(others)),
        cost=cost_of(1.0),
    )(*in_hbm(y, cell_nodes, face_order, *others))
    return (dn, up), y, table, others


def owned_part_kernel(geo, scale, has_prev, has_field, has_upper, *refs):
    refs = list(refs)
    base_ref = refs.pop()
    y_ref = refs.pop(0)
    prev_ref = refs.pop(0) if has_prev else None
    pot_ref = refs.pop(0)
    field_ref = refs.pop(0) if has_field else None
    mats = [refs.pop(0) for _ in range(geo.cells)]
    y = y_ref[...]
    factor = pot_ref[...]
    if has_field:
        factor = factor + field_ref[...]
    value = ((factor - filter_center) * scale) * y
    if has_prev:
        value = value - prev_ref[...]
    base_ref[...] = value
    x = y.astype(BF)
    for c in range(geo.cells):
        w = geo.windows[c]
        own = w.hi - w.lo
        rows = x[w.lo : w.hi, :]
        if w.low:
            rows = jnp.concatenate([rows, x[0 : w.low, :]], axis=0)
        product = dot(mats[c][...], rows) * scale
        base_ref[w.lo : w.hi, :] += product[:own]
        if w.low:
            base_ref[0 : w.low, :] += product[own:]
    if has_upper:
        for upper in refs:
            base_ref[0 : geo.sp, :] += dot(upper[...], x[0 : geo.sp, :]) * scale


def owned_part(geo, scale, y, prev, pot, field, mats, uppers):
    args = [y] + ([prev] if prev is not None else []) + [pot]
    args += [field] if field is not None else []
    args += list(mats) + list(uppers)
    return vmem_call(
        functools.partial(
            owned_part_kernel, geo, scale, prev is not None, field is not None, bool(uppers)
        ),
        sds(y.shape, F32),
        cost=cost_of(2.0),
    )(*args)


def add_halo(geo, scale, y_ref, up_ref, dn_ref, crosses, behinds, uppers, own_up_ref):
    h_up = up_ref[...]
    h_dn = dn_ref[...]
    for at, c in enumerate(geo.touching):
        w = geo.windows[c]
        own = w.hi - w.lo
        product = dot(crosses[at][...], h_up) * scale
        y_ref[w.lo : w.hi, :] += product[:own]
        if w.low:
            y_ref[0 : w.low, :] += product[own:]
    total = None
    for at, c in enumerate(geo.touching):
        w = geo.windows[c]
        first = w.lo - geo.dn_lo
        term = dot(behinds[at][...], h_dn[first : first + w.rows, :])
        total = term if total is None else total + term
        if uppers:
            total = total + dot(uppers[at][...], own_up_ref[...])
    y_ref[0 : geo.sp, :] += total * scale


def write_density(y_ref, occ_ref, table_ref, part_rows, dens_ref):
    parts = dens_ref.shape[0]
    own = y_ref.shape[0]
    y = y_ref[...]
    terms = y * y * occ_ref[...]
    high = terms.astype(BF)
    low = (terms - high.astype(F32)).astype(BF)
    ones = jnp.ones((SUBLANES, terms.shape[1]), BF)
    summed = dot_t(ones, high) + dot_t(ones, low)
    dens_ref[:, 0, 0:own] = jnp.broadcast_to(summed[0:1, :], (parts, own))
    band = lax.axis_index("band")
    for r in range(part_rows):
        row = table_ref[band, r : r + 1, :]
        dens_ref[:, 0, own + r * LANES : own + (r + 1) * LANES] = jnp.broadcast_to(row, (parts, LANES))


def first_finish_kernel(geo, scale, *refs):
    n = len(geo.touching)
    base_ref, up_ref, dn_ref, own_up_ref, matrix_ref = refs[:5]
    crosses, (y_ref, dn_out, up_out) = refs[5 : 5 + n], refs[5 + n : 8 + n]
    outs = refs[8 + n : 8 + 3 * n]
    build_behind(geo, dn_ref, matrix_ref, *refs[-2:], outs)
    y_ref[...] = base_ref[...]
    add_halo(geo, scale, y_ref, up_ref, dn_ref, crosses, outs[:n], outs[n:], own_up_ref)
    write_sends(geo, y_ref, dn_out, up_out)


def first_finish(geo, scale, base, halo, own_up, matrix, crosses):
    shapes = [sds(base.shape, F32), *send_shapes(geo, base.shape[1]), *behind_shapes(geo)]
    y, dn, up, *outs = vmem_call(
        functools.partial(first_finish_kernel, geo, scale),
        shapes,
        [table_scratch(geo), matrix_scratch(geo)],
        cost=cost_of(1.5),
    )(base, halo[0], halo[1], own_up, matrix, *crosses)
    n = len(geo.touching)
    return y, (dn, up), outs[:n], outs[n:]


def finish_kernel(geo, scale, mode, part_rows, *refs):
    refs = list(refs)
    n = len(geo.touching)
    base_ref, up_ref, dn_ref = refs[:3]
    refs = refs[3:]
    crosses, refs = refs[:n], refs[n:]
    behinds, refs = refs[:n], refs[n:]
    halo = (up_ref, dn_ref, crosses, behinds, (), None)
    if mode == "last":
        finish_last(geo, scale, base_ref, halo, *refs)
        return
    if mode == "density":
        occ_ref, table_ref = refs.pop(0), refs.pop(0)
    if mode == "field":
        column_ref, before_ref = refs.pop(0), refs.pop(0)
    y_ref = refs.pop(0)
    if mode == "field":
        y_ref[...] = base_ref[...] + (column_ref[...] * scale) * before_ref[...]
    else:
        y_ref[...] = base_ref[...]
    add_halo(geo, scale, y_ref, *halo)
    if mode == "density":
        _, _, out_hbm, dens, sem = refs
        write_density(y_ref, occ_ref, table_ref, part_rows, dens)
        copy = pltpu.make_async_copy(dens, out_hbm, sem)
        copy.start()
    write_sends(geo, y_ref, refs[0], refs[1])
    if mode == "density":
        copy.wait()


def finish_last(geo, scale, base_ref, halo, *refs):
    extras = (len(refs) - 3) // 2
    sources, out_hbm, targets = refs[:extras], refs[extras], refs[extras + 1 : -2]
    y_ref, sems = refs[-2:]
    top = max(geo.sp, geo.low)
    inner = pl.ds(top, geo.dn_lo - top)
    copies = fetch([(base_ref.at[inner], out_hbm.at[inner]), *zip(sources, targets)], sems)
    edges = [(0, top), (geo.dn_lo, geo.own)]
    for a, b in edges:
        y_ref[a:b, :] = base_ref[a:b, :]
    add_halo(geo, scale, y_ref, *halo)
    for i, (a, b) in enumerate(edges):
        edge = pl.ds(a, b - a)
        copy = pltpu.make_async_copy(y_ref.at[edge], out_hbm.at[edge], sems.at[1 + extras + i])
        copy.start()
        copies.append(copy)
    for copy in copies:
        copy.wait()


def finish(geo, scale, base, halo, crosses, behinds, density=None, field=None, last=None):
    columns = base.shape[1]
    args = [base, halo[0], halo[1], *crosses, *behinds]
    mode, part_rows = "plain", 0
    shapes = [sds(base.shape, F32)]
    scratch = []
    vmem, hbm = pl.BlockSpec(memory_space=pltpu.VMEM), pl.BlockSpec(memory_space=pltpu.HBM)
    out_specs = [vmem, vmem, vmem]
    if last is not None:
        mode = "last"
        args += last
        shapes += [sds(a.shape, a.dtype) for a in last]
        out_specs = [hbm] * len(shapes)
        scratch = [pltpu.VMEM(base.shape, F32), pltpu.SemaphoreType.DMA((3 + len(last),))]
    else:
        shapes += send_shapes(geo, columns)
    if field is not None:
        mode = "field"
        args += list(field)
    if density is not None:
        mode = "density"
        fg, weights, table = density
        part_rows = fg.part_rows
        args += [weights, table]
        spread = (fg.bands * fg.domains, 1, fg.width)
        shapes.append(sds(spread, F32))
        out_specs.append(hbm)
        scratch = [pltpu.VMEM(spread, F32), pltpu.SemaphoreType.DMA(())]
    return vmem_call(
        functools.partial(finish_kernel, geo, scale, mode, part_rows),
        shapes,
        scratch,
        out_specs=out_specs,
        cost=cost_of(1.0),
    )(*args)


class FieldGeometry:
    def __init__(self, bands, domains, own, share, cells, npc):
        self.bands, self.domains, self.own, self.share = bands, domains, own, share
        self.cells, self.npc = cells, npc
        self.block = own // domains
        self.rows = up_to(npc, LANES) // LANES
        self.lines = own // LANES
        self.tiles = self.lines + 1
        nloc = own + share
        self.touched = []
        for c in range(cells):
            nodes = [(c * (nloc // cells) + k) % nloc for k in range(npc)]
            self.touched.append(sorted({node // LANES for node in nodes}))
        self.at_inverse = cells * self.rows
        self.at_face = self.at_inverse + cells * self.tiles
        self.at_screen = up_to(self.at_face + 2, 2) // 2
        self.part_rows = -(-(self.at_screen + self.lines) // bands)
        self.table_rows = up_to(self.part_rows * bands, SUBLANES)
        self.width = own + self.part_rows * LANES
        self.size = self.rows * LANES
        self.at_owner_lane = LANES - domains
        self.fits = (
            domains == SUBLANES
            and own % (domains * SUBLANES) == 0
            and own % LANES == 0
            and self.block <= LANES
            and share <= self.at_owner_lane
            and max(npc, nloc) < CODE_BASE - 1
        )


CODE_BASE = 2048
CODE_BITS = 11


def pieces(length, blocks):
    found = []
    for j in range(blocks):
        done = 0
        while done < length:
            at = j * length + done
            count = min(length - done, LANES - at % LANES)
            found.append((at // LANES, at % LANES, j, done, count))
            done += count
    return found


def column_of(row):
    return jnp.broadcast_to(row, (LANES, LANES)).T


def inverse_row(columns, first):
    sub = lax.broadcasted_iota(I32, (LANES, LANES), 0)
    target = (lax.broadcasted_iota(I32, (LANES, LANES), 1) + first).astype(F32)
    found = jnp.zeros((LANES, LANES), F32)
    for r, column in enumerate(columns):
        found = jnp.where(column == target, (sub + (r * LANES + 1)).astype(F32), found)
    return jnp.sum(found, axis=0, keepdims=True) - 1.0


def field_tables_kernel(fg, *refs):
    nodes_ref, face_ref, owner_ref, screen_ref = refs[:4]
    table_ref, pad, one, spare, packed = refs[5:]
    one[...] = jnp.full(one.shape, -1.0, F32)
    spare[...] = jnp.full(spare.shape, -1.0, F32)
    pad[...] = jnp.full(pad.shape, -1, I32)
    pad[0 : fg.cells, 0 : fg.npc] = nodes_ref[...]
    for c in range(fg.cells):
        columns = []
        for r in range(fg.rows):
            code = pad[c : c + 1, r * LANES : (r + 1) * LANES].astype(F32)
            one[c * fg.rows + r : c * fg.rows + r + 1, :] = code
            columns.append(column_of(code))
        for t in fg.touched[c]:
            at = fg.at_inverse + c * fg.tiles + t
            one[at : at + 1, :] = inverse_row(columns, t * LANES)
    lane = fg.at_owner_lane
    spare[0:1, 0 : fg.share] = face_ref[...].astype(F32)
    spare[1:2, 0 : fg.domains] = owner_ref[...].astype(F32)
    at = fg.at_face
    one[at : at + 1, :] = spare[0:1, :]
    one[at : at + 1, lane:LANES] = owner_ref[...].astype(F32)
    back = inverse_row([column_of(spare[0:1, :])], 0)
    home = inverse_row([column_of(spare[1:2, :])], -lane)
    lanes = lax.broadcasted_iota(I32, (1, LANES), 1)
    one[at + 1 : at + 2, :] = jnp.where(lanes < lane, back, home)
    packed[...] = jnp.zeros(packed.shape, F32)
    half = fg.at_screen
    packed[0:half, :] = (one[0:half, :] + 1.0) + (one[half : 2 * half, :] + 1.0) * CODE_BASE
    packed[half : half + fg.lines, :] = screen_ref[...]
    for b in range(fg.bands):
        table_ref[b, 0 : fg.part_rows, :] = packed[b * fg.part_rows : (b + 1) * fg.part_rows, :]


def field_tables(fg, pois_nodes, pois_face, block_owner, lines, after):
    specs = [pl.BlockSpec(memory_space=pltpu.VMEM)] * 4 + [pl.BlockSpec(memory_space=pl.ANY)]
    return vmem_call(
        functools.partial(field_tables_kernel, fg),
        sds((fg.bands, up_to(fg.part_rows, SUBLANES), LANES), F32),
        [
            pltpu.VMEM((up_to(fg.cells, SUBLANES), fg.size), I32),
            pltpu.VMEM((up_to(2 * fg.at_screen, SUBLANES), LANES), F32),
            pltpu.VMEM((SUBLANES, LANES), F32),
            pltpu.VMEM((fg.table_rows, LANES), F32),
        ],
        in_specs=specs,
        cost=cost_of(1.0),
    )(pois_nodes, pois_face, block_owner, lines, after)


def lanes_of(values, index):
    return jnp.take_along_axis(values, index, axis=1, mode="promise_in_bounds")


def decode(fg, got_ref, codes):
    domains, half, own = fg.domains, fg.at_screen, fg.own

    def tile(at):
        band, row = at // fg.part_rows, at % fg.part_rows
        first = own + row * LANES
        return got_ref[band * domains : (band + 1) * domains, 0, first : first + LANES]

    for at in range(half):
        both = tile(at).astype(I32)
        codes[at] = jnp.bitwise_and(both, CODE_BASE - 1) - 1
        codes[half + at] = jnp.right_shift(both, CODE_BITS) - 1
    screens = [tile(half + g) for g in range(fg.lines)]
    lane = lax.broadcasted_iota(I32, (domains, LANES), 1)
    first, last = fg.at_owner_lane, LANES
    owners = codes[fg.at_face].astype(F32).T[first:last, :]
    inverse = codes[fg.at_face + 1].astype(F32).T[first:last, :]
    back = jnp.where(lane < fg.share, codes[fg.at_face + 1], -1)
    codes[fg.at_face + 1] = pltpu.roll(back, 1, 0)
    places = []
    for q in range(domains):
        block = jnp.broadcast_to(inverse[:, q : q + 1], (domains, LANES)).astype(I32)
        places.append(block * fg.block + lane)
    here = lax.axis_index("domain")
    narrow = lax.broadcasted_iota(I32, (domains, domains), 1)
    mine = jnp.sum(jnp.where(narrow == here, owners, 0.0), axis=1, keepdims=True)
    return places, jnp.broadcast_to(mine, (domains, LANES)).astype(I32), screens


def rows_of(values, index):
    return jnp.take_along_axis(values, index, axis=0, mode="promise_in_bounds")


def lookup(sources, code):
    lane = jnp.bitwise_and(code, LANES - 1)
    which = jnp.right_shift(code, 7)
    total = jnp.zeros(code.shape, F32)
    for b, values in sources:
        total = jnp.where(which == b, lanes_of(values, lane), total)
    return total


def field_source(fg, got_ref, places):
    domains = fg.domains
    density = []
    for g in range(fg.lines):
        at = slice(g * LANES, (g + 1) * LANES)
        total = got_ref[0:domains, 0, at]
        for b in range(1, fg.bands):
            total = total + got_ref[b * domains : (b + 1) * domains, 0, at]
        density.append(total)
    lane = lax.broadcasted_iota(I32, (domains, LANES), 1)
    source = [None] * fg.lines
    for q in range(domains):
        spread = [jnp.broadcast_to(d[q : q + 1, :], (domains, LANES)) for d in density]
        block = lookup(list(enumerate(spread)), places[q])
        for row, start, j, offset, count in pieces(fg.block, domains):
            if j == q:
                moved = pltpu.roll(block, (start - offset) % LANES, 1)
                inside = (lane >= start) & (lane < start + count)
                before = 0.0 if source[row] is None else source[row]
                source[row] = jnp.where(inside, moved, before)
    return source


def field_solve(fg, source, codes, screen, matrix_ref, high_ref, low_ref, rows, copies):
    domains, cells = fg.domains, fg.cells

    def operator(field):
        ahead = pltpu.roll(field[0], domains - 1, 0)
        local = list(field) + [lookup([(0, ahead)], codes[fg.at_face])]
        for r in range(fg.rows):
            for c in range(cells):
                sources = [(t, local[t]) for t in fg.touched[c]]
                rows[c * domains : (c + 1) * domains, r * LANES : (r + 1) * LANES] = lookup(sources, codes[c * fg.rows + r])
            if copies:
                copies.pop(0).wait()
                span = slice(r * LANES, min((r + 1) * LANES, fg.npc))
                full = matrix_ref[span, :]
                top = full.astype(BF)
                high_ref[span, :] = top
                low_ref[span, :] = (full - top.astype(F32)).astype(BF)
        picked = rows[:, 0 : fg.npc]
        high = picked.astype(BF)
        low = (picked - high.astype(F32)).astype(BF)
        both = dot(jnp.concatenate([high, low], axis=0), high_ref[...])
        half_rows = cells * domains
        rows[:, 0 : fg.npc] = both[:half_rows] + (both[half_rows:] + dot(high, low_ref[...]))
        out = [None] * fg.tiles
        for c in range(cells):
            sources = [
                (r, rows[c * domains : (c + 1) * domains, r * LANES : (r + 1) * LANES])
                for r in range(fg.rows)
            ]
            for t in fg.touched[c]:
                term = lookup(sources, codes[fg.at_inverse + c * fg.tiles + t])
                out[t] = term if out[t] is None else out[t] + term
        arriving = pltpu.roll(out[fg.lines], 1, 0)
        out[0] = out[0] + lookup([(0, arriving)], codes[fg.at_face + 1])
        return [screen[g] * field[g] + out[g] for g in range(fg.lines)]

    step_one = [s * (1.0 / solve_center) for s in source]
    applied = operator(step_one)
    residual = [s - a for s, a in zip(source, applied)]
    a1, b1 = weight_one * weight_zero, 2.0 * weight_one / solve_half
    step_two = [a1 * e + b1 * r for e, r in zip(step_one, residual)]
    applied = operator(step_two)
    residual = [r - a for r, a in zip(residual, applied)]
    a2, b2 = weight_two * weight_one, 2.0 * weight_two / solve_half
    step_three = [a2 * e + b2 * r for e, r in zip(step_two, residual)]
    return [(x + y) + z for x, y, z in zip(step_one, step_two, step_three)]


def field_kernel(fg, got_ref, matrix_hbm, column_ref, hartree_ref, codes, rows, mine, matrix_ref, high_ref, low_ref, sems):
    spans = [pl.ds(r * LANES, min(LANES, fg.npc - r * LANES)) for r in range(fg.rows)]
    copies = fetch([(matrix_hbm.at[span], matrix_ref.at[span]) for span in spans], sems)
    places, owner, screens = decode(fg, got_ref, codes)
    source = field_source(fg, got_ref, places)
    solved = field_solve(fg, source, codes, screens, matrix_ref, high_ref, low_ref, rows, copies)
    lane = lax.broadcasted_iota(I32, (fg.domains, LANES), 1)
    block = lookup(list(enumerate(solved)), lane + lax.axis_index("domain") * fg.block)
    mine[...] = rows_of(block, owner)
    for j in range(fg.domains):
        column = column_of(mine[j : j + 1, :])
        column_ref[j * fg.block : (j + 1) * fg.block, :] = column[0 : fg.block, :]
    for row, start, j, offset, count in pieces(fg.block, fg.domains):
        hartree_ref[row : row + 1, start : start + count] = mine[j : j + 1, offset : offset + count]


def field_step(fg, got, matrix):
    tile = (fg.domains, LANES)
    return vmem_call(
        functools.partial(field_kernel, fg),
        [sds((fg.own, LANES), F32), sds((fg.lines, LANES), F32)],
        [
            pltpu.VMEM((2 * fg.at_screen, *tile), I32),
            pltpu.VMEM((fg.cells * fg.domains, fg.size), F32),
            pltpu.VMEM(tile, F32),
            pltpu.VMEM(matrix.shape, F32),
            pltpu.VMEM(matrix.shape, BF),
            pltpu.VMEM(matrix.shape, BF),
            pltpu.SemaphoreType.DMA((fg.rows,)),
        ],
        in_specs=[pl.BlockSpec(memory_space=pltpu.VMEM), pl.BlockSpec(memory_space=pltpu.HBM)],
        cost=cost_of(4.0),
    )(got, *in_hbm(matrix))


def assembled(owned_rows, face_row, terms):
    owned_count = owned_rows.shape[0]
    shared = face_row.shape[0]
    coming = jnp.take(from_behind(owned_rows[:shared], "domain", -1), face_row, axis=0)
    partial_value = terms(jnp.concatenate([owned_rows, coming], axis=0))
    upper_rows = partial_value[owned_count:]
    ordered = jnp.zeros_like(upper_rows).at[face_row].set(upper_rows)
    arrived = from_behind(ordered, "domain", 1)
    return partial_value[:owned_count].at[:shared].add(arrived)


def field_terms(local_rows, pois_matrix, node_ids):
    cell_vals = jnp.take(local_rows, node_ids, axis=0)
    product = jnp.einsum(
        "pq,cq->cp",
        pois_matrix,
        cell_vals,
        precision=lax.Precision.HIGHEST,
        preferred_element_type=F32,
    )
    return jnp.zeros(local_rows.shape, F32).at[node_ids.reshape(-1)].add(product.reshape(-1))


def reshuffle(blocks):
    return lax.all_to_all(blocks, "domain", split_axis=0, concat_axis=0, tiled=True)


def distributed_field(y, occupation, owner_row, pois_matrix, pois_nodes, field_face, screening):
    owned_count = y.shape[0]
    domains = lax.axis_size("domain")
    block_len = owned_count // domains
    partial_value = jnp.dot(
        y * y, occupation, precision=lax.Precision.HIGHEST, preferred_element_type=F32
    )
    summed = lax.psum(partial_value, "band")
    arranged = (
        jnp.zeros((domains, block_len), F32)
        .at[owner_row]
        .set(summed.reshape(domains, block_len))
    )
    source = reshuffle(arranged).reshape(owned_count)

    def field_operator(vector):
        return (
            assembled(
                vector, field_face, lambda local: field_terms(local, pois_matrix, pois_nodes)
            )
            + screening * vector
        )

    step_one = source / solve_center
    residual = source - field_operator(step_one)
    step_two = weight_one * weight_zero * step_one + 2.0 * weight_one / solve_half * residual
    residual = residual - field_operator(step_two)
    step_three = weight_two * weight_one * step_two + 2.0 * weight_two / solve_half * residual
    solved = step_one + step_two + step_three
    returned = reshuffle(solved.reshape(domains, block_len))
    return jnp.take(returned, owner_row, axis=0).reshape(owned_count)


def exchange(sends):
    dn, up = sends
    h_dn = from_behind(dn, "domain", 1)
    h_up = from_behind(up, "domain", -1)
    return h_up, h_dn


def on_device(
    orbitals,
    potential,
    occupation,
    cell_matrix,
    cell_nodes,
    face_order,
    pois_matrix,
    pois_nodes,
    pois_face,
    screening,
    block_owner,
):
    domains = lax.axis_size("domain")
    bands = lax.axis_size("band")
    own, columns = orbitals.shape
    geo = Geometry(own, face_order.shape[1], cell_nodes.shape[0], cell_nodes.shape[1])
    fg = FieldGeometry(bands, domains, own, pois_face.shape[1], pois_nodes.shape[0], pois_nodes.shape[1])
    first, later = 1.0 / filter_half, 2.0 / filter_half

    others = [cell_matrix, potential.reshape(own // LANES, LANES)]
    if fg.fits:
        others += [pois_nodes, pois_face, block_owner, screening.reshape(own // LANES, LANES)]
        others.append(occupation.reshape(1, columns))
    sends, y0, nodes, (matrix, lines, *others) = pack(geo, orbitals, cell_nodes, face_order, *others)
    halo = exchange(sends)
    mats, crosses, pot = own_matrices(geo, nodes, matrix, lines)
    base = owned_part(geo, first, y0, None, pot, None, mats, ())
    y1, sends1, behinds, uppers = first_finish(geo, first, base, halo, sends[1], matrix, crosses)

    halo = exchange(sends1)
    base = owned_part(geo, later, y1, y0, pot, None, mats, uppers)
    if fg.fits:
        *others, weights = others
        table = field_tables(fg, *others, base)
    y2, *sends2 = finish(geo, later, base, halo, crosses, behinds)

    halo = exchange(sends2)
    base = owned_part(geo, later, y2, y1, pot, None, mats, uppers)
    if fg.fits:
        y3, dn, up, spread = finish(
            geo, later, base, halo, crosses, behinds, density=(fg, weights, table)
        )
        dens = lax.all_to_all(spread, ("band", "domain"), 0, 0, tiled=True)
        halo = exchange((dn, up))
        base = owned_part(geo, first, y3, None, pot, None, mats, uppers)
        column, packed = field_step(fg, dens, pois_matrix)
        z1, *sends4 = finish(geo, first, base, halo, crosses, behinds, field=(column, y3))
    else:
        y3, *sends3 = finish(geo, later, base, halo, crosses, behinds)
        halo = exchange(sends3)
        hartree = distributed_field(
            y3, occupation, block_owner[0], pois_matrix, pois_nodes, pois_face[0], screening
        )
        column = jnp.broadcast_to(hartree[:, None], (own, LANES))
        base = owned_part(geo, first, y3, None, pot, column, mats, uppers)
        z1, *sends4 = finish(geo, first, base, halo, crosses, behinds)

    halo = exchange(sends4)
    base = owned_part(geo, later, z1, y3, pot, column, mats, uppers)
    last = [packed] if fg.fits else []
    filtered, *rest = finish(geo, later, base, halo, crosses, behinds, last=last)
    if fg.fits:
        hartree = rest[0].reshape(own)
    return filtered, hartree


def solution(mesh):
    return jax.shard_map(
        on_device,
        mesh=mesh,
        in_specs=(
            P("domain", "band"),
            P("domain"),
            P("band"),
            P(),
            P("domain", None),
            P("domain", None),
            P(),
            P("domain", None),
            P("domain", None),
            P("domain"),
            P("domain", None),
        ),
        out_specs=(P("domain", "band"), P("domain")),
        check_vma=False,
    )
```

```python
import functools

import jax
import jax.numpy as jnp
from jax import lax
from jax.experimental import pallas as pl
from jax.experimental.pallas import tpu as pltpu
from jax.sharding import PartitionSpec as P

filter_center = 1.8
filter_half = 2.7
solve_center = 3.25
solve_half = 2.75
solve_ratio = solve_center / solve_half
weight_zero = 1.0 / solve_ratio
weight_one = 1.0 / (2.0 * solve_ratio - weight_zero)
weight_two = 1.0 / (2.0 * solve_ratio - weight_one)

BF = jnp.bfloat16
F32 = jnp.float32
I32 = jnp.int32
LANES = 128
SUBLANES = 8


def up_to(n, m):
    return -(-n // m) * m


def from_behind(array, axis, by):
    length = lax.axis_size(axis)
    return lax.ppermute(array, axis, [(i, (i + by) % length) for i in range(length)])


class Window:
    def __init__(self, start, npc, own, nloc):
        end = start + npc
        self.lo = start // 16 * 16
        self.hi = min(up_to(min(end, own), 16), own)
        self.touches = end > own
        self.low = up_to(max(0, end - nloc), 16)
        self.rows = self.hi - self.lo + self.low


class Geometry:
    def __init__(self, own, share, cells, npc):
        self.own, self.share, self.cells, self.npc = own, share, cells, npc
        nloc = own + share
        stride = nloc // cells
        self.sp = up_to(share, 16)
        self.npl = up_to(npc, LANES)
        self.windows = [Window(c * stride, npc, own, nloc) for c in range(cells)]
        self.touching = [c for c in range(cells) if self.windows[c].touches]
        self.dn_lo = min(self.windows[c].lo for c in self.touching)
        self.low = max(w.low for w in self.windows)
        self.dn_rows = own - self.dn_lo + self.low
        self.table_rows = up_to(cells, SUBLANES)
        self.table_lanes = up_to(npc, LANES)
        self.table_tiles = self.table_lanes // LANES


def dot(a, b):
    return lax.dot_general(a, b, (((1,), (0,)), ((), ())), preferred_element_type=F32)


def dot_t(a, b):
    return lax.dot_general(a, b, (((1,), (1,)), ((), ())), preferred_element_type=F32)


def vmem_call(kernel, out_shape, scratch=(), in_specs=None, out_specs=None, cost=None):
    kwargs = {}
    if in_specs is not None:
        kwargs["in_specs"] = in_specs
    if out_specs is not None:
        kwargs["out_specs"] = out_specs
    return pl.pallas_call(
        kernel,
        out_shape=out_shape,
        scratch_shapes=list(scratch),
        cost_estimate=cost,
        compiler_params=pltpu.CompilerParams(vmem_limit_bytes=12 * 1024 * 1024),
        **kwargs,
    )


def in_hbm(*arrays):
    return [pltpu.with_memory_space_constraint(a, pltpu.HBM) for a in arrays]


def sds(shape, dtype):
    return jax.ShapeDtypeStruct(shape, dtype)


def one_hot_rows(count, first, nodes):
    ids = lax.broadcasted_iota(I32, (count, nodes.shape[1]), 0) + first
    return jnp.where(ids == nodes, 1.0, 0.0).astype(BF)


def place_table(geo, nodes_ref, face_ref, table, faces):
    table[...] = jnp.full(table.shape, -1, I32)
    table[0 : geo.cells, 0 : geo.npc] = nodes_ref[...]
    faces[...] = jnp.zeros(faces.shape, I32)
    faces[0:1, 0 : geo.share] = face_ref[...]
    for t in range(geo.table_tiles):
        lanes = slice(t * LANES, (t + 1) * LANES)
        nodes = table[:, lanes]
        beyond = nodes - geo.own
        at = jnp.bitwise_and(beyond, LANES - 1)
        which = jnp.right_shift(beyond, 7)
        for f in range(faces.shape[1] // LANES):
            row = jnp.broadcast_to(faces[0:1, f * LANES : (f + 1) * LANES], nodes.shape)
            nodes = jnp.where(which == f, lanes_of(row, at) + geo.own, nodes)
        table[:, lanes] = nodes


def place_matrix(geo, matrix_ref, matrix_pad):
    matrix_pad[...] = jnp.zeros(matrix_pad.shape, F32)
    matrix_pad[0 : geo.npc, 0 : geo.npc] = matrix_ref[...].astype(F32)
    return matrix_pad[...].astype(BF)


def table_scratch(geo):
    return pltpu.VMEM((geo.table_rows, geo.table_lanes), I32)


def matrix_scratch(geo):
    return pltpu.VMEM((geo.npl, geo.npl), F32)


def nodes_of(geo, table, c):
    return table[c : c + 1, 0 : geo.npl]


def owned_picks(geo, c, nodes):
    w = geo.windows[c]
    picks = one_hot_rows(w.hi - w.lo, w.lo, nodes)
    if w.low:
        picks = jnp.concatenate([picks, one_hot_rows(w.low, 0, nodes)], axis=0)
    return picks


def upper_picks(geo, nodes):
    return one_hot_rows(geo.sp, geo.own, nodes)


def own_matrices_kernel(geo, *refs):
    table, matrix_ref, pot_ref = refs[:3]
    outs, matrix_pad = refs[3:-1], refs[-1]
    matrix = place_matrix(geo, matrix_ref, matrix_pad)
    for c in range(geo.cells):
        nodes = nodes_of(geo, table, c)
        own = owned_picks(geo, c, nodes)
        left = dot(own, matrix).astype(BF)
        outs[c][...] = dot_t(left, own).astype(BF)
        if c in geo.touching:
            at = geo.cells + geo.touching.index(c)
            upper = upper_picks(geo, nodes)
            outs[at][...] = dot_t(left, upper).astype(BF)
            left = dot(upper, matrix).astype(BF)
            outs[at + len(geo.touching)][...] = dot_t(left, own).astype(BF)
    column = outs[-1]
    for r in range(geo.own // LANES):
        row = jnp.broadcast_to(pot_ref[r : r + 1, :], (LANES, LANES))
        column[r * LANES : (r + 1) * LANES, :] = row.T


def own_matrices(geo, table, cell_matrix, lines):
    shapes = [sds((w.rows, w.rows), BF) for w in geo.windows]
    shapes += [sds((geo.windows[c].rows, geo.sp), BF) for c in geo.touching]
    shapes += [sds((geo.sp, geo.windows[c].rows), BF) for c in geo.touching]
    shapes += [sds((geo.own, LANES), F32)]
    outs = vmem_call(
        functools.partial(own_matrices_kernel, geo),
        shapes,
        [matrix_scratch(geo)],
        cost=cost_of(2.0),
    )(table, cell_matrix, lines)
    n, m = geo.cells, geo.cells + len(geo.touching)
    return outs[:n], outs[n:m], outs[m:-1], outs[-1]


def build_behind(geo, sent_ref, matrix_ref, table, matrix_pad, behinds, uppers):
    for t in range(geo.table_tiles):
        at = geo.dn_rows + 2 * t * geo.table_rows
        digits = sent_ref[at : at + 2 * geo.table_rows, :].astype(F32)
        value = digits[: geo.table_rows] * LANES + digits[geo.table_rows :] - 1.0
        table[:, t * LANES : (t + 1) * LANES] = value.astype(I32)
    matrix = place_matrix(geo, matrix_ref, matrix_pad)
    for at, c in enumerate(geo.touching):
        nodes = nodes_of(geo, table, c)
        upper = upper_picks(geo, nodes)
        left = dot(upper, matrix).astype(BF)
        behinds[at][...] = dot_t(left, owned_picks(geo, c, nodes)).astype(BF)
        uppers[at][...] = dot_t(left, upper).astype(BF)


def cost_of(us):
    return pl.CostEstimate(flops=0, bytes_accessed=int(us * 3.0e6), transcendentals=0)


def write_rows(geo, y_ref, dn_ref, up_ref):
    top = geo.own - geo.dn_lo
    dn_ref[0:top, :] = y_ref[geo.dn_lo : geo.own, :].astype(BF)
    dn_ref[top : top + geo.low, :] = y_ref[0 : geo.low, :].astype(BF)
    up_ref[...] = y_ref[0 : geo.sp, :].astype(BF)


def window_rows(geo, c, y_ref):
    w = geo.windows[c]
    rows = y_ref[w.lo : w.hi, :].astype(BF)
    if w.low:
        rows = jnp.concatenate([rows, y_ref[0 : w.low, :].astype(BF)], axis=0)
    return rows


def is_even():
    return jnp.bitwise_and(lax.axis_index("domain"), 1) == 0


def write_sends(geo, y_ref, reaches, near_ref, far_ref):
    total = None
    for at, c in enumerate(geo.touching):
        term = dot(reaches[at][...], window_rows(geo, c, y_ref))
        total = term if total is None else total + term
    rows = y_ref[0 : geo.sp, :]
    even = is_even()
    near_ref[...] = jnp.where(even, total, rows).astype(BF)
    far_ref[...] = jnp.where(even, rows, total).astype(BF)


def send_shapes(geo, columns):
    return [sds((geo.sp, columns), BF), sds((geo.sp, columns), BF)]


def fetch(pairs, sems):
    copies = [pltpu.make_async_copy(src, dst, sems.at[i]) for i, (src, dst) in enumerate(pairs)]
    for copy in copies:
        copy.start()
    return copies


def pack_kernel(geo, extra, y_hbm, nodes_hbm, face_hbm, *refs):
    sources, refs = refs[:extra], refs[extra:]
    dn_ref, up_ref, y, table = refs[:4]
    kept, (nodes, face, faces, sems) = refs[4 : 4 + extra], refs[4 + extra :]
    cuts = sorted({0, max(geo.sp, geo.low), geo.dn_lo, geo.own})
    spans = list(zip(cuts[:-1], cuts[1:]))
    pairs = [(nodes_hbm, nodes), (face_hbm, face)]
    pairs += [(y_hbm.at[pl.ds(a, b - a)], y.at[pl.ds(a, b - a)]) for a, b in spans]
    pairs += list(zip(sources, kept))
    copies = fetch(pairs, sems)
    copies[0].wait()
    copies[1].wait()
    place_table(geo, nodes, face, table, faces)
    for t in range(geo.table_tiles):
        at = geo.dn_rows + 2 * t * geo.table_rows
        value = table[:, t * LANES : (t + 1) * LANES] + 1
        high = jnp.right_shift(value, 7).astype(F32)
        low = jnp.bitwise_and(value, LANES - 1).astype(F32)
        digits = jnp.concatenate([high, low], axis=0).astype(BF)
        dn_ref[at : at + 2 * geo.table_rows, :] = digits
    for copy in copies[2:]:
        copy.wait()
    write_rows(geo, y, dn_ref, up_ref)


def pack(geo, y, cell_nodes, face_order, *others):
    up = sds((geo.sp, y.shape[1]), BF)
    rows = geo.dn_rows + 2 * geo.table_rows * geo.table_tiles
    dn, up, y, table, *others = vmem_call(
        functools.partial(pack_kernel, geo, len(others)),
        [
            sds((rows, y.shape[1]), BF),
            up,
            sds(y.shape, F32),
            sds((geo.table_rows, geo.table_lanes), I32),
            *[sds(a.shape, a.dtype) for a in others],
        ],
        [
            pltpu.VMEM(cell_nodes.shape, I32),
            pltpu.VMEM(face_order.shape, I32),
            pltpu.VMEM((1, up_to(geo.share, LANES)), I32),
            pltpu.SemaphoreType.DMA((5 + len(others),)),
        ],
        in_specs=[pl.BlockSpec(memory_space=pltpu.HBM)] * (3 + len(others)),
        cost=cost_of(1.0),
    )(*in_hbm(y, cell_nodes, face_order, *others))
    return (dn, up), y, table, others


def owned_part_kernel(geo, scale, has_prev, has_field, has_upper, *refs):
    refs = list(refs)
    base_ref = refs.pop()
    y_ref = refs.pop(0)
    prev_ref = refs.pop(0) if has_prev else None
    pot_ref = refs.pop(0)
    field_ref = refs.pop(0) if has_field else None
    mats = [refs.pop(0) for _ in range(geo.cells)]
    y = y_ref[...]
    factor = pot_ref[...]
    if has_field:
        factor = factor + field_ref[...]
    value = ((factor - filter_center) * scale) * y
    if has_prev:
        value = value - prev_ref[...]
    base_ref[...] = value
    x = y.astype(BF)
    for c in range(geo.cells):
        w = geo.windows[c]
        own = w.hi - w.lo
        rows = x[w.lo : w.hi, :]
        if w.low:
            rows = jnp.concatenate([rows, x[0 : w.low, :]], axis=0)
        product = dot(mats[c][...], rows) * scale
        base_ref[w.lo : w.hi, :] += product[:own]
        if w.low:
            base_ref[0 : w.low, :] += product[own:]
    if has_upper:
        for upper in refs:
            base_ref[0 : geo.sp, :] += dot(upper[...], x[0 : geo.sp, :]) * scale


def owned_part(geo, scale, y, prev, pot, field, mats, uppers):
    args = [y] + ([prev] if prev is not None else []) + [pot]
    args += [field] if field is not None else []
    args += list(mats) + list(uppers)
    return vmem_call(
        functools.partial(
            owned_part_kernel, geo, scale, prev is not None, field is not None, bool(uppers)
        ),
        sds(y.shape, F32),
        cost=cost_of(2.0),
    )(*args)


def add_upper(geo, scale, y_ref, h_up, crosses):
    for at, c in enumerate(geo.touching):
        w = geo.windows[c]
        own = w.hi - w.lo
        product = dot(crosses[at][...], h_up) * scale
        y_ref[w.lo : w.hi, :] += product[:own]
        if w.low:
            y_ref[0 : w.low, :] += product[own:]


def add_rows(geo, scale, y_ref, h_dn, behinds, uppers, own_up):
    total = None
    for at, c in enumerate(geo.touching):
        w = geo.windows[c]
        first = w.lo - geo.dn_lo
        term = dot(behinds[at][...], h_dn[first : first + w.rows, :])
        term = term + dot(uppers[at][...], own_up)
        total = term if total is None else total + term
    y_ref[0 : geo.sp, :] += total * scale


def add_halo(geo, scale, y_ref, near_ref, far_ref, crosses):
    near, far = near_ref[...].astype(F32), far_ref[...].astype(F32)
    even = is_even()
    y_ref[0 : geo.sp, :] += jnp.where(even, far, near) * scale
    add_upper(geo, scale, y_ref, jnp.where(even, near, far).astype(BF), crosses)


def write_density(y_ref, occ_ref, table_ref, part_rows, dens_ref):
    parts = dens_ref.shape[0]
    own = y_ref.shape[0]
    y = y_ref[...]
    terms = y * y * occ_ref[...]
    high = terms.astype(BF)
    low = (terms - high.astype(F32)).astype(BF)
    ones = jnp.ones((SUBLANES, terms.shape[1]), BF)
    summed = dot_t(ones, high) + dot_t(ones, low)
    dens_ref[:, 0, 0:own] = jnp.broadcast_to(summed[0:1, :], (parts, own))
    band = lax.axis_index("band")
    for r in range(part_rows):
        row = table_ref[band, r : r + 1, :]
        dens_ref[:, 0, own + r * LANES : own + (r + 1) * LANES] = jnp.broadcast_to(row, (parts, LANES))


def first_finish_kernel(geo, scale, *refs):
    n = len(geo.touching)
    base_ref, up_ref, dn_ref, own_up_ref, matrix_ref = refs[:5]
    crosses, reaches, refs = refs[5 : 5 + n], refs[5 + n : 5 + 2 * n], refs[5 + 2 * n :]
    y_ref, near_out, far_out = refs[:3]
    uppers, behinds = refs[3 : 3 + n], refs[3 + n : 3 + 2 * n]
    build_behind(geo, dn_ref, matrix_ref, *refs[-2:], behinds, uppers)
    y_ref[...] = base_ref[...]
    add_upper(geo, scale, y_ref, up_ref[...], crosses)
    add_rows(geo, scale, y_ref, dn_ref[...], behinds, uppers, own_up_ref[...])
    write_sends(geo, y_ref, reaches, near_out, far_out)


def first_finish(geo, scale, base, halo, own_up, matrix, crosses, reaches):
    shapes = [sds(base.shape, F32), *send_shapes(geo, base.shape[1])]
    shapes += [sds((geo.sp, geo.sp), BF) for _ in geo.touching]
    y, near, far, *uppers = vmem_call(
        functools.partial(first_finish_kernel, geo, scale),
        shapes,
        [
            *[pltpu.VMEM((geo.sp, geo.windows[c].rows), BF) for c in geo.touching],
            table_scratch(geo),
            matrix_scratch(geo),
        ],
        cost=cost_of(1.5),
    )(base, halo[0], halo[1], own_up, matrix, *crosses, *reaches)
    return y, (near, far), uppers


def finish_kernel(geo, scale, mode, part_rows, *refs):
    refs = list(refs)
    n = len(geo.touching)
    base_ref, near_ref, far_ref = refs[:3]
    refs = refs[3:]
    crosses, refs = refs[:n], refs[n:]
    halo = (near_ref, far_ref, crosses)
    if mode == "last":
        finish_last(geo, scale, base_ref, halo, *refs)
        return
    reaches, refs = refs[:n], refs[n:]
    if mode == "density":
        occ_ref, table_ref = refs.pop(0), refs.pop(0)
    if mode == "field":
        column_ref, before_ref = refs.pop(0), refs.pop(0)
    y_ref = refs.pop(0)
    if mode == "field":
        y_ref[...] = base_ref[...] + (column_ref[...] * scale) * before_ref[...]
    else:
        y_ref[...] = base_ref[...]
    add_halo(geo, scale, y_ref, *halo)
    if mode == "density":
        _, _, out_hbm, dens, sem = refs
        write_density(y_ref, occ_ref, table_ref, part_rows, dens)
        copy = pltpu.make_async_copy(dens, out_hbm, sem)
        copy.start()
    write_sends(geo, y_ref, reaches, refs[0], refs[1])
    if mode == "density":
        copy.wait()


def finish_last(geo, scale, base_ref, halo, *refs):
    extras = (len(refs) - 3) // 2
    sources, out_hbm, targets = refs[:extras], refs[extras], refs[extras + 1 : -2]
    y_ref, sems = refs[-2:]
    top = max(geo.sp, geo.low)
    inner = pl.ds(top, geo.dn_lo - top)
    copies = fetch([(base_ref.at[inner], out_hbm.at[inner]), *zip(sources, targets)], sems)
    edges = [(0, top), (geo.dn_lo, geo.own)]
    for a, b in edges:
        y_ref[a:b, :] = base_ref[a:b, :]
    add_halo(geo, scale, y_ref, *halo)
    for i, (a, b) in enumerate(edges):
        edge = pl.ds(a, b - a)
        copy = pltpu.make_async_copy(y_ref.at[edge], out_hbm.at[edge], sems.at[1 + extras + i])
        copy.start()
        copies.append(copy)
    for copy in copies:
        copy.wait()


def finish(geo, scale, base, halo, crosses, reaches=(), density=None, field=None, last=None):
    columns = base.shape[1]
    args = [base, halo[0], halo[1], *crosses, *reaches]
    mode, part_rows = "plain", 0
    shapes = [sds(base.shape, F32)]
    scratch = []
    vmem, hbm = pl.BlockSpec(memory_space=pltpu.VMEM), pl.BlockSpec(memory_space=pltpu.HBM)
    out_specs = [vmem, vmem, vmem]
    if last is not None:
        mode = "last"
        args += last
        shapes += [sds(a.shape, a.dtype) for a in last]
        out_specs = [hbm] * len(shapes)
        scratch = [pltpu.VMEM(base.shape, F32), pltpu.SemaphoreType.DMA((3 + len(last),))]
    else:
        shapes += send_shapes(geo, columns)
    if field is not None:
        mode = "field"
        args += list(field)
    if density is not None:
        mode = "density"
        fg, weights, table = density
        part_rows = fg.part_rows
        args += [weights, table]
        spread = (fg.bands * fg.domains, 1, fg.width)
        shapes.append(sds(spread, F32))
        out_specs.append(hbm)
        scratch = [pltpu.VMEM(spread, F32), pltpu.SemaphoreType.DMA(())]
    return vmem_call(
        functools.partial(finish_kernel, geo, scale, mode, part_rows),
        shapes,
        scratch,
        out_specs=out_specs,
        cost=cost_of(1.0),
    )(*args)


class FieldGeometry:
    def __init__(self, bands, domains, own, share, cells, npc):
        self.bands, self.domains, self.own, self.share = bands, domains, own, share
        self.cells, self.npc = cells, npc
        self.block = own // domains
        self.rows = up_to(npc, LANES) // LANES
        self.lines = own // LANES
        self.tiles = self.lines + 1
        nloc = own + share
        self.touched = []
        for c in range(cells):
            nodes = [(c * (nloc // cells) + k) % nloc for k in range(npc)]
            self.touched.append(sorted({node // LANES for node in nodes}))
        self.at_inverse = cells * self.rows
        self.at_face = self.at_inverse + cells * self.tiles
        self.at_screen = up_to(self.at_face + 2, 2) // 2
        self.part_rows = -(-(self.at_screen + self.lines) // bands)
        self.table_rows = up_to(self.part_rows * bands, SUBLANES)
        self.width = own + self.part_rows * LANES
        self.size = self.rows * LANES
        self.at_owner_lane = LANES - domains
        self.fits = (
            domains == SUBLANES
            and own % (domains * SUBLANES) == 0
            and own % LANES == 0
            and self.block <= LANES
            and share <= self.at_owner_lane
            and max(npc, nloc) < CODE_BASE - 1
        )


CODE_BASE = 2048
CODE_BITS = 11


def pieces(length, blocks):
    found = []
    for j in range(blocks):
        done = 0
        while done < length:
            at = j * length + done
            count = min(length - done, LANES - at % LANES)
            found.append((at // LANES, at % LANES, j, done, count))
            done += count
    return found


def column_of(row):
    return jnp.broadcast_to(row, (LANES, LANES)).T


def inverse_row(columns, first):
    sub = lax.broadcasted_iota(I32, (LANES, LANES), 0)
    target = (lax.broadcasted_iota(I32, (LANES, LANES), 1) + first).astype(F32)
    found = jnp.zeros((LANES, LANES), F32)
    for r, column in enumerate(columns):
        found = jnp.where(column == target, (sub + (r * LANES + 1)).astype(F32), found)
    return jnp.sum(found, axis=0, keepdims=True) - 1.0


def field_tables_kernel(fg, *refs):
    nodes_ref, face_ref, owner_ref, screen_ref = refs[:4]
    table_ref, pad, one, spare, packed = refs[5:]
    one[...] = jnp.full(one.shape, -1.0, F32)
    spare[...] = jnp.full(spare.shape, -1.0, F32)
    pad[...] = jnp.full(pad.shape, -1, I32)
    pad[0 : fg.cells, 0 : fg.npc] = nodes_ref[...]
    for c in range(fg.cells):
        columns = []
        for r in range(fg.rows):
            code = pad[c : c + 1, r * LANES : (r + 1) * LANES].astype(F32)
            one[c * fg.rows + r : c * fg.rows + r + 1, :] = code
            columns.append(column_of(code))
        for t in fg.touched[c]:
            at = fg.at_inverse + c * fg.tiles + t
            one[at : at + 1, :] = inverse_row(columns, t * LANES)
    lane = fg.at_owner_lane
    spare[0:1, 0 : fg.share] = face_ref[...].astype(F32)
    spare[1:2, 0 : fg.domains] = owner_ref[...].astype(F32)
    at = fg.at_face
    one[at : at + 1, :] = spare[0:1, :]
    one[at : at + 1, lane:LANES] = owner_ref[...].astype(F32)
    back = inverse_row([column_of(spare[0:1, :])], 0)
    home = inverse_row([column_of(spare[1:2, :])], -lane)
    lanes = lax.broadcasted_iota(I32, (1, LANES), 1)
    one[at + 1 : at + 2, :] = jnp.where(lanes < lane, back, home)
    packed[...] = jnp.zeros(packed.shape, F32)
    half = fg.at_screen
    packed[0:half, :] = (one[0:half, :] + 1.0) + (one[half : 2 * half, :] + 1.0) * CODE_BASE
    packed[half : half + fg.lines, :] = screen_ref[...]
    for b in range(fg.bands):
        table_ref[b, 0 : fg.part_rows, :] = packed[b * fg.part_rows : (b + 1) * fg.part_rows, :]


def field_tables(fg, pois_nodes, pois_face, block_owner, lines, after):
    specs = [pl.BlockSpec(memory_space=pltpu.VMEM)] * 4 + [pl.BlockSpec(memory_space=pl.ANY)]
    return vmem_call(
        functools.partial(field_tables_kernel, fg),
        sds((fg.bands, up_to(fg.part_rows, SUBLANES), LANES), F32),
        [
            pltpu.VMEM((up_to(fg.cells, SUBLANES), fg.size), I32),
            pltpu.VMEM((up_to(2 * fg.at_screen, SUBLANES), LANES), F32),
            pltpu.VMEM((SUBLANES, LANES), F32),
            pltpu.VMEM((fg.table_rows, LANES), F32),
        ],
        in_specs=specs,
        cost=cost_of(1.0),
    )(pois_nodes, pois_face, block_owner, lines, after)


def lanes_of(values, index):
    return jnp.take_along_axis(values, index, axis=1, mode="promise_in_bounds")


def decode(fg, got_ref, codes):
    domains, half, own = fg.domains, fg.at_screen, fg.own

    def tile(at):
        band, row = at // fg.part_rows, at % fg.part_rows
        first = own + row * LANES
        return got_ref[band * domains : (band + 1) * domains, 0, first : first + LANES]

    for at in range(half):
        both = tile(at).astype(I32)
        codes[at] = jnp.bitwise_and(both, CODE_BASE - 1) - 1
        codes[half + at] = jnp.right_shift(both, CODE_BITS) - 1
    screens = [tile(half + g) for g in range(fg.lines)]
    lane = lax.broadcasted_iota(I32, (domains, LANES), 1)
    first, last = fg.at_owner_lane, LANES
    owners = codes[fg.at_face].astype(F32).T[first:last, :]
    inverse = codes[fg.at_face + 1].astype(F32).T[first:last, :]
    back = jnp.where(lane < fg.share, codes[fg.at_face + 1], -1)
    codes[fg.at_face + 1] = pltpu.roll(back, 1, 0)
    places = []
    for q in range(domains):
        block = jnp.broadcast_to(inverse[:, q : q + 1], (domains, LANES)).astype(I32)
        places.append(block * fg.block + lane)
    here = lax.axis_index("domain")
    narrow = lax.broadcasted_iota(I32, (domains, domains), 1)
    mine = jnp.sum(jnp.where(narrow == here, owners, 0.0), axis=1, keepdims=True)
    return places, jnp.broadcast_to(mine, (domains, LANES)).astype(I32), screens


def rows_of(values, index):
    return jnp.take_along_axis(values, index, axis=0, mode="promise_in_bounds")


def lookup(sources, code):
    lane = jnp.bitwise_and(code, LANES - 1)
    which = jnp.right_shift(code, 7)
    total = jnp.zeros(code.shape, F32)
    for b, values in sources:
        total = jnp.where(which == b, lanes_of(values, lane), total)
    return total


def field_source(fg, got_ref, places):
    domains = fg.domains
    density = []
    for g in range(fg.lines):
        at = slice(g * LANES, (g + 1) * LANES)
        total = got_ref[0:domains, 0, at]
        for b in range(1, fg.bands):
            total = total + got_ref[b * domains : (b + 1) * domains, 0, at]
        density.append(total)
    lane = lax.broadcasted_iota(I32, (domains, LANES), 1)
    source = [None] * fg.lines
    for q in range(domains):
        spread = [jnp.broadcast_to(d[q : q + 1, :], (domains, LANES)) for d in density]
        block = lookup(list(enumerate(spread)), places[q])
        for row, start, j, offset, count in pieces(fg.block, domains):
            if j == q:
                moved = pltpu.roll(block, (start - offset) % LANES, 1)
                inside = (lane >= start) & (lane < start + count)
                before = 0.0 if source[row] is None else source[row]
                source[row] = jnp.where(inside, moved, before)
    return source


def field_solve(fg, source, codes, screen, matrix_ref, high_ref, low_ref, rows, copies):
    domains, cells = fg.domains, fg.cells

    def operator(field):
        ahead = pltpu.roll(field[0], domains - 1, 0)
        local = list(field) + [lookup([(0, ahead)], codes[fg.at_face])]
        for r in range(fg.rows):
            for c in range(cells):
                sources = [(t, local[t]) for t in fg.touched[c]]
                rows[c * domains : (c + 1) * domains, r * LANES : (r + 1) * LANES] = lookup(sources, codes[c * fg.rows + r])
            if copies:
                copies.pop(0).wait()
                span = slice(r * LANES, min((r + 1) * LANES, fg.npc))
                full = matrix_ref[span, :]
                top = full.astype(BF)
                high_ref[span, :] = top
                low_ref[span, :] = (full - top.astype(F32)).astype(BF)
        picked = rows[:, 0 : fg.npc]
        high = picked.astype(BF)
        low = (picked - high.astype(F32)).astype(BF)
        both = dot(jnp.concatenate([high, low], axis=0), high_ref[...])
        half_rows = cells * domains
        rows[:, 0 : fg.npc] = both[:half_rows] + (both[half_rows:] + dot(high, low_ref[...]))
        out = [None] * fg.tiles
        for c in range(cells):
            sources = [
                (r, rows[c * domains : (c + 1) * domains, r * LANES : (r + 1) * LANES])
                for r in range(fg.rows)
            ]
            for t in fg.touched[c]:
                term = lookup(sources, codes[fg.at_inverse + c * fg.tiles + t])
                out[t] = term if out[t] is None else out[t] + term
        arriving = pltpu.roll(out[fg.lines], 1, 0)
        out[0] = out[0] + lookup([(0, arriving)], codes[fg.at_face + 1])
        return [screen[g] * field[g] + out[g] for g in range(fg.lines)]

    step_one = [s * (1.0 / solve_center) for s in source]
    applied = operator(step_one)
    residual = [s - a for s, a in zip(source, applied)]
    a1, b1 = weight_one * weight_zero, 2.0 * weight_one / solve_half
    step_two = [a1 * e + b1 * r for e, r in zip(step_one, residual)]
    applied = operator(step_two)
    residual = [r - a for r, a in zip(residual, applied)]
    a2, b2 = weight_two * weight_one, 2.0 * weight_two / solve_half
    step_three = [a2 * e + b2 * r for e, r in zip(step_two, residual)]
    return [(x + y) + z for x, y, z in zip(step_one, step_two, step_three)]


def field_kernel(fg, got_ref, matrix_hbm, column_ref, hartree_ref, codes, rows, mine, matrix_ref, high_ref, low_ref, sems):
    spans = [pl.ds(r * LANES, min(LANES, fg.npc - r * LANES)) for r in range(fg.rows)]
    copies = fetch([(matrix_hbm.at[span], matrix_ref.at[span]) for span in spans], sems)
    places, owner, screens = decode(fg, got_ref, codes)
    source = field_source(fg, got_ref, places)
    solved = field_solve(fg, source, codes, screens, matrix_ref, high_ref, low_ref, rows, copies)
    lane = lax.broadcasted_iota(I32, (fg.domains, LANES), 1)
    block = lookup(list(enumerate(solved)), lane + lax.axis_index("domain") * fg.block)
    mine[...] = rows_of(block, owner)
    for j in range(fg.domains):
        column = column_of(mine[j : j + 1, :])
        column_ref[j * fg.block : (j + 1) * fg.block, :] = column[0 : fg.block, :]
    for row, start, j, offset, count in pieces(fg.block, fg.domains):
        hartree_ref[row : row + 1, start : start + count] = mine[j : j + 1, offset : offset + count]


def field_step(fg, got, matrix):
    tile = (fg.domains, LANES)
    return vmem_call(
        functools.partial(field_kernel, fg),
        [sds((fg.own, LANES), F32), sds((fg.lines, LANES), F32)],
        [
            pltpu.VMEM((2 * fg.at_screen, *tile), I32),
            pltpu.VMEM((fg.cells * fg.domains, fg.size), F32),
            pltpu.VMEM(tile, F32),
            pltpu.VMEM(matrix.shape, F32),
            pltpu.VMEM(matrix.shape, BF),
            pltpu.VMEM(matrix.shape, BF),
            pltpu.SemaphoreType.DMA((fg.rows,)),
        ],
        in_specs=[pl.BlockSpec(memory_space=pltpu.VMEM), pl.BlockSpec(memory_space=pltpu.HBM)],
        cost=cost_of(4.0),
    )(got, *in_hbm(matrix))


def assembled(owned_rows, face_row, terms):
    owned_count = owned_rows.shape[0]
    shared = face_row.shape[0]
    coming = jnp.take(from_behind(owned_rows[:shared], "domain", -1), face_row, axis=0)
    partial_value = terms(jnp.concatenate([owned_rows, coming], axis=0))
    upper_rows = partial_value[owned_count:]
    ordered = jnp.zeros_like(upper_rows).at[face_row].set(upper_rows)
    arrived = from_behind(ordered, "domain", 1)
    return partial_value[:owned_count].at[:shared].add(arrived)


def field_terms(local_rows, pois_matrix, node_ids):
    cell_vals = jnp.take(local_rows, node_ids, axis=0)
    product = jnp.einsum(
        "pq,cq->cp",
        pois_matrix,
        cell_vals,
        precision=lax.Precision.HIGHEST,
        preferred_element_type=F32,
    )
    return jnp.zeros(local_rows.shape, F32).at[node_ids.reshape(-1)].add(product.reshape(-1))


def reshuffle(blocks):
    return lax.all_to_all(blocks, "domain", split_axis=0, concat_axis=0, tiled=True)


def distributed_field(y, occupation, owner_row, pois_matrix, pois_nodes, field_face, screening):
    owned_count = y.shape[0]
    domains = lax.axis_size("domain")
    block_len = owned_count // domains
    partial_value = jnp.dot(
        y * y, occupation, precision=lax.Precision.HIGHEST, preferred_element_type=F32
    )
    summed = lax.psum(partial_value, "band")
    arranged = (
        jnp.zeros((domains, block_len), F32)
        .at[owner_row]
        .set(summed.reshape(domains, block_len))
    )
    source = reshuffle(arranged).reshape(owned_count)

    def field_operator(vector):
        return (
            assembled(
                vector, field_face, lambda local: field_terms(local, pois_matrix, pois_nodes)
            )
            + screening * vector
        )

    step_one = source / solve_center
    residual = source - field_operator(step_one)
    step_two = weight_one * weight_zero * step_one + 2.0 * weight_one / solve_half * residual
    residual = residual - field_operator(step_two)
    step_three = weight_two * weight_one * step_two + 2.0 * weight_two / solve_half * residual
    solved = step_one + step_two + step_three
    returned = reshuffle(solved.reshape(domains, block_len))
    return jnp.take(returned, owner_row, axis=0).reshape(owned_count)


def exchange(sends):
    dn, up = sends
    h_dn = from_behind(dn, "domain", 1)
    h_up = from_behind(up, "domain", -1)
    return h_up, h_dn


def on_device(
    orbitals,
    potential,
    occupation,
    cell_matrix,
    cell_nodes,
    face_order,
    pois_matrix,
    pois_nodes,
    pois_face,
    screening,
    block_owner,
):
    domains = lax.axis_size("domain")
    bands = lax.axis_size("band")
    own, columns = orbitals.shape
    geo = Geometry(own, face_order.shape[1], cell_nodes.shape[0], cell_nodes.shape[1])
    fg = FieldGeometry(bands, domains, own, pois_face.shape[1], pois_nodes.shape[0], pois_nodes.shape[1])
    first, later = 1.0 / filter_half, 2.0 / filter_half

    others = [cell_matrix, potential.reshape(own // LANES, LANES)]
    if fg.fits:
        others += [pois_nodes, pois_face, block_owner, screening.reshape(own // LANES, LANES)]
        others.append(occupation.reshape(1, columns))
    sends, y0, nodes, (matrix, lines, *others) = pack(geo, orbitals, cell_nodes, face_order, *others)
    halo = exchange(sends)
    mats, crosses, reaches, pot = own_matrices(geo, nodes, matrix, lines)
    base = owned_part(geo, first, y0, None, pot, None, mats, ())
    y1, sends1, uppers = first_finish(
        geo, first, base, halo, sends[1], matrix, crosses, reaches
    )

    halo = swap(sends1)
    base = owned_part(geo, later, y1, y0, pot, None, mats, uppers)
    if fg.fits:
        *others, weights = others
        table = field_tables(fg, *others, base)
    y2, *sends2 = finish(geo, later, base, halo, crosses, reaches)

    halo = swap(sends2)
    base = owned_part(geo, later, y2, y1, pot, None, mats, uppers)
    if fg.fits:
        y3, dn, up, spread = finish(
            geo, later, base, halo, crosses, reaches, density=(fg, weights, table)
        )
        dens = lax.all_to_all(spread, ("band", "domain"), 0, 0, tiled=True)
        halo = swap((dn, up))
        base = owned_part(geo, first, y3, None, pot, None, mats, uppers)
        column, packed = field_step(fg, dens, pois_matrix)
        z1, *sends4 = finish(geo, first, base, halo, crosses, reaches, field=(column, y3))
    else:
        y3, *sends3 = finish(geo, later, base, halo, crosses, reaches)
        halo = swap(sends3)
        hartree = distributed_field(
            y3, occupation, block_owner[0], pois_matrix, pois_nodes, pois_face[0], screening
        )
        column = jnp.broadcast_to(hartree[:, None], (own, LANES))
        base = owned_part(geo, first, y3, None, pot, column, mats, uppers)
        z1, *sends4 = finish(geo, first, base, halo, crosses, reaches)

    halo = swap(sends4)
    base = owned_part(geo, later, z1, y3, pot, column, mats, uppers)
    last = [packed] if fg.fits else []
    filtered, *rest = finish(geo, later, base, halo, crosses, last=last)
    if fg.fits:
        hartree = rest[0].reshape(own)
    return filtered, hartree


def swap(sends):
    length = lax.axis_size("domain")
    near, far = sends
    turns = [(i, (i + 1) % length if i % 2 else (i - 1) % length) for i in range(length)]
    far = lax.ppermute(far, "domain", turns)
    near = lax.ppermute(near, "domain", [(i, i ^ 1) for i in range(length)])
    return near, far


def solution(mesh):
    return jax.shard_map(
        on_device,
        mesh=mesh,
        in_specs=(
            P("domain", "band"),
            P("domain"),
            P("band"),
            P(),
            P("domain", None),
            P("domain", None),
            P(),
            P("domain", None),
            P("domain", None),
            P("domain"),
            P("domain", None),
        ),
        out_specs=(P("domain", "band"), P("domain")),
        check_vma=False,
    )
```

```python
import functools

import jax
import jax.numpy as jnp
from jax import lax
from jax.experimental import pallas as pl
from jax.experimental.pallas import tpu as pltpu
from jax.sharding import PartitionSpec as P

filter_center = 1.8
filter_half = 2.7
solve_center = 3.25
solve_half = 2.75
solve_ratio = solve_center / solve_half
weight_zero = 1.0 / solve_ratio
weight_one = 1.0 / (2.0 * solve_ratio - weight_zero)
weight_two = 1.0 / (2.0 * solve_ratio - weight_one)

BF = jnp.bfloat16
F32 = jnp.float32
I32 = jnp.int32
LANES = 128
SUBLANES = 8


def up_to(n, m):
    return -(-n // m) * m


def from_behind(array, axis, by):
    length = lax.axis_size(axis)
    return lax.ppermute(array, axis, [(i, (i + by) % length) for i in range(length)])


class Window:
    def __init__(self, start, npc, own, nloc):
        end = start + npc
        self.lo = start // 16 * 16
        self.hi = min(up_to(min(end, own), 16), own)
        self.touches = end > own
        self.low = up_to(max(0, end - nloc), 16)
        self.rows = self.hi - self.lo + self.low


class Geometry:
    def __init__(self, own, share, cells, npc):
        self.own, self.share, self.cells, self.npc = own, share, cells, npc
        nloc = own + share
        stride = nloc // cells
        self.sp = up_to(share, 16)
        self.npl = up_to(npc, LANES)
        self.windows = [Window(c * stride, npc, own, nloc) for c in range(cells)]
        self.touching = [c for c in range(cells) if self.windows[c].touches]
        self.dn_lo = min(self.windows[c].lo for c in self.touching)
        self.low = max(w.low for w in self.windows)
        self.dn_rows = own - self.dn_lo + self.low
        self.table_rows = up_to(cells, SUBLANES)
        self.table_lanes = up_to(npc, LANES)
        self.table_tiles = self.table_lanes // LANES


def dot(a, b):
    return lax.dot_general(a, b, (((1,), (0,)), ((), ())), preferred_element_type=F32)


def dot_t(a, b):
    return lax.dot_general(a, b, (((1,), (1,)), ((), ())), preferred_element_type=F32)


def vmem_call(kernel, out_shape, scratch=(), in_specs=None, out_specs=None, cost=None):
    kwargs = {}
    if in_specs is not None:
        kwargs["in_specs"] = in_specs
    if out_specs is not None:
        kwargs["out_specs"] = out_specs
    return pl.pallas_call(
        kernel,
        out_shape=out_shape,
        scratch_shapes=list(scratch),
        cost_estimate=cost,
        compiler_params=pltpu.CompilerParams(vmem_limit_bytes=12 * 1024 * 1024),
        **kwargs,
    )


def in_hbm(*arrays):
    return [pltpu.with_memory_space_constraint(a, pltpu.HBM) for a in arrays]


def sds(shape, dtype):
    return jax.ShapeDtypeStruct(shape, dtype)


def one_hot_rows(count, first, nodes):
    ids = lax.broadcasted_iota(I32, (count, nodes.shape[1]), 0) + first
    return jnp.where(ids == nodes, 1.0, 0.0).astype(BF)


def place_table(geo, nodes_ref, face_ref, table, faces):
    table[...] = jnp.full(table.shape, -1, I32)
    table[0 : geo.cells, 0 : geo.npc] = nodes_ref[...]
    faces[...] = jnp.zeros(faces.shape, I32)
    faces[0:1, 0 : geo.share] = face_ref[...]
    for t in range(geo.table_tiles):
        lanes = slice(t * LANES, (t + 1) * LANES)
        nodes = table[:, lanes]
        beyond = nodes - geo.own
        at = jnp.bitwise_and(beyond, LANES - 1)
        which = jnp.right_shift(beyond, 7)
        for f in range(faces.shape[1] // LANES):
            row = jnp.broadcast_to(faces[0:1, f * LANES : (f + 1) * LANES], nodes.shape)
            nodes = jnp.where(which == f, lanes_of(row, at) + geo.own, nodes)
        table[:, lanes] = nodes


def place_matrix(geo, matrix_ref, matrix_pad):
    matrix_pad[...] = jnp.zeros(matrix_pad.shape, F32)
    matrix_pad[0 : geo.npc, 0 : geo.npc] = matrix_ref[...].astype(F32)
    return matrix_pad[...].astype(BF)


def table_scratch(geo):
    return pltpu.VMEM((geo.table_rows, geo.table_lanes), I32)


def matrix_scratch(geo):
    return pltpu.VMEM((geo.npl, geo.npl), F32)


def nodes_of(geo, table, c):
    return table[c : c + 1, 0 : geo.npl]


def owned_picks(geo, c, nodes):
    w = geo.windows[c]
    picks = one_hot_rows(w.hi - w.lo, w.lo, nodes)
    if w.low:
        picks = jnp.concatenate([picks, one_hot_rows(w.low, 0, nodes)], axis=0)
    return picks


def upper_picks(geo, nodes):
    return one_hot_rows(geo.sp, geo.own, nodes)


def own_matrices_kernel(geo, *refs):
    table, matrix_ref, pot_ref = refs[:3]
    outs, matrix_pad = refs[3:-1], refs[-1]
    matrix = place_matrix(geo, matrix_ref, matrix_pad)
    for c in range(geo.cells):
        nodes = nodes_of(geo, table, c)
        own = owned_picks(geo, c, nodes)
        left = dot(own, matrix).astype(BF)
        outs[c][...] = dot_t(left, own).astype(BF)
        if c in geo.touching:
            at = geo.cells + geo.touching.index(c)
            upper = upper_picks(geo, nodes)
            outs[at][...] = dot_t(left, upper).astype(BF)
            left = dot(upper, matrix).astype(BF)
            outs[at + len(geo.touching)][...] = dot_t(left, own).astype(BF)
    column = outs[-1]
    for r in range(geo.own // LANES):
        row = jnp.broadcast_to(pot_ref[r : r + 1, :], (LANES, LANES))
        column[r * LANES : (r + 1) * LANES, :] = row.T


def own_matrices(geo, table, cell_matrix, lines):
    shapes = [sds((w.rows, w.rows), BF) for w in geo.windows]
    shapes += [sds((geo.windows[c].rows, geo.sp), BF) for c in geo.touching]
    shapes += [sds((geo.sp, geo.windows[c].rows), BF) for c in geo.touching]
    shapes += [sds((geo.own, LANES), F32)]
    outs = vmem_call(
        functools.partial(own_matrices_kernel, geo),
        shapes,
        [matrix_scratch(geo)],
        cost=cost_of(2.0),
    )(table, cell_matrix, lines)
    n, m = geo.cells, geo.cells + len(geo.touching)
    return outs[:n], outs[n:m], outs[m:-1], outs[-1]


def build_behind(geo, sent_ref, matrix_ref, table, matrix_pad, behinds, uppers):
    for t in range(geo.table_tiles):
        at = geo.dn_rows + 2 * t * geo.table_rows
        digits = sent_ref[at : at + 2 * geo.table_rows, :].astype(F32)
        value = digits[: geo.table_rows] * LANES + digits[geo.table_rows :] - 1.0
        table[:, t * LANES : (t + 1) * LANES] = value.astype(I32)
    matrix = place_matrix(geo, matrix_ref, matrix_pad)
    for at, c in enumerate(geo.touching):
        nodes = nodes_of(geo, table, c)
        upper = upper_picks(geo, nodes)
        left = dot(upper, matrix).astype(BF)
        behinds[at][...] = dot_t(left, owned_picks(geo, c, nodes)).astype(BF)
        uppers[at][...] = dot_t(left, upper).astype(BF)


def cost_of(us):
    return pl.CostEstimate(flops=0, bytes_accessed=int(us * 3.0e6), transcendentals=0)


def write_rows(geo, y_ref, dn_ref, up_ref):
    top = geo.own - geo.dn_lo
    dn_ref[0:top, :] = y_ref[geo.dn_lo : geo.own, :].astype(BF)
    dn_ref[top : top + geo.low, :] = y_ref[0 : geo.low, :].astype(BF)
    up_ref[...] = y_ref[0 : geo.sp, :].astype(BF)


def window_rows(geo, c, y_ref):
    w = geo.windows[c]
    rows = y_ref[w.lo : w.hi, :].astype(BF)
    if w.low:
        rows = jnp.concatenate([rows, y_ref[0 : w.low, :].astype(BF)], axis=0)
    return rows


def is_even():
    return jnp.bitwise_and(lax.axis_index("domain"), 1) == 0


def write_sends(geo, y_ref, reaches, near_ref, far_ref):
    total = None
    for at, c in enumerate(geo.touching):
        term = dot(reaches[at][...], window_rows(geo, c, y_ref))
        total = term if total is None else total + term
    rows = y_ref[0 : geo.sp, :]
    even = is_even()
    near_ref[...] = jnp.where(even, total, rows).astype(BF)
    far_ref[...] = jnp.where(even, rows, total).astype(BF)


def send_shapes(geo, columns):
    return [sds((geo.sp, columns), BF), sds((geo.sp, columns), BF)]


def fetch(pairs, sems):
    copies = [pltpu.make_async_copy(src, dst, sems.at[i]) for i, (src, dst) in enumerate(pairs)]
    for copy in copies:
        copy.start()
    return copies


def pack_kernel(geo, extra, y_hbm, nodes_hbm, face_hbm, *refs):
    sources, refs = refs[:extra], refs[extra:]
    dn_ref, up_ref, y, table = refs[:4]
    kept, (nodes, face, faces, sems) = refs[4 : 4 + extra], refs[4 + extra :]
    cuts = sorted({0, max(geo.sp, geo.low), geo.dn_lo, geo.own})
    spans = list(zip(cuts[:-1], cuts[1:]))
    pairs = [(nodes_hbm, nodes), (face_hbm, face)]
    pairs += [(y_hbm.at[pl.ds(a, b - a)], y.at[pl.ds(a, b - a)]) for a, b in spans]
    pairs += list(zip(sources, kept))
    copies = fetch(pairs, sems)
    copies[0].wait()
    copies[1].wait()
    place_table(geo, nodes, face, table, faces)
    for t in range(geo.table_tiles):
        at = geo.dn_rows + 2 * t * geo.table_rows
        value = table[:, t * LANES : (t + 1) * LANES] + 1
        high = jnp.right_shift(value, 7).astype(F32)
        low = jnp.bitwise_and(value, LANES - 1).astype(F32)
        digits = jnp.concatenate([high, low], axis=0).astype(BF)
        dn_ref[at : at + 2 * geo.table_rows, :] = digits
    for copy in copies[2:]:
        copy.wait()
    write_rows(geo, y, dn_ref, up_ref)


def pack(geo, y, cell_nodes, face_order, *others):
    up = sds((geo.sp, y.shape[1]), BF)
    rows = geo.dn_rows + 2 * geo.table_rows * geo.table_tiles
    dn, up, y, table, *others = vmem_call(
        functools.partial(pack_kernel, geo, len(others)),
        [
            sds((rows, y.shape[1]), BF),
            up,
            sds(y.shape, F32),
            sds((geo.table_rows, geo.table_lanes), I32),
            *[sds(a.shape, a.dtype) for a in others],
        ],
        [
            pltpu.VMEM(cell_nodes.shape, I32),
            pltpu.VMEM(face_order.shape, I32),
            pltpu.VMEM((1, up_to(geo.share, LANES)), I32),
            pltpu.SemaphoreType.DMA((5 + len(others),)),
        ],
        in_specs=[pl.BlockSpec(memory_space=pltpu.HBM)] * (3 + len(others)),
        cost=cost_of(1.0),
    )(*in_hbm(y, cell_nodes, face_order, *others))
    return (dn, up), y, table, others


def owned_part_kernel(geo, scale, has_prev, has_field, has_upper, *refs):
    refs = list(refs)
    base_ref = refs.pop()
    y_ref = refs.pop(0)
    prev_ref = refs.pop(0) if has_prev else None
    pot_ref = refs.pop(0)
    field_ref = refs.pop(0) if has_field else None
    mats = [refs.pop(0) for _ in range(geo.cells)]
    y = y_ref[...]
    factor = pot_ref[...]
    if has_field:
        factor = factor + field_ref[...]
    value = ((factor - filter_center) * scale) * y
    if has_prev:
        value = value - prev_ref[...]
    base_ref[...] = value
    x = y.astype(BF)
    for c in range(geo.cells):
        w = geo.windows[c]
        own = w.hi - w.lo
        rows = x[w.lo : w.hi, :]
        if w.low:
            rows = jnp.concatenate([rows, x[0 : w.low, :]], axis=0)
        product = dot(mats[c][...], rows) * scale
        base_ref[w.lo : w.hi, :] += product[:own]
        if w.low:
            base_ref[0 : w.low, :] += product[own:]
    if has_upper:
        for upper in refs:
            base_ref[0 : geo.sp, :] += dot(upper[...], x[0 : geo.sp, :]) * scale


def owned_part(geo, scale, y, prev, pot, field, mats, uppers):
    args = [y] + ([prev] if prev is not None else []) + [pot]
    args += [field] if field is not None else []
    args += list(mats) + list(uppers)
    return vmem_call(
        functools.partial(
            owned_part_kernel, geo, scale, prev is not None, field is not None, bool(uppers)
        ),
        sds(y.shape, F32),
        cost=cost_of(2.0),
    )(*args)


def add_upper(geo, scale, y_ref, h_up, crosses):
    for at, c in enumerate(geo.touching):
        w = geo.windows[c]
        own = w.hi - w.lo
        product = dot(crosses[at][...], h_up) * scale
        y_ref[w.lo : w.hi, :] += product[:own]
        if w.low:
            y_ref[0 : w.low, :] += product[own:]


def add_rows(geo, scale, y_ref, h_dn, behinds, uppers, own_up):
    total = None
    for at, c in enumerate(geo.touching):
        w = geo.windows[c]
        first = w.lo - geo.dn_lo
        term = dot(behinds[at][...], h_dn[first : first + w.rows, :])
        term = term + dot(uppers[at][...], own_up)
        total = term if total is None else total + term
    y_ref[0 : geo.sp, :] += total * scale


def add_halo(geo, scale, y_ref, near_ref, far_ref, crosses):
    near, far = near_ref[...].astype(F32), far_ref[...].astype(F32)
    even = is_even()
    y_ref[0 : geo.sp, :] += jnp.where(even, far, near) * scale
    add_upper(geo, scale, y_ref, jnp.where(even, near, far).astype(BF), crosses)


def write_density(y_ref, occ_ref, table_ref, part_rows, dens_ref):
    parts = dens_ref.shape[0]
    own = y_ref.shape[0]
    y = y_ref[...]
    terms = y * y * occ_ref[...]
    high = terms.astype(BF)
    low = (terms - high.astype(F32)).astype(BF)
    ones = jnp.ones((SUBLANES, terms.shape[1]), BF)
    summed = dot_t(ones, high) + dot_t(ones, low)
    dens_ref[:, 0, 0:own] = jnp.broadcast_to(summed[0:1, :], (parts, own))
    band = lax.axis_index("band")
    for r in range(part_rows):
        row = table_ref[band, r : r + 1, :]
        dens_ref[:, 0, own + r * LANES : own + (r + 1) * LANES] = jnp.broadcast_to(row, (parts, LANES))


def behind_kernel(geo, sent_ref, matrix_ref, *refs):
    n = len(geo.touching)
    build_behind(geo, sent_ref, matrix_ref, *refs[2 * n :], refs[:n], refs[n : 2 * n])


def behind_matrices(geo, sent, matrix):
    shapes = [sds((geo.sp, geo.windows[c].rows), BF) for c in geo.touching]
    shapes += [sds((geo.sp, geo.sp), BF) for _ in geo.touching]
    outs = vmem_call(
        functools.partial(behind_kernel, geo),
        shapes,
        [table_scratch(geo), matrix_scratch(geo)],
        cost=cost_of(1.0),
    )(sent, matrix)
    return outs[: len(geo.touching)], outs[len(geo.touching) :]


def first_finish_kernel(geo, scale, *refs):
    n = len(geo.touching)
    base_ref, up_ref, dn_ref, own_up_ref = refs[:4]
    crosses, reaches, behinds, uppers = (refs[4 + i * n : 4 + (i + 1) * n] for i in range(4))
    y_ref, near_out, far_out = refs[4 + 4 * n :]
    y_ref[...] = base_ref[...]
    add_upper(geo, scale, y_ref, up_ref[...], crosses)
    add_rows(geo, scale, y_ref, dn_ref[...], behinds, uppers, own_up_ref[...])
    write_sends(geo, y_ref, reaches, near_out, far_out)


def first_finish(geo, scale, base, halo, own_up, crosses, reaches, behinds, uppers):
    y, near, far = vmem_call(
        functools.partial(first_finish_kernel, geo, scale),
        [sds(base.shape, F32), *send_shapes(geo, base.shape[1])],
        cost=cost_of(0.5),
    )(base, halo[0], halo[1], own_up, *crosses, *reaches, *behinds, *uppers)
    return y, (near, far)


def finish_kernel(geo, scale, mode, part_rows, *refs):
    refs = list(refs)
    n = len(geo.touching)
    base_ref, near_ref, far_ref = refs[:3]
    refs = refs[3:]
    crosses, refs = refs[:n], refs[n:]
    halo = (near_ref, far_ref, crosses)
    if mode == "last":
        finish_last(geo, scale, base_ref, halo, *refs)
        return
    reaches, refs = refs[:n], refs[n:]
    if mode == "density":
        occ_ref, table_ref = refs.pop(0), refs.pop(0)
    y_ref = refs.pop(0)
    y_ref[...] = base_ref[...]
    add_halo(geo, scale, y_ref, *halo)
    if mode == "density":
        _, _, out_hbm, dens, sem = refs
        write_density(y_ref, occ_ref, table_ref, part_rows, dens)
        copy = pltpu.make_async_copy(dens, out_hbm, sem)
        copy.start()
    write_sends(geo, y_ref, reaches, refs[0], refs[1])
    if mode == "density":
        copy.wait()


def finish_last(geo, scale, base_ref, halo, *refs):
    extras = (len(refs) - 3) // 2
    sources, out_hbm, targets = refs[:extras], refs[extras], refs[extras + 1 : -2]
    y_ref, sems = refs[-2:]
    top = max(geo.sp, geo.low)
    inner = pl.ds(top, geo.dn_lo - top)
    copies = fetch([(base_ref.at[inner], out_hbm.at[inner]), *zip(sources, targets)], sems)
    edges = [(0, top), (geo.dn_lo, geo.own)]
    for a, b in edges:
        y_ref[a:b, :] = base_ref[a:b, :]
    add_halo(geo, scale, y_ref, *halo)
    for i, (a, b) in enumerate(edges):
        edge = pl.ds(a, b - a)
        copy = pltpu.make_async_copy(y_ref.at[edge], out_hbm.at[edge], sems.at[1 + extras + i])
        copy.start()
        copies.append(copy)
    for copy in copies:
        copy.wait()


def finish(geo, scale, base, halo, crosses, reaches=(), density=None, last=None):
    columns = base.shape[1]
    args = [base, halo[0], halo[1], *crosses, *reaches]
    mode, part_rows = "plain", 0
    shapes = [sds(base.shape, F32)]
    scratch = []
    vmem, hbm = pl.BlockSpec(memory_space=pltpu.VMEM), pl.BlockSpec(memory_space=pltpu.HBM)
    out_specs = [vmem, vmem, vmem]
    if last is not None:
        mode = "last"
        args += last
        shapes += [sds(a.shape, a.dtype) for a in last]
        out_specs = [hbm] * len(shapes)
        scratch = [pltpu.VMEM(base.shape, F32), pltpu.SemaphoreType.DMA((3 + len(last),))]
    else:
        shapes += send_shapes(geo, columns)
    if density is not None:
        mode = "density"
        fg, weights, table = density
        part_rows = fg.part_rows
        args += [weights, table]
        spread = (fg.bands * fg.domains, 1, fg.width)
        shapes.append(sds(spread, F32))
        out_specs.append(hbm)
        scratch = [pltpu.VMEM(spread, F32), pltpu.SemaphoreType.DMA(())]
    return vmem_call(
        functools.partial(finish_kernel, geo, scale, mode, part_rows),
        shapes,
        scratch,
        out_specs=out_specs,
        cost=cost_of(1.0),
    )(*args)


class FieldGeometry:
    def __init__(self, bands, domains, own, share, cells, npc):
        self.bands, self.domains, self.own, self.share = bands, domains, own, share
        self.cells, self.npc = cells, npc
        self.block = own // domains
        self.rows = up_to(npc, LANES) // LANES
        self.lines = own // LANES
        self.tiles = self.lines + 1
        nloc = own + share
        self.touched = []
        for c in range(cells):
            nodes = [(c * (nloc // cells) + k) % nloc for k in range(npc)]
            self.touched.append(sorted({node // LANES for node in nodes}))
        self.at_inverse = cells * self.rows
        self.at_face = self.at_inverse + cells * self.tiles
        self.at_screen = up_to(self.at_face + 2, 2) // 2
        self.part_rows = -(-(self.at_screen + self.lines) // bands)
        self.table_rows = up_to(self.part_rows * bands, SUBLANES)
        self.width = own + self.part_rows * LANES
        self.size = self.rows * LANES
        self.at_owner_lane = LANES - domains
        self.fits = (
            domains == SUBLANES
            and own % (domains * SUBLANES) == 0
            and own % LANES == 0
            and self.block <= LANES
            and share <= self.at_owner_lane
            and max(npc, nloc) < CODE_BASE - 1
        )


CODE_BASE = 2048
CODE_BITS = 11


def pieces(length, blocks):
    found = []
    for j in range(blocks):
        done = 0
        while done < length:
            at = j * length + done
            count = min(length - done, LANES - at % LANES)
            found.append((at // LANES, at % LANES, j, done, count))
            done += count
    return found


def column_of(row):
    return jnp.broadcast_to(row, (LANES, LANES)).T


def inverse_row(columns, first):
    sub = lax.broadcasted_iota(I32, (LANES, LANES), 0)
    target = (lax.broadcasted_iota(I32, (LANES, LANES), 1) + first).astype(F32)
    found = jnp.zeros((LANES, LANES), F32)
    for r, column in enumerate(columns):
        found = jnp.where(column == target, (sub + (r * LANES + 1)).astype(F32), found)
    return jnp.sum(found, axis=0, keepdims=True) - 1.0


def field_tables_kernel(fg, *refs):
    nodes_ref, face_ref, owner_ref, screen_ref = refs[:4]
    table_ref, pad, one, spare, packed = refs[5:]
    one[...] = jnp.full(one.shape, -1.0, F32)
    spare[...] = jnp.full(spare.shape, -1.0, F32)
    pad[...] = jnp.full(pad.shape, -1, I32)
    pad[0 : fg.cells, 0 : fg.npc] = nodes_ref[...]
    for c in range(fg.cells):
        columns = []
        for r in range(fg.rows):
            code = pad[c : c + 1, r * LANES : (r + 1) * LANES].astype(F32)
            one[c * fg.rows + r : c * fg.rows + r + 1, :] = code
            columns.append(column_of(code))
        for t in fg.touched[c]:
            at = fg.at_inverse + c * fg.tiles + t
            one[at : at + 1, :] = inverse_row(columns, t * LANES)
    lane = fg.at_owner_lane
    spare[0:1, 0 : fg.share] = face_ref[...].astype(F32)
    spare[1:2, 0 : fg.domains] = owner_ref[...].astype(F32)
    at = fg.at_face
    one[at : at + 1, :] = spare[0:1, :]
    one[at : at + 1, lane:LANES] = owner_ref[...].astype(F32)
    back = inverse_row([column_of(spare[0:1, :])], 0)
    home = inverse_row([column_of(spare[1:2, :])], -lane)
    lanes = lax.broadcasted_iota(I32, (1, LANES), 1)
    one[at + 1 : at + 2, :] = jnp.where(lanes < lane, back, home)
    packed[...] = jnp.zeros(packed.shape, F32)
    half = fg.at_screen
    packed[0:half, :] = (one[0:half, :] + 1.0) + (one[half : 2 * half, :] + 1.0) * CODE_BASE
    packed[half : half + fg.lines, :] = screen_ref[...]
    for b in range(fg.bands):
        table_ref[b, 0 : fg.part_rows, :] = packed[b * fg.part_rows : (b + 1) * fg.part_rows, :]


def field_tables(fg, pois_nodes, pois_face, block_owner, lines, after):
    specs = [pl.BlockSpec(memory_space=pltpu.VMEM)] * 4 + [pl.BlockSpec(memory_space=pl.ANY)]
    return vmem_call(
        functools.partial(field_tables_kernel, fg),
        sds((fg.bands, up_to(fg.part_rows, SUBLANES), LANES), F32),
        [
            pltpu.VMEM((up_to(fg.cells, SUBLANES), fg.size), I32),
            pltpu.VMEM((up_to(2 * fg.at_screen, SUBLANES), LANES), F32),
            pltpu.VMEM((SUBLANES, LANES), F32),
            pltpu.VMEM((fg.table_rows, LANES), F32),
        ],
        in_specs=specs,
        cost=cost_of(1.0),
    )(pois_nodes, pois_face, block_owner, lines, after)


def lanes_of(values, index):
    return jnp.take_along_axis(values, index, axis=1, mode="promise_in_bounds")


def decode(fg, got_ref, codes):
    domains, half, own = fg.domains, fg.at_screen, fg.own

    def tile(at):
        band, row = at // fg.part_rows, at % fg.part_rows
        first = own + row * LANES
        return got_ref[band * domains : (band + 1) * domains, 0, first : first + LANES]

    for at in range(half):
        both = tile(at).astype(I32)
        codes[at] = jnp.bitwise_and(both, CODE_BASE - 1) - 1
        codes[half + at] = jnp.right_shift(both, CODE_BITS) - 1
    screens = [tile(half + g) for g in range(fg.lines)]
    lane = lax.broadcasted_iota(I32, (domains, LANES), 1)
    first, last = fg.at_owner_lane, LANES
    owners = codes[fg.at_face].astype(F32).T[first:last, :]
    inverse = codes[fg.at_face + 1].astype(F32).T[first:last, :]
    back = jnp.where(lane < fg.share, codes[fg.at_face + 1], -1)
    codes[fg.at_face + 1] = pltpu.roll(back, 1, 0)
    places = []
    for q in range(domains):
        block = jnp.broadcast_to(inverse[:, q : q + 1], (domains, LANES)).astype(I32)
        places.append(block * fg.block + lane)
    here = lax.axis_index("domain")
    narrow = lax.broadcasted_iota(I32, (domains, domains), 1)
    mine = jnp.sum(jnp.where(narrow == here, owners, 0.0), axis=1, keepdims=True)
    return places, jnp.broadcast_to(mine, (domains, LANES)).astype(I32), screens


def rows_of(values, index):
    return jnp.take_along_axis(values, index, axis=0, mode="promise_in_bounds")


def lookup(sources, code):
    lane = jnp.bitwise_and(code, LANES - 1)
    which = jnp.right_shift(code, 7)
    total = jnp.zeros(code.shape, F32)
    for b, values in sources:
        total = jnp.where(which == b, lanes_of(values, lane), total)
    return total


def field_source(fg, got_ref, places):
    domains = fg.domains
    density = []
    for g in range(fg.lines):
        at = slice(g * LANES, (g + 1) * LANES)
        total = got_ref[0:domains, 0, at]
        for b in range(1, fg.bands):
            total = total + got_ref[b * domains : (b + 1) * domains, 0, at]
        density.append(total)
    lane = lax.broadcasted_iota(I32, (domains, LANES), 1)
    source = [None] * fg.lines
    for q in range(domains):
        spread = [jnp.broadcast_to(d[q : q + 1, :], (domains, LANES)) for d in density]
        block = lookup(list(enumerate(spread)), places[q])
        for row, start, j, offset, count in pieces(fg.block, domains):
            if j == q:
                moved = pltpu.roll(block, (start - offset) % LANES, 1)
                inside = (lane >= start) & (lane < start + count)
                before = 0.0 if source[row] is None else source[row]
                source[row] = jnp.where(inside, moved, before)
    return source


def field_solve(fg, source, codes, screen, matrix_ref, high_ref, low_ref, rows, copies):
    domains, cells = fg.domains, fg.cells

    def operator(field):
        ahead = pltpu.roll(field[0], domains - 1, 0)
        local = list(field) + [lookup([(0, ahead)], codes[fg.at_face])]
        for r in range(fg.rows):
            for c in range(cells):
                sources = [(t, local[t]) for t in fg.touched[c]]
                rows[c * domains : (c + 1) * domains, r * LANES : (r + 1) * LANES] = lookup(sources, codes[c * fg.rows + r])
            if copies:
                copies.pop(0).wait()
                span = slice(r * LANES, min((r + 1) * LANES, fg.npc))
                full = matrix_ref[span, :]
                top = full.astype(BF)
                high_ref[span, :] = top
                low_ref[span, :] = (full - top.astype(F32)).astype(BF)
        picked = rows[:, 0 : fg.npc]
        high = picked.astype(BF)
        low = (picked - high.astype(F32)).astype(BF)
        both = dot(jnp.concatenate([high, low], axis=0), high_ref[...])
        half_rows = cells * domains
        rows[:, 0 : fg.npc] = both[:half_rows] + (both[half_rows:] + dot(high, low_ref[...]))
        out = [None] * fg.tiles
        for c in range(cells):
            sources = [
                (r, rows[c * domains : (c + 1) * domains, r * LANES : (r + 1) * LANES])
                for r in range(fg.rows)
            ]
            for t in fg.touched[c]:
                term = lookup(sources, codes[fg.at_inverse + c * fg.tiles + t])
                out[t] = term if out[t] is None else out[t] + term
        arriving = pltpu.roll(out[fg.lines], 1, 0)
        out[0] = out[0] + lookup([(0, arriving)], codes[fg.at_face + 1])
        return [screen[g] * field[g] + out[g] for g in range(fg.lines)]

    step_one = [s * (1.0 / solve_center) for s in source]
    applied = operator(step_one)
    residual = [s - a for s, a in zip(source, applied)]
    a1, b1 = weight_one * weight_zero, 2.0 * weight_one / solve_half
    step_two = [a1 * e + b1 * r for e, r in zip(step_one, residual)]
    applied = operator(step_two)
    residual = [r - a for r, a in zip(residual, applied)]
    a2, b2 = weight_two * weight_one, 2.0 * weight_two / solve_half
    step_three = [a2 * e + b2 * r for e, r in zip(step_two, residual)]
    return [(x + y) + z for x, y, z in zip(step_one, step_two, step_three)]


def field_kernel(geo, fg, scale, got_ref, matrix_hbm, base_ref, near_ref, far_ref, y_ref, *refs):
    n = len(geo.touching)
    crosses, reaches, refs = refs[:n], refs[n : 2 * n], refs[2 * n :]
    z_ref, near_out, far_out, column_ref, hartree_ref = refs[:5]
    codes, rows, mine, matrix_ref, high_ref, low_ref, sems = refs[5:]
    spans = [pl.ds(r * LANES, min(LANES, fg.npc - r * LANES)) for r in range(fg.rows)]
    copies = fetch([(matrix_hbm.at[span], matrix_ref.at[span]) for span in spans], sems)
    z_ref[...] = base_ref[...]
    add_halo(geo, scale, z_ref, near_ref, far_ref, crosses)
    places, owner, screens = decode(fg, got_ref, codes)
    source = field_source(fg, got_ref, places)
    solved = field_solve(fg, source, codes, screens, matrix_ref, high_ref, low_ref, rows, copies)
    lane = lax.broadcasted_iota(I32, (fg.domains, LANES), 1)
    block = lookup(list(enumerate(solved)), lane + lax.axis_index("domain") * fg.block)
    mine[...] = rows_of(block, owner)
    for j in range(fg.domains):
        at = slice(j * fg.block, (j + 1) * fg.block)
        column = column_of(mine[j : j + 1, :])[0 : fg.block, :]
        column_ref[at, :] = column
        z_ref[at, :] += (column * scale) * y_ref[at, :]
    write_sends(geo, z_ref, reaches, near_out, far_out)
    for row, start, j, offset, count in pieces(fg.block, fg.domains):
        hartree_ref[row : row + 1, start : start + count] = mine[j : j + 1, offset : offset + count]


def field_step(geo, fg, scale, got, matrix, base, halo, y, crosses, reaches):
    tile = (fg.domains, LANES)
    vmem = pl.BlockSpec(memory_space=pltpu.VMEM)
    args = [got, *in_hbm(matrix), base, *halo, y, *crosses, *reaches]
    specs = [vmem] * len(args)
    specs[1] = pl.BlockSpec(memory_space=pltpu.HBM)
    z, near, far, column, lines = vmem_call(
        functools.partial(field_kernel, geo, fg, scale),
        [
            sds(y.shape, F32),
            *send_shapes(geo, y.shape[1]),
            sds((fg.own, LANES), F32),
            sds((fg.lines, LANES), F32),
        ],
        [
            pltpu.VMEM((2 * fg.at_screen, *tile), I32),
            pltpu.VMEM((fg.cells * fg.domains, fg.size), F32),
            pltpu.VMEM(tile, F32),
            pltpu.VMEM(matrix.shape, F32),
            pltpu.VMEM(matrix.shape, BF),
            pltpu.VMEM(matrix.shape, BF),
            pltpu.SemaphoreType.DMA((fg.rows,)),
        ],
        in_specs=specs,
        cost=cost_of(4.0),
    )(*args)
    return z, (near, far), column, lines


def assembled(owned_rows, face_row, terms):
    owned_count = owned_rows.shape[0]
    shared = face_row.shape[0]
    coming = jnp.take(from_behind(owned_rows[:shared], "domain", -1), face_row, axis=0)
    partial_value = terms(jnp.concatenate([owned_rows, coming], axis=0))
    upper_rows = partial_value[owned_count:]
    ordered = jnp.zeros_like(upper_rows).at[face_row].set(upper_rows)
    arrived = from_behind(ordered, "domain", 1)
    return partial_value[:owned_count].at[:shared].add(arrived)


def field_terms(local_rows, pois_matrix, node_ids):
    cell_vals = jnp.take(local_rows, node_ids, axis=0)
    product = jnp.einsum(
        "pq,cq->cp",
        pois_matrix,
        cell_vals,
        precision=lax.Precision.HIGHEST,
        preferred_element_type=F32,
    )
    return jnp.zeros(local_rows.shape, F32).at[node_ids.reshape(-1)].add(product.reshape(-1))


def reshuffle(blocks):
    return lax.all_to_all(blocks, "domain", split_axis=0, concat_axis=0, tiled=True)


def distributed_field(y, occupation, owner_row, pois_matrix, pois_nodes, field_face, screening):
    owned_count = y.shape[0]
    domains = lax.axis_size("domain")
    block_len = owned_count // domains
    partial_value = jnp.dot(
        y * y, occupation, precision=lax.Precision.HIGHEST, preferred_element_type=F32
    )
    summed = lax.psum(partial_value, "band")
    arranged = (
        jnp.zeros((domains, block_len), F32)
        .at[owner_row]
        .set(summed.reshape(domains, block_len))
    )
    source = reshuffle(arranged).reshape(owned_count)

    def field_operator(vector):
        return (
            assembled(
                vector, field_face, lambda local: field_terms(local, pois_matrix, pois_nodes)
            )
            + screening * vector
        )

    step_one = source / solve_center
    residual = source - field_operator(step_one)
    step_two = weight_one * weight_zero * step_one + 2.0 * weight_one / solve_half * residual
    residual = residual - field_operator(step_two)
    step_three = weight_two * weight_one * step_two + 2.0 * weight_two / solve_half * residual
    solved = step_one + step_two + step_three
    returned = reshuffle(solved.reshape(domains, block_len))
    return jnp.take(returned, owner_row, axis=0).reshape(owned_count)


def exchange(sends):
    dn, up = sends
    h_dn = from_behind(dn, "domain", 1)
    h_up = from_behind(up, "domain", -1)
    return h_up, h_dn


def on_device(
    orbitals,
    potential,
    occupation,
    cell_matrix,
    cell_nodes,
    face_order,
    pois_matrix,
    pois_nodes,
    pois_face,
    screening,
    block_owner,
):
    domains = lax.axis_size("domain")
    bands = lax.axis_size("band")
    own, columns = orbitals.shape
    geo = Geometry(own, face_order.shape[1], cell_nodes.shape[0], cell_nodes.shape[1])
    fg = FieldGeometry(bands, domains, own, pois_face.shape[1], pois_nodes.shape[0], pois_nodes.shape[1])
    first, later = 1.0 / filter_half, 2.0 / filter_half

    others = [cell_matrix, potential.reshape(own // LANES, LANES)]
    if fg.fits:
        others += [pois_nodes, pois_face, block_owner, screening.reshape(own // LANES, LANES)]
        others.append(occupation.reshape(1, columns))
    sends, y0, nodes, (matrix, lines, *others) = pack(geo, orbitals, cell_nodes, face_order, *others)
    halo = exchange(sends)
    mats, crosses, reaches, pot = own_matrices(geo, nodes, matrix, lines)
    base = owned_part(geo, first, y0, None, pot, None, mats, ())
    behinds, uppers = behind_matrices(geo, halo[1], matrix)
    y1, sends1 = first_finish(
        geo, first, base, halo, sends[1], crosses, reaches, behinds, uppers
    )

    halo = swap(sends1)
    base = owned_part(geo, later, y1, y0, pot, None, mats, uppers)
    if fg.fits:
        *others, weights = others
        table = field_tables(fg, *others, base)
    y2, *sends2 = finish(geo, later, base, halo, crosses, reaches)

    halo = swap(sends2)
    base = owned_part(geo, later, y2, y1, pot, None, mats, uppers)
    if fg.fits:
        y3, dn, up, spread = finish(
            geo, later, base, halo, crosses, reaches, density=(fg, weights, table)
        )
        dens = lax.all_to_all(spread, ("band", "domain"), 0, 0, tiled=True)
        halo = swap((dn, up))
        base = owned_part(geo, first, y3, None, pot, None, mats, uppers)
        z1, sends4, column, packed = field_step(
            geo, fg, first, dens, pois_matrix, base, halo, y3, crosses, reaches
        )
    else:
        y3, *sends3 = finish(geo, later, base, halo, crosses, reaches)
        halo = swap(sends3)
        hartree = distributed_field(
            y3, occupation, block_owner[0], pois_matrix, pois_nodes, pois_face[0], screening
        )
        column = jnp.broadcast_to(hartree[:, None], (own, LANES))
        base = owned_part(geo, first, y3, None, pot, column, mats, uppers)
        z1, *sends4 = finish(geo, first, base, halo, crosses, reaches)

    halo = swap(sends4)
    base = owned_part(geo, later, z1, y3, pot, column, mats, uppers)
    last = [packed] if fg.fits else []
    filtered, *rest = finish(geo, later, base, halo, crosses, last=last)
    if fg.fits:
        hartree = rest[0].reshape(own)
    return filtered, hartree


def swap(sends):
    length = lax.axis_size("domain")
    near, far = sends
    turns = [(i, (i + 1) % length if i % 2 else (i - 1) % length) for i in range(length)]
    far = lax.ppermute(far, "domain", turns)
    near = lax.ppermute(near, "domain", [(i, i ^ 1) for i in range(length)])
    return near, far


def solution(mesh):
    return jax.shard_map(
        on_device,
        mesh=mesh,
        in_specs=(
            P("domain", "band"),
            P("domain"),
            P("band"),
            P(),
            P("domain", None),
            P("domain", None),
            P(),
            P("domain", None),
            P("domain", None),
            P("domain"),
            P("domain", None),
        ),
        out_specs=(P("domain", "band"), P("domain")),
        check_vma=False,
    )
```

```python
import functools

import jax
import jax.numpy as jnp
from jax import lax
from jax.experimental import pallas as pl
from jax.experimental.pallas import tpu as pltpu
from jax.sharding import PartitionSpec as P

filter_center = 1.8
filter_half = 2.7
solve_center = 3.25
solve_half = 2.75
solve_ratio = solve_center / solve_half
weight_zero = 1.0 / solve_ratio
weight_one = 1.0 / (2.0 * solve_ratio - weight_zero)
weight_two = 1.0 / (2.0 * solve_ratio - weight_one)

BF = jnp.bfloat16
F32 = jnp.float32
I32 = jnp.int32
LANES = 128
SUBLANES = 8


def up_to(n, m):
    return -(-n // m) * m


def from_behind(array, axis, by):
    length = lax.axis_size(axis)
    return lax.ppermute(array, axis, [(i, (i + by) % length) for i in range(length)])


class Window:
    def __init__(self, start, npc, own, nloc):
        end = start + npc
        self.lo = start // 16 * 16
        self.hi = min(up_to(min(end, own), 16), own)
        self.touches = end > own
        self.low = up_to(max(0, end - nloc), 16)
        self.rows = self.hi - self.lo + self.low


class Geometry:
    def __init__(self, own, share, cells, npc):
        self.own, self.share, self.cells, self.npc = own, share, cells, npc
        nloc = own + share
        stride = nloc // cells
        self.sp = up_to(share, 16)
        self.npl = up_to(npc, LANES)
        self.windows = [Window(c * stride, npc, own, nloc) for c in range(cells)]
        self.touching = [c for c in range(cells) if self.windows[c].touches]
        self.dn_lo = min(self.windows[c].lo for c in self.touching)
        self.low = max(w.low for w in self.windows)
        self.dn_rows = own - self.dn_lo + self.low
        self.table_rows = up_to(cells, SUBLANES)
        self.table_lanes = up_to(npc, LANES)
        self.table_tiles = self.table_lanes // LANES


def dot(a, b):
    return lax.dot_general(a, b, (((1,), (0,)), ((), ())), preferred_element_type=F32)


def dot_t(a, b):
    return lax.dot_general(a, b, (((1,), (1,)), ((), ())), preferred_element_type=F32)


def vmem_call(kernel, out_shape, scratch=(), in_specs=None, out_specs=None, cost=None):
    kwargs = {}
    if in_specs is not None:
        kwargs["in_specs"] = in_specs
    if out_specs is not None:
        kwargs["out_specs"] = out_specs
    return pl.pallas_call(
        kernel,
        out_shape=out_shape,
        scratch_shapes=list(scratch),
        cost_estimate=cost,
        compiler_params=pltpu.CompilerParams(vmem_limit_bytes=12 * 1024 * 1024),
        **kwargs,
    )


def in_hbm(*arrays):
    return [pltpu.with_memory_space_constraint(a, pltpu.HBM) for a in arrays]


def sds(shape, dtype):
    return jax.ShapeDtypeStruct(shape, dtype)


def one_hot_rows(count, first, nodes):
    ids = lax.broadcasted_iota(I32, (count, nodes.shape[1]), 0) + first
    return jnp.where(ids == nodes, 1.0, 0.0).astype(BF)


def place_table(geo, nodes_ref, face_ref, table, faces):
    table[...] = jnp.full(table.shape, -1, I32)
    table[0 : geo.cells, 0 : geo.npc] = nodes_ref[...]
    faces[...] = jnp.zeros(faces.shape, I32)
    faces[0:1, 0 : geo.share] = face_ref[...]
    for t in range(geo.table_tiles):
        lanes = slice(t * LANES, (t + 1) * LANES)
        nodes = table[:, lanes]
        beyond = nodes - geo.own
        at = jnp.bitwise_and(beyond, LANES - 1)
        which = jnp.right_shift(beyond, 7)
        for f in range(faces.shape[1] // LANES):
            row = jnp.broadcast_to(faces[0:1, f * LANES : (f + 1) * LANES], nodes.shape)
            nodes = jnp.where(which == f, lanes_of(row, at) + geo.own, nodes)
        table[:, lanes] = nodes


def place_matrix(geo, matrix_ref, matrix_pad):
    matrix_pad[...] = jnp.zeros(matrix_pad.shape, F32)
    matrix_pad[0 : geo.npc, 0 : geo.npc] = matrix_ref[...].astype(F32)
    return matrix_pad[...].astype(BF)


def table_scratch(geo):
    return pltpu.VMEM((geo.table_rows, geo.table_lanes), I32)


def matrix_scratch(geo):
    return pltpu.VMEM((geo.npl, geo.npl), F32)


def nodes_of(geo, table, c):
    return table[c : c + 1, 0 : geo.npl]


def owned_picks(geo, c, nodes):
    w = geo.windows[c]
    picks = one_hot_rows(w.hi - w.lo, w.lo, nodes)
    if w.low:
        picks = jnp.concatenate([picks, one_hot_rows(w.low, 0, nodes)], axis=0)
    return picks


def upper_picks(geo, nodes):
    return one_hot_rows(geo.sp, geo.own, nodes)


def own_matrices_kernel(geo, *refs):
    table, matrix_ref, pot_ref = refs[:3]
    outs, matrix_pad = refs[3:-1], refs[-1]
    matrix = place_matrix(geo, matrix_ref, matrix_pad)
    for c in range(geo.cells):
        nodes = nodes_of(geo, table, c)
        own = owned_picks(geo, c, nodes)
        left = dot(own, matrix).astype(BF)
        outs[c][...] = dot_t(left, own).astype(BF)
        if c in geo.touching:
            at = geo.cells + geo.touching.index(c)
            upper = upper_picks(geo, nodes)
            outs[at][...] = dot_t(left, upper).astype(BF)
            left = dot(upper, matrix).astype(BF)
            outs[at + len(geo.touching)][...] = dot_t(left, own).astype(BF)
    column = outs[-1]
    for r in range(geo.own // LANES):
        row = jnp.broadcast_to(pot_ref[r : r + 1, :], (LANES, LANES))
        column[r * LANES : (r + 1) * LANES, :] = row.T


def own_matrices(geo, table, cell_matrix, lines):
    shapes = [sds((w.rows, w.rows), BF) for w in geo.windows]
    shapes += [sds((geo.windows[c].rows, geo.sp), BF) for c in geo.touching]
    shapes += [sds((geo.sp, geo.windows[c].rows), BF) for c in geo.touching]
    shapes += [sds((geo.own, LANES), F32)]
    outs = vmem_call(
        functools.partial(own_matrices_kernel, geo),
        shapes,
        [matrix_scratch(geo)],
        cost=cost_of(2.0),
    )(table, cell_matrix, lines)
    n, m = geo.cells, geo.cells + len(geo.touching)
    return outs[:n], outs[n:m], outs[m:-1], outs[-1]


def build_behind(geo, sent_ref, matrix_ref, table, matrix_pad, behinds, uppers):
    for t in range(geo.table_tiles):
        at = geo.dn_rows + 2 * t * geo.table_rows
        digits = sent_ref[at : at + 2 * geo.table_rows, :].astype(F32)
        value = digits[: geo.table_rows] * LANES + digits[geo.table_rows :] - 1.0
        table[:, t * LANES : (t + 1) * LANES] = value.astype(I32)
    matrix = place_matrix(geo, matrix_ref, matrix_pad)
    for at, c in enumerate(geo.touching):
        nodes = nodes_of(geo, table, c)
        upper = upper_picks(geo, nodes)
        left = dot(upper, matrix).astype(BF)
        behinds[at][...] = dot_t(left, owned_picks(geo, c, nodes)).astype(BF)
        uppers[at][...] = dot_t(left, upper).astype(BF)


def cost_of(us):
    return pl.CostEstimate(flops=0, bytes_accessed=int(us * 3.0e6), transcendentals=0)


def write_rows(geo, y_ref, dn_ref, up_ref):
    top = geo.own - geo.dn_lo
    dn_ref[0:top, :] = y_ref[geo.dn_lo : geo.own, :].astype(BF)
    dn_ref[top : top + geo.low, :] = y_ref[0 : geo.low, :].astype(BF)
    up_ref[...] = y_ref[0 : geo.sp, :].astype(BF)


def window_rows(geo, c, y_ref):
    w = geo.windows[c]
    rows = y_ref[w.lo : w.hi, :].astype(BF)
    if w.low:
        rows = jnp.concatenate([rows, y_ref[0 : w.low, :].astype(BF)], axis=0)
    return rows


def is_even():
    return jnp.bitwise_and(lax.axis_index("domain"), 1) == 0


def write_sends(geo, y_ref, reaches, near_ref, far_ref):
    total = None
    for at, c in enumerate(geo.touching):
        term = dot(reaches[at][...], window_rows(geo, c, y_ref))
        total = term if total is None else total + term
    rows = y_ref[0 : geo.sp, :]
    even = is_even()
    near_ref[...] = jnp.where(even, total, rows).astype(BF)
    far_ref[...] = jnp.where(even, rows, total).astype(BF)


def send_shapes(geo, columns):
    return [sds((geo.sp, columns), BF), sds((geo.sp, columns), BF)]


def fetch(pairs, sems):
    copies = [pltpu.make_async_copy(src, dst, sems.at[i]) for i, (src, dst) in enumerate(pairs)]
    for copy in copies:
        copy.start()
    return copies


def pack_kernel(geo, extra, y_hbm, nodes_hbm, face_hbm, *refs):
    sources, refs = refs[:extra], refs[extra:]
    dn_ref, up_ref, y, table = refs[:4]
    kept, (nodes, face, faces, sems) = refs[4 : 4 + extra], refs[4 + extra :]
    cuts = sorted({0, max(geo.sp, geo.low), geo.dn_lo, geo.own})
    spans = list(zip(cuts[:-1], cuts[1:]))
    pairs = [(nodes_hbm, nodes), (face_hbm, face)]
    pairs += [(y_hbm.at[pl.ds(a, b - a)], y.at[pl.ds(a, b - a)]) for a, b in spans]
    pairs += list(zip(sources, kept))
    copies = fetch(pairs, sems)
    copies[0].wait()
    copies[1].wait()
    place_table(geo, nodes, face, table, faces)
    for t in range(geo.table_tiles):
        at = geo.dn_rows + 2 * t * geo.table_rows
        value = table[:, t * LANES : (t + 1) * LANES] + 1
        high = jnp.right_shift(value, 7).astype(F32)
        low = jnp.bitwise_and(value, LANES - 1).astype(F32)
        digits = jnp.concatenate([high, low], axis=0).astype(BF)
        dn_ref[at : at + 2 * geo.table_rows, :] = digits
    for copy in copies[2:]:
        copy.wait()
    write_rows(geo, y, dn_ref, up_ref)


def pack(geo, y, cell_nodes, face_order, *others):
    up = sds((geo.sp, y.shape[1]), BF)
    rows = geo.dn_rows + 2 * geo.table_rows * geo.table_tiles
    dn, up, y, table, *others = vmem_call(
        functools.partial(pack_kernel, geo, len(others)),
        [
            sds((rows, y.shape[1]), BF),
            up,
            sds(y.shape, F32),
            sds((geo.table_rows, geo.table_lanes), I32),
            *[sds(a.shape, a.dtype) for a in others],
        ],
        [
            pltpu.VMEM(cell_nodes.shape, I32),
            pltpu.VMEM(face_order.shape, I32),
            pltpu.VMEM((1, up_to(geo.share, LANES)), I32),
            pltpu.SemaphoreType.DMA((5 + len(others),)),
        ],
        in_specs=[pl.BlockSpec(memory_space=pltpu.HBM)] * (3 + len(others)),
        cost=cost_of(1.0),
    )(*in_hbm(y, cell_nodes, face_order, *others))
    return (dn, up), y, table, others


def owned_part_kernel(geo, scale, has_prev, has_field, has_upper, *refs):
    refs = list(refs)
    base_ref = refs.pop()
    y_ref = refs.pop(0)
    prev_ref = refs.pop(0) if has_prev else None
    pot_ref = refs.pop(0)
    field_ref = refs.pop(0) if has_field else None
    mats = [refs.pop(0) for _ in range(geo.cells)]
    y = y_ref[...]
    factor = pot_ref[...]
    if has_field:
        factor = factor + field_ref[...]
    value = ((factor - filter_center) * scale) * y
    if has_prev:
        value = value - prev_ref[...]
    base_ref[...] = value
    x = y.astype(BF)
    for c in range(geo.cells):
        w = geo.windows[c]
        own = w.hi - w.lo
        rows = x[w.lo : w.hi, :]
        if w.low:
            rows = jnp.concatenate([rows, x[0 : w.low, :]], axis=0)
        product = dot(mats[c][...], rows) * scale
        base_ref[w.lo : w.hi, :] += product[:own]
        if w.low:
            base_ref[0 : w.low, :] += product[own:]
    if has_upper:
        for upper in refs:
            base_ref[0 : geo.sp, :] += dot(upper[...], x[0 : geo.sp, :]) * scale


def owned_part(geo, scale, y, prev, pot, field, mats, uppers):
    args = [y] + ([prev] if prev is not None else []) + [pot]
    args += [field] if field is not None else []
    args += list(mats) + list(uppers)
    return vmem_call(
        functools.partial(
            owned_part_kernel, geo, scale, prev is not None, field is not None, bool(uppers)
        ),
        sds(y.shape, F32),
        cost=cost_of(2.0),
    )(*args)


def add_upper(geo, scale, y_ref, h_up, crosses):
    for at, c in enumerate(geo.touching):
        w = geo.windows[c]
        own = w.hi - w.lo
        product = dot(crosses[at][...], h_up) * scale
        y_ref[w.lo : w.hi, :] += product[:own]
        if w.low:
            y_ref[0 : w.low, :] += product[own:]


def add_rows(geo, scale, y_ref, h_dn, behinds, uppers, own_up):
    total = None
    for at, c in enumerate(geo.touching):
        w = geo.windows[c]
        first = w.lo - geo.dn_lo
        term = dot(behinds[at][...], h_dn[first : first + w.rows, :])
        term = term + dot(uppers[at][...], own_up)
        total = term if total is None else total + term
    y_ref[0 : geo.sp, :] += total * scale


def add_halo(geo, scale, y_ref, near_ref, far_ref, crosses):
    near, far = near_ref[...].astype(F32), far_ref[...].astype(F32)
    even = is_even()
    y_ref[0 : geo.sp, :] += jnp.where(even, far, near) * scale
    add_upper(geo, scale, y_ref, jnp.where(even, near, far).astype(BF), crosses)


def write_density(y_ref, occ_ref, table_ref, part_rows, dens_ref):
    parts = dens_ref.shape[0]
    own = y_ref.shape[0]
    y = y_ref[...]
    terms = y * y * occ_ref[...]
    high = terms.astype(BF)
    low = (terms - high.astype(F32)).astype(BF)
    ones = jnp.ones((SUBLANES, terms.shape[1]), BF)
    summed = dot_t(ones, high) + dot_t(ones, low)
    dens_ref[:, 0, 0:own] = jnp.broadcast_to(summed[0:1, :], (parts, own))
    band = lax.axis_index("band")
    for r in range(part_rows):
        row = table_ref[band, r : r + 1, :]
        dens_ref[:, 0, own + r * LANES : own + (r + 1) * LANES] = jnp.broadcast_to(row, (parts, LANES))


def behind_kernel(geo, scale, sent_ref, matrix_ref, base_ref, own_up_ref, *refs):
    n = len(geo.touching)
    uppers, out_ref, behinds, rest = refs[:n], refs[n], refs[n + 1 : 2 * n + 1], refs[2 * n + 1 :]
    build_behind(geo, sent_ref, matrix_ref, *rest, behinds, uppers)
    out_ref[...] = base_ref[...]
    add_rows(geo, scale, out_ref, sent_ref[...], behinds, uppers, own_up_ref[...])


def behind_sums(geo, scale, sent, matrix, base, own_up):
    *uppers, base = vmem_call(
        functools.partial(behind_kernel, geo, scale),
        [sds((geo.sp, geo.sp), BF) for _ in geo.touching] + [sds(base.shape, F32)],
        [
            *[pltpu.VMEM((geo.sp, geo.windows[c].rows), BF) for c in geo.touching],
            table_scratch(geo),
            matrix_scratch(geo),
        ],
        cost=cost_of(1.0),
    )(sent, matrix, base, own_up)
    return uppers, base


def first_finish_kernel(geo, scale, *refs):
    n = len(geo.touching)
    base_ref, up_ref = refs[:2]
    crosses, reaches = refs[2 : 2 + n], refs[2 + n : 2 + 2 * n]
    y_ref, near_out, far_out = refs[2 + 2 * n :]
    y_ref[...] = base_ref[...]
    add_upper(geo, scale, y_ref, up_ref[...], crosses)
    write_sends(geo, y_ref, reaches, near_out, far_out)


def first_finish(geo, scale, base, h_up, crosses, reaches):
    y, near, far = vmem_call(
        functools.partial(first_finish_kernel, geo, scale),
        [sds(base.shape, F32), *send_shapes(geo, base.shape[1])],
        cost=cost_of(0.5),
    )(base, h_up, *crosses, *reaches)
    return y, (near, far)


def finish_kernel(geo, scale, mode, part_rows, *refs):
    refs = list(refs)
    n = len(geo.touching)
    base_ref, near_ref, far_ref = refs[:3]
    refs = refs[3:]
    crosses, refs = refs[:n], refs[n:]
    halo = (near_ref, far_ref, crosses)
    if mode == "last":
        finish_last(geo, scale, base_ref, halo, *refs)
        return
    reaches, refs = refs[:n], refs[n:]
    if mode == "density":
        occ_ref, table_ref = refs.pop(0), refs.pop(0)
    y_ref = refs.pop(0)
    y_ref[...] = base_ref[...]
    add_halo(geo, scale, y_ref, *halo)
    if mode == "density":
        _, _, out_hbm, dens, sem = refs
        write_density(y_ref, occ_ref, table_ref, part_rows, dens)
        copy = pltpu.make_async_copy(dens, out_hbm, sem)
        copy.start()
    write_sends(geo, y_ref, reaches, refs[0], refs[1])
    if mode == "density":
        copy.wait()


def finish_last(geo, scale, base_ref, halo, *refs):
    extras = (len(refs) - 3) // 2
    sources, out_hbm, targets = refs[:extras], refs[extras], refs[extras + 1 : -2]
    y_ref, sems = refs[-2:]
    top = max(geo.sp, geo.low)
    inner = pl.ds(top, geo.dn_lo - top)
    copies = fetch([(base_ref.at[inner], out_hbm.at[inner]), *zip(sources, targets)], sems)
    edges = [(0, top), (geo.dn_lo, geo.own)]
    for a, b in edges:
        y_ref[a:b, :] = base_ref[a:b, :]
    add_halo(geo, scale, y_ref, *halo)
    for i, (a, b) in enumerate(edges):
        edge = pl.ds(a, b - a)
        copy = pltpu.make_async_copy(y_ref.at[edge], out_hbm.at[edge], sems.at[1 + extras + i])
        copy.start()
        copies.append(copy)
    for copy in copies:
        copy.wait()


def finish(geo, scale, base, halo, crosses, reaches=(), density=None, last=None):
    columns = base.shape[1]
    args = [base, halo[0], halo[1], *crosses, *reaches]
    mode, part_rows = "plain", 0
    shapes = [sds(base.shape, F32)]
    scratch = []
    vmem, hbm = pl.BlockSpec(memory_space=pltpu.VMEM), pl.BlockSpec(memory_space=pltpu.HBM)
    out_specs = [vmem, vmem, vmem]
    if last is not None:
        mode = "last"
        args += last
        shapes += [sds(a.shape, a.dtype) for a in last]
        out_specs = [hbm] * len(shapes)
        scratch = [pltpu.VMEM(base.shape, F32), pltpu.SemaphoreType.DMA((3 + len(last),))]
    else:
        shapes += send_shapes(geo, columns)
    if density is not None:
        mode = "density"
        fg, weights, table = density
        part_rows = fg.part_rows
        args += [weights, table]
        spread = (fg.bands * fg.domains, 1, fg.width)
        shapes.append(sds(spread, F32))
        out_specs.append(hbm)
        scratch = [pltpu.VMEM(spread, F32), pltpu.SemaphoreType.DMA(())]
    return vmem_call(
        functools.partial(finish_kernel, geo, scale, mode, part_rows),
        shapes,
        scratch,
        out_specs=out_specs,
        cost=cost_of(1.0),
    )(*args)


class FieldGeometry:
    def __init__(self, bands, domains, own, share, cells, npc):
        self.bands, self.domains, self.own, self.share = bands, domains, own, share
        self.cells, self.npc = cells, npc
        self.block = own // domains
        self.rows = up_to(npc, LANES) // LANES
        self.lines = own // LANES
        self.tiles = self.lines + 1
        nloc = own + share
        self.touched = []
        for c in range(cells):
            nodes = [(c * (nloc // cells) + k) % nloc for k in range(npc)]
            self.touched.append(sorted({node // LANES for node in nodes}))
        self.at_inverse = cells * self.rows
        self.at_face = self.at_inverse + cells * self.tiles
        self.at_screen = up_to(self.at_face + 2, 2) // 2
        self.part_rows = -(-(self.at_screen + self.lines) // bands)
        self.table_rows = up_to(self.part_rows * bands, SUBLANES)
        self.width = own + self.part_rows * LANES
        self.size = self.rows * LANES
        self.at_owner_lane = LANES - domains
        self.fits = (
            domains == SUBLANES
            and own % (domains * SUBLANES) == 0
            and own % LANES == 0
            and self.block <= LANES
            and share <= self.at_owner_lane
            and max(npc, nloc) < CODE_BASE - 1
        )


CODE_BASE = 2048
CODE_BITS = 11


def pieces(length, blocks):
    found = []
    for j in range(blocks):
        done = 0
        while done < length:
            at = j * length + done
            count = min(length - done, LANES - at % LANES)
            found.append((at // LANES, at % LANES, j, done, count))
            done += count
    return found


def column_of(row):
    return jnp.broadcast_to(row, (LANES, LANES)).T


def inverse_row(columns, first):
    sub = lax.broadcasted_iota(I32, (LANES, LANES), 0)
    target = (lax.broadcasted_iota(I32, (LANES, LANES), 1) + first).astype(F32)
    found = jnp.zeros((LANES, LANES), F32)
    for r, column in enumerate(columns):
        found = jnp.where(column == target, (sub + (r * LANES + 1)).astype(F32), found)
    return jnp.sum(found, axis=0, keepdims=True) - 1.0


def field_tables_kernel(fg, *refs):
    nodes_ref, face_ref, owner_ref, screen_ref = refs[:4]
    table_ref, pad, one, spare, packed = refs[5:]
    one[...] = jnp.full(one.shape, -1.0, F32)
    spare[...] = jnp.full(spare.shape, -1.0, F32)
    pad[...] = jnp.full(pad.shape, -1, I32)
    pad[0 : fg.cells, 0 : fg.npc] = nodes_ref[...]
    for c in range(fg.cells):
        columns = []
        for r in range(fg.rows):
            code = pad[c : c + 1, r * LANES : (r + 1) * LANES].astype(F32)
            one[c * fg.rows + r : c * fg.rows + r + 1, :] = code
            columns.append(column_of(code))
        for t in fg.touched[c]:
            at = fg.at_inverse + c * fg.tiles + t
            one[at : at + 1, :] = inverse_row(columns, t * LANES)
    lane = fg.at_owner_lane
    spare[0:1, 0 : fg.share] = face_ref[...].astype(F32)
    spare[1:2, 0 : fg.domains] = owner_ref[...].astype(F32)
    at = fg.at_face
    one[at : at + 1, :] = spare[0:1, :]
    one[at : at + 1, lane:LANES] = owner_ref[...].astype(F32)
    back = inverse_row([column_of(spare[0:1, :])], 0)
    home = inverse_row([column_of(spare[1:2, :])], -lane)
    lanes = lax.broadcasted_iota(I32, (1, LANES), 1)
    one[at + 1 : at + 2, :] = jnp.where(lanes < lane, back, home)
    packed[...] = jnp.zeros(packed.shape, F32)
    half = fg.at_screen
    packed[0:half, :] = (one[0:half, :] + 1.0) + (one[half : 2 * half, :] + 1.0) * CODE_BASE
    packed[half : half + fg.lines, :] = screen_ref[...]
    for b in range(fg.bands):
        table_ref[b, 0 : fg.part_rows, :] = packed[b * fg.part_rows : (b + 1) * fg.part_rows, :]


def field_tables(fg, pois_nodes, pois_face, block_owner, lines, after):
    specs = [pl.BlockSpec(memory_space=pltpu.VMEM)] * 4 + [pl.BlockSpec(memory_space=pl.ANY)]
    return vmem_call(
        functools.partial(field_tables_kernel, fg),
        sds((fg.bands, up_to(fg.part_rows, SUBLANES), LANES), F32),
        [
            pltpu.VMEM((up_to(fg.cells, SUBLANES), fg.size), I32),
            pltpu.VMEM((up_to(2 * fg.at_screen, SUBLANES), LANES), F32),
            pltpu.VMEM((SUBLANES, LANES), F32),
            pltpu.VMEM((fg.table_rows, LANES), F32),
        ],
        in_specs=specs,
        cost=cost_of(1.0),
    )(pois_nodes, pois_face, block_owner, lines, after)


def lanes_of(values, index):
    return jnp.take_along_axis(values, index, axis=1, mode="promise_in_bounds")


def decode(fg, got_ref, codes):
    domains, half, own = fg.domains, fg.at_screen, fg.own

    def tile(at):
        band, row = at // fg.part_rows, at % fg.part_rows
        first = own + row * LANES
        return got_ref[band * domains : (band + 1) * domains, 0, first : first + LANES]

    for at in range(half):
        both = tile(at).astype(I32)
        codes[at] = jnp.bitwise_and(both, CODE_BASE - 1) - 1
        codes[half + at] = jnp.right_shift(both, CODE_BITS) - 1
    screens = [tile(half + g) for g in range(fg.lines)]
    lane = lax.broadcasted_iota(I32, (domains, LANES), 1)
    first, last = fg.at_owner_lane, LANES
    owners = codes[fg.at_face].astype(F32).T[first:last, :]
    inverse = codes[fg.at_face + 1].astype(F32).T[first:last, :]
    back = jnp.where(lane < fg.share, codes[fg.at_face + 1], -1)
    codes[fg.at_face + 1] = pltpu.roll(back, 1, 0)
    places = []
    for q in range(domains):
        block = jnp.broadcast_to(inverse[:, q : q + 1], (domains, LANES)).astype(I32)
        places.append(block * fg.block + lane)
    here = lax.axis_index("domain")
    narrow = lax.broadcasted_iota(I32, (domains, domains), 1)
    mine = jnp.sum(jnp.where(narrow == here, owners, 0.0), axis=1, keepdims=True)
    return places, jnp.broadcast_to(mine, (domains, LANES)).astype(I32), screens


def rows_of(values, index):
    return jnp.take_along_axis(values, index, axis=0, mode="promise_in_bounds")


def lookup(sources, code):
    lane = jnp.bitwise_and(code, LANES - 1)
    which = jnp.right_shift(code, 7)
    total = jnp.zeros(code.shape, F32)
    for b, values in sources:
        total = jnp.where(which == b, lanes_of(values, lane), total)
    return total


def field_source(fg, got_ref, places):
    domains = fg.domains
    density = []
    for g in range(fg.lines):
        at = slice(g * LANES, (g + 1) * LANES)
        total = got_ref[0:domains, 0, at]
        for b in range(1, fg.bands):
            total = total + got_ref[b * domains : (b + 1) * domains, 0, at]
        density.append(total)
    lane = lax.broadcasted_iota(I32, (domains, LANES), 1)
    source = [None] * fg.lines
    for q in range(domains):
        spread = [jnp.broadcast_to(d[q : q + 1, :], (domains, LANES)) for d in density]
        block = lookup(list(enumerate(spread)), places[q])
        for row, start, j, offset, count in pieces(fg.block, domains):
            if j == q:
                moved = pltpu.roll(block, (start - offset) % LANES, 1)
                inside = (lane >= start) & (lane < start + count)
                before = 0.0 if source[row] is None else source[row]
                source[row] = jnp.where(inside, moved, before)
    return source


def field_solve(fg, source, codes, screen, matrix_ref, weight_ref, rows, copies):
    domains, cells = fg.domains, fg.cells

    def operator(field):
        ahead = pltpu.roll(field[0], domains - 1, 0)
        local = list(field) + [lookup([(0, ahead)], codes[fg.at_face])]
        for r in range(fg.rows):
            for c in range(cells):
                sources = [(t, local[t]) for t in fg.touched[c]]
                rows[c * domains : (c + 1) * domains, r * LANES : (r + 1) * LANES] = lookup(sources, codes[c * fg.rows + r])
            if copies:
                copies.pop(0).wait()
                span = slice(r * LANES, min((r + 1) * LANES, fg.npc))
                weight_ref[span, :] = matrix_ref[span, :].astype(BF)
        picked = rows[:, 0 : fg.npc]
        high = picked.astype(BF)
        low = (picked - high.astype(F32)).astype(BF)
        both = dot(jnp.concatenate([high, low], axis=0), weight_ref[...])
        half_rows = cells * domains
        rows[:, 0 : fg.npc] = both[:half_rows] + both[half_rows:]
        out = [None] * fg.tiles
        for c in range(cells):
            sources = [
                (r, rows[c * domains : (c + 1) * domains, r * LANES : (r + 1) * LANES])
                for r in range(fg.rows)
            ]
            for t in fg.touched[c]:
                term = lookup(sources, codes[fg.at_inverse + c * fg.tiles + t])
                out[t] = term if out[t] is None else out[t] + term
        arriving = pltpu.roll(out[fg.lines], 1, 0)
        out[0] = out[0] + lookup([(0, arriving)], codes[fg.at_face + 1])
        return [screen[g] * field[g] + out[g] for g in range(fg.lines)]

    step_one = [s * (1.0 / solve_center) for s in source]
    applied = operator(step_one)
    residual = [s - a for s, a in zip(source, applied)]
    a1, b1 = weight_one * weight_zero, 2.0 * weight_one / solve_half
    step_two = [a1 * e + b1 * r for e, r in zip(step_one, residual)]
    applied = operator(step_two)
    residual = [r - a for r, a in zip(residual, applied)]
    a2, b2 = weight_two * weight_one, 2.0 * weight_two / solve_half
    step_three = [a2 * e + b2 * r for e, r in zip(step_two, residual)]
    return [(x + y) + z for x, y, z in zip(step_one, step_two, step_three)]


def field_kernel(geo, fg, scale, got_ref, matrix_hbm, base_ref, near_ref, far_ref, y_ref, *refs):
    n = len(geo.touching)
    crosses, reaches, refs = refs[:n], refs[n : 2 * n], refs[2 * n :]
    z_ref, near_out, far_out, column_ref, hartree_ref = refs[:5]
    codes, rows, mine, matrix_ref, weight_ref, sems = refs[5:]
    spans = [pl.ds(r * LANES, min(LANES, fg.npc - r * LANES)) for r in range(fg.rows)]
    copies = fetch([(matrix_hbm.at[span], matrix_ref.at[span]) for span in spans], sems)
    z_ref[...] = base_ref[...]
    add_halo(geo, scale, z_ref, near_ref, far_ref, crosses)
    places, owner, screens = decode(fg, got_ref, codes)
    source = field_source(fg, got_ref, places)
    solved = field_solve(fg, source, codes, screens, matrix_ref, weight_ref, rows, copies)
    lane = lax.broadcasted_iota(I32, (fg.domains, LANES), 1)
    block = lookup(list(enumerate(solved)), lane + lax.axis_index("domain") * fg.block)
    mine[...] = rows_of(block, owner)
    for j in range(fg.domains):
        at = slice(j * fg.block, (j + 1) * fg.block)
        column = column_of(mine[j : j + 1, :])[0 : fg.block, :]
        column_ref[at, :] = column
        z_ref[at, :] += (column * scale) * y_ref[at, :]
    write_sends(geo, z_ref, reaches, near_out, far_out)
    for row, start, j, offset, count in pieces(fg.block, fg.domains):
        hartree_ref[row : row + 1, start : start + count] = mine[j : j + 1, offset : offset + count]


def field_step(geo, fg, scale, got, matrix, base, halo, y, crosses, reaches):
    tile = (fg.domains, LANES)
    vmem = pl.BlockSpec(memory_space=pltpu.VMEM)
    args = [got, *in_hbm(matrix), base, *halo, y, *crosses, *reaches]
    specs = [vmem] * len(args)
    specs[1] = pl.BlockSpec(memory_space=pltpu.HBM)
    z, near, far, column, lines = vmem_call(
        functools.partial(field_kernel, geo, fg, scale),
        [
            sds(y.shape, F32),
            *send_shapes(geo, y.shape[1]),
            sds((fg.own, LANES), F32),
            sds((fg.lines, LANES), F32),
        ],
        [
            pltpu.VMEM((2 * fg.at_screen, *tile), I32),
            pltpu.VMEM((fg.cells * fg.domains, fg.size), F32),
            pltpu.VMEM(tile, F32),
            pltpu.VMEM(matrix.shape, F32),
            pltpu.VMEM(matrix.shape, BF),
            pltpu.SemaphoreType.DMA((fg.rows,)),
        ],
        in_specs=specs,
        cost=cost_of(4.0),
    )(*args)
    return z, (near, far), column, lines


def assembled(owned_rows, face_row, terms):
    owned_count = owned_rows.shape[0]
    shared = face_row.shape[0]
    coming = jnp.take(from_behind(owned_rows[:shared], "domain", -1), face_row, axis=0)
    partial_value = terms(jnp.concatenate([owned_rows, coming], axis=0))
    upper_rows = partial_value[owned_count:]
    ordered = jnp.zeros_like(upper_rows).at[face_row].set(upper_rows)
    arrived = from_behind(ordered, "domain", 1)
    return partial_value[:owned_count].at[:shared].add(arrived)


def field_terms(local_rows, pois_matrix, node_ids):
    cell_vals = jnp.take(local_rows, node_ids, axis=0)
    product = jnp.einsum(
        "pq,cq->cp",
        pois_matrix,
        cell_vals,
        precision=lax.Precision.HIGHEST,
        preferred_element_type=F32,
    )
    return jnp.zeros(local_rows.shape, F32).at[node_ids.reshape(-1)].add(product.reshape(-1))


def reshuffle(blocks):
    return lax.all_to_all(blocks, "domain", split_axis=0, concat_axis=0, tiled=True)


def distributed_field(y, occupation, owner_row, pois_matrix, pois_nodes, field_face, screening):
    owned_count = y.shape[0]
    domains = lax.axis_size("domain")
    block_len = owned_count // domains
    partial_value = jnp.dot(
        y * y, occupation, precision=lax.Precision.HIGHEST, preferred_element_type=F32
    )
    summed = lax.psum(partial_value, "band")
    arranged = (
        jnp.zeros((domains, block_len), F32)
        .at[owner_row]
        .set(summed.reshape(domains, block_len))
    )
    source = reshuffle(arranged).reshape(owned_count)

    def field_operator(vector):
        return (
            assembled(
                vector, field_face, lambda local: field_terms(local, pois_matrix, pois_nodes)
            )
            + screening * vector
        )

    step_one = source / solve_center
    residual = source - field_operator(step_one)
    step_two = weight_one * weight_zero * step_one + 2.0 * weight_one / solve_half * residual
    residual = residual - field_operator(step_two)
    step_three = weight_two * weight_one * step_two + 2.0 * weight_two / solve_half * residual
    solved = step_one + step_two + step_three
    returned = reshuffle(solved.reshape(domains, block_len))
    return jnp.take(returned, owner_row, axis=0).reshape(owned_count)


def exchange(sends):
    dn, up = sends
    h_dn = from_behind(dn, "domain", 1)
    h_up = from_behind(up, "domain", -1)
    return h_up, h_dn


def on_device(
    orbitals,
    potential,
    occupation,
    cell_matrix,
    cell_nodes,
    face_order,
    pois_matrix,
    pois_nodes,
    pois_face,
    screening,
    block_owner,
):
    domains = lax.axis_size("domain")
    bands = lax.axis_size("band")
    own, columns = orbitals.shape
    geo = Geometry(own, face_order.shape[1], cell_nodes.shape[0], cell_nodes.shape[1])
    fg = FieldGeometry(bands, domains, own, pois_face.shape[1], pois_nodes.shape[0], pois_nodes.shape[1])
    first, later = 1.0 / filter_half, 2.0 / filter_half

    others = [cell_matrix, potential.reshape(own // LANES, LANES)]
    if fg.fits:
        others += [pois_nodes, pois_face, block_owner, screening.reshape(own // LANES, LANES)]
        others.append(occupation.reshape(1, columns))
    sends, y0, nodes, (matrix, lines, *others) = pack(geo, orbitals, cell_nodes, face_order, *others)
    halo = exchange(sends)
    mats, crosses, reaches, pot = own_matrices(geo, nodes, matrix, lines)
    base = owned_part(geo, first, y0, None, pot, None, mats, ())
    uppers, base = behind_sums(geo, first, halo[1], matrix, base, sends[1])
    y1, sends1 = first_finish(geo, first, base, halo[0], crosses, reaches)

    halo = swap(sends1)
    base = owned_part(geo, later, y1, y0, pot, None, mats, uppers)
    if fg.fits:
        *others, weights = others
        table = field_tables(fg, *others, base)
    y2, *sends2 = finish(geo, later, base, halo, crosses, reaches)

    halo = swap(sends2)
    base = owned_part(geo, later, y2, y1, pot, None, mats, uppers)
    if fg.fits:
        y3, dn, up, spread = finish(
            geo, later, base, halo, crosses, reaches, density=(fg, weights, table)
        )
        dens = lax.all_to_all(spread, ("band", "domain"), 0, 0, tiled=True)
        halo = swap((dn, up))
        base = owned_part(geo, first, y3, None, pot, None, mats, uppers)
        z1, sends4, column, packed = field_step(
            geo, fg, first, dens, pois_matrix, base, halo, y3, crosses, reaches
        )
    else:
        y3, *sends3 = finish(geo, later, base, halo, crosses, reaches)
        halo = swap(sends3)
        hartree = distributed_field(
            y3, occupation, block_owner[0], pois_matrix, pois_nodes, pois_face[0], screening
        )
        column = jnp.broadcast_to(hartree[:, None], (own, LANES))
        base = owned_part(geo, first, y3, None, pot, column, mats, uppers)
        z1, *sends4 = finish(geo, first, base, halo, crosses, reaches)

    halo = swap(sends4)
    base = owned_part(geo, later, z1, y3, pot, column, mats, uppers)
    last = [packed] if fg.fits else []
    filtered, *rest = finish(geo, later, base, halo, crosses, last=last)
    if fg.fits:
        hartree = rest[0].reshape(own)
    return filtered, hartree


def swap(sends):
    length = lax.axis_size("domain")
    near, far = sends
    turns = [(i, (i + 1) % length if i % 2 else (i - 1) % length) for i in range(length)]
    far = lax.ppermute(far, "domain", turns)
    near = lax.ppermute(near, "domain", [(i, i ^ 1) for i in range(length)])
    return near, far


def solution(mesh):
    return jax.shard_map(
        on_device,
        mesh=mesh,
        in_specs=(
            P("domain", "band"),
            P("domain"),
            P("band"),
            P(),
            P("domain", None),
            P("domain", None),
            P(),
            P("domain", None),
            P("domain", None),
            P("domain"),
            P("domain", None),
        ),
        out_specs=(P("domain", "band"), P("domain")),
        check_vma=False,
    )
```

```python
import functools

import jax
import jax.numpy as jnp
from jax import lax
from jax.experimental import pallas as pl
from jax.experimental.pallas import tpu as pltpu
from jax.sharding import PartitionSpec as P

filter_center = 1.8
filter_half = 2.7
solve_center = 3.25
solve_half = 2.75
solve_ratio = solve_center / solve_half
weight_zero = 1.0 / solve_ratio
weight_one = 1.0 / (2.0 * solve_ratio - weight_zero)
weight_two = 1.0 / (2.0 * solve_ratio - weight_one)

BF = jnp.bfloat16
F32 = jnp.float32
I32 = jnp.int32
LANES = 128
SUBLANES = 8


def up_to(n, m):
    return -(-n // m) * m


def from_behind(array, axis, by):
    length = lax.axis_size(axis)
    return lax.ppermute(array, axis, [(i, (i + by) % length) for i in range(length)])


class Window:
    def __init__(self, start, npc, own, nloc):
        end = start + npc
        self.lo = start // 16 * 16
        self.hi = min(up_to(min(end, own), 16), own)
        self.touches = end > own
        self.low = up_to(max(0, end - nloc), 16)
        self.rows = self.hi - self.lo + self.low


class Geometry:
    def __init__(self, own, share, cells, npc):
        self.own, self.share, self.cells, self.npc = own, share, cells, npc
        nloc = own + share
        stride = nloc // cells
        self.sp = up_to(share, 16)
        self.npl = up_to(npc, LANES)
        self.windows = [Window(c * stride, npc, own, nloc) for c in range(cells)]
        self.touching = [c for c in range(cells) if self.windows[c].touches]
        self.dn_lo = min(self.windows[c].lo for c in self.touching)
        self.low = max(w.low for w in self.windows)
        self.dn_rows = own - self.dn_lo + self.low
        self.table_rows = up_to(cells, SUBLANES)
        self.table_lanes = up_to(npc, LANES)
        self.table_tiles = self.table_lanes // LANES


def dot(a, b):
    return lax.dot_general(a, b, (((1,), (0,)), ((), ())), preferred_element_type=F32)


def dot_t(a, b):
    return lax.dot_general(a, b, (((1,), (1,)), ((), ())), preferred_element_type=F32)


def vmem_call(kernel, out_shape, scratch=(), in_specs=None, out_specs=None, cost=None):
    kwargs = {}
    if in_specs is not None:
        kwargs["in_specs"] = in_specs
    if out_specs is not None:
        kwargs["out_specs"] = out_specs
    return pl.pallas_call(
        kernel,
        out_shape=out_shape,
        scratch_shapes=list(scratch),
        cost_estimate=cost,
        compiler_params=pltpu.CompilerParams(vmem_limit_bytes=12 * 1024 * 1024),
        **kwargs,
    )


def in_hbm(*arrays):
    return [pltpu.with_memory_space_constraint(a, pltpu.HBM) for a in arrays]


def sds(shape, dtype):
    return jax.ShapeDtypeStruct(shape, dtype)


def one_hot_rows(count, first, nodes):
    ids = lax.broadcasted_iota(I32, (count, nodes.shape[1]), 0) + first
    return jnp.where(ids == nodes, 1.0, 0.0).astype(BF)


def place_table(geo, nodes_ref, face_ref, table, faces):
    table[...] = jnp.full(table.shape, -1, I32)
    table[0 : geo.cells, 0 : geo.npc] = nodes_ref[...]
    faces[...] = jnp.zeros(faces.shape, I32)
    faces[0:1, 0 : geo.share] = face_ref[...]
    for t in range(geo.table_tiles):
        lanes = slice(t * LANES, (t + 1) * LANES)
        nodes = table[:, lanes]
        beyond = nodes - geo.own
        at = jnp.bitwise_and(beyond, LANES - 1)
        which = jnp.right_shift(beyond, 7)
        for f in range(faces.shape[1] // LANES):
            row = jnp.broadcast_to(faces[0:1, f * LANES : (f + 1) * LANES], nodes.shape)
            nodes = jnp.where(which == f, lanes_of(row, at) + geo.own, nodes)
        table[:, lanes] = nodes


def place_matrix(geo, matrix_ref, matrix_pad):
    matrix_pad[...] = jnp.zeros(matrix_pad.shape, F32)
    matrix_pad[0 : geo.npc, 0 : geo.npc] = matrix_ref[...].astype(F32)
    return matrix_pad[...].astype(BF)


def table_scratch(geo):
    return pltpu.VMEM((geo.table_rows, geo.table_lanes), I32)


def matrix_scratch(geo):
    return pltpu.VMEM((geo.npl, geo.npl), F32)


def nodes_of(geo, table, c):
    return table[c : c + 1, 0 : geo.npl]


def owned_picks(geo, c, nodes):
    w = geo.windows[c]
    picks = one_hot_rows(w.hi - w.lo, w.lo, nodes)
    if w.low:
        picks = jnp.concatenate([picks, one_hot_rows(w.low, 0, nodes)], axis=0)
    return picks


def upper_picks(geo, nodes):
    return one_hot_rows(geo.sp, geo.own, nodes)


def own_matrices_kernel(geo, *refs):
    table, matrix_ref, pot_ref = refs[:3]
    outs, matrix_pad = refs[3:-1], refs[-1]
    matrix = place_matrix(geo, matrix_ref, matrix_pad)
    for c in range(geo.cells):
        nodes = nodes_of(geo, table, c)
        own = owned_picks(geo, c, nodes)
        left = dot(own, matrix).astype(BF)
        outs[c][...] = dot_t(left, own).astype(BF)
        if c in geo.touching:
            at = geo.cells + geo.touching.index(c)
            upper = upper_picks(geo, nodes)
            outs[at][...] = dot_t(left, upper).astype(BF)
            left = dot(upper, matrix).astype(BF)
            outs[at + len(geo.touching)][...] = dot_t(left, own).astype(BF)
    column = outs[-1]
    for r in range(geo.own // LANES):
        row = jnp.broadcast_to(pot_ref[r : r + 1, :], (LANES, LANES))
        column[r * LANES : (r + 1) * LANES, :] = row.T


def own_matrices(geo, table, cell_matrix, lines):
    shapes = [sds((w.rows, w.rows), BF) for w in geo.windows]
    shapes += [sds((geo.windows[c].rows, geo.sp), BF) for c in geo.touching]
    shapes += [sds((geo.sp, geo.windows[c].rows), BF) for c in geo.touching]
    shapes += [sds((geo.own, LANES), F32)]
    outs = vmem_call(
        functools.partial(own_matrices_kernel, geo),
        shapes,
        [matrix_scratch(geo)],
        cost=cost_of(2.0),
    )(table, cell_matrix, lines)
    n, m = geo.cells, geo.cells + len(geo.touching)
    return outs[:n], outs[n:m], outs[m:-1], outs[-1]


def build_behind(geo, sent_ref, matrix_ref, table, matrix_pad, behinds, uppers):
    for t in range(geo.table_tiles):
        at = geo.dn_rows + 2 * t * geo.table_rows
        digits = sent_ref[at : at + 2 * geo.table_rows, :].astype(F32)
        value = digits[: geo.table_rows] * LANES + digits[geo.table_rows :] - 1.0
        table[:, t * LANES : (t + 1) * LANES] = value.astype(I32)
    matrix = place_matrix(geo, matrix_ref, matrix_pad)
    for at, c in enumerate(geo.touching):
        nodes = nodes_of(geo, table, c)
        upper = upper_picks(geo, nodes)
        left = dot(upper, matrix).astype(BF)
        behinds[at][...] = dot_t(left, owned_picks(geo, c, nodes)).astype(BF)
        uppers[at][...] = dot_t(left, upper).astype(BF)


def cost_of(us):
    return pl.CostEstimate(flops=0, bytes_accessed=int(us * 3.0e6), transcendentals=0)


def write_rows(geo, y_ref, dn_ref, up_ref):
    top = geo.own - geo.dn_lo
    dn_ref[0:top, :] = y_ref[geo.dn_lo : geo.own, :].astype(BF)
    dn_ref[top : top + geo.low, :] = y_ref[0 : geo.low, :].astype(BF)
    up_ref[...] = y_ref[0 : geo.sp, :].astype(BF)


def window_rows(geo, c, y_ref):
    w = geo.windows[c]
    rows = y_ref[w.lo : w.hi, :].astype(BF)
    if w.low:
        rows = jnp.concatenate([rows, y_ref[0 : w.low, :].astype(BF)], axis=0)
    return rows


def is_even():
    return jnp.bitwise_and(lax.axis_index("domain"), 1) == 0


def write_sends(geo, y_ref, reaches, near_ref, far_ref):
    total = None
    for at, c in enumerate(geo.touching):
        term = dot(reaches[at][...], window_rows(geo, c, y_ref))
        total = term if total is None else total + term
    rows = y_ref[0 : geo.sp, :]
    even = is_even()
    near_ref[...] = jnp.where(even, total, rows).astype(BF)
    far_ref[...] = jnp.where(even, rows, total).astype(BF)


def send_shapes(geo, columns):
    return [sds((geo.sp, columns), BF), sds((geo.sp, columns), BF)]


def fetch(pairs, sems):
    copies = [pltpu.make_async_copy(src, dst, sems.at[i]) for i, (src, dst) in enumerate(pairs)]
    for copy in copies:
        copy.start()
    return copies


def pack_kernel(geo, extra, y_hbm, nodes_hbm, face_hbm, *refs):
    sources, refs = refs[:extra], refs[extra:]
    dn_ref, up_ref, y, table = refs[:4]
    kept, (nodes, face, faces, sems) = refs[4 : 4 + extra], refs[4 + extra :]
    cuts = sorted({0, max(geo.sp, geo.low), geo.dn_lo, geo.own})
    spans = list(zip(cuts[:-1], cuts[1:]))
    pairs = [(nodes_hbm, nodes), (face_hbm, face)]
    pairs += [(y_hbm.at[pl.ds(a, b - a)], y.at[pl.ds(a, b - a)]) for a, b in spans]
    pairs += list(zip(sources, kept))
    copies = fetch(pairs, sems)
    copies[0].wait()
    copies[1].wait()
    place_table(geo, nodes, face, table, faces)
    for t in range(geo.table_tiles):
        at = geo.dn_rows + 2 * t * geo.table_rows
        value = table[:, t * LANES : (t + 1) * LANES] + 1
        high = jnp.right_shift(value, 7).astype(F32)
        low = jnp.bitwise_and(value, LANES - 1).astype(F32)
        digits = jnp.concatenate([high, low], axis=0).astype(BF)
        dn_ref[at : at + 2 * geo.table_rows, :] = digits
    for copy in copies[2:]:
        copy.wait()
    write_rows(geo, y, dn_ref, up_ref)


def pack(geo, y, cell_nodes, face_order, *others):
    up = sds((geo.sp, y.shape[1]), BF)
    rows = geo.dn_rows + 2 * geo.table_rows * geo.table_tiles
    dn, up, y, table, *others = vmem_call(
        functools.partial(pack_kernel, geo, len(others)),
        [
            sds((rows, y.shape[1]), BF),
            up,
            sds(y.shape, F32),
            sds((geo.table_rows, geo.table_lanes), I32),
            *[sds(a.shape, a.dtype) for a in others],
        ],
        [
            pltpu.VMEM(cell_nodes.shape, I32),
            pltpu.VMEM(face_order.shape, I32),
            pltpu.VMEM((1, up_to(geo.share, LANES)), I32),
            pltpu.SemaphoreType.DMA((5 + len(others),)),
        ],
        in_specs=[pl.BlockSpec(memory_space=pltpu.HBM)] * (3 + len(others)),
        cost=cost_of(1.0),
    )(*in_hbm(y, cell_nodes, face_order, *others))
    return (dn, up), y, table, others


def owned_part_kernel(geo, scale, has_prev, has_field, has_upper, *refs):
    refs = list(refs)
    base_ref = refs.pop()
    y_ref = refs.pop(0)
    prev_ref = refs.pop(0) if has_prev else None
    pot_ref = refs.pop(0)
    field_ref = refs.pop(0) if has_field else None
    mats = [refs.pop(0) for _ in range(geo.cells)]
    y = y_ref[...]
    factor = pot_ref[...]
    if has_field:
        factor = factor + field_ref[...]
    value = ((factor - filter_center) * scale) * y
    if has_prev:
        value = value - prev_ref[...]
    base_ref[...] = value
    x = y.astype(BF)
    for c in range(geo.cells):
        w = geo.windows[c]
        own = w.hi - w.lo
        rows = x[w.lo : w.hi, :]
        if w.low:
            rows = jnp.concatenate([rows, x[0 : w.low, :]], axis=0)
        product = dot(mats[c][...], rows) * scale
        base_ref[w.lo : w.hi, :] += product[:own]
        if w.low:
            base_ref[0 : w.low, :] += product[own:]
    if has_upper:
        for upper in refs:
            base_ref[0 : geo.sp, :] += dot(upper[...], x[0 : geo.sp, :]) * scale


def owned_part(geo, scale, y, prev, pot, field, mats, uppers):
    args = [y] + ([prev] if prev is not None else []) + [pot]
    args += [field] if field is not None else []
    args += list(mats) + list(uppers)
    return vmem_call(
        functools.partial(
            owned_part_kernel, geo, scale, prev is not None, field is not None, bool(uppers)
        ),
        sds(y.shape, F32),
        cost=cost_of(2.0),
    )(*args)


def add_upper(geo, scale, y_ref, h_up, crosses):
    for at, c in enumerate(geo.touching):
        w = geo.windows[c]
        own = w.hi - w.lo
        product = dot(crosses[at][...], h_up) * scale
        y_ref[w.lo : w.hi, :] += product[:own]
        if w.low:
            y_ref[0 : w.low, :] += product[own:]


def add_rows(geo, scale, y_ref, h_dn, behinds, uppers, own_up):
    total = None
    for at, c in enumerate(geo.touching):
        w = geo.windows[c]
        first = w.lo - geo.dn_lo
        term = dot(behinds[at][...], h_dn[first : first + w.rows, :])
        term = term + dot(uppers[at][...], own_up)
        total = term if total is None else total + term
    y_ref[0 : geo.sp, :] += total * scale


def add_halo(geo, scale, y_ref, near_ref, far_ref, crosses):
    near, far = near_ref[...].astype(F32), far_ref[...].astype(F32)
    even = is_even()
    y_ref[0 : geo.sp, :] += jnp.where(even, far, near) * scale
    add_upper(geo, scale, y_ref, jnp.where(even, near, far).astype(BF), crosses)


def write_density(y_ref, occ_ref, table_ref, part_rows, dens_ref):
    parts = dens_ref.shape[0]
    own = y_ref.shape[0]
    y = y_ref[...]
    terms = y * y * occ_ref[...]
    high = terms.astype(BF)
    low = (terms - high.astype(F32)).astype(BF)
    ones = jnp.ones((SUBLANES, terms.shape[1]), BF)
    summed = dot_t(ones, high) + dot_t(ones, low)
    dens_ref[:, 0, 0:own] = jnp.broadcast_to(summed[0:1, :], (parts, own))
    band = lax.axis_index("band")
    for r in range(part_rows):
        row = table_ref[band, r : r + 1, :]
        dens_ref[:, 0, own + r * LANES : own + (r + 1) * LANES] = jnp.broadcast_to(row, (parts, LANES))


def behind_kernel(geo, scale, sent_ref, matrix_ref, base_ref, own_up_ref, *refs):
    n = len(geo.touching)
    uppers, out_ref, behinds, rest = refs[:n], refs[n], refs[n + 1 : 2 * n + 1], refs[2 * n + 1 :]
    build_behind(geo, sent_ref, matrix_ref, *rest, behinds, uppers)
    out_ref[...] = base_ref[...]
    add_rows(geo, scale, out_ref, sent_ref[...], behinds, uppers, own_up_ref[...])


def behind_sums(geo, scale, sent, matrix, base, own_up):
    *uppers, base = vmem_call(
        functools.partial(behind_kernel, geo, scale),
        [sds((geo.sp, geo.sp), BF) for _ in geo.touching] + [sds(base.shape, F32)],
        [
            *[pltpu.VMEM((geo.sp, geo.windows[c].rows), BF) for c in geo.touching],
            table_scratch(geo),
            matrix_scratch(geo),
        ],
        cost=cost_of(1.0),
    )(sent, matrix, base, own_up)
    return uppers, base


def first_finish_kernel(geo, scale, *refs):
    n = len(geo.touching)
    base_ref, up_ref = refs[:2]
    crosses, reaches = refs[2 : 2 + n], refs[2 + n : 2 + 2 * n]
    y_ref, near_out, far_out = refs[2 + 2 * n :]
    y_ref[...] = base_ref[...]
    add_upper(geo, scale, y_ref, up_ref[...], crosses)
    write_sends(geo, y_ref, reaches, near_out, far_out)


def first_finish(geo, scale, base, h_up, crosses, reaches):
    y, near, far = vmem_call(
        functools.partial(first_finish_kernel, geo, scale),
        [sds(base.shape, F32), *send_shapes(geo, base.shape[1])],
        cost=cost_of(0.5),
    )(base, h_up, *crosses, *reaches)
    return y, (near, far)


def finish_kernel(geo, scale, mode, part_rows, *refs):
    refs = list(refs)
    n = len(geo.touching)
    base_ref, near_ref, far_ref = refs[:3]
    refs = refs[3:]
    crosses, refs = refs[:n], refs[n:]
    halo = (near_ref, far_ref, crosses)
    if mode == "last":
        finish_last(geo, scale, base_ref, halo, *refs)
        return
    reaches, refs = refs[:n], refs[n:]
    if mode == "density":
        occ_ref, table_ref = refs.pop(0), refs.pop(0)
    y_ref = refs.pop(0)
    y_ref[...] = base_ref[...]
    add_halo(geo, scale, y_ref, *halo)
    if mode == "density":
        _, _, out_hbm, dens, sem = refs
        write_density(y_ref, occ_ref, table_ref, part_rows, dens)
        copy = pltpu.make_async_copy(dens, out_hbm, sem)
        copy.start()
    write_sends(geo, y_ref, reaches, refs[0], refs[1])
    if mode == "density":
        copy.wait()


def finish_last(geo, scale, base_ref, halo, *refs):
    extras = (len(refs) - 3) // 2
    sources, out_hbm, targets = refs[:extras], refs[extras], refs[extras + 1 : -2]
    y_ref, sems = refs[-2:]
    top = max(geo.sp, geo.low)
    inner = pl.ds(top, geo.dn_lo - top)
    copies = fetch([(base_ref.at[inner], out_hbm.at[inner]), *zip(sources, targets)], sems)
    edges = [(0, top), (geo.dn_lo, geo.own)]
    for a, b in edges:
        y_ref[a:b, :] = base_ref[a:b, :]
    add_halo(geo, scale, y_ref, *halo)
    for i, (a, b) in enumerate(edges):
        edge = pl.ds(a, b - a)
        copy = pltpu.make_async_copy(y_ref.at[edge], out_hbm.at[edge], sems.at[1 + extras + i])
        copy.start()
        copies.append(copy)
    for copy in copies:
        copy.wait()


def finish(geo, scale, base, halo, crosses, reaches=(), density=None, last=None):
    columns = base.shape[1]
    args = [base, halo[0], halo[1], *crosses, *reaches]
    mode, part_rows = "plain", 0
    shapes = [sds(base.shape, F32)]
    scratch = []
    vmem, hbm = pl.BlockSpec(memory_space=pltpu.VMEM), pl.BlockSpec(memory_space=pltpu.HBM)
    out_specs = [vmem, vmem, vmem]
    if last is not None:
        mode = "last"
        args += last
        shapes += [sds(a.shape, a.dtype) for a in last]
        out_specs = [hbm] * len(shapes)
        scratch = [pltpu.VMEM(base.shape, F32), pltpu.SemaphoreType.DMA((3 + len(last),))]
    else:
        shapes += send_shapes(geo, columns)
    if density is not None:
        mode = "density"
        fg, weights, table = density
        part_rows = fg.part_rows
        args += [weights, table]
        spread = (fg.bands * fg.domains, 1, fg.width)
        shapes.append(sds(spread, F32))
        out_specs.append(hbm)
        scratch = [pltpu.VMEM(spread, F32), pltpu.SemaphoreType.DMA(())]
    return vmem_call(
        functools.partial(finish_kernel, geo, scale, mode, part_rows),
        shapes,
        scratch,
        out_specs=out_specs,
        cost=cost_of(1.0),
    )(*args)


class FieldGeometry:
    def __init__(self, bands, domains, own, share, cells, npc):
        self.bands, self.domains, self.own, self.share = bands, domains, own, share
        self.cells, self.npc = cells, npc
        self.block = own // domains
        self.rows = up_to(npc, LANES) // LANES
        self.lines = own // LANES
        self.tiles = self.lines + 1
        nloc = own + share
        self.touched = []
        for c in range(cells):
            nodes = [(c * (nloc // cells) + k) % nloc for k in range(npc)]
            self.touched.append(sorted({node // LANES for node in nodes}))
        self.at_inverse = cells * self.rows
        self.at_face = self.at_inverse + cells * self.tiles
        self.at_screen = up_to(self.at_face + 2, 2) // 2
        self.part_rows = -(-(self.at_screen + self.lines) // bands)
        self.table_rows = up_to(self.part_rows * bands, SUBLANES)
        self.width = own + self.part_rows * LANES
        self.size = self.rows * LANES
        self.at_owner_lane = LANES - domains
        self.fits = (
            domains == SUBLANES
            and own % (domains * SUBLANES) == 0
            and own % LANES == 0
            and self.block <= LANES
            and share <= self.at_owner_lane
            and max(npc, nloc) < CODE_BASE - 1
        )


CODE_BASE = 2048
CODE_BITS = 11


def pieces(length, blocks):
    found = []
    for j in range(blocks):
        done = 0
        while done < length:
            at = j * length + done
            count = min(length - done, LANES - at % LANES)
            found.append((at // LANES, at % LANES, j, done, count))
            done += count
    return found


def column_of(row):
    return jnp.broadcast_to(row, (LANES, LANES)).T


def inverse_row(columns, first):
    sub = lax.broadcasted_iota(I32, (LANES, LANES), 0)
    target = (lax.broadcasted_iota(I32, (LANES, LANES), 1) + first).astype(F32)
    found = jnp.zeros((LANES, LANES), F32)
    for r, column in enumerate(columns):
        found = jnp.where(column == target, (sub + (r * LANES + 1)).astype(F32), found)
    return jnp.sum(found, axis=0, keepdims=True) - 1.0


def field_tables_kernel(fg, *refs):
    nodes_ref, face_ref, owner_ref, screen_ref = refs[:4]
    table_ref, pad, one, spare, packed = refs[5:]
    one[...] = jnp.full(one.shape, -1.0, F32)
    spare[...] = jnp.full(spare.shape, -1.0, F32)
    pad[...] = jnp.full(pad.shape, -1, I32)
    pad[0 : fg.cells, 0 : fg.npc] = nodes_ref[...]
    for c in range(fg.cells):
        columns = []
        for r in range(fg.rows):
            code = pad[c : c + 1, r * LANES : (r + 1) * LANES].astype(F32)
            one[c * fg.rows + r : c * fg.rows + r + 1, :] = code
            columns.append(column_of(code))
        for t in fg.touched[c]:
            at = fg.at_inverse + c * fg.tiles + t
            one[at : at + 1, :] = inverse_row(columns, t * LANES)
    lane = fg.at_owner_lane
    spare[0:1, 0 : fg.share] = face_ref[...].astype(F32)
    spare[1:2, 0 : fg.domains] = owner_ref[...].astype(F32)
    at = fg.at_face
    one[at : at + 1, :] = spare[0:1, :]
    one[at : at + 1, lane:LANES] = owner_ref[...].astype(F32)
    back = inverse_row([column_of(spare[0:1, :])], 0)
    home = inverse_row([column_of(spare[1:2, :])], -lane)
    lanes = lax.broadcasted_iota(I32, (1, LANES), 1)
    one[at + 1 : at + 2, :] = jnp.where(lanes < lane, back, home)
    packed[...] = jnp.zeros(packed.shape, F32)
    half = fg.at_screen
    packed[0:half, :] = (one[0:half, :] + 1.0) + (one[half : 2 * half, :] + 1.0) * CODE_BASE
    packed[half : half + fg.lines, :] = screen_ref[...]
    for b in range(fg.bands):
        table_ref[b, 0 : fg.part_rows, :] = packed[b * fg.part_rows : (b + 1) * fg.part_rows, :]


def field_tables(fg, pois_nodes, pois_face, block_owner, lines, after):
    specs = [pl.BlockSpec(memory_space=pltpu.VMEM)] * 4 + [pl.BlockSpec(memory_space=pl.ANY)]
    return vmem_call(
        functools.partial(field_tables_kernel, fg),
        sds((fg.bands, up_to(fg.part_rows, SUBLANES), LANES), F32),
        [
            pltpu.VMEM((up_to(fg.cells, SUBLANES), fg.size), I32),
            pltpu.VMEM((up_to(2 * fg.at_screen, SUBLANES), LANES), F32),
            pltpu.VMEM((SUBLANES, LANES), F32),
            pltpu.VMEM((fg.table_rows, LANES), F32),
        ],
        in_specs=specs,
        cost=cost_of(1.0),
    )(pois_nodes, pois_face, block_owner, lines, after)


def lanes_of(values, index):
    return jnp.take_along_axis(values, index, axis=1, mode="promise_in_bounds")


def got_tile(fg, got_ref, band, line):
    lines = fg.width // LANES
    return got_ref[pl.ds(band * fg.domains * lines + line, fg.domains, stride=lines), :]


def decode(fg, got_ref, codes):
    domains, half = fg.domains, fg.at_screen

    def tile(at):
        return got_tile(fg, got_ref, at // fg.part_rows, fg.lines + at % fg.part_rows)

    for at in range(half):
        both = tile(at).astype(I32)
        codes[at] = jnp.bitwise_and(both, CODE_BASE - 1) - 1
        codes[half + at] = jnp.right_shift(both, CODE_BITS) - 1
    screens = [tile(half + g) for g in range(fg.lines)]
    lane = lax.broadcasted_iota(I32, (domains, LANES), 1)
    first, last = fg.at_owner_lane, LANES
    owners = codes[fg.at_face].astype(F32).T[first:last, :]
    inverse = codes[fg.at_face + 1].astype(F32).T[first:last, :]
    back = jnp.where(lane < fg.share, codes[fg.at_face + 1], -1)
    codes[fg.at_face + 1] = pltpu.roll(back, 1, 0)
    places = []
    for q in range(domains):
        block = jnp.broadcast_to(inverse[:, q : q + 1], (domains, LANES)).astype(I32)
        places.append(block * fg.block + lane)
    here = lax.axis_index("domain")
    narrow = lax.broadcasted_iota(I32, (domains, domains), 1)
    mine = jnp.sum(jnp.where(narrow == here, owners, 0.0), axis=1, keepdims=True)
    return places, jnp.broadcast_to(mine, (domains, LANES)).astype(I32), screens


def rows_of(values, index):
    return jnp.take_along_axis(values, index, axis=0, mode="promise_in_bounds")


def lookup(sources, code):
    lane = jnp.bitwise_and(code, LANES - 1)
    which = jnp.right_shift(code, 7)
    total = jnp.zeros(code.shape, F32)
    for b, values in sources:
        total = jnp.where(which == b, lanes_of(values, lane), total)
    return total


def field_source(fg, got_ref, places):
    domains = fg.domains
    density = []
    for g in range(fg.lines):
        total = got_tile(fg, got_ref, 0, g)
        for b in range(1, fg.bands):
            total = total + got_tile(fg, got_ref, b, g)
        density.append(total)
    lane = lax.broadcasted_iota(I32, (domains, LANES), 1)
    source = [None] * fg.lines
    for q in range(domains):
        spread = [jnp.broadcast_to(d[q : q + 1, :], (domains, LANES)) for d in density]
        block = lookup(list(enumerate(spread)), places[q])
        for row, start, j, offset, count in pieces(fg.block, domains):
            if j == q:
                moved = pltpu.roll(block, (start - offset) % LANES, 1)
                inside = (lane >= start) & (lane < start + count)
                before = 0.0 if source[row] is None else source[row]
                source[row] = jnp.where(inside, moved, before)
    return source


def field_solve(fg, source, codes, screen, matrix_ref, high_ref, low_ref, rows, copies):
    domains, cells = fg.domains, fg.cells

    def operator(field):
        ahead = pltpu.roll(field[0], domains - 1, 0)
        local = list(field) + [lookup([(0, ahead)], codes[fg.at_face])]
        for r in range(fg.rows):
            for c in range(cells):
                sources = [(t, local[t]) for t in fg.touched[c]]
                rows[c * domains : (c + 1) * domains, r * LANES : (r + 1) * LANES] = lookup(sources, codes[c * fg.rows + r])
            if copies:
                copies.pop(0).wait()
                span = slice(r * LANES, min((r + 1) * LANES, fg.npc))
                full = matrix_ref[span, :]
                top = full.astype(BF)
                high_ref[span, :] = top
                low_ref[span, :] = (full - top.astype(F32)).astype(BF)
        picked = rows[:, 0 : fg.npc]
        high = picked.astype(BF)
        low = (picked - high.astype(F32)).astype(BF)
        both = dot(jnp.concatenate([high, low], axis=0), high_ref[...])
        half_rows = cells * domains
        rows[:, 0 : fg.npc] = both[:half_rows] + (both[half_rows:] + dot(high, low_ref[...]))
        out = [None] * fg.tiles
        for c in range(cells):
            sources = [
                (r, rows[c * domains : (c + 1) * domains, r * LANES : (r + 1) * LANES])
                for r in range(fg.rows)
            ]
            for t in fg.touched[c]:
                term = lookup(sources, codes[fg.at_inverse + c * fg.tiles + t])
                out[t] = term if out[t] is None else out[t] + term
        arriving = pltpu.roll(out[fg.lines], 1, 0)
        out[0] = out[0] + lookup([(0, arriving)], codes[fg.at_face + 1])
        return [screen[g] * field[g] + out[g] for g in range(fg.lines)]

    step_one = [s * (1.0 / solve_center) for s in source]
    applied = operator(step_one)
    residual = [s - a for s, a in zip(source, applied)]
    a1, b1 = weight_one * weight_zero, 2.0 * weight_one / solve_half
    step_two = [a1 * e + b1 * r for e, r in zip(step_one, residual)]
    applied = operator(step_two)
    residual = [r - a for r, a in zip(residual, applied)]
    a2, b2 = weight_two * weight_one, 2.0 * weight_two / solve_half
    step_three = [a2 * e + b2 * r for e, r in zip(step_two, residual)]
    return [(x + y) + z for x, y, z in zip(step_one, step_two, step_three)]


def field_kernel(geo, fg, scale, got_ref, matrix_hbm, base_ref, near_ref, far_ref, y_ref, *refs):
    n = len(geo.touching)
    crosses, reaches, refs = refs[:n], refs[n : 2 * n], refs[2 * n :]
    z_ref, near_out, far_out, column_ref, hartree_ref = refs[:5]
    codes, rows, mine, matrix_ref, high_ref, low_ref, sems = refs[5:]
    spans = [pl.ds(r * LANES, min(LANES, fg.npc - r * LANES)) for r in range(fg.rows)]
    copies = fetch([(matrix_hbm.at[span], matrix_ref.at[span]) for span in spans], sems)
    z_ref[...] = base_ref[...]
    add_halo(geo, scale, z_ref, near_ref, far_ref, crosses)
    places, owner, screens = decode(fg, got_ref, codes)
    source = field_source(fg, got_ref, places)
    solved = field_solve(fg, source, codes, screens, matrix_ref, high_ref, low_ref, rows, copies)
    lane = lax.broadcasted_iota(I32, (fg.domains, LANES), 1)
    block = lookup(list(enumerate(solved)), lane + lax.axis_index("domain") * fg.block)
    mine[...] = rows_of(block, owner)
    for j in range(fg.domains):
        at = slice(j * fg.block, (j + 1) * fg.block)
        column = column_of(mine[j : j + 1, :])[0 : fg.block, :]
        column_ref[at, :] = column
        z_ref[at, :] += (column * scale) * y_ref[at, :]
    write_sends(geo, z_ref, reaches, near_out, far_out)
    for row, start, j, offset, count in pieces(fg.block, fg.domains):
        hartree_ref[row : row + 1, start : start + count] = mine[j : j + 1, offset : offset + count]


def field_step(geo, fg, scale, got, matrix, base, halo, y, crosses, reaches):
    tile = (fg.domains, LANES)
    vmem = pl.BlockSpec(memory_space=pltpu.VMEM)
    got = got.reshape(got.shape[0] * fg.width // LANES, LANES)
    args = [got, *in_hbm(matrix), base, *halo, y, *crosses, *reaches]
    specs = [vmem] * len(args)
    specs[1] = pl.BlockSpec(memory_space=pltpu.HBM)
    z, near, far, column, lines = vmem_call(
        functools.partial(field_kernel, geo, fg, scale),
        [
            sds(y.shape, F32),
            *send_shapes(geo, y.shape[1]),
            sds((fg.own, LANES), F32),
            sds((fg.lines, LANES), F32),
        ],
        [
            pltpu.VMEM((2 * fg.at_screen, *tile), I32),
            pltpu.VMEM((fg.cells * fg.domains, fg.size), F32),
            pltpu.VMEM(tile, F32),
            pltpu.VMEM(matrix.shape, F32),
            pltpu.VMEM(matrix.shape, BF),
            pltpu.VMEM(matrix.shape, BF),
            pltpu.SemaphoreType.DMA((fg.rows,)),
        ],
        in_specs=specs,
        cost=cost_of(4.0),
    )(*args)
    return z, (near, far), column, lines


def assembled(owned_rows, face_row, terms):
    owned_count = owned_rows.shape[0]
    shared = face_row.shape[0]
    coming = jnp.take(from_behind(owned_rows[:shared], "domain", -1), face_row, axis=0)
    partial_value = terms(jnp.concatenate([owned_rows, coming], axis=0))
    upper_rows = partial_value[owned_count:]
    ordered = jnp.zeros_like(upper_rows).at[face_row].set(upper_rows)
    arrived = from_behind(ordered, "domain", 1)
    return partial_value[:owned_count].at[:shared].add(arrived)


def field_terms(local_rows, pois_matrix, node_ids):
    cell_vals = jnp.take(local_rows, node_ids, axis=0)
    product = jnp.einsum(
        "pq,cq->cp",
        pois_matrix,
        cell_vals,
        precision=lax.Precision.HIGHEST,
        preferred_element_type=F32,
    )
    return jnp.zeros(local_rows.shape, F32).at[node_ids.reshape(-1)].add(product.reshape(-1))


def reshuffle(blocks):
    return lax.all_to_all(blocks, "domain", split_axis=0, concat_axis=0, tiled=True)


def distributed_field(y, occupation, owner_row, pois_matrix, pois_nodes, field_face, screening):
    owned_count = y.shape[0]
    domains = lax.axis_size("domain")
    block_len = owned_count // domains
    partial_value = jnp.dot(
        y * y, occupation, precision=lax.Precision.HIGHEST, preferred_element_type=F32
    )
    summed = lax.psum(partial_value, "band")
    arranged = (
        jnp.zeros((domains, block_len), F32)
        .at[owner_row]
        .set(summed.reshape(domains, block_len))
    )
    source = reshuffle(arranged).reshape(owned_count)

    def field_operator(vector):
        return (
            assembled(
                vector, field_face, lambda local: field_terms(local, pois_matrix, pois_nodes)
            )
            + screening * vector
        )

    step_one = source / solve_center
    residual = source - field_operator(step_one)
    step_two = weight_one * weight_zero * step_one + 2.0 * weight_one / solve_half * residual
    residual = residual - field_operator(step_two)
    step_three = weight_two * weight_one * step_two + 2.0 * weight_two / solve_half * residual
    solved = step_one + step_two + step_three
    returned = reshuffle(solved.reshape(domains, block_len))
    return jnp.take(returned, owner_row, axis=0).reshape(owned_count)


def exchange(sends):
    dn, up = sends
    h_dn = from_behind(dn, "domain", 1)
    h_up = from_behind(up, "domain", -1)
    return h_up, h_dn


def on_device(
    orbitals,
    potential,
    occupation,
    cell_matrix,
    cell_nodes,
    face_order,
    pois_matrix,
    pois_nodes,
    pois_face,
    screening,
    block_owner,
):
    domains = lax.axis_size("domain")
    bands = lax.axis_size("band")
    own, columns = orbitals.shape
    geo = Geometry(own, face_order.shape[1], cell_nodes.shape[0], cell_nodes.shape[1])
    fg = FieldGeometry(bands, domains, own, pois_face.shape[1], pois_nodes.shape[0], pois_nodes.shape[1])
    first, later = 1.0 / filter_half, 2.0 / filter_half

    others = [cell_matrix, potential.reshape(own // LANES, LANES)]
    if fg.fits:
        others += [pois_nodes, pois_face, block_owner, screening.reshape(own // LANES, LANES)]
        others.append(occupation.reshape(1, columns))
    sends, y0, nodes, (matrix, lines, *others) = pack(geo, orbitals, cell_nodes, face_order, *others)
    halo = exchange(sends)
    mats, crosses, reaches, pot = own_matrices(geo, nodes, matrix, lines)
    base = owned_part(geo, first, y0, None, pot, None, mats, ())
    uppers, base = behind_sums(geo, first, halo[1], matrix, base, sends[1])
    y1, sends1 = first_finish(geo, first, base, halo[0], crosses, reaches)

    halo = swap(sends1)
    base = owned_part(geo, later, y1, y0, pot, None, mats, uppers)
    if fg.fits:
        *others, weights = others
        table = field_tables(fg, *others, base)
    y2, *sends2 = finish(geo, later, base, halo, crosses, reaches)

    halo = swap(sends2)
    base = owned_part(geo, later, y2, y1, pot, None, mats, uppers)
    if fg.fits:
        y3, dn, up, spread = finish(
            geo, later, base, halo, crosses, reaches, density=(fg, weights, table)
        )
        dens = lax.all_to_all(spread, ("band", "domain"), 0, 0, tiled=True)
        halo = swap((dn, up))
        base = owned_part(geo, first, y3, None, pot, None, mats, uppers)
        z1, sends4, column, packed = field_step(
            geo, fg, first, dens, pois_matrix, base, halo, y3, crosses, reaches
        )
    else:
        y3, *sends3 = finish(geo, later, base, halo, crosses, reaches)
        halo = swap(sends3)
        hartree = distributed_field(
            y3, occupation, block_owner[0], pois_matrix, pois_nodes, pois_face[0], screening
        )
        column = jnp.broadcast_to(hartree[:, None], (own, LANES))
        base = owned_part(geo, first, y3, None, pot, column, mats, uppers)
        z1, *sends4 = finish(geo, first, base, halo, crosses, reaches)

    halo = swap(sends4)
    base = owned_part(geo, later, z1, y3, pot, column, mats, uppers)
    last = [packed] if fg.fits else []
    filtered, *rest = finish(geo, later, base, halo, crosses, last=last)
    if fg.fits:
        hartree = rest[0].reshape(own)
    return filtered, hartree


def swap(sends):
    length = lax.axis_size("domain")
    near, far = sends
    turns = [(i, (i + 1) % length if i % 2 else (i - 1) % length) for i in range(length)]
    far = lax.ppermute(far, "domain", turns)
    near = lax.ppermute(near, "domain", [(i, i ^ 1) for i in range(length)])
    return near, far


def solution(mesh):
    return jax.shard_map(
        on_device,
        mesh=mesh,
        in_specs=(
            P("domain", "band"),
            P("domain"),
            P("band"),
            P(),
            P("domain", None),
            P("domain", None),
            P(),
            P("domain", None),
            P("domain", None),
            P("domain"),
            P("domain", None),
        ),
        out_specs=(P("domain", "band"), P("domain")),
        check_vma=False,
    )
```

```python
import functools

import jax
import jax.numpy as jnp
from jax import lax
from jax.experimental import pallas as pl
from jax.experimental.pallas import tpu as pltpu
from jax.sharding import PartitionSpec as P

filter_center = 1.8
filter_half = 2.7
solve_center = 3.25
solve_half = 2.75
solve_ratio = solve_center / solve_half
weight_zero = 1.0 / solve_ratio
weight_one = 1.0 / (2.0 * solve_ratio - weight_zero)
weight_two = 1.0 / (2.0 * solve_ratio - weight_one)

BF = jnp.bfloat16
F32 = jnp.float32
I32 = jnp.int32
LANES = 128
SUBLANES = 8


def up_to(n, m):
    return -(-n // m) * m


def from_behind(array, axis, by):
    length = lax.axis_size(axis)
    return lax.ppermute(array, axis, [(i, (i + by) % length) for i in range(length)])


class Window:
    def __init__(self, start, npc, own, nloc):
        end = start + npc
        self.lo = start // 16 * 16
        self.hi = min(up_to(min(end, own), 16), own)
        self.touches = end > own
        self.low = up_to(max(0, end - nloc), 16)
        self.rows = self.hi - self.lo + self.low


class Geometry:
    def __init__(self, own, share, cells, npc):
        self.own, self.share, self.cells, self.npc = own, share, cells, npc
        nloc = own + share
        stride = nloc // cells
        self.sp = up_to(share, 16)
        self.npl = up_to(npc, LANES)
        self.windows = [Window(c * stride, npc, own, nloc) for c in range(cells)]
        self.touching = [c for c in range(cells) if self.windows[c].touches]
        self.dn_lo = min(self.windows[c].lo for c in self.touching)
        self.low = max(w.low for w in self.windows)
        self.dn_rows = own - self.dn_lo + self.low
        self.table_rows = up_to(cells, SUBLANES)
        self.table_lanes = up_to(npc, LANES)
        self.table_tiles = self.table_lanes // LANES


def dot(a, b):
    return lax.dot_general(a, b, (((1,), (0,)), ((), ())), preferred_element_type=F32)


def dot_t(a, b):
    return lax.dot_general(a, b, (((1,), (1,)), ((), ())), preferred_element_type=F32)


def vmem_call(kernel, out_shape, scratch=(), in_specs=None, out_specs=None, cost=None):
    kwargs = {}
    if in_specs is not None:
        kwargs["in_specs"] = in_specs
    if out_specs is not None:
        kwargs["out_specs"] = out_specs
    return pl.pallas_call(
        kernel,
        out_shape=out_shape,
        scratch_shapes=list(scratch),
        cost_estimate=cost,
        compiler_params=pltpu.CompilerParams(vmem_limit_bytes=12 * 1024 * 1024),
        **kwargs,
    )


def in_hbm(*arrays):
    return [pltpu.with_memory_space_constraint(a, pltpu.HBM) for a in arrays]


def sds(shape, dtype):
    return jax.ShapeDtypeStruct(shape, dtype)


def one_hot_rows(count, first, nodes):
    ids = lax.broadcasted_iota(I32, (count, nodes.shape[1]), 0) + first
    return jnp.where(ids == nodes, 1.0, 0.0).astype(BF)


def place_table(geo, nodes_ref, face_ref, table, faces):
    table[...] = jnp.full(table.shape, -1, I32)
    table[0 : geo.cells, 0 : geo.npc] = nodes_ref[...]
    faces[...] = jnp.zeros(faces.shape, I32)
    faces[0:1, 0 : geo.share] = face_ref[...]
    for t in range(geo.table_tiles):
        lanes = slice(t * LANES, (t + 1) * LANES)
        nodes = table[:, lanes]
        beyond = nodes - geo.own
        at = jnp.bitwise_and(beyond, LANES - 1)
        which = jnp.right_shift(beyond, 7)
        for f in range(faces.shape[1] // LANES):
            row = jnp.broadcast_to(faces[0:1, f * LANES : (f + 1) * LANES], nodes.shape)
            nodes = jnp.where(which == f, lanes_of(row, at) + geo.own, nodes)
        table[:, lanes] = nodes


def place_matrix(geo, matrix_ref, matrix_pad):
    matrix_pad[...] = jnp.zeros(matrix_pad.shape, F32)
    matrix_pad[0 : geo.npc, 0 : geo.npc] = matrix_ref[...].astype(F32)
    return matrix_pad[...].astype(BF)


def table_scratch(geo):
    return pltpu.VMEM((geo.table_rows, geo.table_lanes), I32)


def matrix_scratch(geo):
    return pltpu.VMEM((geo.npl, geo.npl), F32)


def nodes_of(geo, table, c):
    return table[c : c + 1, 0 : geo.npl]


def owned_picks(geo, c, nodes):
    w = geo.windows[c]
    picks = one_hot_rows(w.hi - w.lo, w.lo, nodes)
    if w.low:
        picks = jnp.concatenate([picks, one_hot_rows(w.low, 0, nodes)], axis=0)
    return picks


def upper_picks(geo, nodes):
    return one_hot_rows(geo.sp, geo.own, nodes)


def own_matrices_kernel(geo, *refs):
    table, matrix_ref, pot_ref = refs[:3]
    outs, matrix_pad = refs[3:-1], refs[-1]
    matrix = place_matrix(geo, matrix_ref, matrix_pad)
    for c in range(geo.cells):
        nodes = nodes_of(geo, table, c)
        own = owned_picks(geo, c, nodes)
        left = dot(own, matrix).astype(BF)
        outs[c][...] = dot_t(left, own).astype(BF)
        if c in geo.touching:
            at = geo.cells + geo.touching.index(c)
            upper = upper_picks(geo, nodes)
            outs[at][...] = dot_t(left, upper).astype(BF)
            left = dot(upper, matrix).astype(BF)
            outs[at + len(geo.touching)][...] = dot_t(left, own).astype(BF)
    column = outs[-1]
    for r in range(geo.own // LANES):
        row = jnp.broadcast_to(pot_ref[r : r + 1, :], (LANES, LANES))
        column[r * LANES : (r + 1) * LANES, :] = row.T


def own_matrices(geo, table, cell_matrix, lines):
    shapes = [sds((w.rows, w.rows), BF) for w in geo.windows]
    shapes += [sds((geo.windows[c].rows, geo.sp), BF) for c in geo.touching]
    shapes += [sds((geo.sp, geo.windows[c].rows), BF) for c in geo.touching]
    shapes += [sds((geo.own, LANES), F32)]
    outs = vmem_call(
        functools.partial(own_matrices_kernel, geo),
        shapes,
        [matrix_scratch(geo)],
        cost=cost_of(2.0),
    )(table, cell_matrix, lines)
    n, m = geo.cells, geo.cells + len(geo.touching)
    return outs[:n], outs[n:m], outs[m:-1], outs[-1]


def build_behind(geo, sent_ref, matrix_ref, table, matrix_pad, behinds, uppers):
    for t in range(geo.table_tiles):
        at = geo.dn_rows + 2 * t * geo.table_rows
        digits = sent_ref[at : at + 2 * geo.table_rows, :].astype(F32)
        value = digits[: geo.table_rows] * LANES + digits[geo.table_rows :] - 1.0
        table[:, t * LANES : (t + 1) * LANES] = value.astype(I32)
    matrix = place_matrix(geo, matrix_ref, matrix_pad)
    for at, c in enumerate(geo.touching):
        nodes = nodes_of(geo, table, c)
        upper = upper_picks(geo, nodes)
        left = dot(upper, matrix).astype(BF)
        behinds[at][...] = dot_t(left, owned_picks(geo, c, nodes)).astype(BF)
        uppers[at][...] = dot_t(left, upper).astype(BF)


def cost_of(us):
    return pl.CostEstimate(flops=0, bytes_accessed=int(us * 3.0e6), transcendentals=0)


def write_rows(geo, y_ref, dn_ref, up_ref):
    top = geo.own - geo.dn_lo
    dn_ref[0:top, :] = y_ref[geo.dn_lo : geo.own, :].astype(BF)
    dn_ref[top : top + geo.low, :] = y_ref[0 : geo.low, :].astype(BF)
    up_ref[...] = y_ref[0 : geo.sp, :].astype(BF)


def window_rows(geo, c, y_ref):
    w = geo.windows[c]
    rows = y_ref[w.lo : w.hi, :].astype(BF)
    if w.low:
        rows = jnp.concatenate([rows, y_ref[0 : w.low, :].astype(BF)], axis=0)
    return rows


def is_even():
    return jnp.bitwise_and(lax.axis_index("domain"), 1) == 0


def write_sends(geo, y_ref, reaches, near_ref, far_ref):
    total = None
    for at, c in enumerate(geo.touching):
        term = dot(reaches[at][...], window_rows(geo, c, y_ref))
        total = term if total is None else total + term
    rows = y_ref[0 : geo.sp, :]
    even = is_even()
    near_ref[...] = jnp.where(even, total, rows).astype(BF)
    far_ref[...] = jnp.where(even, rows, total).astype(BF)


def send_shapes(geo, columns):
    return [sds((geo.sp, columns), BF), sds((geo.sp, columns), BF)]


def fetch(pairs, sems):
    copies = [pltpu.make_async_copy(src, dst, sems.at[i]) for i, (src, dst) in enumerate(pairs)]
    for copy in copies:
        copy.start()
    return copies


def pack_kernel(geo, extra, y_hbm, nodes_hbm, face_hbm, *refs):
    sources, refs = refs[:extra], refs[extra:]
    dn_ref, up_ref, y, table = refs[:4]
    kept, (nodes, face, faces, sems) = refs[4 : 4 + extra], refs[4 + extra :]
    cuts = sorted({0, max(geo.sp, geo.low), geo.dn_lo, geo.own})
    spans = list(zip(cuts[:-1], cuts[1:]))
    pairs = [(nodes_hbm, nodes), (face_hbm, face)]
    pairs += [(y_hbm.at[pl.ds(a, b - a)], y.at[pl.ds(a, b - a)]) for a, b in spans]
    pairs += list(zip(sources, kept))
    copies = fetch(pairs, sems)
    copies[0].wait()
    copies[1].wait()
    place_table(geo, nodes, face, table, faces)
    for t in range(geo.table_tiles):
        at = geo.dn_rows + 2 * t * geo.table_rows
        value = table[:, t * LANES : (t + 1) * LANES] + 1
        high = jnp.right_shift(value, 7).astype(F32)
        low = jnp.bitwise_and(value, LANES - 1).astype(F32)
        digits = jnp.concatenate([high, low], axis=0).astype(BF)
        dn_ref[at : at + 2 * geo.table_rows, :] = digits
    for copy in copies[2:]:
        copy.wait()
    write_rows(geo, y, dn_ref, up_ref)


def pack(geo, y, cell_nodes, face_order, *others):
    up = sds((geo.sp, y.shape[1]), BF)
    rows = geo.dn_rows + 2 * geo.table_rows * geo.table_tiles
    dn, up, y, table, *others = vmem_call(
        functools.partial(pack_kernel, geo, len(others)),
        [
            sds((rows, y.shape[1]), BF),
            up,
            sds(y.shape, F32),
            sds((geo.table_rows, geo.table_lanes), I32),
            *[sds(a.shape, a.dtype) for a in others],
        ],
        [
            pltpu.VMEM(cell_nodes.shape, I32),
            pltpu.VMEM(face_order.shape, I32),
            pltpu.VMEM((1, up_to(geo.share, LANES)), I32),
            pltpu.SemaphoreType.DMA((5 + len(others),)),
        ],
        in_specs=[pl.BlockSpec(memory_space=pltpu.HBM)] * (3 + len(others)),
        cost=cost_of(1.0),
    )(*in_hbm(y, cell_nodes, face_order, *others))
    return (dn, up), y, table, others


def owned_part_kernel(geo, scale, has_prev, has_field, has_upper, far, *refs):
    refs = list(refs)
    if far:
        places, sems = refs[-2 - geo.cells : -1], refs[-1]
        refs = refs[: -2 - geo.cells]
    base_ref = refs.pop()
    y_ref = refs.pop(0)
    prev_ref = refs.pop(0) if has_prev else None
    pot_ref = refs.pop(0)
    field_ref = refs.pop(0) if has_field else None
    mats = [refs.pop(0) for _ in range(geo.cells)]
    if far:
        copies = fetch(list(zip([pot_ref, *mats], places)), sems)
        pot_ref, mats = places[0], places[1:]
        for copy in copies:
            copy.wait()
    y = y_ref[...]
    factor = pot_ref[...]
    if has_field:
        factor = factor + field_ref[...]
    value = ((factor - filter_center) * scale) * y
    if has_prev:
        value = value - prev_ref[...]
    base_ref[...] = value
    x = y.astype(BF)
    for c in range(geo.cells):
        w = geo.windows[c]
        own = w.hi - w.lo
        rows = x[w.lo : w.hi, :]
        if w.low:
            rows = jnp.concatenate([rows, x[0 : w.low, :]], axis=0)
        product = dot(mats[c][...], rows) * scale
        base_ref[w.lo : w.hi, :] += product[:own]
        if w.low:
            base_ref[0 : w.low, :] += product[own:]
    if has_upper:
        for upper in refs:
            base_ref[0 : geo.sp, :] += dot(upper[...], x[0 : geo.sp, :]) * scale


def owned_part(geo, scale, y, prev, pot, field, mats, uppers, far=False):
    vmem, hbm = pl.BlockSpec(memory_space=pltpu.VMEM), pl.BlockSpec(memory_space=pltpu.HBM)
    place, scratch = vmem, []
    if far:
        place = hbm
        scratch = [pltpu.VMEM(a.shape, a.dtype) for a in [pot, *mats]]
        scratch.append(pltpu.SemaphoreType.DMA((1 + len(mats),)))
        pot, *mats = in_hbm(pot, *mats)
    args = [y] + ([prev] if prev is not None else []) + [pot]
    args += [field] if field is not None else []
    args += list(mats) + list(uppers)
    specs = [vmem] * (2 if prev is not None else 1) + [place]
    specs += [vmem] * (0 if field is None else 1)
    specs += [place] * len(mats) + [vmem] * len(uppers)
    return vmem_call(
        functools.partial(
            owned_part_kernel, geo, scale, prev is not None, field is not None, bool(uppers), far
        ),
        sds(y.shape, F32),
        scratch,
        in_specs=specs,
        cost=cost_of(2.0),
    )(*args)


def add_upper(geo, scale, y_ref, h_up, crosses):
    for at, c in enumerate(geo.touching):
        w = geo.windows[c]
        own = w.hi - w.lo
        product = dot(crosses[at][...], h_up) * scale
        y_ref[w.lo : w.hi, :] += product[:own]
        if w.low:
            y_ref[0 : w.low, :] += product[own:]


def add_rows(geo, scale, y_ref, h_dn, behinds, uppers, own_up):
    total = None
    for at, c in enumerate(geo.touching):
        w = geo.windows[c]
        first = w.lo - geo.dn_lo
        term = dot(behinds[at][...], h_dn[first : first + w.rows, :])
        term = term + dot(uppers[at][...], own_up)
        total = term if total is None else total + term
    y_ref[0 : geo.sp, :] += total * scale


def add_halo(geo, scale, y_ref, near_ref, far_ref, crosses):
    near, far = near_ref[...].astype(F32), far_ref[...].astype(F32)
    even = is_even()
    y_ref[0 : geo.sp, :] += jnp.where(even, far, near) * scale
    add_upper(geo, scale, y_ref, jnp.where(even, near, far).astype(BF), crosses)


def write_density(y_ref, occ_ref, table_ref, part_rows, dens_ref):
    parts = dens_ref.shape[0]
    own = y_ref.shape[0]
    y = y_ref[...]
    terms = y * y * occ_ref[...]
    high = terms.astype(BF)
    low = (terms - high.astype(F32)).astype(BF)
    ones = jnp.ones((SUBLANES, terms.shape[1]), BF)
    summed = dot_t(ones, high) + dot_t(ones, low)
    dens_ref[:, 0, 0:own] = jnp.broadcast_to(summed[0:1, :], (parts, own))
    band = lax.axis_index("band")
    for r in range(part_rows):
        row = table_ref[band, r : r + 1, :]
        dens_ref[:, 0, own + r * LANES : own + (r + 1) * LANES] = jnp.broadcast_to(row, (parts, LANES))


def behind_kernel(geo, scale, sent_ref, matrix_ref, base_ref, own_up_ref, *refs):
    n = len(geo.touching)
    uppers, out_ref, behinds, rest = refs[:n], refs[n], refs[n + 1 : 2 * n + 1], refs[2 * n + 1 :]
    build_behind(geo, sent_ref, matrix_ref, *rest, behinds, uppers)
    out_ref[...] = base_ref[...]
    add_rows(geo, scale, out_ref, sent_ref[...], behinds, uppers, own_up_ref[...])


def behind_sums(geo, scale, sent, matrix, base, own_up):
    *uppers, base = vmem_call(
        functools.partial(behind_kernel, geo, scale),
        [sds((geo.sp, geo.sp), BF) for _ in geo.touching] + [sds(base.shape, F32)],
        [
            *[pltpu.VMEM((geo.sp, geo.windows[c].rows), BF) for c in geo.touching],
            table_scratch(geo),
            matrix_scratch(geo),
        ],
        cost=cost_of(1.0),
    )(sent, matrix, base, own_up)
    return uppers, base


def first_finish_kernel(geo, scale, *refs):
    n = len(geo.touching)
    base_ref, up_ref = refs[:2]
    crosses, reaches = refs[2 : 2 + n], refs[2 + n : 2 + 2 * n]
    y_ref, near_out, far_out = refs[2 + 2 * n :]
    y_ref[...] = base_ref[...]
    add_upper(geo, scale, y_ref, up_ref[...], crosses)
    write_sends(geo, y_ref, reaches, near_out, far_out)


def first_finish(geo, scale, base, h_up, crosses, reaches):
    y, near, far = vmem_call(
        functools.partial(first_finish_kernel, geo, scale),
        [sds(base.shape, F32), *send_shapes(geo, base.shape[1])],
        cost=cost_of(0.5),
    )(base, h_up, *crosses, *reaches)
    return y, (near, far)


def finish_kernel(geo, scale, mode, part_rows, *refs):
    refs = list(refs)
    n = len(geo.touching)
    base_ref, near_ref, far_ref = refs[:3]
    refs = refs[3:]
    crosses, refs = refs[:n], refs[n:]
    halo = (near_ref, far_ref, crosses)
    if mode == "last":
        finish_last(geo, scale, base_ref, halo, *refs)
        return
    reaches, refs = refs[:n], refs[n:]
    if mode == "density":
        occ_ref, table_ref = refs.pop(0), refs.pop(0)
    y_ref = refs.pop(0)
    y_ref[...] = base_ref[...]
    add_halo(geo, scale, y_ref, *halo)
    if mode == "density":
        _, _, out_hbm, dens, sem = refs
        write_density(y_ref, occ_ref, table_ref, part_rows, dens)
        copy = pltpu.make_async_copy(dens, out_hbm, sem)
        copy.start()
    write_sends(geo, y_ref, reaches, refs[0], refs[1])
    if mode == "density":
        copy.wait()


def finish_last(geo, scale, base_ref, halo, *refs):
    extras = (len(refs) - 3) // 2
    sources, out_hbm, targets = refs[:extras], refs[extras], refs[extras + 1 : -2]
    y_ref, sems = refs[-2:]
    top = max(geo.sp, geo.low)
    inner = pl.ds(top, geo.dn_lo - top)
    copies = fetch([(base_ref.at[inner], out_hbm.at[inner]), *zip(sources, targets)], sems)
    edges = [(0, top), (geo.dn_lo, geo.own)]
    for a, b in edges:
        y_ref[a:b, :] = base_ref[a:b, :]
    add_halo(geo, scale, y_ref, *halo)
    for i, (a, b) in enumerate(edges):
        edge = pl.ds(a, b - a)
        copy = pltpu.make_async_copy(y_ref.at[edge], out_hbm.at[edge], sems.at[1 + extras + i])
        copy.start()
        copies.append(copy)
    for copy in copies:
        copy.wait()


def finish(geo, scale, base, halo, crosses, reaches=(), density=None, last=None):
    columns = base.shape[1]
    args = [base, halo[0], halo[1], *crosses, *reaches]
    mode, part_rows = "plain", 0
    shapes = [sds(base.shape, F32)]
    scratch = []
    vmem, hbm = pl.BlockSpec(memory_space=pltpu.VMEM), pl.BlockSpec(memory_space=pltpu.HBM)
    out_specs = [vmem, vmem, vmem]
    if last is not None:
        mode = "last"
        args += last
        shapes += [sds(a.shape, a.dtype) for a in last]
        out_specs = [hbm] * len(shapes)
        scratch = [pltpu.VMEM(base.shape, F32), pltpu.SemaphoreType.DMA((3 + len(last),))]
    else:
        shapes += send_shapes(geo, columns)
    if density is not None:
        mode = "density"
        fg, weights, table = density
        part_rows = fg.part_rows
        args += [weights, table]
        spread = (fg.bands * fg.domains, 1, fg.width)
        shapes.append(sds(spread, F32))
        out_specs.append(hbm)
        scratch = [pltpu.VMEM(spread, F32), pltpu.SemaphoreType.DMA(())]
    return vmem_call(
        functools.partial(finish_kernel, geo, scale, mode, part_rows),
        shapes,
        scratch,
        out_specs=out_specs,
        cost=cost_of(1.0),
    )(*args)


class FieldGeometry:
    def __init__(self, bands, domains, own, share, cells, npc):
        self.bands, self.domains, self.own, self.share = bands, domains, own, share
        self.cells, self.npc = cells, npc
        self.block = own // domains
        self.rows = up_to(npc, LANES) // LANES
        self.lines = own // LANES
        self.tiles = self.lines + 1
        nloc = own + share
        self.touched = []
        for c in range(cells):
            nodes = [(c * (nloc // cells) + k) % nloc for k in range(npc)]
            self.touched.append(sorted({node // LANES for node in nodes}))
        self.at_inverse = cells * self.rows
        self.at_face = self.at_inverse + cells * self.tiles
        self.at_screen = up_to(self.at_face + 2, 2) // 2
        self.part_rows = -(-(self.at_screen + self.lines) // bands)
        self.table_rows = up_to(self.part_rows * bands, SUBLANES)
        self.width = own + self.part_rows * LANES
        self.size = self.rows * LANES
        self.at_owner_lane = LANES - domains
        self.fits = (
            domains == SUBLANES
            and own % (domains * SUBLANES) == 0
            and own % LANES == 0
            and self.block <= LANES
            and share <= self.at_owner_lane
            and max(npc, nloc) < CODE_BASE - 1
        )


CODE_BASE = 2048
CODE_BITS = 11


def pieces(length, blocks):
    found = []
    for j in range(blocks):
        done = 0
        while done < length:
            at = j * length + done
            count = min(length - done, LANES - at % LANES)
            found.append((at // LANES, at % LANES, j, done, count))
            done += count
    return found


def column_of(row):
    return jnp.broadcast_to(row, (LANES, LANES)).T


def inverse_row(columns, first):
    sub = lax.broadcasted_iota(I32, (LANES, LANES), 0)
    target = (lax.broadcasted_iota(I32, (LANES, LANES), 1) + first).astype(F32)
    found = jnp.zeros((LANES, LANES), F32)
    for r, column in enumerate(columns):
        found = jnp.where(column == target, (sub + (r * LANES + 1)).astype(F32), found)
    return jnp.sum(found, axis=0, keepdims=True) - 1.0


def field_tables_kernel(fg, *refs):
    nodes_ref, face_ref, owner_ref, screen_ref = refs[:4]
    table_ref, pad, one, spare, packed = refs[5:]
    one[...] = jnp.full(one.shape, -1.0, F32)
    spare[...] = jnp.full(spare.shape, -1.0, F32)
    pad[...] = jnp.full(pad.shape, -1, I32)
    pad[0 : fg.cells, 0 : fg.npc] = nodes_ref[...]
    for c in range(fg.cells):
        columns = []
        for r in range(fg.rows):
            code = pad[c : c + 1, r * LANES : (r + 1) * LANES].astype(F32)
            one[c * fg.rows + r : c * fg.rows + r + 1, :] = code
            columns.append(column_of(code))
        for t in fg.touched[c]:
            at = fg.at_inverse + c * fg.tiles + t
            one[at : at + 1, :] = inverse_row(columns, t * LANES)
    lane = fg.at_owner_lane
    spare[0:1, 0 : fg.share] = face_ref[...].astype(F32)
    spare[1:2, 0 : fg.domains] = owner_ref[...].astype(F32)
    at = fg.at_face
    one[at : at + 1, :] = spare[0:1, :]
    one[at : at + 1, lane:LANES] = owner_ref[...].astype(F32)
    back = inverse_row([column_of(spare[0:1, :])], 0)
    home = inverse_row([column_of(spare[1:2, :])], -lane)
    lanes = lax.broadcasted_iota(I32, (1, LANES), 1)
    one[at + 1 : at + 2, :] = jnp.where(lanes < lane, back, home)
    packed[...] = jnp.zeros(packed.shape, F32)
    half = fg.at_screen
    packed[0:half, :] = (one[0:half, :] + 1.0) + (one[half : 2 * half, :] + 1.0) * CODE_BASE
    packed[half : half + fg.lines, :] = screen_ref[...]
    for b in range(fg.bands):
        table_ref[b, 0 : fg.part_rows, :] = packed[b * fg.part_rows : (b + 1) * fg.part_rows, :]


def field_tables(fg, pois_nodes, pois_face, block_owner, lines, after):
    specs = [pl.BlockSpec(memory_space=pltpu.VMEM)] * 4 + [pl.BlockSpec(memory_space=pl.ANY)]
    return vmem_call(
        functools.partial(field_tables_kernel, fg),
        sds((fg.bands, up_to(fg.part_rows, SUBLANES), LANES), F32),
        [
            pltpu.VMEM((up_to(fg.cells, SUBLANES), fg.size), I32),
            pltpu.VMEM((up_to(2 * fg.at_screen, SUBLANES), LANES), F32),
            pltpu.VMEM((SUBLANES, LANES), F32),
            pltpu.VMEM((fg.table_rows, LANES), F32),
        ],
        in_specs=specs,
        cost=cost_of(1.0),
    )(pois_nodes, pois_face, block_owner, lines, after)


def lanes_of(values, index):
    return jnp.take_along_axis(values, index, axis=1, mode="promise_in_bounds")


def got_tile(fg, got_ref, band, line):
    lines = fg.width // LANES
    return got_ref[pl.ds(band * fg.domains * lines + line, fg.domains, stride=lines), :]


def decode(fg, got_ref, codes):
    domains, half = fg.domains, fg.at_screen

    def tile(at):
        return got_tile(fg, got_ref, at // fg.part_rows, fg.lines + at % fg.part_rows)

    for at in range(half):
        both = tile(at).astype(I32)
        codes[at] = jnp.bitwise_and(both, CODE_BASE - 1) - 1
        codes[half + at] = jnp.right_shift(both, CODE_BITS) - 1
    screens = [tile(half + g) for g in range(fg.lines)]
    lane = lax.broadcasted_iota(I32, (domains, LANES), 1)
    first, last = fg.at_owner_lane, LANES
    owners = codes[fg.at_face].astype(F32).T[first:last, :]
    inverse = codes[fg.at_face + 1].astype(F32).T[first:last, :]
    back = jnp.where(lane < fg.share, codes[fg.at_face + 1], -1)
    codes[fg.at_face + 1] = pltpu.roll(back, 1, 0)
    places = []
    for q in range(domains):
        block = jnp.broadcast_to(inverse[:, q : q + 1], (domains, LANES)).astype(I32)
        places.append(block * fg.block + lane)
    here = lax.axis_index("domain")
    narrow = lax.broadcasted_iota(I32, (domains, domains), 1)
    mine = jnp.sum(jnp.where(narrow == here, owners, 0.0), axis=1, keepdims=True)
    return places, jnp.broadcast_to(mine, (domains, LANES)).astype(I32), screens


def rows_of(values, index):
    return jnp.take_along_axis(values, index, axis=0, mode="promise_in_bounds")


def lookup(sources, code):
    lane = jnp.bitwise_and(code, LANES - 1)
    which = jnp.right_shift(code, 7)
    total = jnp.zeros(code.shape, F32)
    for b, values in sources:
        total = jnp.where(which == b, lanes_of(values, lane), total)
    return total


def field_source(fg, got_ref, places):
    domains = fg.domains
    density = []
    for g in range(fg.lines):
        total = got_tile(fg, got_ref, 0, g)
        for b in range(1, fg.bands):
            total = total + got_tile(fg, got_ref, b, g)
        density.append(total)
    lane = lax.broadcasted_iota(I32, (domains, LANES), 1)
    source = [None] * fg.lines
    for q in range(domains):
        spread = [jnp.broadcast_to(d[q : q + 1, :], (domains, LANES)) for d in density]
        block = lookup(list(enumerate(spread)), places[q])
        for row, start, j, offset, count in pieces(fg.block, domains):
            if j == q:
                moved = pltpu.roll(block, (start - offset) % LANES, 1)
                inside = (lane >= start) & (lane < start + count)
                before = 0.0 if source[row] is None else source[row]
                source[row] = jnp.where(inside, moved, before)
    return source


def field_solve(fg, source, codes, screen, matrix_ref, high_ref, low_ref, rows, copies):
    domains, cells = fg.domains, fg.cells

    def operator(field):
        ahead = pltpu.roll(field[0], domains - 1, 0)
        local = list(field) + [lookup([(0, ahead)], codes[fg.at_face])]
        for r in range(fg.rows):
            for c in range(cells):
                sources = [(t, local[t]) for t in fg.touched[c]]
                rows[c * domains : (c + 1) * domains, r * LANES : (r + 1) * LANES] = lookup(sources, codes[c * fg.rows + r])
        picked = rows[:, 0 : fg.npc]
        high = picked.astype(BF)
        low = (picked - high.astype(F32)).astype(BF)
        both = dot(jnp.concatenate([high, low], axis=0), high_ref[...])
        half_rows = cells * domains
        for r in range(fg.rows if copies else 0):
            copies.pop(0).wait()
            span = slice(r * LANES, min((r + 1) * LANES, fg.npc))
            rest = matrix_ref[span, :] - high_ref[span, :].astype(F32)
            low_ref[span, :] = rest.astype(BF)
        rows[:, 0 : fg.npc] = both[:half_rows] + (both[half_rows:] + dot(high, low_ref[...]))
        out = [None] * fg.tiles
        for c in range(cells):
            sources = [
                (r, rows[c * domains : (c + 1) * domains, r * LANES : (r + 1) * LANES])
                for r in range(fg.rows)
            ]
            for t in fg.touched[c]:
                term = lookup(sources, codes[fg.at_inverse + c * fg.tiles + t])
                out[t] = term if out[t] is None else out[t] + term
        arriving = pltpu.roll(out[fg.lines], 1, 0)
        out[0] = out[0] + lookup([(0, arriving)], codes[fg.at_face + 1])
        return [screen[g] * field[g] + out[g] for g in range(fg.lines)]

    step_one = [s * (1.0 / solve_center) for s in source]
    applied = operator(step_one)
    residual = [s - a for s, a in zip(source, applied)]
    a1, b1 = weight_one * weight_zero, 2.0 * weight_one / solve_half
    step_two = [a1 * e + b1 * r for e, r in zip(step_one, residual)]
    applied = operator(step_two)
    residual = [r - a for r, a in zip(residual, applied)]
    a2, b2 = weight_two * weight_one, 2.0 * weight_two / solve_half
    step_three = [a2 * e + b2 * r for e, r in zip(step_two, residual)]
    return [(x + y) + z for x, y, z in zip(step_one, step_two, step_three)]


def field_top_kernel(fg, matrix_hbm, after_ref, top_ref, matrix_ref, sems):
    del after_ref
    spans = [pl.ds(r * LANES, min(LANES, fg.npc - r * LANES)) for r in range(fg.rows)]
    copies = fetch([(matrix_hbm.at[span], matrix_ref.at[span]) for span in spans], sems)
    for r, copy in enumerate(copies):
        copy.wait()
        span = slice(r * LANES, min((r + 1) * LANES, fg.npc))
        top_ref[span, :] = matrix_ref[span, :].astype(BF)


def field_top(fg, matrix, after):
    return vmem_call(
        functools.partial(field_top_kernel, fg),
        sds(matrix.shape, BF),
        [pltpu.VMEM(matrix.shape, F32), pltpu.SemaphoreType.DMA((fg.rows,))],
        in_specs=[pl.BlockSpec(memory_space=pltpu.HBM), pl.BlockSpec(memory_space=pl.ANY)],
        cost=cost_of(1.5),
    )(*in_hbm(matrix), after)


def field_kernel(geo, fg, scale, got_ref, matrix_hbm, high_ref, base_ref, near_ref, far_ref, y_ref, *refs):
    n = len(geo.touching)
    crosses, reaches, refs = refs[:n], refs[n : 2 * n], refs[2 * n :]
    z_ref, near_out, far_out, column_ref, hartree_ref = refs[:5]
    codes, rows, mine, matrix_ref, low_ref, sems = refs[5:]
    spans = [pl.ds(r * LANES, min(LANES, fg.npc - r * LANES)) for r in range(fg.rows)]
    copies = fetch([(matrix_hbm.at[span], matrix_ref.at[span]) for span in spans], sems)
    z_ref[...] = base_ref[...]
    add_halo(geo, scale, z_ref, near_ref, far_ref, crosses)
    places, owner, screens = decode(fg, got_ref, codes)
    source = field_source(fg, got_ref, places)
    solved = field_solve(fg, source, codes, screens, matrix_ref, high_ref, low_ref, rows, copies)
    lane = lax.broadcasted_iota(I32, (fg.domains, LANES), 1)
    block = lookup(list(enumerate(solved)), lane + lax.axis_index("domain") * fg.block)
    mine[...] = rows_of(block, owner)
    for j in range(fg.domains):
        at = slice(j * fg.block, (j + 1) * fg.block)
        column = column_of(mine[j : j + 1, :])[0 : fg.block, :]
        column_ref[at, :] = column
        z_ref[at, :] += (column * scale) * y_ref[at, :]
    write_sends(geo, z_ref, reaches, near_out, far_out)
    for row, start, j, offset, count in pieces(fg.block, fg.domains):
        hartree_ref[row : row + 1, start : start + count] = mine[j : j + 1, offset : offset + count]


def field_step(geo, fg, scale, got, matrix, top, base, halo, y, crosses, reaches):
    tile = (fg.domains, LANES)
    vmem = pl.BlockSpec(memory_space=pltpu.VMEM)
    got = got.reshape(got.shape[0] * fg.width // LANES, LANES)
    args = [got, *in_hbm(matrix), top, base, *halo, y, *crosses, *reaches]
    specs = [vmem] * len(args)
    specs[1] = pl.BlockSpec(memory_space=pltpu.HBM)
    z, near, far, column, lines = vmem_call(
        functools.partial(field_kernel, geo, fg, scale),
        [
            sds(y.shape, F32),
            *send_shapes(geo, y.shape[1]),
            sds((fg.own, LANES), F32),
            sds((fg.lines, LANES), F32),
        ],
        [
            pltpu.VMEM((2 * fg.at_screen, *tile), I32),
            pltpu.VMEM((fg.cells * fg.domains, fg.size), F32),
            pltpu.VMEM(tile, F32),
            pltpu.VMEM(matrix.shape, F32),
            pltpu.VMEM(matrix.shape, BF),
            pltpu.SemaphoreType.DMA((fg.rows,)),
        ],
        in_specs=specs,
        cost=cost_of(4.0),
    )(*args)
    return z, (near, far), column, lines


def assembled(owned_rows, face_row, terms):
    owned_count = owned_rows.shape[0]
    shared = face_row.shape[0]
    coming = jnp.take(from_behind(owned_rows[:shared], "domain", -1), face_row, axis=0)
    partial_value = terms(jnp.concatenate([owned_rows, coming], axis=0))
    upper_rows = partial_value[owned_count:]
    ordered = jnp.zeros_like(upper_rows).at[face_row].set(upper_rows)
    arrived = from_behind(ordered, "domain", 1)
    return partial_value[:owned_count].at[:shared].add(arrived)


def field_terms(local_rows, pois_matrix, node_ids):
    cell_vals = jnp.take(local_rows, node_ids, axis=0)
    product = jnp.einsum(
        "pq,cq->cp",
        pois_matrix,
        cell_vals,
        precision=lax.Precision.HIGHEST,
        preferred_element_type=F32,
    )
    return jnp.zeros(local_rows.shape, F32).at[node_ids.reshape(-1)].add(product.reshape(-1))


def reshuffle(blocks):
    return lax.all_to_all(blocks, "domain", split_axis=0, concat_axis=0, tiled=True)


def distributed_field(y, occupation, owner_row, pois_matrix, pois_nodes, field_face, screening):
    owned_count = y.shape[0]
    domains = lax.axis_size("domain")
    block_len = owned_count // domains
    partial_value = jnp.dot(
        y * y, occupation, precision=lax.Precision.HIGHEST, preferred_element_type=F32
    )
    summed = lax.psum(partial_value, "band")
    arranged = (
        jnp.zeros((domains, block_len), F32)
        .at[owner_row]
        .set(summed.reshape(domains, block_len))
    )
    source = reshuffle(arranged).reshape(owned_count)

    def field_operator(vector):
        return (
            assembled(
                vector, field_face, lambda local: field_terms(local, pois_matrix, pois_nodes)
            )
            + screening * vector
        )

    step_one = source / solve_center
    residual = source - field_operator(step_one)
    step_two = weight_one * weight_zero * step_one + 2.0 * weight_one / solve_half * residual
    residual = residual - field_operator(step_two)
    step_three = weight_two * weight_one * step_two + 2.0 * weight_two / solve_half * residual
    solved = step_one + step_two + step_three
    returned = reshuffle(solved.reshape(domains, block_len))
    return jnp.take(returned, owner_row, axis=0).reshape(owned_count)


def exchange(sends):
    dn, up = sends
    h_dn = from_behind(dn, "domain", 1)
    h_up = from_behind(up, "domain", -1)
    return h_up, h_dn


def on_device(
    orbitals,
    potential,
    occupation,
    cell_matrix,
    cell_nodes,
    face_order,
    pois_matrix,
    pois_nodes,
    pois_face,
    screening,
    block_owner,
):
    domains = lax.axis_size("domain")
    bands = lax.axis_size("band")
    own, columns = orbitals.shape
    geo = Geometry(own, face_order.shape[1], cell_nodes.shape[0], cell_nodes.shape[1])
    fg = FieldGeometry(bands, domains, own, pois_face.shape[1], pois_nodes.shape[0], pois_nodes.shape[1])
    first, later = 1.0 / filter_half, 2.0 / filter_half

    others = [cell_matrix, potential.reshape(own // LANES, LANES)]
    if fg.fits:
        others += [pois_nodes, pois_face, block_owner, screening.reshape(own // LANES, LANES)]
        others.append(occupation.reshape(1, columns))
    sends, y0, nodes, (matrix, lines, *others) = pack(geo, orbitals, cell_nodes, face_order, *others)
    halo = exchange(sends)
    mats, crosses, reaches, pot = own_matrices(geo, nodes, matrix, lines)
    base = owned_part(geo, first, y0, None, pot, None, mats, ())
    uppers, base = behind_sums(geo, first, halo[1], matrix, base, sends[1])
    y1, sends1 = first_finish(geo, first, base, halo[0], crosses, reaches)

    halo = swap(sends1)
    base = owned_part(geo, later, y1, y0, pot, None, mats, uppers)
    if fg.fits:
        *others, weights = others
        table = field_tables(fg, *others, base)
    y2, *sends2 = finish(geo, later, base, halo, crosses, reaches)

    halo = swap(sends2)
    base = owned_part(geo, later, y2, y1, pot, None, mats, uppers)
    if fg.fits:
        y3, dn, up, spread = finish(
            geo, later, base, halo, crosses, reaches, density=(fg, weights, table)
        )
        dens = lax.all_to_all(spread, ("band", "domain"), 0, 0, tiled=True)
        halo = swap((dn, up))
        base = owned_part(geo, first, y3, None, pot, None, mats, uppers)
        top = field_top(fg, pois_matrix, base)
        z1, sends4, column, packed = field_step(
            geo, fg, first, dens, pois_matrix, top, base, halo, y3, crosses, reaches
        )
    else:
        y3, *sends3 = finish(geo, later, base, halo, crosses, reaches)
        halo = swap(sends3)
        hartree = distributed_field(
            y3, occupation, block_owner[0], pois_matrix, pois_nodes, pois_face[0], screening
        )
        column = jnp.broadcast_to(hartree[:, None], (own, LANES))
        base = owned_part(geo, first, y3, None, pot, column, mats, uppers)
        z1, *sends4 = finish(geo, first, base, halo, crosses, reaches)

    halo = swap(sends4)
    base = owned_part(geo, later, z1, y3, pot, column, mats, uppers, far=fg.fits)
    last = [packed] if fg.fits else []
    filtered, *rest = finish(geo, later, base, halo, crosses, last=last)
    if fg.fits:
        hartree = rest[0].reshape(own)
    return filtered, hartree


def swap(sends):
    length = lax.axis_size("domain")
    near, far = sends
    turns = [(i, (i + 1) % length if i % 2 else (i - 1) % length) for i in range(length)]
    far = lax.ppermute(far, "domain", turns)
    near = lax.ppermute(near, "domain", [(i, i ^ 1) for i in range(length)])
    return near, far


def solution(mesh):
    return jax.shard_map(
        on_device,
        mesh=mesh,
        in_specs=(
            P("domain", "band"),
            P("domain"),
            P("band"),
            P(),
            P("domain", None),
            P("domain", None),
            P(),
            P("domain", None),
            P("domain", None),
            P("domain"),
            P("domain", None),
        ),
        out_specs=(P("domain", "band"), P("domain")),
        check_vma=False,
    )
```

```python
import functools

import jax
import jax.numpy as jnp
from jax import lax
from jax.experimental import pallas as pl
from jax.experimental.pallas import tpu as pltpu
from jax.sharding import PartitionSpec as P

filter_center = 1.8
filter_half = 2.7
solve_center = 3.25
solve_half = 2.75
solve_ratio = solve_center / solve_half
weight_zero = 1.0 / solve_ratio
weight_one = 1.0 / (2.0 * solve_ratio - weight_zero)
weight_two = 1.0 / (2.0 * solve_ratio - weight_one)

BF = jnp.bfloat16
F32 = jnp.float32
I32 = jnp.int32
LANES = 128
SUBLANES = 8


def up_to(n, m):
    return -(-n // m) * m


def from_behind(array, axis, by):
    length = lax.axis_size(axis)
    return lax.ppermute(array, axis, [(i, (i + by) % length) for i in range(length)])


class Window:
    def __init__(self, start, npc, own, nloc):
        end = start + npc
        self.lo = start // 16 * 16
        self.hi = min(up_to(min(end, own), 16), own)
        self.touches = end > own
        self.low = up_to(max(0, end - nloc), 16)
        self.rows = self.hi - self.lo + self.low


class Geometry:
    def __init__(self, own, share, cells, npc):
        self.own, self.share, self.cells, self.npc = own, share, cells, npc
        nloc = own + share
        stride = nloc // cells
        self.sp = up_to(share, 16)
        self.npl = up_to(npc, LANES)
        self.windows = [Window(c * stride, npc, own, nloc) for c in range(cells)]
        self.touching = [c for c in range(cells) if self.windows[c].touches]
        self.dn_lo = min(self.windows[c].lo for c in self.touching)
        self.low = max(w.low for w in self.windows)
        self.dn_rows = own - self.dn_lo + self.low
        self.table_rows = up_to(cells, SUBLANES)
        self.table_lanes = up_to(npc, LANES)
        self.table_tiles = self.table_lanes // LANES


def dot(a, b):
    return lax.dot_general(a, b, (((1,), (0,)), ((), ())), preferred_element_type=F32)


def dot_t(a, b):
    return lax.dot_general(a, b, (((1,), (1,)), ((), ())), preferred_element_type=F32)


def vmem_call(kernel, out_shape, scratch=(), in_specs=None, out_specs=None, cost=None):
    kwargs = {}
    if in_specs is not None:
        kwargs["in_specs"] = in_specs
    if out_specs is not None:
        kwargs["out_specs"] = out_specs
    return pl.pallas_call(
        kernel,
        out_shape=out_shape,
        scratch_shapes=list(scratch),
        cost_estimate=cost,
        compiler_params=pltpu.CompilerParams(vmem_limit_bytes=12 * 1024 * 1024),
        **kwargs,
    )


def in_hbm(*arrays):
    return [pltpu.with_memory_space_constraint(a, pltpu.HBM) for a in arrays]


def sds(shape, dtype):
    return jax.ShapeDtypeStruct(shape, dtype)


def one_hot_rows(count, first, nodes):
    ids = lax.broadcasted_iota(I32, (count, nodes.shape[1]), 0) + first
    return jnp.where(ids == nodes, 1.0, 0.0).astype(BF)


def place_table(geo, nodes_ref, face_ref, table, faces):
    table[...] = jnp.full(table.shape, -1, I32)
    table[0 : geo.cells, 0 : geo.npc] = nodes_ref[...]
    faces[...] = jnp.zeros(faces.shape, I32)
    faces[0:1, 0 : geo.share] = face_ref[...]
    for t in range(geo.table_tiles):
        lanes = slice(t * LANES, (t + 1) * LANES)
        nodes = table[:, lanes]
        beyond = nodes - geo.own
        at = jnp.bitwise_and(beyond, LANES - 1)
        which = jnp.right_shift(beyond, 7)
        for f in range(faces.shape[1] // LANES):
            row = jnp.broadcast_to(faces[0:1, f * LANES : (f + 1) * LANES], nodes.shape)
            nodes = jnp.where(which == f, lanes_of(row, at) + geo.own, nodes)
        table[:, lanes] = nodes


def place_matrix(geo, matrix_ref, matrix_pad):
    matrix_pad[...] = jnp.zeros(matrix_pad.shape, F32)
    matrix_pad[0 : geo.npc, 0 : geo.npc] = matrix_ref[...].astype(F32)
    return matrix_pad[...].astype(BF)


def table_scratch(geo):
    return pltpu.VMEM((geo.table_rows, geo.table_lanes), I32)


def matrix_scratch(geo):
    return pltpu.VMEM((geo.npl, geo.npl), F32)


def nodes_of(geo, table, c):
    return table[c : c + 1, 0 : geo.npl]


def owned_picks(geo, c, nodes):
    w = geo.windows[c]
    picks = one_hot_rows(w.hi - w.lo, w.lo, nodes)
    if w.low:
        picks = jnp.concatenate([picks, one_hot_rows(w.low, 0, nodes)], axis=0)
    return picks


def upper_picks(geo, nodes):
    return one_hot_rows(geo.sp, geo.own, nodes)


def own_matrices_kernel(geo, *refs):
    table, matrix_ref, pot_ref = refs[:3]
    outs, matrix_pad = refs[3:-1], refs[-1]
    matrix = place_matrix(geo, matrix_ref, matrix_pad)
    for c in range(geo.cells):
        nodes = nodes_of(geo, table, c)
        own = owned_picks(geo, c, nodes)
        left = dot(own, matrix).astype(BF)
        outs[c][...] = dot_t(left, own).astype(BF)
        if c in geo.touching:
            at = geo.cells + geo.touching.index(c)
            upper = upper_picks(geo, nodes)
            outs[at][...] = dot_t(left, upper).astype(BF)
            left = dot(upper, matrix).astype(BF)
            outs[at + len(geo.touching)][...] = dot_t(left, own).astype(BF)
    column = outs[-1]
    for r in range(geo.own // LANES):
        row = jnp.broadcast_to(pot_ref[r : r + 1, :], (LANES, LANES))
        column[r * LANES : (r + 1) * LANES, :] = row.T


def own_matrices(geo, table, cell_matrix, lines):
    shapes = [sds((w.rows, w.rows), BF) for w in geo.windows]
    shapes += [sds((geo.windows[c].rows, geo.sp), BF) for c in geo.touching]
    shapes += [sds((geo.sp, geo.windows[c].rows), BF) for c in geo.touching]
    shapes += [sds((geo.own, LANES), F32)]
    outs = vmem_call(
        functools.partial(own_matrices_kernel, geo),
        shapes,
        [matrix_scratch(geo)],
        cost=cost_of(2.0),
    )(table, cell_matrix, lines)
    n, m = geo.cells, geo.cells + len(geo.touching)
    return outs[:n], outs[n:m], outs[m:-1], outs[-1]


def build_behind(geo, sent_ref, matrix_ref, table, matrix_pad, behinds, uppers):
    for t in range(geo.table_tiles):
        at = geo.dn_rows + 2 * t * geo.table_rows
        digits = sent_ref[at : at + 2 * geo.table_rows, :].astype(F32)
        value = digits[: geo.table_rows] * LANES + digits[geo.table_rows :] - 1.0
        table[:, t * LANES : (t + 1) * LANES] = value.astype(I32)
    matrix = place_matrix(geo, matrix_ref, matrix_pad)
    for at, c in enumerate(geo.touching):
        nodes = nodes_of(geo, table, c)
        upper = upper_picks(geo, nodes)
        left = dot(upper, matrix).astype(BF)
        behinds[at][...] = dot_t(left, owned_picks(geo, c, nodes)).astype(BF)
        uppers[at][...] = dot_t(left, upper).astype(BF)


def cost_of(us):
    return pl.CostEstimate(flops=0, bytes_accessed=int(us * 3.0e6), transcendentals=0)


def write_rows(geo, y_ref, dn_ref, up_ref):
    top = geo.own - geo.dn_lo
    dn_ref[0:top, :] = y_ref[geo.dn_lo : geo.own, :].astype(BF)
    dn_ref[top : top + geo.low, :] = y_ref[0 : geo.low, :].astype(BF)
    up_ref[...] = y_ref[0 : geo.sp, :].astype(BF)


def window_rows(geo, c, y_ref):
    w = geo.windows[c]
    rows = y_ref[w.lo : w.hi, :].astype(BF)
    if w.low:
        rows = jnp.concatenate([rows, y_ref[0 : w.low, :].astype(BF)], axis=0)
    return rows


def is_even():
    return jnp.bitwise_and(lax.axis_index("domain"), 1) == 0


def write_sends(geo, y_ref, reaches, near_ref, far_ref):
    total = None
    for at, c in enumerate(geo.touching):
        term = dot(reaches[at][...], window_rows(geo, c, y_ref))
        total = term if total is None else total + term
    rows = y_ref[0 : geo.sp, :]
    even = is_even()
    near_ref[...] = jnp.where(even, total, rows).astype(BF)
    far_ref[...] = jnp.where(even, rows, total).astype(BF)


def send_shapes(geo, columns):
    return [sds((geo.sp, columns), BF), sds((geo.sp, columns), BF)]


def fetch(pairs, sems):
    copies = [pltpu.make_async_copy(src, dst, sems.at[i]) for i, (src, dst) in enumerate(pairs)]
    for copy in copies:
        copy.start()
    return copies


def pack_kernel(geo, extra, y_hbm, nodes_hbm, face_hbm, *refs):
    sources, refs = refs[:extra], refs[extra:]
    dn_ref, up_ref, y, table = refs[:4]
    kept, (nodes, face, faces, sems) = refs[4 : 4 + extra], refs[4 + extra :]
    cuts = sorted({0, max(geo.sp, geo.low), geo.dn_lo, geo.own})
    spans = list(zip(cuts[:-1], cuts[1:]))
    pairs = [(nodes_hbm, nodes), (face_hbm, face)]
    pairs += [(y_hbm.at[pl.ds(a, b - a)], y.at[pl.ds(a, b - a)]) for a, b in spans]
    pairs += list(zip(sources, kept))
    copies = fetch(pairs, sems)
    copies[0].wait()
    copies[1].wait()
    place_table(geo, nodes, face, table, faces)
    for t in range(geo.table_tiles):
        at = geo.dn_rows + 2 * t * geo.table_rows
        value = table[:, t * LANES : (t + 1) * LANES] + 1
        high = jnp.right_shift(value, 7).astype(F32)
        low = jnp.bitwise_and(value, LANES - 1).astype(F32)
        digits = jnp.concatenate([high, low], axis=0).astype(BF)
        dn_ref[at : at + 2 * geo.table_rows, :] = digits
    for copy in copies[2:]:
        copy.wait()
    write_rows(geo, y, dn_ref, up_ref)


def pack(geo, y, cell_nodes, face_order, *others):
    up = sds((geo.sp, y.shape[1]), BF)
    rows = geo.dn_rows + 2 * geo.table_rows * geo.table_tiles
    dn, up, y, table, *others = vmem_call(
        functools.partial(pack_kernel, geo, len(others)),
        [
            sds((rows, y.shape[1]), BF),
            up,
            sds(y.shape, F32),
            sds((geo.table_rows, geo.table_lanes), I32),
            *[sds(a.shape, a.dtype) for a in others],
        ],
        [
            pltpu.VMEM(cell_nodes.shape, I32),
            pltpu.VMEM(face_order.shape, I32),
            pltpu.VMEM((1, up_to(geo.share, LANES)), I32),
            pltpu.SemaphoreType.DMA((5 + len(others),)),
        ],
        in_specs=[pl.BlockSpec(memory_space=pltpu.HBM)] * (3 + len(others)),
        cost=cost_of(1.0),
    )(*in_hbm(y, cell_nodes, face_order, *others))
    return (dn, up), y, table, others


def owned_part_kernel(geo, scale, has_prev, has_field, has_upper, far, *refs):
    refs = list(refs)
    if far:
        places, sems = refs[-2 - geo.cells : -1], refs[-1]
        refs = refs[: -2 - geo.cells]
    base_ref = refs.pop()
    y_ref = refs.pop(0)
    prev_ref = refs.pop(0) if has_prev else None
    pot_ref = refs.pop(0)
    field_ref = refs.pop(0) if has_field else None
    mats = [refs.pop(0) for _ in range(geo.cells)]
    if far:
        copies = fetch(list(zip([pot_ref, *mats], places)), sems)
        pot_ref, mats = places[0], places[1:]
        for copy in copies:
            copy.wait()
    y = y_ref[...]
    factor = pot_ref[...]
    if has_field:
        factor = factor + field_ref[...]
    value = ((factor - filter_center) * scale) * y
    if has_prev:
        value = value - prev_ref[...]
    base_ref[...] = value
    x = y.astype(BF)
    for c in range(geo.cells):
        w = geo.windows[c]
        own = w.hi - w.lo
        rows = x[w.lo : w.hi, :]
        if w.low:
            rows = jnp.concatenate([rows, x[0 : w.low, :]], axis=0)
        product = dot(mats[c][...], rows) * scale
        base_ref[w.lo : w.hi, :] += product[:own]
        if w.low:
            base_ref[0 : w.low, :] += product[own:]
    if has_upper:
        for upper in refs:
            base_ref[0 : geo.sp, :] += dot(upper[...], x[0 : geo.sp, :]) * scale


def owned_part(geo, scale, y, prev, pot, field, mats, uppers, far=False):
    vmem, hbm = pl.BlockSpec(memory_space=pltpu.VMEM), pl.BlockSpec(memory_space=pltpu.HBM)
    place, scratch = vmem, []
    if far:
        place = hbm
        scratch = [pltpu.VMEM(a.shape, a.dtype) for a in [pot, *mats]]
        scratch.append(pltpu.SemaphoreType.DMA((1 + len(mats),)))
        pot, *mats = in_hbm(pot, *mats)
    args = [y] + ([prev] if prev is not None else []) + [pot]
    args += [field] if field is not None else []
    args += list(mats) + list(uppers)
    specs = [vmem] * (2 if prev is not None else 1) + [place]
    specs += [vmem] * (0 if field is None else 1)
    specs += [place] * len(mats) + [vmem] * len(uppers)
    return vmem_call(
        functools.partial(
            owned_part_kernel, geo, scale, prev is not None, field is not None, bool(uppers), far
        ),
        sds(y.shape, F32),
        scratch,
        in_specs=specs,
        cost=cost_of(2.0),
    )(*args)


def add_upper(geo, scale, y_ref, h_up, crosses):
    for at, c in enumerate(geo.touching):
        w = geo.windows[c]
        own = w.hi - w.lo
        product = dot(crosses[at][...], h_up) * scale
        y_ref[w.lo : w.hi, :] += product[:own]
        if w.low:
            y_ref[0 : w.low, :] += product[own:]


def add_rows(geo, scale, y_ref, h_dn, behinds, uppers, own_up):
    total = None
    for at, c in enumerate(geo.touching):
        w = geo.windows[c]
        first = w.lo - geo.dn_lo
        term = dot(behinds[at][...], h_dn[first : first + w.rows, :])
        term = term + dot(uppers[at][...], own_up)
        total = term if total is None else total + term
    y_ref[0 : geo.sp, :] += total * scale


def add_halo(geo, scale, y_ref, near_ref, far_ref, crosses):
    near, far = near_ref[...].astype(F32), far_ref[...].astype(F32)
    even = is_even()
    y_ref[0 : geo.sp, :] += jnp.where(even, far, near) * scale
    add_upper(geo, scale, y_ref, jnp.where(even, near, far).astype(BF), crosses)


def write_density(y_ref, occ_ref, table_ref, part_rows, dens_ref):
    parts = dens_ref.shape[0]
    own = y_ref.shape[0]
    y = y_ref[...]
    terms = y * y * occ_ref[...]
    high = terms.astype(BF)
    low = (terms - high.astype(F32)).astype(BF)
    ones = jnp.ones((SUBLANES, terms.shape[1]), BF)
    summed = dot_t(ones, high) + dot_t(ones, low)
    dens_ref[:, 0, 0:own] = jnp.broadcast_to(summed[0:1, :], (parts, own))
    band = lax.axis_index("band")
    for r in range(part_rows):
        row = table_ref[band, r : r + 1, :]
        dens_ref[:, 0, own + r * LANES : own + (r + 1) * LANES] = jnp.broadcast_to(row, (parts, LANES))


def behind_kernel(geo, scale, sent_ref, matrix_ref, base_ref, own_up_ref, *refs):
    n = len(geo.touching)
    uppers, out_ref, behinds, rest = refs[:n], refs[n], refs[n + 1 : 2 * n + 1], refs[2 * n + 1 :]
    build_behind(geo, sent_ref, matrix_ref, *rest, behinds, uppers)
    out_ref[...] = base_ref[...]
    add_rows(geo, scale, out_ref, sent_ref[...], behinds, uppers, own_up_ref[...])


def behind_sums(geo, scale, sent, matrix, base, own_up):
    *uppers, base = vmem_call(
        functools.partial(behind_kernel, geo, scale),
        [sds((geo.sp, geo.sp), BF) for _ in geo.touching] + [sds(base.shape, F32)],
        [
            *[pltpu.VMEM((geo.sp, geo.windows[c].rows), BF) for c in geo.touching],
            table_scratch(geo),
            matrix_scratch(geo),
        ],
        cost=cost_of(1.0),
    )(sent, matrix, base, own_up)
    return uppers, base


def first_finish_kernel(geo, scale, *refs):
    n = len(geo.touching)
    base_ref, up_ref = refs[:2]
    crosses, reaches = refs[2 : 2 + n], refs[2 + n : 2 + 2 * n]
    y_ref, near_out, far_out = refs[2 + 2 * n :]
    y_ref[...] = base_ref[...]
    add_upper(geo, scale, y_ref, up_ref[...], crosses)
    write_sends(geo, y_ref, reaches, near_out, far_out)


def first_finish(geo, scale, base, h_up, crosses, reaches):
    y, near, far = vmem_call(
        functools.partial(first_finish_kernel, geo, scale),
        [sds(base.shape, F32), *send_shapes(geo, base.shape[1])],
        cost=cost_of(0.5),
    )(base, h_up, *crosses, *reaches)
    return y, (near, far)


def finish_kernel(geo, scale, mode, part_rows, *refs):
    refs = list(refs)
    n = len(geo.touching)
    base_ref, near_ref, far_ref = refs[:3]
    refs = refs[3:]
    crosses, refs = refs[:n], refs[n:]
    halo = (near_ref, far_ref, crosses)
    if mode == "last":
        finish_last(geo, scale, base_ref, halo, *refs)
        return
    reaches, refs = refs[:n], refs[n:]
    if mode == "density":
        occ_ref, table_ref = refs.pop(0), refs.pop(0)
    y_ref = refs.pop(0)
    y_ref[...] = base_ref[...]
    add_halo(geo, scale, y_ref, *halo)
    if mode == "density":
        _, _, out_hbm, dens, sem = refs
        write_density(y_ref, occ_ref, table_ref, part_rows, dens)
        copy = pltpu.make_async_copy(dens, out_hbm, sem)
        copy.start()
    write_sends(geo, y_ref, reaches, refs[0], refs[1])
    if mode == "density":
        copy.wait()


def finish_last(geo, scale, base_ref, halo, *refs):
    extras = (len(refs) - 3) // 2
    sources, out_hbm, targets = refs[:extras], refs[extras], refs[extras + 1 : -2]
    y_ref, sems = refs[-2:]
    top = max(geo.sp, geo.low)
    inner = pl.ds(top, geo.dn_lo - top)
    copies = fetch([(base_ref.at[inner], out_hbm.at[inner]), *zip(sources, targets)], sems)
    edges = [(0, top), (geo.dn_lo, geo.own)]
    for a, b in edges:
        y_ref[a:b, :] = base_ref[a:b, :]
    add_halo(geo, scale, y_ref, *halo)
    for i, (a, b) in enumerate(edges):
        edge = pl.ds(a, b - a)
        copy = pltpu.make_async_copy(y_ref.at[edge], out_hbm.at[edge], sems.at[1 + extras + i])
        copy.start()
        copies.append(copy)
    for copy in copies:
        copy.wait()


def finish(geo, scale, base, halo, crosses, reaches=(), density=None, last=None):
    columns = base.shape[1]
    args = [base, halo[0], halo[1], *crosses, *reaches]
    mode, part_rows = "plain", 0
    shapes = [sds(base.shape, F32)]
    scratch = []
    vmem, hbm = pl.BlockSpec(memory_space=pltpu.VMEM), pl.BlockSpec(memory_space=pltpu.HBM)
    out_specs = [vmem, vmem, vmem]
    if last is not None:
        mode = "last"
        args += last
        shapes += [sds(a.shape, a.dtype) for a in last]
        out_specs = [hbm] * len(shapes)
        scratch = [pltpu.VMEM(base.shape, F32), pltpu.SemaphoreType.DMA((3 + len(last),))]
    else:
        shapes += send_shapes(geo, columns)
    if density is not None:
        mode = "density"
        fg, weights, table = density
        part_rows = fg.part_rows
        args += [weights, table]
        spread = (fg.bands * fg.domains, 1, fg.width)
        shapes.append(sds(spread, F32))
        out_specs.append(hbm)
        scratch = [pltpu.VMEM(spread, F32), pltpu.SemaphoreType.DMA(())]
    return vmem_call(
        functools.partial(finish_kernel, geo, scale, mode, part_rows),
        shapes,
        scratch,
        out_specs=out_specs,
        cost=cost_of(1.0),
    )(*args)


class FieldGeometry:
    def __init__(self, bands, domains, own, share, cells, npc):
        self.bands, self.domains, self.own, self.share = bands, domains, own, share
        self.cells, self.npc = cells, npc
        self.block = own // domains
        self.rows = up_to(npc, LANES) // LANES
        self.lines = own // LANES
        self.tiles = self.lines + 1
        nloc = own + share
        self.touched = []
        for c in range(cells):
            nodes = [(c * (nloc // cells) + k) % nloc for k in range(npc)]
            self.touched.append(sorted({node // LANES for node in nodes}))
        self.at_inverse = cells * self.rows
        self.at_face = self.at_inverse + cells * self.tiles
        self.at_screen = up_to(self.at_face + 2, 2) // 2
        self.part_rows = -(-(self.at_screen + self.lines) // bands)
        self.table_rows = up_to(self.part_rows * bands, SUBLANES)
        self.width = own + self.part_rows * LANES
        self.size = self.rows * LANES
        self.at_owner_lane = LANES - domains
        self.fits = (
            domains == SUBLANES
            and own % (domains * SUBLANES) == 0
            and own % LANES == 0
            and self.block <= LANES
            and share <= self.at_owner_lane
            and max(npc, nloc) < CODE_BASE - 1
        )


CODE_BASE = 2048
CODE_BITS = 11


def pieces(length, blocks):
    found = []
    for j in range(blocks):
        done = 0
        while done < length:
            at = j * length + done
            count = min(length - done, LANES - at % LANES)
            found.append((at // LANES, at % LANES, j, done, count))
            done += count
    return found


def column_of(row):
    return jnp.broadcast_to(row, (LANES, LANES)).T


def inverse_row(columns, first):
    sub = lax.broadcasted_iota(I32, (LANES, LANES), 0)
    target = (lax.broadcasted_iota(I32, (LANES, LANES), 1) + first).astype(F32)
    found = jnp.zeros((LANES, LANES), F32)
    for r, column in enumerate(columns):
        found = jnp.where(column == target, (sub + (r * LANES + 1)).astype(F32), found)
    return jnp.sum(found, axis=0, keepdims=True) - 1.0


def field_tables_kernel(fg, *refs):
    nodes_ref, face_ref, owner_ref, screen_ref = refs[:4]
    table_ref, pad, one, spare, packed = refs[5:]
    one[...] = jnp.full(one.shape, -1.0, F32)
    spare[...] = jnp.full(spare.shape, -1.0, F32)
    pad[...] = jnp.full(pad.shape, -1, I32)
    pad[0 : fg.cells, 0 : fg.npc] = nodes_ref[...]
    for c in range(fg.cells):
        columns = []
        for r in range(fg.rows):
            code = pad[c : c + 1, r * LANES : (r + 1) * LANES].astype(F32)
            one[c * fg.rows + r : c * fg.rows + r + 1, :] = code
            columns.append(column_of(code))
        for t in fg.touched[c]:
            at = fg.at_inverse + c * fg.tiles + t
            one[at : at + 1, :] = inverse_row(columns, t * LANES)
    lane = fg.at_owner_lane
    spare[0:1, 0 : fg.share] = face_ref[...].astype(F32)
    spare[1:2, 0 : fg.domains] = owner_ref[...].astype(F32)
    at = fg.at_face
    one[at : at + 1, :] = spare[0:1, :]
    one[at : at + 1, lane:LANES] = owner_ref[...].astype(F32)
    back = inverse_row([column_of(spare[0:1, :])], 0)
    home = inverse_row([column_of(spare[1:2, :])], -lane)
    lanes = lax.broadcasted_iota(I32, (1, LANES), 1)
    one[at + 1 : at + 2, :] = jnp.where(lanes < lane, back, home)
    packed[...] = jnp.zeros(packed.shape, F32)
    half = fg.at_screen
    packed[0:half, :] = (one[0:half, :] + 1.0) + (one[half : 2 * half, :] + 1.0) * CODE_BASE
    packed[half : half + fg.lines, :] = screen_ref[...]
    for b in range(fg.bands):
        table_ref[b, 0 : fg.part_rows, :] = packed[b * fg.part_rows : (b + 1) * fg.part_rows, :]


def field_tables(fg, pois_nodes, pois_face, block_owner, lines, after):
    specs = [pl.BlockSpec(memory_space=pltpu.VMEM)] * 4 + [pl.BlockSpec(memory_space=pl.ANY)]
    return vmem_call(
        functools.partial(field_tables_kernel, fg),
        sds((fg.bands, up_to(fg.part_rows, SUBLANES), LANES), F32),
        [
            pltpu.VMEM((up_to(fg.cells, SUBLANES), fg.size), I32),
            pltpu.VMEM((up_to(2 * fg.at_screen, SUBLANES), LANES), F32),
            pltpu.VMEM((SUBLANES, LANES), F32),
            pltpu.VMEM((fg.table_rows, LANES), F32),
        ],
        in_specs=specs,
        cost=cost_of(1.0),
    )(pois_nodes, pois_face, block_owner, lines, after)


def lanes_of(values, index):
    return jnp.take_along_axis(values, index, axis=1, mode="promise_in_bounds")


def got_tile(fg, got_ref, band, line):
    lines = fg.width // LANES
    return got_ref[pl.ds(band * fg.domains * lines + line, fg.domains, stride=lines), :]


def decode(fg, got_ref, codes):
    domains, half = fg.domains, fg.at_screen

    def tile(at):
        return got_tile(fg, got_ref, at // fg.part_rows, fg.lines + at % fg.part_rows)

    for at in range(half):
        both = tile(at).astype(I32)
        codes[at] = jnp.bitwise_and(both, CODE_BASE - 1) - 1
        codes[half + at] = jnp.right_shift(both, CODE_BITS) - 1
    screens = [tile(half + g) for g in range(fg.lines)]
    lane = lax.broadcasted_iota(I32, (domains, LANES), 1)
    first, last = fg.at_owner_lane, LANES
    owners = codes[fg.at_face].astype(F32).T[first:last, :]
    inverse = codes[fg.at_face + 1].astype(F32).T[first:last, :]
    back = jnp.where(lane < fg.share, codes[fg.at_face + 1], -1)
    codes[fg.at_face + 1] = pltpu.roll(back, 1, 0)
    places = []
    for q in range(domains):
        block = jnp.broadcast_to(inverse[:, q : q + 1], (domains, LANES)).astype(I32)
        places.append(block * fg.block + lane)
    here = lax.axis_index("domain")
    narrow = lax.broadcasted_iota(I32, (domains, domains), 1)
    mine = jnp.sum(jnp.where(narrow == here, owners, 0.0), axis=1, keepdims=True)
    return places, jnp.broadcast_to(mine, (domains, LANES)).astype(I32), screens


def rows_of(values, index):
    return jnp.take_along_axis(values, index, axis=0, mode="promise_in_bounds")


def lookup(sources, code):
    lane = jnp.bitwise_and(code, LANES - 1)
    which = jnp.right_shift(code, 7)
    total = jnp.zeros(code.shape, F32)
    for b, values in sources:
        total = jnp.where(which == b, lanes_of(values, lane), total)
    return total


def field_source(fg, got_ref, places):
    domains = fg.domains
    density = []
    for g in range(fg.lines):
        total = got_tile(fg, got_ref, 0, g)
        for b in range(1, fg.bands):
            total = total + got_tile(fg, got_ref, b, g)
        density.append(total)
    lane = lax.broadcasted_iota(I32, (domains, LANES), 1)
    source = [None] * fg.lines
    for q in range(domains):
        spread = [jnp.broadcast_to(d[q : q + 1, :], (domains, LANES)) for d in density]
        block = lookup(list(enumerate(spread)), places[q])
        for row, start, j, offset, count in pieces(fg.block, domains):
            if j == q:
                moved = pltpu.roll(block, (start - offset) % LANES, 1)
                inside = (lane >= start) & (lane < start + count)
                before = 0.0 if source[row] is None else source[row]
                source[row] = jnp.where(inside, moved, before)
    return source


def field_solve(fg, source, codes, screen, high_ref, low_ref, rows, copies):
    domains, cells = fg.domains, fg.cells

    def operator(field):
        ahead = pltpu.roll(field[0], domains - 1, 0)
        local = list(field) + [lookup([(0, ahead)], codes[fg.at_face])]
        for r in range(fg.rows):
            for c in range(cells):
                sources = [(t, local[t]) for t in fg.touched[c]]
                rows[c * domains : (c + 1) * domains, r * LANES : (r + 1) * LANES] = lookup(sources, codes[c * fg.rows + r])
        picked = rows[:, 0 : fg.npc]
        high = picked.astype(BF)
        low = (picked - high.astype(F32)).astype(BF)
        both = dot(jnp.concatenate([high, low], axis=0), high_ref[...])
        half_rows = cells * domains
        if copies:
            copies.pop().wait()
        rows[:, 0 : fg.npc] = both[:half_rows] + (both[half_rows:] + dot(high, low_ref[...]))
        out = [None] * fg.tiles
        for c in range(cells):
            sources = [
                (r, rows[c * domains : (c + 1) * domains, r * LANES : (r + 1) * LANES])
                for r in range(fg.rows)
            ]
            for t in fg.touched[c]:
                term = lookup(sources, codes[fg.at_inverse + c * fg.tiles + t])
                out[t] = term if out[t] is None else out[t] + term
        arriving = pltpu.roll(out[fg.lines], 1, 0)
        out[0] = out[0] + lookup([(0, arriving)], codes[fg.at_face + 1])
        return [screen[g] * field[g] + out[g] for g in range(fg.lines)]

    step_one = [s * (1.0 / solve_center) for s in source]
    applied = operator(step_one)
    residual = [s - a for s, a in zip(source, applied)]
    a1, b1 = weight_one * weight_zero, 2.0 * weight_one / solve_half
    step_two = [a1 * e + b1 * r for e, r in zip(step_one, residual)]
    applied = operator(step_two)
    residual = [r - a for r, a in zip(residual, applied)]
    a2, b2 = weight_two * weight_one, 2.0 * weight_two / solve_half
    step_three = [a2 * e + b2 * r for e, r in zip(step_two, residual)]
    return [(x + y) + z for x, y, z in zip(step_one, step_two, step_three)]


def field_parts_kernel(fg, matrix_hbm, after_ref, top_ref, low_ref, matrix_ref, sems):
    del after_ref
    spans = [pl.ds(r * LANES, min(LANES, fg.npc - r * LANES)) for r in range(fg.rows)]
    copies = fetch([(matrix_hbm.at[span], matrix_ref.at[span]) for span in spans], sems)
    for r, copy in enumerate(copies):
        copy.wait()
        span = slice(r * LANES, min((r + 1) * LANES, fg.npc))
        full = matrix_ref[span, :]
        top = full.astype(BF)
        top_ref[span, :] = top
        low_ref[span, :] = (full - top.astype(F32)).astype(BF)


def field_parts(fg, matrix, after):
    hbm = pl.BlockSpec(memory_space=pltpu.HBM)
    return vmem_call(
        functools.partial(field_parts_kernel, fg),
        [sds(matrix.shape, BF), sds(matrix.shape, BF)],
        [
            pltpu.VMEM(matrix.shape, F32),
            pltpu.SemaphoreType.DMA((fg.rows,)),
        ],
        in_specs=[hbm, pl.BlockSpec(memory_space=pl.ANY)],
        cost=cost_of(2.5),
    )(*in_hbm(matrix), after)


def field_kernel(geo, fg, scale, got_ref, low_hbm, high_ref, base_ref, near_ref, far_ref, y_ref, *refs):
    n = len(geo.touching)
    crosses, reaches, refs = refs[:n], refs[n : 2 * n], refs[2 * n :]
    z_ref, near_out, far_out, column_ref, hartree_ref = refs[:5]
    codes, rows, mine, low_ref, sems = refs[5:]
    copies = fetch([(low_hbm, low_ref)], sems)
    z_ref[...] = base_ref[...]
    add_halo(geo, scale, z_ref, near_ref, far_ref, crosses)
    places, owner, screens = decode(fg, got_ref, codes)
    source = field_source(fg, got_ref, places)
    solved = field_solve(fg, source, codes, screens, high_ref, low_ref, rows, copies)
    lane = lax.broadcasted_iota(I32, (fg.domains, LANES), 1)
    block = lookup(list(enumerate(solved)), lane + lax.axis_index("domain") * fg.block)
    mine[...] = rows_of(block, owner)
    for j in range(fg.domains):
        at = slice(j * fg.block, (j + 1) * fg.block)
        column = column_of(mine[j : j + 1, :])[0 : fg.block, :]
        column_ref[at, :] = column
        z_ref[at, :] += (column * scale) * y_ref[at, :]
    write_sends(geo, z_ref, reaches, near_out, far_out)
    for row, start, j, offset, count in pieces(fg.block, fg.domains):
        hartree_ref[row : row + 1, start : start + count] = mine[j : j + 1, offset : offset + count]


def field_step(geo, fg, scale, got, top, rest, base, halo, y, crosses, reaches):
    tile = (fg.domains, LANES)
    vmem = pl.BlockSpec(memory_space=pltpu.VMEM)
    got = got.reshape(got.shape[0] * fg.width // LANES, LANES)
    args = [got, *in_hbm(rest), top, base, *halo, y, *crosses, *reaches]
    specs = [vmem] * len(args)
    specs[1] = pl.BlockSpec(memory_space=pltpu.HBM)
    z, near, far, column, lines = vmem_call(
        functools.partial(field_kernel, geo, fg, scale),
        [
            sds(y.shape, F32),
            *send_shapes(geo, y.shape[1]),
            sds((fg.own, LANES), F32),
            sds((fg.lines, LANES), F32),
        ],
        [
            pltpu.VMEM((2 * fg.at_screen, *tile), I32),
            pltpu.VMEM((fg.cells * fg.domains, fg.size), F32),
            pltpu.VMEM(tile, F32),
            pltpu.VMEM(rest.shape, BF),
            pltpu.SemaphoreType.DMA((1,)),
        ],
        in_specs=specs,
        cost=cost_of(4.0),
    )(*args)
    return z, (near, far), column, lines


def assembled(owned_rows, face_row, terms):
    owned_count = owned_rows.shape[0]
    shared = face_row.shape[0]
    coming = jnp.take(from_behind(owned_rows[:shared], "domain", -1), face_row, axis=0)
    partial_value = terms(jnp.concatenate([owned_rows, coming], axis=0))
    upper_rows = partial_value[owned_count:]
    ordered = jnp.zeros_like(upper_rows).at[face_row].set(upper_rows)
    arrived = from_behind(ordered, "domain", 1)
    return partial_value[:owned_count].at[:shared].add(arrived)


def field_terms(local_rows, pois_matrix, node_ids):
    cell_vals = jnp.take(local_rows, node_ids, axis=0)
    product = jnp.einsum(
        "pq,cq->cp",
        pois_matrix,
        cell_vals,
        precision=lax.Precision.HIGHEST,
        preferred_element_type=F32,
    )
    return jnp.zeros(local_rows.shape, F32).at[node_ids.reshape(-1)].add(product.reshape(-1))


def reshuffle(blocks):
    return lax.all_to_all(blocks, "domain", split_axis=0, concat_axis=0, tiled=True)


def distributed_field(y, occupation, owner_row, pois_matrix, pois_nodes, field_face, screening):
    owned_count = y.shape[0]
    domains = lax.axis_size("domain")
    block_len = owned_count // domains
    partial_value = jnp.dot(
        y * y, occupation, precision=lax.Precision.HIGHEST, preferred_element_type=F32
    )
    summed = lax.psum(partial_value, "band")
    arranged = (
        jnp.zeros((domains, block_len), F32)
        .at[owner_row]
        .set(summed.reshape(domains, block_len))
    )
    source = reshuffle(arranged).reshape(owned_count)

    def field_operator(vector):
        return (
            assembled(
                vector, field_face, lambda local: field_terms(local, pois_matrix, pois_nodes)
            )
            + screening * vector
        )

    step_one = source / solve_center
    residual = source - field_operator(step_one)
    step_two = weight_one * weight_zero * step_one + 2.0 * weight_one / solve_half * residual
    residual = residual - field_operator(step_two)
    step_three = weight_two * weight_one * step_two + 2.0 * weight_two / solve_half * residual
    solved = step_one + step_two + step_three
    returned = reshuffle(solved.reshape(domains, block_len))
    return jnp.take(returned, owner_row, axis=0).reshape(owned_count)


def exchange(sends):
    dn, up = sends
    h_dn = from_behind(dn, "domain", 1)
    h_up = from_behind(up, "domain", -1)
    return h_up, h_dn


def on_device(
    orbitals,
    potential,
    occupation,
    cell_matrix,
    cell_nodes,
    face_order,
    pois_matrix,
    pois_nodes,
    pois_face,
    screening,
    block_owner,
):
    domains = lax.axis_size("domain")
    bands = lax.axis_size("band")
    own, columns = orbitals.shape
    geo = Geometry(own, face_order.shape[1], cell_nodes.shape[0], cell_nodes.shape[1])
    fg = FieldGeometry(bands, domains, own, pois_face.shape[1], pois_nodes.shape[0], pois_nodes.shape[1])
    first, later = 1.0 / filter_half, 2.0 / filter_half

    others = [cell_matrix, potential.reshape(own // LANES, LANES)]
    if fg.fits:
        others += [pois_nodes, pois_face, block_owner, screening.reshape(own // LANES, LANES)]
        others.append(occupation.reshape(1, columns))
    sends, y0, nodes, (matrix, lines, *others) = pack(geo, orbitals, cell_nodes, face_order, *others)
    halo = exchange(sends)
    mats, crosses, reaches, pot = own_matrices(geo, nodes, matrix, lines)
    base = owned_part(geo, first, y0, None, pot, None, mats, ())
    uppers, base = behind_sums(geo, first, halo[1], matrix, base, sends[1])
    y1, sends1 = first_finish(geo, first, base, halo[0], crosses, reaches)

    halo = swap(sends1)
    base = owned_part(geo, later, y1, y0, pot, None, mats, uppers)
    if fg.fits:
        *others, weights = others
        table = field_tables(fg, *others, base)
    y2, *sends2 = finish(geo, later, base, halo, crosses, reaches)

    halo = swap(sends2)
    base = owned_part(geo, later, y2, y1, pot, None, mats, uppers)
    if fg.fits:
        y3, dn, up, spread = finish(
            geo, later, base, halo, crosses, reaches, density=(fg, weights, table)
        )
        dens = lax.all_to_all(spread, ("band", "domain"), 0, 0, tiled=True)
        halo = swap((dn, up))
        base = owned_part(geo, first, y3, None, pot, None, mats, uppers)
        top, rest = field_parts(fg, pois_matrix, base)
        z1, sends4, column, packed = field_step(
            geo, fg, first, dens, top, rest, base, halo, y3, crosses, reaches
        )
    else:
        y3, *sends3 = finish(geo, later, base, halo, crosses, reaches)
        halo = swap(sends3)
        hartree = distributed_field(
            y3, occupation, block_owner[0], pois_matrix, pois_nodes, pois_face[0], screening
        )
        column = jnp.broadcast_to(hartree[:, None], (own, LANES))
        base = owned_part(geo, first, y3, None, pot, column, mats, uppers)
        z1, *sends4 = finish(geo, first, base, halo, crosses, reaches)

    halo = swap(sends4)
    base = owned_part(geo, later, z1, y3, pot, column, mats, uppers, far=fg.fits)
    last = [packed] if fg.fits else []
    filtered, *rest = finish(geo, later, base, halo, crosses, last=last)
    if fg.fits:
        hartree = rest[0].reshape(own)
    return filtered, hartree


def swap(sends):
    length = lax.axis_size("domain")
    near, far = sends
    turns = [(i, (i + 1) % length if i % 2 else (i - 1) % length) for i in range(length)]
    far = lax.ppermute(far, "domain", turns)
    near = lax.ppermute(near, "domain", [(i, i ^ 1) for i in range(length)])
    return near, far


def solution(mesh):
    return jax.shard_map(
        on_device,
        mesh=mesh,
        in_specs=(
            P("domain", "band"),
            P("domain"),
            P("band"),
            P(),
            P("domain", None),
            P("domain", None),
            P(),
            P("domain", None),
            P("domain", None),
            P("domain"),
            P("domain", None),
        ),
        out_specs=(P("domain", "band"), P("domain")),
        check_vma=False,
    )
```

```python
import functools

import jax
import jax.numpy as jnp
from jax import lax
from jax.experimental import pallas as pl
from jax.experimental.pallas import tpu as pltpu
from jax.sharding import PartitionSpec as P

filter_center = 1.8
filter_half = 2.7
solve_center = 3.25
solve_half = 2.75
solve_ratio = solve_center / solve_half
weight_zero = 1.0 / solve_ratio
weight_one = 1.0 / (2.0 * solve_ratio - weight_zero)
weight_two = 1.0 / (2.0 * solve_ratio - weight_one)

BF = jnp.bfloat16
F32 = jnp.float32
I32 = jnp.int32
LANES = 128
SUBLANES = 8


def up_to(n, m):
    return -(-n // m) * m


def from_behind(array, axis, by):
    length = lax.axis_size(axis)
    return lax.ppermute(array, axis, [(i, (i + by) % length) for i in range(length)])


class Window:
    def __init__(self, start, npc, own, nloc):
        end = start + npc
        self.lo = start // 16 * 16
        self.hi = min(up_to(min(end, own), 16), own)
        self.touches = end > own
        self.low = up_to(max(0, end - nloc), 16)
        self.rows = self.hi - self.lo + self.low


class Geometry:
    def __init__(self, own, share, cells, npc):
        self.own, self.share, self.cells, self.npc = own, share, cells, npc
        nloc = own + share
        stride = nloc // cells
        self.sp = up_to(share, 16)
        self.npl = up_to(npc, LANES)
        self.windows = [Window(c * stride, npc, own, nloc) for c in range(cells)]
        self.touching = [c for c in range(cells) if self.windows[c].touches]
        self.dn_lo = min(self.windows[c].lo for c in self.touching)
        self.low = max(w.low for w in self.windows)
        self.dn_rows = own - self.dn_lo + self.low
        self.table_rows = up_to(cells, SUBLANES)
        self.table_lanes = up_to(npc, LANES)
        self.table_tiles = self.table_lanes // LANES


def dot(a, b):
    return lax.dot_general(a, b, (((1,), (0,)), ((), ())), preferred_element_type=F32)


def dot_t(a, b):
    return lax.dot_general(a, b, (((1,), (1,)), ((), ())), preferred_element_type=F32)


def vmem_call(kernel, out_shape, scratch=(), in_specs=None, out_specs=None, cost=None):
    kwargs = {}
    if in_specs is not None:
        kwargs["in_specs"] = in_specs
    if out_specs is not None:
        kwargs["out_specs"] = out_specs
    return pl.pallas_call(
        kernel,
        out_shape=out_shape,
        scratch_shapes=list(scratch),
        cost_estimate=cost,
        compiler_params=pltpu.CompilerParams(vmem_limit_bytes=12 * 1024 * 1024),
        **kwargs,
    )


def in_hbm(*arrays):
    return [pltpu.with_memory_space_constraint(a, pltpu.HBM) for a in arrays]


def sds(shape, dtype):
    return jax.ShapeDtypeStruct(shape, dtype)


def one_hot_rows(count, first, nodes):
    ids = lax.broadcasted_iota(I32, (count, nodes.shape[1]), 0) + first
    return jnp.where(ids == nodes, 1.0, 0.0).astype(BF)


def place_table(geo, nodes_ref, face_ref, table, faces):
    table[...] = jnp.full(table.shape, -1, I32)
    table[0 : geo.cells, 0 : geo.npc] = nodes_ref[...]
    faces[...] = jnp.zeros(faces.shape, I32)
    faces[0:1, 0 : geo.share] = face_ref[...]
    for t in range(geo.table_tiles):
        lanes = slice(t * LANES, (t + 1) * LANES)
        nodes = table[:, lanes]
        beyond = nodes - geo.own
        at = jnp.bitwise_and(beyond, LANES - 1)
        which = jnp.right_shift(beyond, 7)
        for f in range(faces.shape[1] // LANES):
            row = jnp.broadcast_to(faces[0:1, f * LANES : (f + 1) * LANES], nodes.shape)
            nodes = jnp.where(which == f, lanes_of(row, at) + geo.own, nodes)
        table[:, lanes] = nodes


def place_matrix(geo, matrix_ref, matrix_pad):
    matrix_pad[...] = jnp.zeros(matrix_pad.shape, F32)
    matrix_pad[0 : geo.npc, 0 : geo.npc] = matrix_ref[...].astype(F32)
    return matrix_pad[...].astype(BF)


def table_scratch(geo):
    return pltpu.VMEM((geo.table_rows, geo.table_lanes), I32)


def matrix_scratch(geo):
    return pltpu.VMEM((geo.npl, geo.npl), F32)


def nodes_of(geo, table, c):
    return table[c : c + 1, 0 : geo.npl]


def owned_picks(geo, c, nodes):
    w = geo.windows[c]
    picks = one_hot_rows(w.hi - w.lo, w.lo, nodes)
    if w.low:
        picks = jnp.concatenate([picks, one_hot_rows(w.low, 0, nodes)], axis=0)
    return picks


def upper_picks(geo, nodes):
    return one_hot_rows(geo.sp, geo.own, nodes)


def own_matrices_kernel(geo, *refs):
    table, matrix_ref, pot_ref = refs[:3]
    outs, matrix_pad = refs[3:-1], refs[-1]
    matrix = place_matrix(geo, matrix_ref, matrix_pad)
    for c in range(geo.cells):
        nodes = nodes_of(geo, table, c)
        own = owned_picks(geo, c, nodes)
        left = dot(own, matrix).astype(BF)
        outs[c][...] = dot_t(left, own).astype(BF)
        if c in geo.touching:
            at = geo.cells + geo.touching.index(c)
            upper = upper_picks(geo, nodes)
            outs[at][...] = dot_t(left, upper).astype(BF)
            left = dot(upper, matrix).astype(BF)
            outs[at + len(geo.touching)][...] = dot_t(left, own).astype(BF)
    column = outs[-1]
    for r in range(geo.own // LANES):
        row = jnp.broadcast_to(pot_ref[r : r + 1, :], (LANES, LANES))
        column[r * LANES : (r + 1) * LANES, :] = row.T


def own_matrices(geo, table, cell_matrix, lines):
    shapes = [sds((w.rows, w.rows), BF) for w in geo.windows]
    shapes += [sds((geo.windows[c].rows, geo.sp), BF) for c in geo.touching]
    shapes += [sds((geo.sp, geo.windows[c].rows), BF) for c in geo.touching]
    shapes += [sds((geo.own, LANES), F32)]
    outs = vmem_call(
        functools.partial(own_matrices_kernel, geo),
        shapes,
        [matrix_scratch(geo)],
        cost=cost_of(2.0),
    )(table, cell_matrix, lines)
    n, m = geo.cells, geo.cells + len(geo.touching)
    return outs[:n], outs[n:m], outs[m:-1], outs[-1]


def build_behind(geo, sent_ref, matrix_ref, table, matrix_pad, behinds, uppers):
    for t in range(geo.table_tiles):
        at = geo.dn_rows + 2 * t * geo.table_rows
        digits = sent_ref[at : at + 2 * geo.table_rows, :].astype(F32)
        value = digits[: geo.table_rows] * LANES + digits[geo.table_rows :] - 1.0
        table[:, t * LANES : (t + 1) * LANES] = value.astype(I32)
    matrix = place_matrix(geo, matrix_ref, matrix_pad)
    for at, c in enumerate(geo.touching):
        nodes = nodes_of(geo, table, c)
        upper = upper_picks(geo, nodes)
        left = dot(upper, matrix).astype(BF)
        behinds[at][...] = dot_t(left, owned_picks(geo, c, nodes)).astype(BF)
        uppers[at][...] = dot_t(left, upper).astype(BF)


def cost_of(us):
    return pl.CostEstimate(flops=0, bytes_accessed=int(us * 3.0e6), transcendentals=0)


def write_rows(geo, y_ref, dn_ref, up_ref):
    top = geo.own - geo.dn_lo
    dn_ref[0:top, :] = y_ref[geo.dn_lo : geo.own, :].astype(BF)
    dn_ref[top : top + geo.low, :] = y_ref[0 : geo.low, :].astype(BF)
    up_ref[...] = y_ref[0 : geo.sp, :].astype(BF)


def window_rows(geo, c, y_ref):
    w = geo.windows[c]
    rows = y_ref[w.lo : w.hi, :].astype(BF)
    if w.low:
        rows = jnp.concatenate([rows, y_ref[0 : w.low, :].astype(BF)], axis=0)
    return rows


def is_even():
    return jnp.bitwise_and(lax.axis_index("domain"), 1) == 0


def write_sends(geo, y_ref, reaches, near_ref, far_ref):
    total = None
    for at, c in enumerate(geo.touching):
        term = dot(reaches[at][...], window_rows(geo, c, y_ref))
        total = term if total is None else total + term
    rows = y_ref[0 : geo.sp, :]
    even = is_even()
    near_ref[...] = jnp.where(even, total, rows).astype(BF)
    far_ref[...] = jnp.where(even, rows, total).astype(BF)


def send_shapes(geo, columns):
    return [sds((geo.sp, columns), BF), sds((geo.sp, columns), BF)]


def fetch(pairs, sems):
    copies = [pltpu.make_async_copy(src, dst, sems.at[i]) for i, (src, dst) in enumerate(pairs)]
    for copy in copies:
        copy.start()
    return copies


def pack_kernel(geo, extra, y_hbm, nodes_hbm, face_hbm, *refs):
    sources, refs = refs[:extra], refs[extra:]
    dn_ref, up_ref, y, table = refs[:4]
    kept, (nodes, face, faces, sems) = refs[4 : 4 + extra], refs[4 + extra :]
    cuts = sorted({0, max(geo.sp, geo.low), geo.dn_lo, geo.own})
    spans = list(zip(cuts[:-1], cuts[1:]))
    pairs = [(nodes_hbm, nodes), (face_hbm, face)]
    pairs += [(y_hbm.at[pl.ds(a, b - a)], y.at[pl.ds(a, b - a)]) for a, b in spans]
    pairs += list(zip(sources, kept))
    copies = fetch(pairs, sems)
    copies[0].wait()
    copies[1].wait()
    place_table(geo, nodes, face, table, faces)
    for t in range(geo.table_tiles):
        at = geo.dn_rows + 2 * t * geo.table_rows
        value = table[:, t * LANES : (t + 1) * LANES] + 1
        high = jnp.right_shift(value, 7).astype(F32)
        low = jnp.bitwise_and(value, LANES - 1).astype(F32)
        digits = jnp.concatenate([high, low], axis=0).astype(BF)
        dn_ref[at : at + 2 * geo.table_rows, :] = digits
    for copy in copies[2:]:
        copy.wait()
    write_rows(geo, y, dn_ref, up_ref)


def pack(geo, y, cell_nodes, face_order, *others):
    up = sds((geo.sp, y.shape[1]), BF)
    rows = geo.dn_rows + 2 * geo.table_rows * geo.table_tiles
    dn, up, y, table, *others = vmem_call(
        functools.partial(pack_kernel, geo, len(others)),
        [
            sds((rows, y.shape[1]), BF),
            up,
            sds(y.shape, F32),
            sds((geo.table_rows, geo.table_lanes), I32),
            *[sds(a.shape, a.dtype) for a in others],
        ],
        [
            pltpu.VMEM(cell_nodes.shape, I32),
            pltpu.VMEM(face_order.shape, I32),
            pltpu.VMEM((1, up_to(geo.share, LANES)), I32),
            pltpu.SemaphoreType.DMA((5 + len(others),)),
        ],
        in_specs=[pl.BlockSpec(memory_space=pltpu.HBM)] * (3 + len(others)),
        cost=cost_of(1.0),
    )(*in_hbm(y, cell_nodes, face_order, *others))
    return (dn, up), y, table, others


def owned_part_kernel(geo, scale, has_prev, has_field, has_upper, far, *refs):
    refs = list(refs)
    if far:
        places, sems = refs[-2 - geo.cells : -1], refs[-1]
        refs = refs[: -2 - geo.cells]
    base_ref = refs.pop()
    y_ref = refs.pop(0)
    prev_ref = refs.pop(0) if has_prev else None
    pot_ref = refs.pop(0)
    field_ref = refs.pop(0) if has_field else None
    mats = [refs.pop(0) for _ in range(geo.cells)]
    if far:
        copies = fetch(list(zip([pot_ref, *mats], places)), sems)
        pot_ref, mats = places[0], places[1:]
        for copy in copies:
            copy.wait()
    y = y_ref[...]
    factor = pot_ref[...]
    if has_field:
        factor = factor + field_ref[...]
    value = ((factor - filter_center) * scale) * y
    if has_prev:
        value = value - prev_ref[...]
    base_ref[...] = value
    x = y.astype(BF)
    for c in range(geo.cells):
        w = geo.windows[c]
        own = w.hi - w.lo
        rows = x[w.lo : w.hi, :]
        if w.low:
            rows = jnp.concatenate([rows, x[0 : w.low, :]], axis=0)
        product = dot(mats[c][...], rows) * scale
        base_ref[w.lo : w.hi, :] += product[:own]
        if w.low:
            base_ref[0 : w.low, :] += product[own:]
    if has_upper:
        for upper in refs:
            base_ref[0 : geo.sp, :] += dot(upper[...], x[0 : geo.sp, :]) * scale


def owned_part(geo, scale, y, prev, pot, field, mats, uppers, far=False):
    vmem, hbm = pl.BlockSpec(memory_space=pltpu.VMEM), pl.BlockSpec(memory_space=pltpu.HBM)
    place, scratch = vmem, []
    if far:
        place = hbm
        scratch = [pltpu.VMEM(a.shape, a.dtype) for a in [pot, *mats]]
        scratch.append(pltpu.SemaphoreType.DMA((1 + len(mats),)))
        pot, *mats = in_hbm(pot, *mats)
    args = [y] + ([prev] if prev is not None else []) + [pot]
    args += [field] if field is not None else []
    args += list(mats) + list(uppers)
    specs = [vmem] * (2 if prev is not None else 1) + [place]
    specs += [vmem] * (0 if field is None else 1)
    specs += [place] * len(mats) + [vmem] * len(uppers)
    return vmem_call(
        functools.partial(
            owned_part_kernel, geo, scale, prev is not None, field is not None, bool(uppers), far
        ),
        sds(y.shape, F32),
        scratch,
        in_specs=specs,
        cost=cost_of(2.0),
    )(*args)


def add_upper(geo, scale, y_ref, h_up, crosses):
    for at, c in enumerate(geo.touching):
        w = geo.windows[c]
        own = w.hi - w.lo
        product = dot(crosses[at][...], h_up) * scale
        y_ref[w.lo : w.hi, :] += product[:own]
        if w.low:
            y_ref[0 : w.low, :] += product[own:]


def add_rows(geo, scale, y_ref, h_dn, behinds, uppers, own_up):
    total = None
    for at, c in enumerate(geo.touching):
        w = geo.windows[c]
        first = w.lo - geo.dn_lo
        term = dot(behinds[at][...], h_dn[first : first + w.rows, :])
        term = term + dot(uppers[at][...], own_up)
        total = term if total is None else total + term
    y_ref[0 : geo.sp, :] += total * scale


def add_halo(geo, scale, y_ref, near_ref, far_ref, crosses):
    near, far = near_ref[...].astype(F32), far_ref[...].astype(F32)
    even = is_even()
    y_ref[0 : geo.sp, :] += jnp.where(even, far, near) * scale
    add_upper(geo, scale, y_ref, jnp.where(even, near, far).astype(BF), crosses)


def write_tables(own, table_ref, part_rows, dens_ref):
    parts = dens_ref.shape[0]
    band = lax.axis_index("band")
    for r in range(part_rows):
        row = table_ref[band, r : r + 1, :]
        dens_ref[:, 0, own + r * LANES : own + (r + 1) * LANES] = jnp.broadcast_to(row, (parts, LANES))


def write_density(y_ref, occ_ref, dens_ref):
    parts = dens_ref.shape[0]
    own = y_ref.shape[0]
    y = y_ref[...]
    terms = y * y * occ_ref[...]
    high = terms.astype(BF)
    low = (terms - high.astype(F32)).astype(BF)
    ones = jnp.ones((SUBLANES, terms.shape[1]), BF)
    summed = dot_t(ones, high) + dot_t(ones, low)
    dens_ref[:, 0, 0:own] = jnp.broadcast_to(summed[0:1, :], (parts, own))


def behind_kernel(geo, scale, sent_ref, matrix_ref, base_ref, own_up_ref, *refs):
    n = len(geo.touching)
    uppers, out_ref, behinds, rest = refs[:n], refs[n], refs[n + 1 : 2 * n + 1], refs[2 * n + 1 :]
    build_behind(geo, sent_ref, matrix_ref, *rest, behinds, uppers)
    out_ref[...] = base_ref[...]
    add_rows(geo, scale, out_ref, sent_ref[...], behinds, uppers, own_up_ref[...])


def behind_sums(geo, scale, sent, matrix, base, own_up):
    *uppers, base = vmem_call(
        functools.partial(behind_kernel, geo, scale),
        [sds((geo.sp, geo.sp), BF) for _ in geo.touching] + [sds(base.shape, F32)],
        [
            *[pltpu.VMEM((geo.sp, geo.windows[c].rows), BF) for c in geo.touching],
            table_scratch(geo),
            matrix_scratch(geo),
        ],
        cost=cost_of(1.0),
    )(sent, matrix, base, own_up)
    return uppers, base


def first_finish_kernel(geo, scale, *refs):
    n = len(geo.touching)
    base_ref, up_ref = refs[:2]
    crosses, reaches = refs[2 : 2 + n], refs[2 + n : 2 + 2 * n]
    y_ref, near_out, far_out = refs[2 + 2 * n :]
    y_ref[...] = base_ref[...]
    add_upper(geo, scale, y_ref, up_ref[...], crosses)
    write_sends(geo, y_ref, reaches, near_out, far_out)


def first_finish(geo, scale, base, h_up, crosses, reaches):
    y, near, far = vmem_call(
        functools.partial(first_finish_kernel, geo, scale),
        [sds(base.shape, F32), *send_shapes(geo, base.shape[1])],
        cost=cost_of(0.5),
    )(base, h_up, *crosses, *reaches)
    return y, (near, far)


def finish_kernel(geo, scale, mode, part_rows, *refs):
    refs = list(refs)
    n = len(geo.touching)
    base_ref, near_ref, far_ref = refs[:3]
    refs = refs[3:]
    crosses, refs = refs[:n], refs[n:]
    halo = (near_ref, far_ref, crosses)
    if mode == "last":
        finish_last(geo, scale, base_ref, halo, *refs)
        return
    reaches, refs = refs[:n], refs[n:]
    if mode == "density":
        occ_ref, table_ref = refs.pop(0), refs.pop(0)
    y_ref = refs.pop(0)
    if mode == "density":
        _, _, out_hbm, dens, sems = refs
        spans = [pl.ds(geo.own, part_rows * LANES), pl.ds(0, geo.own)]
        copies = [
            pltpu.make_async_copy(dens.at[:, :, span], out_hbm.at[:, :, span], sems.at[i])
            for i, span in enumerate(spans)
        ]
        write_tables(geo.own, table_ref, part_rows, dens)
        copies[0].start()
    y_ref[...] = base_ref[...]
    add_halo(geo, scale, y_ref, *halo)
    if mode == "density":
        write_density(y_ref, occ_ref, dens)
        copies[1].start()
    write_sends(geo, y_ref, reaches, refs[0], refs[1])
    if mode == "density":
        for copy in copies:
            copy.wait()


def finish_last(geo, scale, base_ref, halo, *refs):
    extras = (len(refs) - 3) // 2
    sources, out_hbm, targets = refs[:extras], refs[extras], refs[extras + 1 : -2]
    y_ref, sems = refs[-2:]
    top = max(geo.sp, geo.low)
    inner = pl.ds(top, geo.dn_lo - top)
    copies = fetch([(base_ref.at[inner], out_hbm.at[inner]), *zip(sources, targets)], sems)
    edges = [(0, top), (geo.dn_lo, geo.own)]
    for a, b in edges:
        y_ref[a:b, :] = base_ref[a:b, :]
    add_halo(geo, scale, y_ref, *halo)
    for i, (a, b) in enumerate(edges):
        edge = pl.ds(a, b - a)
        copy = pltpu.make_async_copy(y_ref.at[edge], out_hbm.at[edge], sems.at[1 + extras + i])
        copy.start()
        copies.append(copy)
    for copy in copies:
        copy.wait()


def finish(geo, scale, base, halo, crosses, reaches=(), density=None, last=None):
    columns = base.shape[1]
    args = [base, halo[0], halo[1], *crosses, *reaches]
    mode, part_rows = "plain", 0
    shapes = [sds(base.shape, F32)]
    scratch = []
    vmem, hbm = pl.BlockSpec(memory_space=pltpu.VMEM), pl.BlockSpec(memory_space=pltpu.HBM)
    out_specs = [vmem, vmem, vmem]
    if last is not None:
        mode = "last"
        args += last
        shapes += [sds(a.shape, a.dtype) for a in last]
        out_specs = [hbm] * len(shapes)
        scratch = [pltpu.VMEM(base.shape, F32), pltpu.SemaphoreType.DMA((3 + len(last),))]
    else:
        shapes += send_shapes(geo, columns)
    if density is not None:
        mode = "density"
        fg, weights, table = density
        part_rows = fg.part_rows
        args += [weights, table]
        spread = (fg.bands * fg.domains, 1, fg.width)
        shapes.append(sds(spread, F32))
        out_specs.append(hbm)
        scratch = [pltpu.VMEM(spread, F32), pltpu.SemaphoreType.DMA((2,))]
    return vmem_call(
        functools.partial(finish_kernel, geo, scale, mode, part_rows),
        shapes,
        scratch,
        out_specs=out_specs,
        cost=cost_of(1.0),
    )(*args)


class FieldGeometry:
    def __init__(self, bands, domains, own, share, cells, npc):
        self.bands, self.domains, self.own, self.share = bands, domains, own, share
        self.cells, self.npc = cells, npc
        self.block = own // domains
        self.rows = up_to(npc, LANES) // LANES
        self.lines = own // LANES
        self.tiles = self.lines + 1
        nloc = own + share
        self.touched = []
        for c in range(cells):
            nodes = [(c * (nloc // cells) + k) % nloc for k in range(npc)]
            self.touched.append(sorted({node // LANES for node in nodes}))
        self.at_inverse = cells * self.rows
        self.at_face = self.at_inverse + cells * self.tiles
        self.at_screen = up_to(self.at_face + 2, 2) // 2
        self.part_rows = -(-(self.at_screen + self.lines) // bands)
        self.table_rows = up_to(self.part_rows * bands, SUBLANES)
        self.width = own + self.part_rows * LANES
        self.size = self.rows * LANES
        self.at_owner_lane = LANES - domains
        self.fits = (
            domains == SUBLANES
            and own % (domains * SUBLANES) == 0
            and own % LANES == 0
            and self.block <= LANES
            and share <= self.at_owner_lane
            and max(npc, nloc) < CODE_BASE - 1
        )


CODE_BASE = 2048
CODE_BITS = 11


def pieces(length, blocks):
    found = []
    for j in range(blocks):
        done = 0
        while done < length:
            at = j * length + done
            count = min(length - done, LANES - at % LANES)
            found.append((at // LANES, at % LANES, j, done, count))
            done += count
    return found


def column_of(row):
    return jnp.broadcast_to(row, (LANES, LANES)).T


def inverse_row(columns, first):
    sub = lax.broadcasted_iota(I32, (LANES, LANES), 0)
    target = (lax.broadcasted_iota(I32, (LANES, LANES), 1) + first).astype(F32)
    found = jnp.zeros((LANES, LANES), F32)
    for r, column in enumerate(columns):
        found = jnp.where(column == target, (sub + (r * LANES + 1)).astype(F32), found)
    return jnp.sum(found, axis=0, keepdims=True) - 1.0


def field_tables_kernel(fg, *refs):
    nodes_ref, face_ref, owner_ref, screen_ref = refs[:4]
    table_ref, pad, one, spare, packed = refs[5:]
    one[...] = jnp.full(one.shape, -1.0, F32)
    spare[...] = jnp.full(spare.shape, -1.0, F32)
    pad[...] = jnp.full(pad.shape, -1, I32)
    pad[0 : fg.cells, 0 : fg.npc] = nodes_ref[...]
    for c in range(fg.cells):
        columns = []
        for r in range(fg.rows):
            code = pad[c : c + 1, r * LANES : (r + 1) * LANES].astype(F32)
            one[c * fg.rows + r : c * fg.rows + r + 1, :] = code
            columns.append(column_of(code))
        for t in fg.touched[c]:
            at = fg.at_inverse + c * fg.tiles + t
            one[at : at + 1, :] = inverse_row(columns, t * LANES)
    lane = fg.at_owner_lane
    spare[0:1, 0 : fg.share] = face_ref[...].astype(F32)
    spare[1:2, 0 : fg.domains] = owner_ref[...].astype(F32)
    at = fg.at_face
    one[at : at + 1, :] = spare[0:1, :]
    one[at : at + 1, lane:LANES] = owner_ref[...].astype(F32)
    back = inverse_row([column_of(spare[0:1, :])], 0)
    home = inverse_row([column_of(spare[1:2, :])], -lane)
    lanes = lax.broadcasted_iota(I32, (1, LANES), 1)
    one[at + 1 : at + 2, :] = jnp.where(lanes < lane, back, home)
    packed[...] = jnp.zeros(packed.shape, F32)
    half = fg.at_screen
    packed[0:half, :] = (one[0:half, :] + 1.0) + (one[half : 2 * half, :] + 1.0) * CODE_BASE
    packed[half : half + fg.lines, :] = screen_ref[...]
    for b in range(fg.bands):
        table_ref[b, 0 : fg.part_rows, :] = packed[b * fg.part_rows : (b + 1) * fg.part_rows, :]


def field_tables(fg, pois_nodes, pois_face, block_owner, lines, after):
    specs = [pl.BlockSpec(memory_space=pltpu.VMEM)] * 4 + [pl.BlockSpec(memory_space=pl.ANY)]
    return vmem_call(
        functools.partial(field_tables_kernel, fg),
        sds((fg.bands, up_to(fg.part_rows, SUBLANES), LANES), F32),
        [
            pltpu.VMEM((up_to(fg.cells, SUBLANES), fg.size), I32),
            pltpu.VMEM((up_to(2 * fg.at_screen, SUBLANES), LANES), F32),
            pltpu.VMEM((SUBLANES, LANES), F32),
            pltpu.VMEM((fg.table_rows, LANES), F32),
        ],
        in_specs=specs,
        cost=cost_of(1.0),
    )(pois_nodes, pois_face, block_owner, lines, after)


def lanes_of(values, index):
    return jnp.take_along_axis(values, index, axis=1, mode="promise_in_bounds")


def got_tile(fg, got_ref, band, line):
    lines = fg.width // LANES
    return got_ref[pl.ds(band * fg.domains * lines + line, fg.domains, stride=lines), :]


def decode(fg, got_ref, codes):
    domains, half = fg.domains, fg.at_screen

    def tile(at):
        return got_tile(fg, got_ref, at // fg.part_rows, fg.lines + at % fg.part_rows)

    for at in range(half):
        both = tile(at).astype(I32)
        codes[at] = jnp.bitwise_and(both, CODE_BASE - 1) - 1
        codes[half + at] = jnp.right_shift(both, CODE_BITS) - 1
    screens = [tile(half + g) for g in range(fg.lines)]
    lane = lax.broadcasted_iota(I32, (domains, LANES), 1)
    first, last = fg.at_owner_lane, LANES
    owners = codes[fg.at_face].astype(F32).T[first:last, :]
    inverse = codes[fg.at_face + 1].astype(F32).T[first:last, :]
    back = jnp.where(lane < fg.share, codes[fg.at_face + 1], -1)
    codes[fg.at_face + 1] = pltpu.roll(back, 1, 0)
    places = []
    for q in range(domains):
        block = jnp.broadcast_to(inverse[:, q : q + 1], (domains, LANES)).astype(I32)
        places.append(block * fg.block + lane)
    here = lax.axis_index("domain")
    narrow = lax.broadcasted_iota(I32, (domains, domains), 1)
    mine = jnp.sum(jnp.where(narrow == here, owners, 0.0), axis=1, keepdims=True)
    return places, jnp.broadcast_to(mine, (domains, LANES)).astype(I32), screens


def rows_of(values, index):
    return jnp.take_along_axis(values, index, axis=0, mode="promise_in_bounds")


def lookup(sources, code):
    lane = jnp.bitwise_and(code, LANES - 1)
    which = jnp.right_shift(code, 7)
    total = jnp.zeros(code.shape, F32)
    for b, values in sources:
        total = jnp.where(which == b, lanes_of(values, lane), total)
    return total


def field_source(fg, got_ref, places):
    domains = fg.domains
    density = []
    for g in range(fg.lines):
        total = got_tile(fg, got_ref, 0, g)
        for b in range(1, fg.bands):
            total = total + got_tile(fg, got_ref, b, g)
        density.append(total)
    lane = lax.broadcasted_iota(I32, (domains, LANES), 1)
    source = [None] * fg.lines
    for q in range(domains):
        spread = [jnp.broadcast_to(d[q : q + 1, :], (domains, LANES)) for d in density]
        block = lookup(list(enumerate(spread)), places[q])
        for row, start, j, offset, count in pieces(fg.block, domains):
            if j == q:
                moved = pltpu.roll(block, (start - offset) % LANES, 1)
                inside = (lane >= start) & (lane < start + count)
                before = 0.0 if source[row] is None else source[row]
                source[row] = jnp.where(inside, moved, before)
    return source


def field_solve(fg, source, codes, screen, high_ref, low_ref, rows, copies):
    domains, cells = fg.domains, fg.cells

    def operator(field):
        ahead = pltpu.roll(field[0], domains - 1, 0)
        local = list(field) + [lookup([(0, ahead)], codes[fg.at_face])]
        for r in range(fg.rows):
            for c in range(cells):
                sources = [(t, local[t]) for t in fg.touched[c]]
                rows[c * domains : (c + 1) * domains, r * LANES : (r + 1) * LANES] = lookup(sources, codes[c * fg.rows + r])
        picked = rows[:, 0 : fg.npc]
        high = picked.astype(BF)
        low = (picked - high.astype(F32)).astype(BF)
        both = dot(jnp.concatenate([high, low], axis=0), high_ref[...])
        half_rows = cells * domains
        if copies:
            copies.pop().wait()
        rows[:, 0 : fg.npc] = both[:half_rows] + (both[half_rows:] + dot(high, low_ref[...]))
        out = [None] * fg.tiles
        for c in range(cells):
            sources = [
                (r, rows[c * domains : (c + 1) * domains, r * LANES : (r + 1) * LANES])
                for r in range(fg.rows)
            ]
            for t in fg.touched[c]:
                term = lookup(sources, codes[fg.at_inverse + c * fg.tiles + t])
                out[t] = term if out[t] is None else out[t] + term
        arriving = pltpu.roll(out[fg.lines], 1, 0)
        out[0] = out[0] + lookup([(0, arriving)], codes[fg.at_face + 1])
        return [screen[g] * field[g] + out[g] for g in range(fg.lines)]

    step_one = [s * (1.0 / solve_center) for s in source]
    applied = operator(step_one)
    residual = [s - a for s, a in zip(source, applied)]
    a1, b1 = weight_one * weight_zero, 2.0 * weight_one / solve_half
    step_two = [a1 * e + b1 * r for e, r in zip(step_one, residual)]
    applied = operator(step_two)
    residual = [r - a for r, a in zip(residual, applied)]
    a2, b2 = weight_two * weight_one, 2.0 * weight_two / solve_half
    step_three = [a2 * e + b2 * r for e, r in zip(step_two, residual)]
    return [(x + y) + z for x, y, z in zip(step_one, step_two, step_three)]


def field_parts_kernel(fg, matrix_hbm, after_ref, top_ref, low_ref, matrix_ref, sems):
    del after_ref
    spans = [pl.ds(r * LANES, min(LANES, fg.npc - r * LANES)) for r in range(fg.rows)]
    copies = fetch([(matrix_hbm.at[span], matrix_ref.at[span]) for span in spans], sems)
    for r, copy in enumerate(copies):
        copy.wait()
        span = slice(r * LANES, min((r + 1) * LANES, fg.npc))
        full = matrix_ref[span, :]
        top = full.astype(BF)
        top_ref[span, :] = top
        low_ref[span, :] = (full - top.astype(F32)).astype(BF)


def field_parts(fg, matrix, after):
    hbm = pl.BlockSpec(memory_space=pltpu.HBM)
    return vmem_call(
        functools.partial(field_parts_kernel, fg),
        [sds(matrix.shape, BF), sds(matrix.shape, BF)],
        [
            pltpu.VMEM(matrix.shape, F32),
            pltpu.SemaphoreType.DMA((fg.rows,)),
        ],
        in_specs=[hbm, pl.BlockSpec(memory_space=pl.ANY)],
        cost=cost_of(2.5),
    )(*in_hbm(matrix), after)


def field_kernel(geo, fg, scale, got_ref, low_hbm, high_ref, base_ref, near_ref, far_ref, y_ref, *refs):
    n = len(geo.touching)
    crosses, reaches, refs = refs[:n], refs[n : 2 * n], refs[2 * n :]
    z_ref, near_out, far_out, column_ref, hartree_ref = refs[:5]
    codes, rows, mine, low_ref, sems = refs[5:]
    copies = fetch([(low_hbm, low_ref)], sems)
    z_ref[...] = base_ref[...]
    add_halo(geo, scale, z_ref, near_ref, far_ref, crosses)
    places, owner, screens = decode(fg, got_ref, codes)
    source = field_source(fg, got_ref, places)
    solved = field_solve(fg, source, codes, screens, high_ref, low_ref, rows, copies)
    lane = lax.broadcasted_iota(I32, (fg.domains, LANES), 1)
    block = lookup(list(enumerate(solved)), lane + lax.axis_index("domain") * fg.block)
    mine[...] = rows_of(block, owner)
    for j in range(fg.domains):
        at = slice(j * fg.block, (j + 1) * fg.block)
        column = column_of(mine[j : j + 1, :])[0 : fg.block, :]
        column_ref[at, :] = column
        z_ref[at, :] += (column * scale) * y_ref[at, :]
    write_sends(geo, z_ref, reaches, near_out, far_out)
    for row, start, j, offset, count in pieces(fg.block, fg.domains):
        hartree_ref[row : row + 1, start : start + count] = mine[j : j + 1, offset : offset + count]


def field_step(geo, fg, scale, got, top, rest, base, halo, y, crosses, reaches):
    tile = (fg.domains, LANES)
    vmem = pl.BlockSpec(memory_space=pltpu.VMEM)
    got = got.reshape(got.shape[0] * fg.width // LANES, LANES)
    args = [got, *in_hbm(rest), top, base, *halo, y, *crosses, *reaches]
    specs = [vmem] * len(args)
    specs[1] = pl.BlockSpec(memory_space=pltpu.HBM)
    z, near, far, column, lines = vmem_call(
        functools.partial(field_kernel, geo, fg, scale),
        [
            sds(y.shape, F32),
            *send_shapes(geo, y.shape[1]),
            sds((fg.own, LANES), F32),
            sds((fg.lines, LANES), F32),
        ],
        [
            pltpu.VMEM((2 * fg.at_screen, *tile), I32),
            pltpu.VMEM((fg.cells * fg.domains, fg.size), F32),
            pltpu.VMEM(tile, F32),
            pltpu.VMEM(rest.shape, BF),
            pltpu.SemaphoreType.DMA((1,)),
        ],
        in_specs=specs,
        cost=cost_of(4.0),
    )(*args)
    return z, (near, far), column, lines


def assembled(owned_rows, face_row, terms):
    owned_count = owned_rows.shape[0]
    shared = face_row.shape[0]
    coming = jnp.take(from_behind(owned_rows[:shared], "domain", -1), face_row, axis=0)
    partial_value = terms(jnp.concatenate([owned_rows, coming], axis=0))
    upper_rows = partial_value[owned_count:]
    ordered = jnp.zeros_like(upper_rows).at[face_row].set(upper_rows)
    arrived = from_behind(ordered, "domain", 1)
    return partial_value[:owned_count].at[:shared].add(arrived)


def field_terms(local_rows, pois_matrix, node_ids):
    cell_vals = jnp.take(local_rows, node_ids, axis=0)
    product = jnp.einsum(
        "pq,cq->cp",
        pois_matrix,
        cell_vals,
        precision=lax.Precision.HIGHEST,
        preferred_element_type=F32,
    )
    return jnp.zeros(local_rows.shape, F32).at[node_ids.reshape(-1)].add(product.reshape(-1))


def reshuffle(blocks):
    return lax.all_to_all(blocks, "domain", split_axis=0, concat_axis=0, tiled=True)


def distributed_field(y, occupation, owner_row, pois_matrix, pois_nodes, field_face, screening):
    owned_count = y.shape[0]
    domains = lax.axis_size("domain")
    block_len = owned_count // domains
    partial_value = jnp.dot(
        y * y, occupation, precision=lax.Precision.HIGHEST, preferred_element_type=F32
    )
    summed = lax.psum(partial_value, "band")
    arranged = (
        jnp.zeros((domains, block_len), F32)
        .at[owner_row]
        .set(summed.reshape(domains, block_len))
    )
    source = reshuffle(arranged).reshape(owned_count)

    def field_operator(vector):
        return (
            assembled(
                vector, field_face, lambda local: field_terms(local, pois_matrix, pois_nodes)
            )
            + screening * vector
        )

    step_one = source / solve_center
    residual = source - field_operator(step_one)
    step_two = weight_one * weight_zero * step_one + 2.0 * weight_one / solve_half * residual
    residual = residual - field_operator(step_two)
    step_three = weight_two * weight_one * step_two + 2.0 * weight_two / solve_half * residual
    solved = step_one + step_two + step_three
    returned = reshuffle(solved.reshape(domains, block_len))
    return jnp.take(returned, owner_row, axis=0).reshape(owned_count)


def exchange(sends):
    dn, up = sends
    h_dn = from_behind(dn, "domain", 1)
    h_up = from_behind(up, "domain", -1)
    return h_up, h_dn


def on_device(
    orbitals,
    potential,
    occupation,
    cell_matrix,
    cell_nodes,
    face_order,
    pois_matrix,
    pois_nodes,
    pois_face,
    screening,
    block_owner,
):
    domains = lax.axis_size("domain")
    bands = lax.axis_size("band")
    own, columns = orbitals.shape
    geo = Geometry(own, face_order.shape[1], cell_nodes.shape[0], cell_nodes.shape[1])
    fg = FieldGeometry(bands, domains, own, pois_face.shape[1], pois_nodes.shape[0], pois_nodes.shape[1])
    first, later = 1.0 / filter_half, 2.0 / filter_half

    others = [cell_matrix, potential.reshape(own // LANES, LANES)]
    if fg.fits:
        others += [pois_nodes, pois_face, block_owner, screening.reshape(own // LANES, LANES)]
        others.append(occupation.reshape(1, columns))
    sends, y0, nodes, (matrix, lines, *others) = pack(geo, orbitals, cell_nodes, face_order, *others)
    halo = exchange(sends)
    mats, crosses, reaches, pot = own_matrices(geo, nodes, matrix, lines)
    base = owned_part(geo, first, y0, None, pot, None, mats, ())
    uppers, base = behind_sums(geo, first, halo[1], matrix, base, sends[1])
    y1, sends1 = first_finish(geo, first, base, halo[0], crosses, reaches)

    halo = swap(sends1)
    base = owned_part(geo, later, y1, y0, pot, None, mats, uppers)
    if fg.fits:
        *others, weights = others
        table = field_tables(fg, *others, base)
    y2, *sends2 = finish(geo, later, base, halo, crosses, reaches)

    halo = swap(sends2)
    base = owned_part(geo, later, y2, y1, pot, None, mats, uppers)
    if fg.fits:
        y3, dn, up, spread = finish(
            geo, later, base, halo, crosses, reaches, density=(fg, weights, table)
        )
        dens = lax.all_to_all(spread, ("band", "domain"), 0, 0, tiled=True)
        halo = swap((dn, up))
        base = owned_part(geo, first, y3, None, pot, None, mats, uppers)
        top, rest = field_parts(fg, pois_matrix, base)
        z1, sends4, column, packed = field_step(
            geo, fg, first, dens, top, rest, base, halo, y3, crosses, reaches
        )
    else:
        y3, *sends3 = finish(geo, later, base, halo, crosses, reaches)
        halo = swap(sends3)
        hartree = distributed_field(
            y3, occupation, block_owner[0], pois_matrix, pois_nodes, pois_face[0], screening
        )
        column = jnp.broadcast_to(hartree[:, None], (own, LANES))
        base = owned_part(geo, first, y3, None, pot, column, mats, uppers)
        z1, *sends4 = finish(geo, first, base, halo, crosses, reaches)

    halo = swap(sends4)
    base = owned_part(geo, later, z1, y3, pot, column, mats, uppers, far=fg.fits)
    last = [packed] if fg.fits else []
    filtered, *rest = finish(geo, later, base, halo, crosses, last=last)
    if fg.fits:
        hartree = rest[0].reshape(own)
    return filtered, hartree


def swap(sends):
    length = lax.axis_size("domain")
    near, far = sends
    turns = [(i, (i + 1) % length if i % 2 else (i - 1) % length) for i in range(length)]
    far = lax.ppermute(far, "domain", turns)
    near = lax.ppermute(near, "domain", [(i, i ^ 1) for i in range(length)])
    return near, far


def solution(mesh):
    return jax.shard_map(
        on_device,
        mesh=mesh,
        in_specs=(
            P("domain", "band"),
            P("domain"),
            P("band"),
            P(),
            P("domain", None),
            P("domain", None),
            P(),
            P("domain", None),
            P("domain", None),
            P("domain"),
            P("domain", None),
        ),
        out_specs=(P("domain", "band"), P("domain")),
        check_vma=False,
    )
```

```python
import functools

import jax
import jax.numpy as jnp
from jax import lax
from jax.experimental import pallas as pl
from jax.experimental.pallas import tpu as pltpu
from jax.sharding import PartitionSpec as P

filter_center = 1.8
filter_half = 2.7
solve_center = 3.25
solve_half = 2.75
solve_ratio = solve_center / solve_half
weight_zero = 1.0 / solve_ratio
weight_one = 1.0 / (2.0 * solve_ratio - weight_zero)
weight_two = 1.0 / (2.0 * solve_ratio - weight_one)

BF = jnp.bfloat16
F32 = jnp.float32
I32 = jnp.int32
LANES = 128
SUBLANES = 8


def up_to(n, m):
    return -(-n // m) * m


def from_behind(array, axis, by):
    length = lax.axis_size(axis)
    return lax.ppermute(array, axis, [(i, (i + by) % length) for i in range(length)])


class Window:
    def __init__(self, start, npc, own, nloc):
        end = start + npc
        self.lo = start // 16 * 16
        self.hi = min(up_to(min(end, own), 16), own)
        self.touches = end > own
        self.low = up_to(max(0, end - nloc), 16)
        self.rows = self.hi - self.lo + self.low


class Geometry:
    def __init__(self, own, share, cells, npc):
        self.own, self.share, self.cells, self.npc = own, share, cells, npc
        nloc = own + share
        stride = nloc // cells
        self.sp = up_to(share, 16)
        self.npl = up_to(npc, LANES)
        self.windows = [Window(c * stride, npc, own, nloc) for c in range(cells)]
        self.touching = [c for c in range(cells) if self.windows[c].touches]
        self.dn_lo = min(self.windows[c].lo for c in self.touching)
        self.low = max(w.low for w in self.windows)
        self.dn_rows = own - self.dn_lo + self.low
        self.table_rows = up_to(cells, SUBLANES)
        self.table_lanes = up_to(npc, LANES)
        self.table_tiles = self.table_lanes // LANES


def dot(a, b):
    return lax.dot_general(a, b, (((1,), (0,)), ((), ())), preferred_element_type=F32)


def dot_t(a, b):
    return lax.dot_general(a, b, (((1,), (1,)), ((), ())), preferred_element_type=F32)


def vmem_call(kernel, out_shape, scratch=(), in_specs=None, out_specs=None, cost=None):
    kwargs = {}
    if in_specs is not None:
        kwargs["in_specs"] = in_specs
    if out_specs is not None:
        kwargs["out_specs"] = out_specs
    return pl.pallas_call(
        kernel,
        out_shape=out_shape,
        scratch_shapes=list(scratch),
        cost_estimate=cost,
        compiler_params=pltpu.CompilerParams(vmem_limit_bytes=12 * 1024 * 1024),
        **kwargs,
    )


def in_hbm(*arrays):
    return [pltpu.with_memory_space_constraint(a, pltpu.HBM) for a in arrays]


def sds(shape, dtype):
    return jax.ShapeDtypeStruct(shape, dtype)


def one_hot_rows(count, first, nodes):
    ids = lax.broadcasted_iota(I32, (count, nodes.shape[1]), 0) + first
    return jnp.where(ids == nodes, 1.0, 0.0).astype(BF)


def place_table(geo, nodes_ref, face_ref, table, faces):
    table[...] = jnp.full(table.shape, -1, I32)
    table[0 : geo.cells, 0 : geo.npc] = nodes_ref[...]
    faces[...] = jnp.zeros(faces.shape, I32)
    faces[0:1, 0 : geo.share] = face_ref[...]
    for t in range(geo.table_tiles):
        lanes = slice(t * LANES, (t + 1) * LANES)
        nodes = table[:, lanes]
        beyond = nodes - geo.own
        at = jnp.bitwise_and(beyond, LANES - 1)
        which = jnp.right_shift(beyond, 7)
        for f in range(faces.shape[1] // LANES):
            row = jnp.broadcast_to(faces[0:1, f * LANES : (f + 1) * LANES], nodes.shape)
            nodes = jnp.where(which == f, lanes_of(row, at) + geo.own, nodes)
        table[:, lanes] = nodes


def place_matrix(geo, matrix_ref, matrix_pad):
    matrix_pad[...] = jnp.zeros(matrix_pad.shape, F32)
    matrix_pad[0 : geo.npc, 0 : geo.npc] = matrix_ref[...].astype(F32)
    return matrix_pad[...].astype(BF)


def table_scratch(geo):
    return pltpu.VMEM((geo.table_rows, geo.table_lanes), I32)


def matrix_scratch(geo):
    return pltpu.VMEM((geo.npl, geo.npl), F32)


def nodes_of(geo, table, c):
    return table[c : c + 1, 0 : geo.npl]


def owned_picks(geo, c, nodes):
    w = geo.windows[c]
    picks = one_hot_rows(w.hi - w.lo, w.lo, nodes)
    if w.low:
        picks = jnp.concatenate([picks, one_hot_rows(w.low, 0, nodes)], axis=0)
    return picks


def upper_picks(geo, nodes):
    return one_hot_rows(geo.sp, geo.own, nodes)


def own_matrices_kernel(geo, *refs):
    table, matrix_ref, pot_ref = refs[:3]
    outs, matrix_pad = refs[3:-1], refs[-1]
    matrix = place_matrix(geo, matrix_ref, matrix_pad)
    for c in range(geo.cells):
        nodes = nodes_of(geo, table, c)
        own = owned_picks(geo, c, nodes)
        left = dot(own, matrix).astype(BF)
        outs[c][...] = dot_t(left, own).astype(BF)
        if c in geo.touching:
            at = geo.cells + geo.touching.index(c)
            upper = upper_picks(geo, nodes)
            outs[at][...] = dot_t(left, upper).astype(BF)
            left = dot(upper, matrix).astype(BF)
            outs[at + len(geo.touching)][...] = dot_t(left, own).astype(BF)
    column = outs[-1]
    for r in range(geo.own // LANES):
        row = jnp.broadcast_to(pot_ref[r : r + 1, :], (LANES, LANES))
        column[r * LANES : (r + 1) * LANES, :] = row.T


def own_matrices(geo, table, cell_matrix, lines):
    shapes = [sds((w.rows, w.rows), BF) for w in geo.windows]
    shapes += [sds((geo.windows[c].rows, geo.sp), BF) for c in geo.touching]
    shapes += [sds((geo.sp, geo.windows[c].rows), BF) for c in geo.touching]
    shapes += [sds((geo.own, LANES), F32)]
    outs = vmem_call(
        functools.partial(own_matrices_kernel, geo),
        shapes,
        [matrix_scratch(geo)],
        cost=cost_of(2.0),
    )(table, cell_matrix, lines)
    n, m = geo.cells, geo.cells + len(geo.touching)
    return outs[:n], outs[n:m], outs[m:-1], outs[-1]


def build_behind(geo, sent_ref, matrix_ref, table, matrix_pad, behinds, uppers):
    for t in range(geo.table_tiles):
        at = geo.dn_rows + 2 * t * geo.table_rows
        digits = sent_ref[at : at + 2 * geo.table_rows, :].astype(F32)
        value = digits[: geo.table_rows] * LANES + digits[geo.table_rows :] - 1.0
        table[:, t * LANES : (t + 1) * LANES] = value.astype(I32)
    matrix = place_matrix(geo, matrix_ref, matrix_pad)
    for at, c in enumerate(geo.touching):
        nodes = nodes_of(geo, table, c)
        upper = upper_picks(geo, nodes)
        left = dot(upper, matrix).astype(BF)
        behinds[at][...] = dot_t(left, owned_picks(geo, c, nodes)).astype(BF)
        uppers[at][...] = dot_t(left, upper).astype(BF)


def cost_of(us):
    return pl.CostEstimate(flops=0, bytes_accessed=int(us * 3.0e6), transcendentals=0)


def write_rows(geo, y_ref, dn_ref, up_ref):
    top = geo.own - geo.dn_lo
    dn_ref[0:top, :] = y_ref[geo.dn_lo : geo.own, :].astype(BF)
    dn_ref[top : top + geo.low, :] = y_ref[0 : geo.low, :].astype(BF)
    up_ref[...] = y_ref[0 : geo.sp, :].astype(BF)


def window_rows(geo, c, y_ref):
    w = geo.windows[c]
    rows = y_ref[w.lo : w.hi, :].astype(BF)
    if w.low:
        rows = jnp.concatenate([rows, y_ref[0 : w.low, :].astype(BF)], axis=0)
    return rows


def is_even():
    return jnp.bitwise_and(lax.axis_index("domain"), 1) == 0


def write_sends(geo, y_ref, reaches, near_ref, far_ref):
    total = None
    for at, c in enumerate(geo.touching):
        term = dot(reaches[at][...], window_rows(geo, c, y_ref))
        total = term if total is None else total + term
    rows = y_ref[0 : geo.sp, :]
    even = is_even()
    near_ref[...] = jnp.where(even, total, rows).astype(BF)
    far_ref[...] = jnp.where(even, rows, total).astype(BF)


def send_shapes(geo, columns):
    return [sds((geo.sp, columns), BF), sds((geo.sp, columns), BF)]


def fetch(pairs, sems):
    copies = [pltpu.make_async_copy(src, dst, sems.at[i]) for i, (src, dst) in enumerate(pairs)]
    for copy in copies:
        copy.start()
    return copies


def pack_kernel(geo, extra, y_hbm, nodes_hbm, face_hbm, *refs):
    sources, refs = refs[:extra], refs[extra:]
    dn_ref, up_ref, y, table = refs[:4]
    kept, (nodes, face, faces, sems) = refs[4 : 4 + extra], refs[4 + extra :]
    cuts = sorted({0, max(geo.sp, geo.low), geo.dn_lo, geo.own})
    spans = list(zip(cuts[:-1], cuts[1:]))
    pairs = [(y_hbm.at[pl.ds(a, b - a)], y.at[pl.ds(a, b - a)]) for a, b in spans]
    pairs += [(nodes_hbm, nodes), (face_hbm, face)]
    pairs += list(zip(sources, kept))
    copies = fetch(pairs, sems)
    first = len(spans)
    for copy in copies[:first]:
        copy.wait()
    write_rows(geo, y, dn_ref, up_ref)
    for copy in copies[first : first + 2]:
        copy.wait()
    place_table(geo, nodes, face, table, faces)
    for t in range(geo.table_tiles):
        at = geo.dn_rows + 2 * t * geo.table_rows
        value = table[:, t * LANES : (t + 1) * LANES] + 1
        high = jnp.right_shift(value, 7).astype(F32)
        low = jnp.bitwise_and(value, LANES - 1).astype(F32)
        digits = jnp.concatenate([high, low], axis=0).astype(BF)
        dn_ref[at : at + 2 * geo.table_rows, :] = digits
    for copy in copies[first + 2 :]:
        copy.wait()


def pack(geo, y, cell_nodes, face_order, *others):
    up = sds((geo.sp, y.shape[1]), BF)
    rows = geo.dn_rows + 2 * geo.table_rows * geo.table_tiles
    dn, up, y, table, *others = vmem_call(
        functools.partial(pack_kernel, geo, len(others)),
        [
            sds((rows, y.shape[1]), BF),
            up,
            sds(y.shape, F32),
            sds((geo.table_rows, geo.table_lanes), I32),
            *[sds(a.shape, a.dtype) for a in others],
        ],
        [
            pltpu.VMEM(cell_nodes.shape, I32),
            pltpu.VMEM(face_order.shape, I32),
            pltpu.VMEM((1, up_to(geo.share, LANES)), I32),
            pltpu.SemaphoreType.DMA((5 + len(others),)),
        ],
        in_specs=[pl.BlockSpec(memory_space=pltpu.HBM)] * (3 + len(others)),
        cost=cost_of(1.0),
    )(*in_hbm(y, cell_nodes, face_order, *others))
    return (dn, up), y, table, others


def owned_part_kernel(geo, scale, has_prev, has_field, has_upper, far, *refs):
    refs = list(refs)
    if far:
        places, sems = refs[-2 - geo.cells : -1], refs[-1]
        refs = refs[: -2 - geo.cells]
    base_ref = refs.pop()
    y_ref = refs.pop(0)
    prev_ref = refs.pop(0) if has_prev else None
    pot_ref = refs.pop(0)
    field_ref = refs.pop(0) if has_field else None
    mats = [refs.pop(0) for _ in range(geo.cells)]
    if far:
        copies = fetch(list(zip([pot_ref, *mats], places)), sems)
        pot_ref, mats = places[0], places[1:]
        for copy in copies:
            copy.wait()
    y = y_ref[...]
    factor = pot_ref[...]
    if has_field:
        factor = factor + field_ref[...]
    value = ((factor - filter_center) * scale) * y
    if has_prev:
        value = value - prev_ref[...]
    base_ref[...] = value
    x = y.astype(BF)
    for c in range(geo.cells):
        w = geo.windows[c]
        own = w.hi - w.lo
        rows = x[w.lo : w.hi, :]
        if w.low:
            rows = jnp.concatenate([rows, x[0 : w.low, :]], axis=0)
        product = dot(mats[c][...], rows) * scale
        base_ref[w.lo : w.hi, :] += product[:own]
        if w.low:
            base_ref[0 : w.low, :] += product[own:]
    if has_upper:
        for upper in refs:
            base_ref[0 : geo.sp, :] += dot(upper[...], x[0 : geo.sp, :]) * scale


def owned_part(geo, scale, y, prev, pot, field, mats, uppers, far=False):
    vmem, hbm = pl.BlockSpec(memory_space=pltpu.VMEM), pl.BlockSpec(memory_space=pltpu.HBM)
    place, scratch = vmem, []
    if far:
        place = hbm
        scratch = [pltpu.VMEM(a.shape, a.dtype) for a in [pot, *mats]]
        scratch.append(pltpu.SemaphoreType.DMA((1 + len(mats),)))
        pot, *mats = in_hbm(pot, *mats)
    args = [y] + ([prev] if prev is not None else []) + [pot]
    args += [field] if field is not None else []
    args += list(mats) + list(uppers)
    specs = [vmem] * (2 if prev is not None else 1) + [place]
    specs += [vmem] * (0 if field is None else 1)
    specs += [place] * len(mats) + [vmem] * len(uppers)
    return vmem_call(
        functools.partial(
            owned_part_kernel, geo, scale, prev is not None, field is not None, bool(uppers), far
        ),
        sds(y.shape, F32),
        scratch,
        in_specs=specs,
        cost=cost_of(2.0),
    )(*args)


def add_upper(geo, scale, y_ref, h_up, crosses):
    for at, c in enumerate(geo.touching):
        w = geo.windows[c]
        own = w.hi - w.lo
        product = dot(crosses[at][...], h_up) * scale
        y_ref[w.lo : w.hi, :] += product[:own]
        if w.low:
            y_ref[0 : w.low, :] += product[own:]


def add_rows(geo, scale, y_ref, h_dn, behinds, uppers, own_up):
    total = None
    for at, c in enumerate(geo.touching):
        w = geo.windows[c]
        first = w.lo - geo.dn_lo
        term = dot(behinds[at][...], h_dn[first : first + w.rows, :])
        term = term + dot(uppers[at][...], own_up)
        total = term if total is None else total + term
    y_ref[0 : geo.sp, :] += total * scale


def add_halo(geo, scale, y_ref, near_ref, far_ref, crosses):
    near, far = near_ref[...].astype(F32), far_ref[...].astype(F32)
    even = is_even()
    y_ref[0 : geo.sp, :] += jnp.where(even, far, near) * scale
    add_upper(geo, scale, y_ref, jnp.where(even, near, far).astype(BF), crosses)


def write_tables(own, table_ref, part_rows, dens_ref):
    parts = dens_ref.shape[0]
    band = lax.axis_index("band")
    for r in range(part_rows):
        row = table_ref[band, r : r + 1, :]
        dens_ref[:, 0, own + r * LANES : own + (r + 1) * LANES] = jnp.broadcast_to(row, (parts, LANES))


def write_density(y_ref, occ_ref, dens_ref):
    parts = dens_ref.shape[0]
    own = y_ref.shape[0]
    y = y_ref[...]
    terms = y * y * occ_ref[...]
    high = terms.astype(BF)
    low = (terms - high.astype(F32)).astype(BF)
    ones = jnp.ones((SUBLANES, terms.shape[1]), BF)
    summed = dot_t(ones, high) + dot_t(ones, low)
    dens_ref[:, 0, 0:own] = jnp.broadcast_to(summed[0:1, :], (parts, own))


def behind_kernel(geo, scale, sent_ref, matrix_ref, base_ref, own_up_ref, *refs):
    n = len(geo.touching)
    uppers, out_ref, behinds, rest = refs[:n], refs[n], refs[n + 1 : 2 * n + 1], refs[2 * n + 1 :]
    build_behind(geo, sent_ref, matrix_ref, *rest, behinds, uppers)
    out_ref[...] = base_ref[...]
    add_rows(geo, scale, out_ref, sent_ref[...], behinds, uppers, own_up_ref[...])


def behind_sums(geo, scale, sent, matrix, base, own_up):
    *uppers, base = vmem_call(
        functools.partial(behind_kernel, geo, scale),
        [sds((geo.sp, geo.sp), BF) for _ in geo.touching] + [sds(base.shape, F32)],
        [
            *[pltpu.VMEM((geo.sp, geo.windows[c].rows), BF) for c in geo.touching],
            table_scratch(geo),
            matrix_scratch(geo),
        ],
        cost=cost_of(1.0),
    )(sent, matrix, base, own_up)
    return uppers, base


def first_finish_kernel(geo, scale, *refs):
    n = len(geo.touching)
    base_ref, up_ref = refs[:2]
    crosses, reaches = refs[2 : 2 + n], refs[2 + n : 2 + 2 * n]
    y_ref, near_out, far_out = refs[2 + 2 * n :]
    y_ref[...] = base_ref[...]
    add_upper(geo, scale, y_ref, up_ref[...], crosses)
    write_sends(geo, y_ref, reaches, near_out, far_out)


def first_finish(geo, scale, base, h_up, crosses, reaches):
    y, near, far = vmem_call(
        functools.partial(first_finish_kernel, geo, scale),
        [sds(base.shape, F32), *send_shapes(geo, base.shape[1])],
        cost=cost_of(0.5),
    )(base, h_up, *crosses, *reaches)
    return y, (near, far)


def finish_kernel(geo, scale, mode, part_rows, *refs):
    refs = list(refs)
    n = len(geo.touching)
    base_ref, near_ref, far_ref = refs[:3]
    refs = refs[3:]
    crosses, refs = refs[:n], refs[n:]
    halo = (near_ref, far_ref, crosses)
    if mode == "last":
        finish_last(geo, scale, base_ref, halo, *refs)
        return
    reaches, refs = refs[:n], refs[n:]
    if mode == "density":
        occ_ref, table_ref = refs.pop(0), refs.pop(0)
    y_ref = refs.pop(0)
    if mode == "density":
        _, _, out_hbm, dens, sems = refs
        spans = [pl.ds(geo.own, part_rows * LANES), pl.ds(0, geo.own)]
        copies = [
            pltpu.make_async_copy(dens.at[:, :, span], out_hbm.at[:, :, span], sems.at[i])
            for i, span in enumerate(spans)
        ]
        write_tables(geo.own, table_ref, part_rows, dens)
        copies[0].start()
    y_ref[...] = base_ref[...]
    add_halo(geo, scale, y_ref, *halo)
    if mode == "density":
        write_density(y_ref, occ_ref, dens)
        copies[1].start()
    write_sends(geo, y_ref, reaches, refs[0], refs[1])
    if mode == "density":
        for copy in copies:
            copy.wait()


def finish_last(geo, scale, base_ref, halo, *refs):
    extras = (len(refs) - 3) // 2
    sources, out_hbm, targets = refs[:extras], refs[extras], refs[extras + 1 : -2]
    y_ref, sems = refs[-2:]
    top = max(geo.sp, geo.low)
    inner = pl.ds(top, geo.dn_lo - top)
    copies = fetch([(base_ref.at[inner], out_hbm.at[inner]), *zip(sources, targets)], sems)
    edges = [(0, top), (geo.dn_lo, geo.own)]
    for a, b in edges:
        y_ref[a:b, :] = base_ref[a:b, :]
    add_halo(geo, scale, y_ref, *halo)
    for i, (a, b) in enumerate(edges):
        edge = pl.ds(a, b - a)
        copy = pltpu.make_async_copy(y_ref.at[edge], out_hbm.at[edge], sems.at[1 + extras + i])
        copy.start()
        copies.append(copy)
    for copy in copies:
        copy.wait()


def finish(geo, scale, base, halo, crosses, reaches=(), density=None, last=None):
    columns = base.shape[1]
    args = [base, halo[0], halo[1], *crosses, *reaches]
    mode, part_rows = "plain", 0
    shapes = [sds(base.shape, F32)]
    scratch = []
    vmem, hbm = pl.BlockSpec(memory_space=pltpu.VMEM), pl.BlockSpec(memory_space=pltpu.HBM)
    out_specs = [vmem, vmem, vmem]
    if last is not None:
        mode = "last"
        args += last
        shapes += [sds(a.shape, a.dtype) for a in last]
        out_specs = [hbm] * len(shapes)
        scratch = [pltpu.VMEM(base.shape, F32), pltpu.SemaphoreType.DMA((3 + len(last),))]
    else:
        shapes += send_shapes(geo, columns)
    if density is not None:
        mode = "density"
        fg, weights, table = density
        part_rows = fg.part_rows
        args += [weights, table]
        spread = (fg.bands * fg.domains, 1, fg.width)
        shapes.append(sds(spread, F32))
        out_specs.append(hbm)
        scratch = [pltpu.VMEM(spread, F32), pltpu.SemaphoreType.DMA((2,))]
    return vmem_call(
        functools.partial(finish_kernel, geo, scale, mode, part_rows),
        shapes,
        scratch,
        out_specs=out_specs,
        cost=cost_of(1.0),
    )(*args)


class FieldGeometry:
    def __init__(self, bands, domains, own, share, cells, npc):
        self.bands, self.domains, self.own, self.share = bands, domains, own, share
        self.cells, self.npc = cells, npc
        self.block = own // domains
        self.rows = up_to(npc, LANES) // LANES
        self.lines = own // LANES
        self.tiles = self.lines + 1
        nloc = own + share
        self.touched = []
        for c in range(cells):
            nodes = [(c * (nloc // cells) + k) % nloc for k in range(npc)]
            self.touched.append(sorted({node // LANES for node in nodes}))
        self.at_inverse = cells * self.rows
        self.at_face = self.at_inverse + cells * self.tiles
        self.at_screen = up_to(self.at_face + 2, 2) // 2
        self.part_rows = -(-(self.at_screen + self.lines) // bands)
        self.table_rows = up_to(self.part_rows * bands, SUBLANES)
        self.width = own + self.part_rows * LANES
        self.size = self.rows * LANES
        self.at_owner_lane = LANES - domains
        self.fits = (
            domains == SUBLANES
            and own % (domains * SUBLANES) == 0
            and own % LANES == 0
            and self.block <= LANES
            and share <= self.at_owner_lane
            and max(npc, nloc) < CODE_BASE - 1
        )


CODE_BASE = 2048
CODE_BITS = 11


def pieces(length, blocks):
    found = []
    for j in range(blocks):
        done = 0
        while done < length:
            at = j * length + done
            count = min(length - done, LANES - at % LANES)
            found.append((at // LANES, at % LANES, j, done, count))
            done += count
    return found


def column_of(row):
    return jnp.broadcast_to(row, (LANES, LANES)).T


def inverse_row(columns, first):
    sub = lax.broadcasted_iota(I32, (LANES, LANES), 0)
    target = (lax.broadcasted_iota(I32, (LANES, LANES), 1) + first).astype(F32)
    found = jnp.zeros((LANES, LANES), F32)
    for r, column in enumerate(columns):
        found = jnp.where(column == target, (sub + (r * LANES + 1)).astype(F32), found)
    return jnp.sum(found, axis=0, keepdims=True) - 1.0


def field_tables_kernel(fg, *refs):
    nodes_ref, face_ref, owner_ref, screen_ref = refs[:4]
    table_ref, pad, one, spare, packed = refs[5:]
    one[...] = jnp.full(one.shape, -1.0, F32)
    spare[...] = jnp.full(spare.shape, -1.0, F32)
    pad[...] = jnp.full(pad.shape, -1, I32)
    pad[0 : fg.cells, 0 : fg.npc] = nodes_ref[...]
    for c in range(fg.cells):
        columns = []
        for r in range(fg.rows):
            code = pad[c : c + 1, r * LANES : (r + 1) * LANES].astype(F32)
            one[c * fg.rows + r : c * fg.rows + r + 1, :] = code
            columns.append(column_of(code))
        for t in fg.touched[c]:
            at = fg.at_inverse + c * fg.tiles + t
            one[at : at + 1, :] = inverse_row(columns, t * LANES)
    lane = fg.at_owner_lane
    spare[0:1, 0 : fg.share] = face_ref[...].astype(F32)
    spare[1:2, 0 : fg.domains] = owner_ref[...].astype(F32)
    at = fg.at_face
    one[at : at + 1, :] = spare[0:1, :]
    one[at : at + 1, lane:LANES] = owner_ref[...].astype(F32)
    back = inverse_row([column_of(spare[0:1, :])], 0)
    home = inverse_row([column_of(spare[1:2, :])], -lane)
    lanes = lax.broadcasted_iota(I32, (1, LANES), 1)
    one[at + 1 : at + 2, :] = jnp.where(lanes < lane, back, home)
    packed[...] = jnp.zeros(packed.shape, F32)
    half = fg.at_screen
    packed[0:half, :] = (one[0:half, :] + 1.0) + (one[half : 2 * half, :] + 1.0) * CODE_BASE
    packed[half : half + fg.lines, :] = screen_ref[...]
    for b in range(fg.bands):
        table_ref[b, 0 : fg.part_rows, :] = packed[b * fg.part_rows : (b + 1) * fg.part_rows, :]


def field_tables(fg, pois_nodes, pois_face, block_owner, lines, after):
    specs = [pl.BlockSpec(memory_space=pltpu.VMEM)] * 4 + [pl.BlockSpec(memory_space=pl.ANY)]
    return vmem_call(
        functools.partial(field_tables_kernel, fg),
        sds((fg.bands, up_to(fg.part_rows, SUBLANES), LANES), F32),
        [
            pltpu.VMEM((up_to(fg.cells, SUBLANES), fg.size), I32),
            pltpu.VMEM((up_to(2 * fg.at_screen, SUBLANES), LANES), F32),
            pltpu.VMEM((SUBLANES, LANES), F32),
            pltpu.VMEM((fg.table_rows, LANES), F32),
        ],
        in_specs=specs,
        cost=cost_of(1.0),
    )(pois_nodes, pois_face, block_owner, lines, after)


def lanes_of(values, index):
    return jnp.take_along_axis(values, index, axis=1, mode="promise_in_bounds")


def got_tile(fg, got_ref, band, line):
    lines = fg.width // LANES
    return got_ref[pl.ds(band * fg.domains * lines + line, fg.domains, stride=lines), :]


def decode(fg, got_ref, codes):
    domains, half = fg.domains, fg.at_screen

    def tile(at):
        return got_tile(fg, got_ref, at // fg.part_rows, fg.lines + at % fg.part_rows)

    for at in range(half):
        both = tile(at).astype(I32)
        codes[at] = jnp.bitwise_and(both, CODE_BASE - 1) - 1
        codes[half + at] = jnp.right_shift(both, CODE_BITS) - 1
    screens = [tile(half + g) for g in range(fg.lines)]
    lane = lax.broadcasted_iota(I32, (domains, LANES), 1)
    first, last = fg.at_owner_lane, LANES
    owners = codes[fg.at_face].astype(F32).T[first:last, :]
    inverse = codes[fg.at_face + 1].astype(F32).T[first:last, :]
    back = jnp.where(lane < fg.share, codes[fg.at_face + 1], -1)
    codes[fg.at_face + 1] = pltpu.roll(back, 1, 0)
    places = []
    for q in range(domains):
        block = jnp.broadcast_to(inverse[:, q : q + 1], (domains, LANES)).astype(I32)
        places.append(block * fg.block + lane)
    here = lax.axis_index("domain")
    narrow = lax.broadcasted_iota(I32, (domains, domains), 1)
    mine = jnp.sum(jnp.where(narrow == here, owners, 0.0), axis=1, keepdims=True)
    return places, jnp.broadcast_to(mine, (domains, LANES)).astype(I32), screens


def rows_of(values, index):
    return jnp.take_along_axis(values, index, axis=0, mode="promise_in_bounds")


def lookup(sources, code):
    lane = jnp.bitwise_and(code, LANES - 1)
    which = jnp.right_shift(code, 7)
    total = jnp.zeros(code.shape, F32)
    for b, values in sources:
        total = jnp.where(which == b, lanes_of(values, lane), total)
    return total


def field_source(fg, got_ref, places):
    domains = fg.domains
    density = []
    for g in range(fg.lines):
        total = got_tile(fg, got_ref, 0, g)
        for b in range(1, fg.bands):
            total = total + got_tile(fg, got_ref, b, g)
        density.append(total)
    lane = lax.broadcasted_iota(I32, (domains, LANES), 1)
    source = [None] * fg.lines
    for q in range(domains):
        spread = [jnp.broadcast_to(d[q : q + 1, :], (domains, LANES)) for d in density]
        block = lookup(list(enumerate(spread)), places[q])
        for row, start, j, offset, count in pieces(fg.block, domains):
            if j == q:
                moved = pltpu.roll(block, (start - offset) % LANES, 1)
                inside = (lane >= start) & (lane < start + count)
                before = 0.0 if source[row] is None else source[row]
                source[row] = jnp.where(inside, moved, before)
    return source


def field_solve(fg, source, codes, screen, high_ref, low_ref, rows, copies):
    domains, cells = fg.domains, fg.cells

    def operator(field):
        ahead = pltpu.roll(field[0], domains - 1, 0)
        local = list(field) + [lookup([(0, ahead)], codes[fg.at_face])]
        for r in range(fg.rows):
            for c in range(cells):
                sources = [(t, local[t]) for t in fg.touched[c]]
                rows[c * domains : (c + 1) * domains, r * LANES : (r + 1) * LANES] = lookup(sources, codes[c * fg.rows + r])
        picked = rows[:, 0 : fg.npc]
        high = picked.astype(BF)
        low = (picked - high.astype(F32)).astype(BF)
        both = dot(jnp.concatenate([high, low], axis=0), high_ref[...])
        half_rows = cells * domains
        if copies:
            copies.pop().wait()
        rows[:, 0 : fg.npc] = both[:half_rows] + (both[half_rows:] + dot(high, low_ref[...]))
        out = [None] * fg.tiles
        for c in range(cells):
            sources = [
                (r, rows[c * domains : (c + 1) * domains, r * LANES : (r + 1) * LANES])
                for r in range(fg.rows)
            ]
            for t in fg.touched[c]:
                term = lookup(sources, codes[fg.at_inverse + c * fg.tiles + t])
                out[t] = term if out[t] is None else out[t] + term
        arriving = pltpu.roll(out[fg.lines], 1, 0)
        out[0] = out[0] + lookup([(0, arriving)], codes[fg.at_face + 1])
        return [screen[g] * field[g] + out[g] for g in range(fg.lines)]

    step_one = [s * (1.0 / solve_center) for s in source]
    applied = operator(step_one)
    residual = [s - a for s, a in zip(source, applied)]
    a1, b1 = weight_one * weight_zero, 2.0 * weight_one / solve_half
    step_two = [a1 * e + b1 * r for e, r in zip(step_one, residual)]
    applied = operator(step_two)
    residual = [r - a for r, a in zip(residual, applied)]
    a2, b2 = weight_two * weight_one, 2.0 * weight_two / solve_half
    step_three = [a2 * e + b2 * r for e, r in zip(step_two, residual)]
    return [(x + y) + z for x, y, z in zip(step_one, step_two, step_three)]


def field_parts_kernel(fg, matrix_hbm, after_ref, top_ref, low_ref, matrix_ref, sems):
    del after_ref
    spans = [pl.ds(r * LANES, min(LANES, fg.npc - r * LANES)) for r in range(fg.rows)]
    copies = fetch([(matrix_hbm.at[span], matrix_ref.at[span]) for span in spans], sems)
    for r, copy in enumerate(copies):
        copy.wait()
        span = slice(r * LANES, min((r + 1) * LANES, fg.npc))
        full = matrix_ref[span, :]
        top = full.astype(BF)
        top_ref[span, :] = top
        low_ref[span, :] = (full - top.astype(F32)).astype(BF)


def field_parts(fg, matrix, after):
    hbm = pl.BlockSpec(memory_space=pltpu.HBM)
    return vmem_call(
        functools.partial(field_parts_kernel, fg),
        [sds(matrix.shape, BF), sds(matrix.shape, BF)],
        [
            pltpu.VMEM(matrix.shape, F32),
            pltpu.SemaphoreType.DMA((fg.rows,)),
        ],
        in_specs=[hbm, pl.BlockSpec(memory_space=pl.ANY)],
        cost=cost_of(2.5),
    )(*in_hbm(matrix), after)


def field_kernel(geo, fg, scale, got_ref, low_hbm, high_ref, base_ref, near_ref, far_ref, y_ref, *refs):
    n = len(geo.touching)
    crosses, reaches, refs = refs[:n], refs[n : 2 * n], refs[2 * n :]
    z_ref, near_out, far_out, column_ref, hartree_ref = refs[:5]
    codes, rows, mine, low_ref, sems = refs[5:]
    copies = fetch([(low_hbm, low_ref)], sems)
    z_ref[...] = base_ref[...]
    add_halo(geo, scale, z_ref, near_ref, far_ref, crosses)
    places, owner, screens = decode(fg, got_ref, codes)
    source = field_source(fg, got_ref, places)
    solved = field_solve(fg, source, codes, screens, high_ref, low_ref, rows, copies)
    lane = lax.broadcasted_iota(I32, (fg.domains, LANES), 1)
    block = lookup(list(enumerate(solved)), lane + lax.axis_index("domain") * fg.block)
    mine[...] = rows_of(block, owner)
    for j in range(fg.domains):
        at = slice(j * fg.block, (j + 1) * fg.block)
        column = column_of(mine[j : j + 1, :])[0 : fg.block, :]
        column_ref[at, :] = column
        z_ref[at, :] += (column * scale) * y_ref[at, :]
    write_sends(geo, z_ref, reaches, near_out, far_out)
    for row, start, j, offset, count in pieces(fg.block, fg.domains):
        hartree_ref[row : row + 1, start : start + count] = mine[j : j + 1, offset : offset + count]


def field_step(geo, fg, scale, got, top, rest, base, halo, y, crosses, reaches):
    tile = (fg.domains, LANES)
    vmem = pl.BlockSpec(memory_space=pltpu.VMEM)
    got = got.reshape(got.shape[0] * fg.width // LANES, LANES)
    args = [got, *in_hbm(rest), top, base, *halo, y, *crosses, *reaches]
    specs = [vmem] * len(args)
    specs[1] = pl.BlockSpec(memory_space=pltpu.HBM)
    z, near, far, column, lines = vmem_call(
        functools.partial(field_kernel, geo, fg, scale),
        [
            sds(y.shape, F32),
            *send_shapes(geo, y.shape[1]),
            sds((fg.own, LANES), F32),
            sds((fg.lines, LANES), F32),
        ],
        [
            pltpu.VMEM((2 * fg.at_screen, *tile), I32),
            pltpu.VMEM((fg.cells * fg.domains, fg.size), F32),
            pltpu.VMEM(tile, F32),
            pltpu.VMEM(rest.shape, BF),
            pltpu.SemaphoreType.DMA((1,)),
        ],
        in_specs=specs,
        cost=cost_of(4.0),
    )(*args)
    return z, (near, far), column, lines


def assembled(owned_rows, face_row, terms):
    owned_count = owned_rows.shape[0]
    shared = face_row.shape[0]
    coming = jnp.take(from_behind(owned_rows[:shared], "domain", -1), face_row, axis=0)
    partial_value = terms(jnp.concatenate([owned_rows, coming], axis=0))
    upper_rows = partial_value[owned_count:]
    ordered = jnp.zeros_like(upper_rows).at[face_row].set(upper_rows)
    arrived = from_behind(ordered, "domain", 1)
    return partial_value[:owned_count].at[:shared].add(arrived)


def field_terms(local_rows, pois_matrix, node_ids):
    cell_vals = jnp.take(local_rows, node_ids, axis=0)
    product = jnp.einsum(
        "pq,cq->cp",
        pois_matrix,
        cell_vals,
        precision=lax.Precision.HIGHEST,
        preferred_element_type=F32,
    )
    return jnp.zeros(local_rows.shape, F32).at[node_ids.reshape(-1)].add(product.reshape(-1))


def reshuffle(blocks):
    return lax.all_to_all(blocks, "domain", split_axis=0, concat_axis=0, tiled=True)


def distributed_field(y, occupation, owner_row, pois_matrix, pois_nodes, field_face, screening):
    owned_count = y.shape[0]
    domains = lax.axis_size("domain")
    block_len = owned_count // domains
    partial_value = jnp.dot(
        y * y, occupation, precision=lax.Precision.HIGHEST, preferred_element_type=F32
    )
    summed = lax.psum(partial_value, "band")
    arranged = (
        jnp.zeros((domains, block_len), F32)
        .at[owner_row]
        .set(summed.reshape(domains, block_len))
    )
    source = reshuffle(arranged).reshape(owned_count)

    def field_operator(vector):
        return (
            assembled(
                vector, field_face, lambda local: field_terms(local, pois_matrix, pois_nodes)
            )
            + screening * vector
        )

    step_one = source / solve_center
    residual = source - field_operator(step_one)
    step_two = weight_one * weight_zero * step_one + 2.0 * weight_one / solve_half * residual
    residual = residual - field_operator(step_two)
    step_three = weight_two * weight_one * step_two + 2.0 * weight_two / solve_half * residual
    solved = step_one + step_two + step_three
    returned = reshuffle(solved.reshape(domains, block_len))
    return jnp.take(returned, owner_row, axis=0).reshape(owned_count)


def exchange(sends):
    dn, up = sends
    h_dn = from_behind(dn, "domain", 1)
    h_up = from_behind(up, "domain", -1)
    return h_up, h_dn


def on_device(
    orbitals,
    potential,
    occupation,
    cell_matrix,
    cell_nodes,
    face_order,
    pois_matrix,
    pois_nodes,
    pois_face,
    screening,
    block_owner,
):
    domains = lax.axis_size("domain")
    bands = lax.axis_size("band")
    own, columns = orbitals.shape
    geo = Geometry(own, face_order.shape[1], cell_nodes.shape[0], cell_nodes.shape[1])
    fg = FieldGeometry(bands, domains, own, pois_face.shape[1], pois_nodes.shape[0], pois_nodes.shape[1])
    first, later = 1.0 / filter_half, 2.0 / filter_half

    others = [cell_matrix, potential.reshape(own // LANES, LANES)]
    if fg.fits:
        others += [pois_nodes, pois_face, block_owner, screening.reshape(own // LANES, LANES)]
        others.append(occupation.reshape(1, columns))
    sends, y0, nodes, (matrix, lines, *others) = pack(geo, orbitals, cell_nodes, face_order, *others)
    halo = exchange(sends)
    mats, crosses, reaches, pot = own_matrices(geo, nodes, matrix, lines)
    base = owned_part(geo, first, y0, None, pot, None, mats, ())
    uppers, base = behind_sums(geo, first, halo[1], matrix, base, sends[1])
    y1, sends1 = first_finish(geo, first, base, halo[0], crosses, reaches)

    halo = swap(sends1)
    base = owned_part(geo, later, y1, y0, pot, None, mats, uppers)
    if fg.fits:
        *others, weights = others
        table = field_tables(fg, *others, base)
    y2, *sends2 = finish(geo, later, base, halo, crosses, reaches)

    halo = swap(sends2)
    base = owned_part(geo, later, y2, y1, pot, None, mats, uppers)
    if fg.fits:
        y3, dn, up, spread = finish(
            geo, later, base, halo, crosses, reaches, density=(fg, weights, table)
        )
        dens = lax.all_to_all(spread, ("band", "domain"), 0, 0, tiled=True)
        halo = swap((dn, up))
        base = owned_part(geo, first, y3, None, pot, None, mats, uppers)
        top, rest = field_parts(fg, pois_matrix, base)
        z1, sends4, column, packed = field_step(
            geo, fg, first, dens, top, rest, base, halo, y3, crosses, reaches
        )
    else:
        y3, *sends3 = finish(geo, later, base, halo, crosses, reaches)
        halo = swap(sends3)
        hartree = distributed_field(
            y3, occupation, block_owner[0], pois_matrix, pois_nodes, pois_face[0], screening
        )
        column = jnp.broadcast_to(hartree[:, None], (own, LANES))
        base = owned_part(geo, first, y3, None, pot, column, mats, uppers)
        z1, *sends4 = finish(geo, first, base, halo, crosses, reaches)

    halo = swap(sends4)
    base = owned_part(geo, later, z1, y3, pot, column, mats, uppers, far=fg.fits)
    last = [packed] if fg.fits else []
    filtered, *rest = finish(geo, later, base, halo, crosses, last=last)
    if fg.fits:
        hartree = rest[0].reshape(own)
    return filtered, hartree


def swap(sends):
    length = lax.axis_size("domain")
    near, far = sends
    turns = [(i, (i + 1) % length if i % 2 else (i - 1) % length) for i in range(length)]
    far = lax.ppermute(far, "domain", turns)
    near = lax.ppermute(near, "domain", [(i, i ^ 1) for i in range(length)])
    return near, far


def solution(mesh):
    return jax.shard_map(
        on_device,
        mesh=mesh,
        in_specs=(
            P("domain", "band"),
            P("domain"),
            P("band"),
            P(),
            P("domain", None),
            P("domain", None),
            P(),
            P("domain", None),
            P("domain", None),
            P("domain"),
            P("domain", None),
        ),
        out_specs=(P("domain", "band"), P("domain")),
        check_vma=False,
    )
```
